32 devices in a mesh: dp: 4 (over y, x), ctx: 8 (over z, core).
Axes of the slice: x: 2, y: 2, z: 4, core: 2. Of those that a mesh axis runs over, the one named last changes fastest.
Arguments:
- block_input: bfloat16 [4, 1024, 1024], P('dp', 'ctx'), may hold values from -6 to 6
- segment_ids: int32 [4, 1024], P('dp', 'ctx'), may hold values from 0 to 3, never falling along the last dimension, each value on 1 to 512 neighbouring positions
- out_cotangent: bfloat16 [4, 1024, 1024], P('dp', 'ctx'), may hold values from -6 to 6
- attention_in: bfloat16 [1024, 768], P(('dp', 'ctx')), may hold values from -0.1875 to 0.1875
- mixer_in: bfloat16 [1024, 3328], P(('dp', 'ctx')), may hold values from -0.1875 to 0.1875
- step_in: bfloat16 [1024, 24], P(('dp', 'ctx')), may hold values from -0.1875 to 0.1875
- attention_out: bfloat16 [512, 1024], P(('dp', 'ctx')), may hold values from -2 to 2
- mixer_out: bfloat16 [1536, 1024], P(('dp', 'ctx')), may hold values from -0.3125 to 0.3125
- gate_up: bfloat16 [1024, 4096], P(('dp', 'ctx')), may hold values from -0.1875 to 0.1875
- down_weight: bfloat16 [2048, 1024], P(('dp', 'ctx')), may hold values from -0.125 to 0.125
- gain_mixing: float32 [1024], replicated, may hold values from 0.5 to 1.5
- gain_feed: float32 [1024], replicated, may hold values from 0.5 to 1.5
- decay_log: float32 [24], replicated, may hold values from 0 to 2.77
- step_bias: float32 [24], replicated, may hold values from -6.9 to -2.25
- skip_gain: float32 [24], replicated, may hold values from 0.5 to 2
- conv_weight: float32 [4, 1792], replicated, may hold values from -2 to 2
- conv_bias: float32 [1792], replicated, may hold values from -0.5 to 0.5
Outputs:
- output: bfloat16 [4, 1024, 1024], P('dp', 'ctx')
- input_grad: float32 [4, 1024, 1024], P('dp', 'ctx')
- grad_attention_in: float32 [1024, 768], P(('dp', 'ctx'))
- grad_mixer_in: float32 [1024, 3328], P(('dp', 'ctx'))
- grad_step_in: float32 [1024, 24], P(('dp', 'ctx'))
- grad_attention_out: float32 [512, 1024], P(('dp', 'ctx'))
- grad_mixer_out: float32 [1536, 1024], P(('dp', 'ctx'))
- grad_gate_up: float32 [1024, 4096], P(('dp', 'ctx'))
- grad_down_weight: float32 [2048, 1024], P(('dp', 'ctx'))
- grad_gain_mixing: float32 [1024], replicated
- grad_gain_feed: float32 [1024], replicated
- grad_decay_log: float32 [24], replicated
- grad_step_bias: float32 [24], replicated
- grad_skip_gain: float32 [24], replicated
- grad_conv_weight: float32 [4, 1792], replicated
- grad_conv_bias: float32 [1792], replicated
The draws below stay inside these ranges and needn't reach their ends.
Inputs may be any that keep to these rules, and one draw needn't show every extreme that they name: `segment_ids`: segment ids never fall along a sequence; each document holds 1 to 512 tokens and one holds exactly 512.
All inputs are finite; a program needn't handle non-finite values.
Results may differ from the reference program's by a relative error of at most 0.013.
Values may be sent and summed in bfloat16 or wider, within the bound.
A program may use at most 192 MiB of HBM per device.

```python
import math
import jax
import jax.numpy as jnp
import numpy as np
from jax import lax

D = 1024
FF = 2048
HEADS_Q = 8
HEADS_KV = 2
HEAD = 64
SSM_HEADS = 24
SSM_HEAD = 64
STATE = 128
TOK = 128
SSM_INNER = 1536
CONV_WIDTH = 1792
LENGTH = 1024
NSEQ = 4
DOCS = 4
DOC_MOST = 512


def raised(values, key, source, target, parts, factor):
    def block_of(position):
        return (jnp.arange(values.shape[position]) // (values.shape[position] // parts)).reshape((-1,) + (1,) * (values.ndim - 1 - position))

    one_side = jax.random.permutation(key, parts)[block_of(target)]
    other_side = (block_of(target) + parts // 2) % parts
    return jnp.where((block_of(source) == one_side) | (block_of(source) == other_side), factor * values, values)


def block_scale(own_key, extent, cuts, smallest, largest):
    loudness = 1.0
    for axis_at, parts in cuts:
        steps = jax.random.uniform(jax.random.fold_in(jax.random.fold_in(own_key, 6), axis_at), (parts,), jnp.float32, smallest / len(cuts), largest / len(cuts))
        loudness = loudness * jnp.repeat(jnp.exp(steps), extent[axis_at] // parts).reshape((-1,) + (1,) * (len(extent) - 1 - axis_at))
    return loudness


def split_up(amount, total, reach, skew):
    weights = [(1 << 20) // math.isqrt(rank ** skew) + 1 for rank in range(2, amount + 1)]
    spare, counts = total - reach - (amount - 1), [1] * (amount - 1)
    while spare > 0:
        free = [i for i in range(amount - 1) if counts[i] < reach]
        mass, budget = sum([weights[i] for i in free]), spare
        for i in free:
            extra = min(reach - counts[i], max(1, budget * weights[i] // mass), spare)
            counts[i] = counts[i] + extra
            spare = spare - extra
    return np.array([reach] + counts)


def uneven_parts(key, number_of, total, most, skew):
    if number_of == 2:
        one = jax.random.randint(key, (), max(1, total - most), min(most, total - 1) + 1)
        return jnp.stack([one, total - one])
    lengths = jnp.asarray(split_up(number_of, total, most, skew), jnp.int32)
    couples = (number_of - 1) // 2
    donor, taker = lengths[1:1 + 2 * couples:2], lengths[2:2 + 2 * couples:2]
    slack = jnp.minimum(donor - 1, most - taker)
    passed = jax.random.randint(jax.random.fold_in(key, 1), (couples,), 0, 1 << 20) % (slack + 1)
    lengths = lengths.at[1:1 + 2 * couples:2].set(donor - passed).at[2:2 + 2 * couples:2].set(taker + passed)
    return lengths[jax.random.permutation(jax.random.fold_in(key, 2), number_of)]


def centred(stream_key, extent, deviation, reach, pieces=(), held_as=jnp.bfloat16):
    drawn = deviation * jax.random.normal(stream_key, extent, jnp.float32)
    if pieces:
        drawn = drawn * block_scale(stream_key, extent, pieces, -0.22, 0.18)
    return jnp.clip(drawn, -reach, reach).astype(held_as)


def gaussian_with(own_key, dims, scale, reach, shards, heavy, held_as=jnp.bfloat16):
    entries = scale * jax.random.normal(own_key, dims, jnp.float32)
    if shards:
        entries = entries * block_scale(own_key, dims, shards, -0.22, 0.18)
    return jnp.clip(raised(entries, jax.random.fold_in(own_key, 3), *heavy), -reach, reach).astype(held_as)


def setup_inputs(seed: int = 0) -> dict:
    streams_of = jax.random.split(jax.random.key(seed), 18)
    return {
        "block_input": gaussian_with(streams_of[0], (NSEQ, LENGTH, D), 1.0, 6.0, ((0, 4), (1, 8)), (1, 2, 8, 2.0)),
        "segment_ids": jax.vmap(lambda own: jnp.searchsorted(jnp.cumsum(uneven_parts(own, DOCS, LENGTH, DOC_MOST, 2)), jnp.arange(LENGTH), side="right"))(jax.random.split(streams_of[1], NSEQ)).reshape((NSEQ, LENGTH)).astype(jnp.int32),
        "out_cotangent": centred(streams_of[2], (NSEQ, LENGTH, D), 1.0, 6.0, ((0, 4), (1, 8))),
        "attention_in": centred(streams_of[3], (D, HEADS_Q * HEAD + 2 * HEADS_KV * HEAD), D ** -0.5, 0.1875, ((0, 32),)),
        "mixer_in": centred(streams_of[4], (D, 2 * SSM_INNER + 2 * STATE), D ** -0.5, 0.1875, ((0, 32),)),
        "step_in": centred(streams_of[5], (D, SSM_HEADS), D ** -0.5, 0.1875, ((0, 32),)),
        "attention_out": centred(streams_of[6], (HEADS_Q * HEAD, D), 8 ** -0.5, 2.0, ((0, 32),)),
        "mixer_out": centred(streams_of[7], (SSM_INNER, D), (SSM_INNER // 4) ** -0.5, 0.3125, ((0, 32),)),
        "gate_up": centred(streams_of[8], (D, 2 * FF), D ** -0.5, 0.1875, ((0, 32),)),
        "down_weight": centred(streams_of[9], (FF, D), FF ** -0.5, 0.125, ((0, 32),)),
        "gain_mixing": jnp.clip(1.0 + 0.1 * jax.random.normal(streams_of[10], (D,), jnp.float32), 0.5, 1.5),
        "gain_feed": jnp.clip(1.0 + 0.1 * jax.random.normal(streams_of[11], (D,), jnp.float32), 0.5, 1.5),
        "decay_log": jnp.clip(jax.random.uniform(streams_of[12], (SSM_HEADS,), jnp.float32, 0.0, 2.77), 0.0, 2.77),
        "step_bias": jnp.clip(jax.random.uniform(streams_of[13], (SSM_HEADS,), jnp.float32, -6.9, -2.25), -6.9, -2.25),
        "skip_gain": jnp.clip(jax.random.uniform(streams_of[14], (SSM_HEADS,), jnp.float32, 0.5, 2.0), 0.5, 2.0),
        "conv_weight": centred(streams_of[15], (4, CONV_WIDTH), 0.5, 2.0, (), jnp.float32),
        "conv_bias": jnp.clip(jax.random.uniform(streams_of[16], (CONV_WIDTH,), jnp.float32, -0.5, 0.5), -0.5, 0.5),
    }


highest = lax.Precision.HIGHEST

def rms_scale(values, gain):
    return values * lax.rsqrt(lax.optimization_barrier(jnp.mean(values * values, axis=-1, keepdims=True)) + 1e-05) * gain

def silu_slope(values):
    sigma = jax.nn.sigmoid(values)
    return sigma * (1.0 + values * (1.0 - sigma))

def conv_rows(rows, conv_weight, conv_bias, segments):
    width = rows.shape[1]
    pre = conv_bias + conv_weight[3] * rows
    for offset in (1, 2, 3):
        shifted = jnp.concatenate([jnp.zeros((offset, width), rows.dtype), rows[:-offset]], axis=0)
        keep_mask = jnp.concatenate([jnp.zeros((offset,), bool), segments[offset:] == segments[:-offset]])
        pre = pre + jnp.where(keep_mask[:, None], shifted, 0.0) * conv_weight[3 - offset]
    return jax.nn.silu(pre)

def ssd_local(inner, write_map, read_map, step_raw, decay_log, step_bias, skip_gain, starts, segments):
    step = jax.nn.softplus(step_raw + step_bias)
    rates = step * -jnp.exp(decay_log)
    running = jnp.cumsum(rates, axis=0)
    places = jnp.arange(segments.shape[0])
    same = (segments[:, None] == segments[None, :]) & (places[None, :] <= places[:, None])
    spans = jnp.where(same[None], running.T[:, :, None] - running.T[:, None, :], -1e+30)
    intersection = jnp.dot(read_map, write_map.T, precision=highest)
    mixing = jnp.exp(spans) * intersection[None] * step.T[:, None, :]
    result = jnp.einsum('hts,shp->thp', mixing, inner, precision=highest) + skip_gain[None, :, None] * inner
    before = jnp.cumsum(starts.astype(jnp.int32)) == 0
    carried = jnp.where(before[:, None], jnp.exp(running), 0.0)
    tails = jnp.where((segments == segments[-1])[:, None], jnp.exp(running[-1][None, :] - running), 0.0)
    state = jnp.einsum('sh,shp,sn->hpn', tails * step, inner, write_map, precision=highest)
    return (result, state, carried[-1], carried)

def add_state(result, carried, read_map, state_in):
    return result + carried[:, :, None] * jnp.einsum('hpn,tn->thp', state_in, read_map, precision=highest)

def ssd_block(inner, write_map, read_map, step_raw, decay_log, step_bias, skip_gain, starts, segments, state_in):
    result, state, decay_total, carried = ssd_local(inner, write_map, read_map, step_raw, decay_log, step_bias, skip_gain, starts, segments)
    return (add_state(result, carried, read_map, state_in), decay_total[:, None, None] * state_in + state)

def ssd_sequence(inner, write_map, read_map, step_raw, decay_log, step_bias, skip_gain, starts, segments):
    count = inner.shape[0] // TOK

    def shaped(array):
        return array.reshape((count, TOK) + array.shape[1:])

    def advance(state, item):
        result, state = ssd_block(item[0], item[1], item[2], item[3], decay_log, step_bias, skip_gain, item[4], item[5], state)
        return (state, result)
    initial = jnp.zeros((inner.shape[1], inner.shape[2], write_map.shape[1]), jnp.float32)
    _, results = lax.scan(advance, initial, (shaped(inner), shaped(write_map), shaped(read_map), shaped(step_raw), shaped(starts), shaped(segments)))
    return results.reshape(inner.shape)

def head_forward(queries, keys, values, allowed):
    scores = jnp.dot(queries, keys.T, preferred_element_type=jnp.float32) * HEAD ** (-0.5)
    masked = jnp.where(allowed, scores, -1e+30)
    top = lax.optimization_barrier(jnp.max(masked, axis=1, keepdims=True))
    total = lax.optimization_barrier(jnp.sum(jnp.where(allowed, jnp.exp(masked - top), 0.0), axis=1, keepdims=True))
    log_total = top + jnp.log(total)
    probs = jnp.where(allowed, jnp.exp(scores - log_total), 0.0).astype(jnp.bfloat16)
    return (jnp.dot(probs, values, preferred_element_type=jnp.float32).astype(jnp.bfloat16), log_total)

def head_backward(queries, keys, values, log_total, attended, attended_grad, allowed):
    scores = jnp.dot(queries, keys.T, preferred_element_type=jnp.float32) * HEAD ** (-0.5)
    probs = jnp.where(allowed, jnp.exp(scores - log_total), 0.0)
    deltas = lax.optimization_barrier(jnp.sum(attended_grad.astype(jnp.float32) * attended.astype(jnp.float32), axis=1, keepdims=True))
    value_grad = jnp.dot(probs.astype(jnp.bfloat16).T, attended_grad, preferred_element_type=jnp.float32)
    prob_grad = jnp.dot(attended_grad, values.T, preferred_element_type=jnp.float32)
    score_grad = (probs * (prob_grad - deltas)).astype(jnp.bfloat16)
    query_grad = jnp.dot(score_grad, keys, preferred_element_type=jnp.float32) * HEAD ** (-0.5)
    key_grad = jnp.dot(score_grad.T, queries, preferred_element_type=jnp.float32) * HEAD ** (-0.5)
    return (query_grad, key_grad, value_grad)

def one_sequence(sequence, segments, cotangent, weights, smalls):
    attention_in, mixer_in, step_in, attention_out, mixer_out, gate_up, down_weight = weights
    gain_mixing, gain_feed, decay_log, step_bias, skip_gain, conv_weight, conv_bias = smalls
    length = sequence.shape[0]
    query_width = HEADS_Q * HEAD
    key_width = HEADS_KV * HEAD
    groups = HEADS_Q // HEADS_KV
    places = jnp.arange(length)
    allowed = (places[None, :] <= places[:, None]) & (segments[None, :] == segments[:, None])
    starts = jnp.concatenate([jnp.ones((1,), bool), segments[1:] != segments[:-1]])
    source = sequence.astype(jnp.float32)
    normed = rms_scale(source, gain_mixing).astype(jnp.bfloat16)
    projected = jnp.dot(normed, attention_in, preferred_element_type=jnp.float32).astype(jnp.bfloat16)
    mixed_in = jnp.dot(normed, mixer_in, preferred_element_type=jnp.float32)
    step_raw = jnp.dot(normed, step_in, preferred_element_type=jnp.float32)
    gate_part = mixed_in[:, :SSM_INNER]
    conv_in = mixed_in[:, SSM_INNER:]

    def conv_map(rows_v, weight_v, bias_v):
        return conv_rows(rows_v, weight_v, bias_v, segments)
    converted, pull_conv = jax.vjp(conv_map, conv_in, conv_weight, conv_bias)
    inner = converted[:, :SSM_INNER].reshape(length, SSM_HEADS, SSM_HEAD)
    write_map = converted[:, SSM_INNER:SSM_INNER + STATE]
    read_map = converted[:, SSM_INNER + STATE:]

    def scan_map(inner_v, write_v, read_v, step_v, decay_v, bias_v, skip_v):
        return ssd_sequence(inner_v, write_v, read_v, step_v, decay_v, bias_v, skip_v, starts, segments)
    scanned, pull_scan = jax.vjp(scan_map, inner, write_map, read_map, step_raw, decay_log, step_bias, skip_gain)
    flat_scan = scanned.reshape(length, SSM_INNER)
    gated = (flat_scan * jax.nn.silu(gate_part)).astype(jnp.bfloat16)
    queries = projected[:, :query_width].reshape(length, HEADS_Q, HEAD).transpose(1, 0, 2)
    keys = jnp.repeat(projected[:, query_width:query_width + key_width].reshape(length, HEADS_KV, HEAD).transpose(1, 0, 2), groups, axis=0)
    values = jnp.repeat(projected[:, query_width + key_width:].reshape(length, HEADS_KV, HEAD).transpose(1, 0, 2), groups, axis=0)
    attended, log_totals = lax.map(lambda item: head_forward(item[0], item[1], item[2], allowed), (queries, keys, values))
    attended_flat = attended.transpose(1, 0, 2).reshape(length, query_width)
    residual = source + jnp.dot(attended_flat, attention_out, preferred_element_type=jnp.float32) + jnp.dot(gated, mixer_out, preferred_element_type=jnp.float32)
    normed_two = rms_scale(residual, gain_feed).astype(jnp.bfloat16)
    gate_values = jnp.dot(normed_two, gate_up, preferred_element_type=jnp.float32)
    gate_in = gate_values[:, :FF]
    up_in = gate_values[:, FF:]
    active = (jax.nn.silu(gate_in) * up_in).astype(jnp.bfloat16)
    output = (residual + jnp.dot(active, down_weight, preferred_element_type=jnp.float32)).astype(jnp.bfloat16)
    grad_down_weight = jnp.dot(active.T, cotangent, preferred_element_type=jnp.float32)
    active_grad = jnp.dot(cotangent, down_weight.T, preferred_element_type=jnp.float32)
    gate_grad = jnp.concatenate([active_grad * up_in * silu_slope(gate_in), active_grad * jax.nn.silu(gate_in)], axis=1).astype(jnp.bfloat16)
    grad_gate_up = jnp.dot(normed_two.T, gate_grad, preferred_element_type=jnp.float32)
    normed_two_grad = jnp.dot(gate_grad, gate_up.T, preferred_element_type=jnp.float32)
    _, pull_two = jax.vjp(rms_scale, residual, gain_feed)
    residual_part, grad_gain_feed = pull_two(normed_two_grad)
    residual_grad = cotangent.astype(jnp.float32) + residual_part
    residual_half = residual_grad.astype(jnp.bfloat16)
    grad_attention_out = jnp.dot(attended_flat.T, residual_half, preferred_element_type=jnp.float32)
    grad_mixer_out = jnp.dot(gated.T, residual_half, preferred_element_type=jnp.float32)
    attended_grad = jnp.dot(residual_half, attention_out.T, preferred_element_type=jnp.float32).astype(jnp.bfloat16)
    gated_grad = jnp.dot(residual_half, mixer_out.T, preferred_element_type=jnp.float32)
    gate_part_grad = gated_grad * flat_scan * silu_slope(gate_part)
    scan_grad = (gated_grad * jax.nn.silu(gate_part)).reshape(length, SSM_HEADS, SSM_HEAD)
    pulled = pull_scan(scan_grad)
    converted_grad = jnp.concatenate([pulled[0].reshape(length, SSM_INNER), pulled[1], pulled[2]], axis=1)
    conv_in_grad, grad_conv_weight, grad_conv_bias = pull_conv(converted_grad)
    mixer_grad = jnp.concatenate([gate_part_grad, conv_in_grad], axis=1).astype(jnp.bfloat16)
    step_grad_half = pulled[3].astype(jnp.bfloat16)
    grad_heads = attended_grad.reshape(length, HEADS_Q, HEAD).transpose(1, 0, 2)
    query_grad, key_grad, value_grad = lax.map(lambda item: head_backward(item[0], item[1], item[2], item[3], item[4], item[5], allowed), (queries, keys, values, log_totals, attended, grad_heads))
    query_grad = query_grad.transpose(1, 0, 2).reshape(length, query_width)
    key_grad = lax.optimization_barrier(jnp.sum(key_grad.reshape(HEADS_KV, groups, length, HEAD), axis=1)).transpose(1, 0, 2).reshape(length, key_width)
    value_grad = lax.optimization_barrier(jnp.sum(value_grad.reshape(HEADS_KV, groups, length, HEAD), axis=1)).transpose(1, 0, 2).reshape(length, key_width)
    projected_grad = jnp.concatenate([query_grad, key_grad, value_grad], axis=1).astype(jnp.bfloat16)
    grad_attention_in = jnp.dot(normed.T, projected_grad, preferred_element_type=jnp.float32)
    grad_mixer_in = jnp.dot(normed.T, mixer_grad, preferred_element_type=jnp.float32)
    grad_step_in = jnp.dot(normed.T, step_grad_half, preferred_element_type=jnp.float32)
    normed_grad = jnp.dot(projected_grad, attention_in.T, preferred_element_type=jnp.float32) + jnp.dot(mixer_grad, mixer_in.T, preferred_element_type=jnp.float32) + jnp.dot(step_grad_half, step_in.T, preferred_element_type=jnp.float32)
    _, pull_one = jax.vjp(rms_scale, source, gain_mixing)
    source_part, grad_gain_mixing = pull_one(normed_grad)
    input_grad = residual_grad + source_part
    grads = (grad_attention_in, grad_mixer_in, grad_step_in, grad_attention_out, grad_mixer_out, grad_gate_up, grad_down_weight, grad_gain_mixing, grad_gain_feed, pulled[4], pulled[5], pulled[6], grad_conv_weight, grad_conv_bias)
    return (output, input_grad, grads)

def reference(block_input, segment_ids, out_cotangent, attention_in, mixer_in, step_in, attention_out, mixer_out, gate_up, down_weight, gain_mixing, gain_feed, decay_log, step_bias, skip_gain, conv_weight, conv_bias):
    weights = (attention_in, mixer_in, step_in, attention_out, mixer_out, gate_up, down_weight)
    smalls = (gain_mixing, gain_feed, decay_log, step_bias, skip_gain, conv_weight, conv_bias)

    def advance(totals, item):
        output, input_grad, grads = one_sequence(item[0], item[1], item[2], weights, smalls)
        return (tuple((total + grad for total, grad in zip(totals, grads))), (output, input_grad))
    start = tuple((jnp.zeros(weight.shape, jnp.float32) for weight in weights + smalls))
    totals, results = lax.scan(advance, start, (block_input, segment_ids, out_cotangent))
    return (results[0], results[1], totals[0], totals[1], totals[2], totals[3], totals[4], totals[5], totals[6], totals[7], totals[8], totals[9], totals[10], totals[11], totals[12], totals[13])
```

```python
import math

import jax
import jax.numpy as jnp
from jax import lax
from jax.sharding import PartitionSpec as P

FF = 2048
HEADS_Q = 8
HEADS_KV = 2
HEAD = 64
SSM_HEADS = 24
SSM_HEAD = 64
STATE = 128
SSM_INNER = 1536


highest = lax.Precision.HIGHEST


def from_behind(block, axis, distance):
    devices = range(lax.axis_size(axis))
    route = [(i - distance, i) for i in devices if i - distance in devices]
    return lax.ppermute(block, axis, route)


def carried_in(value, axis, join, neutral, backward):
    count, mine = (lax.axis_size(axis), lax.axis_index(axis))
    pieces = jax.tree.map(lambda part: lax.all_gather(part, axis), value)
    if backward:
        pieces = jax.tree.map(lambda part: part[::-1], pieces)
        mine = count - 1 - mine
    so_far = jax.tree.map(
        lambda part, zero: jnp.full_like(part, 0) + jnp.asarray(zero, part.dtype), value, neutral
    )

    def hop(position, so_far):
        longer = join(so_far, jax.tree.map(lambda part: part[position], pieces))
        return jax.tree.map(lambda new, old: jnp.where(position < mine, new, old), longer, so_far)

    return lax.fori_loop(0, count - 1, hop, so_far)


def carried_by_heads(decays, state, backward):
    count, mine = (lax.axis_size("ctx"), lax.axis_index("ctx"))
    seq_count, heads = decays.shape[1:]
    share = heads // count
    own = lax.dynamic_slice_in_dim(decays, mine * share, share, axis=2)
    pieces = lax.all_to_all(state, "ctx", split_axis=1, concat_axis=0, tiled=True)
    pieces = pieces.reshape((count, seq_count, share) + state.shape[2:])
    order = list(range(count))[::-1] if backward else list(range(count))
    so_far = jnp.zeros_like(pieces[0])
    reached = [None] * count
    for position in order:
        reached[position] = so_far
        so_far = own[position][:, :, None, None] * so_far + pieces[position]
    return lax.all_to_all(
        jnp.concatenate(reached, axis=0), "ctx", split_axis=0, concat_axis=1, tiled=True
    )


def fold_shape(owned, rows, width):
    step = math.gcd(owned, rows)
    return (step, owned // step, rows // step, width // (rows // step))


def fold_rows(array, owned, rows):
    step, across, down, part = fold_shape(owned, rows, array.shape[1])
    blocks = array.reshape(-1, owned, array.shape[1])
    columns = [
        jnp.concatenate(
            [blocks[:, i * step : (i + 1) * step, j * part : (j + 1) * part] for j in range(down)],
            axis=1,
        )
        for i in range(across)
    ]
    return jnp.concatenate(columns, axis=2).reshape(-1, across * part)


def unfold_rows(array, owned, rows, width):
    step, across, down, part = fold_shape(owned, rows, width)
    blocks = array.reshape(-1, rows, across * part)
    lines = [
        jnp.concatenate(
            [blocks[:, j * step : (j + 1) * step, i * part : (i + 1) * part] for j in range(down)],
            axis=2,
        )
        for i in range(across)
    ]
    return jnp.concatenate(lines, axis=1).reshape(-1, width)


def pad_columns(array):
    return jnp.pad(array, ((0, 0), (0, -array.shape[1] % 128)))


def cut_columns(array, widths):
    pieces, at = ([], 0)
    for width in widths:
        pieces.append(array[:, at : at + width])
        at += width
    return pieces


def rms_scale(values, gain):
    return values * lax.rsqrt(jnp.mean(values * values, axis=-1, keepdims=True) + 1e-05) * gain


def silu_slope(values):
    sigma = jax.nn.sigmoid(values)
    return sigma * (1.0 + values * (1.0 - sigma))


def ssd_local(
    inner, write_map, read_map, step_raw, decay_log, step_bias, skip_gain, starts, segments
):
    step = jax.nn.softplus(step_raw + step_bias)
    rates = step * -jnp.exp(decay_log)
    places = jnp.arange(segments.shape[0])
    lower = places[None, :] <= places[:, None]
    running = jnp.dot(lower.astype(jnp.float32), rates, precision=highest)
    same = (segments[:, None] == segments[None, :]) & lower
    spans = jnp.where(same[None], running.T[:, :, None] - running.T[:, None, :], -1e30)
    intersection = jnp.dot(read_map, write_map.T, precision=highest)
    mixing = jnp.exp(spans) * intersection[None] * step.T[:, None, :]
    result = (
        jnp.einsum("hts,shp->thp", mixing, inner, precision=highest)
        + skip_gain[None, :, None] * inner
    )
    before = jnp.sum((lower & starts[None, :]).astype(jnp.int32), axis=1) == 0
    carried = jnp.where(before[:, None], jnp.exp(running), 0.0)
    tails = jnp.where(
        (segments == segments[-1])[:, None], jnp.exp(running[-1][None, :] - running), 0.0
    )
    state = jnp.einsum("sh,shp,sn->hpn", tails * step, inner, write_map, precision=highest)
    return (result, state, carried[-1], carried)


def add_state(result, carried, read_map, state_in):
    return result + carried[:, :, None] * jnp.einsum(
        "hpn,tn->thp", state_in, read_map, precision=highest
    )


def ssd_block(
    inner,
    write_map,
    read_map,
    step_raw,
    decay_log,
    step_bias,
    skip_gain,
    starts,
    segments,
    state_in,
):
    result, state, decay_total, carried = ssd_local(
        inner, write_map, read_map, step_raw, decay_log, step_bias, skip_gain, starts, segments
    )
    return (
        add_state(result, carried, read_map, state_in),
        decay_total[:, None, None] * state_in + state,
    )


def chain(earlier, later):
    return (earlier[0] * later[0], later[0][:, :, None, None] * earlier[1] + later[1])


def over_blocks(step, start, items):
    if items[2].shape[0] > 1:
        return lax.scan(step, start, items)
    carry, result = step(start, (items[0][0], items[1][0], 0))
    return (carry, None if result is None else result[None])


def group_queries(flat, seq_count, tok_count):
    groups = HEADS_Q // HEADS_KV
    shaped = flat.reshape(seq_count, tok_count, HEADS_KV, groups, HEAD)
    return shaped.transpose(0, 2, 3, 1, 4).reshape(seq_count, HEADS_KV, groups * tok_count, HEAD)


def ungroup(grouped, seq_count, tok_count):
    groups = HEADS_Q // HEADS_KV
    shaped = grouped.reshape(seq_count, HEADS_KV, groups, tok_count, HEAD)
    return shaped.transpose(0, 3, 1, 2, 4).reshape(seq_count * tok_count, HEADS_Q * HEAD)


def local(
    block_input,
    segment_ids,
    out_cotangent,
    attention_in,
    mixer_in,
    step_in,
    attention_out,
    mixer_out,
    gate_up,
    down_weight,
    gain_mixing,
    gain_feed,
    decay_log,
    step_bias,
    skip_gain,
    conv_weight,
    conv_bias,
):
    seq_count, tok_count, width = block_input.shape
    row_count = seq_count * tok_count
    length = tok_count * lax.axis_size("ctx")
    block = length if length <= 1024 else 512
    blocks = length // block
    groups = HEADS_Q // HEADS_KV
    query_width = HEADS_Q * HEAD
    key_width = HEADS_KV * HEAD
    score_scale = HEAD ** (-0.5)
    query_rows = groups * tok_count
    first = lax.axis_index("ctx") * tok_count
    own_rows = attention_in.shape[0]
    axes = ("dp", "ctx")
    entry = jnp.concatenate([attention_in, mixer_in, pad_columns(step_in)], axis=1)
    full_attention_in, full_mixer_in, full_step_in = cut_columns(
        lax.all_gather(entry, axes, axis=0, tiled=True),
        (attention_in.shape[1], mixer_in.shape[1], step_in.shape[1]),
    )
    tall = (attention_out, mixer_out, down_weight)
    folded = [fold_rows(weight, weight.shape[0], own_rows) for weight in tall]
    rest = lax.all_gather(
        jnp.concatenate(folded + [gate_up], axis=1), axes, axis=0, tiled=True
    )
    rest = cut_columns(rest, [weight.shape[1] for weight in folded] + [gate_up.shape[1]])
    full_attention_out, full_mixer_out, full_down = (
        unfold_rows(part, weight.shape[0], own_rows, width) for part, weight in zip(rest, tall)
    )
    full_gate_up = rest[3]
    source = block_input.reshape(row_count, width).astype(jnp.float32)
    normed = rms_scale(source, gain_mixing).astype(jnp.bfloat16)
    projected = jnp.dot(normed, full_attention_in, preferred_element_type=jnp.float32).astype(
        jnp.bfloat16
    )
    mixed_in = jnp.dot(normed, full_mixer_in, preferred_element_type=jnp.float32)
    step_raw = jnp.dot(normed, full_step_in, preferred_element_type=jnp.float32).reshape(
        seq_count, tok_count, SSM_HEADS
    )
    queries = group_queries(projected[:, :query_width], seq_count, tok_count)
    local_keys = (
        projected[:, query_width:].reshape(seq_count, tok_count, 2 * key_width).transpose(1, 0, 2)
    )
    local_segments = segment_ids.T
    keys_all, segments_all = (
        lax.all_gather(local_keys, "ctx", axis=0, tiled=True),
        lax.all_gather(local_segments, "ctx", axis=0, tiled=True),
    )
    query_pos = first + jnp.arange(query_rows) % tok_count
    query_segments = jnp.tile(segment_ids, (1, groups))
    segment_blocks = segments_all.reshape(blocks, block, seq_count)
    block_ids = jnp.arange(blocks)

    def scores_of(key_block, seg_block, block_id):
        keys = key_block[:, :, :key_width].reshape(block, seq_count, HEADS_KV, HEAD)
        scores = (
            jnp.einsum("sgrd,ksgd->sgrk", queries, keys, preferred_element_type=jnp.float32)
            * score_scale
        )
        key_pos = block_id * block + jnp.arange(block)
        allowed = (key_pos[None, None, None, :] <= query_pos[None, None, :, None]) & (
            seg_block.T[:, None, None, :] == query_segments[:, None, :, None]
        )
        return (scores, allowed)

    key_blocks = keys_all.reshape(blocks, block, seq_count, 2 * key_width)

    def gather_stats(carry, item):
        top, total = carry
        scores, allowed = scores_of(item[0], item[1], item[2])
        masked = jnp.where(allowed, scores, -1e30)
        new_top = jnp.maximum(top, jnp.max(masked, axis=-1))
        total = total * jnp.exp(top - new_top) + jnp.sum(
            jnp.where(allowed, jnp.exp(masked - new_top[..., None]), 0.0), axis=-1
        )
        return ((new_top, total), None)

    start_top = jnp.full((seq_count, HEADS_KV, query_rows), -1e30, jnp.float32)
    (top, total), _ = over_blocks(
        gather_stats,
        (start_top, jnp.zeros_like(start_top)),
        (key_blocks, segment_blocks, block_ids),
    )
    log_total = top + jnp.log(total)

    def weigh_values(accum, item):
        scores, allowed = scores_of(item[0], item[1], item[2])
        values = item[0][:, :, key_width:].reshape(block, seq_count, HEADS_KV, HEAD)
        probs = jnp.where(allowed, jnp.exp(scores - log_total[..., None]), 0.0).astype(jnp.bfloat16)
        return (
            accum
            + jnp.einsum("sgrk,ksgd->sgrd", probs, values, preferred_element_type=jnp.float32),
            None,
        )

    attended, _ = over_blocks(
        weigh_values, jnp.zeros(queries.shape, jnp.float32), (key_blocks, segment_blocks, block_ids)
    )
    attended = attended.astype(jnp.bfloat16)
    attended_flat = ungroup(attended, seq_count, tok_count)
    gate_part = mixed_in[:, :SSM_INNER]
    conv_width = mixed_in.shape[1] - SSM_INNER
    conv_in = mixed_in[:, SSM_INNER:].reshape(seq_count, tok_count, conv_width)
    positions = first + jnp.arange(tok_count)
    before_rows = from_behind(conv_in[:, tok_count - 3 :, :], "ctx", 1)
    extended = jnp.concatenate([before_rows, conv_in], axis=1)
    pre = conv_bias + conv_weight[3] * conv_in
    keep_masks = []
    for offset in (1, 2, 3):
        earlier_ids = segments_all[jnp.maximum(positions - offset, 0)].T
        keep_mask = (positions >= offset)[None, :] & (earlier_ids == segment_ids)
        keep_masks.append(keep_mask)
        pre = (
            pre
            + jnp.where(keep_mask[..., None], extended[:, 3 - offset : 3 - offset + tok_count], 0.0)
            * conv_weight[3 - offset]
        )
    converted = jax.nn.silu(pre)
    inner = converted[..., :SSM_INNER].reshape(seq_count, tok_count, SSM_HEADS, SSM_HEAD)
    write_map = converted[..., SSM_INNER : SSM_INNER + STATE]
    read_map = converted[..., SSM_INNER + STATE :]
    starts = (positions == 0)[None, :] | jnp.logical_not(keep_masks[0])
    local_map = jax.vmap(ssd_local, in_axes=(0, 0, 0, 0, None, None, None, 0, 0))
    partial_out, partial_state, decay_total, carried = local_map(
        inner, write_map, read_map, step_raw, decay_log, step_bias, skip_gain, starts, segment_ids
    )
    by_heads = SSM_HEADS % lax.axis_size("ctx") == 0
    if by_heads:
        decays = lax.all_gather(decay_total, "ctx")
        state_in = carried_by_heads(decays, partial_state, False)
    else:
        unit = (jnp.ones_like(decay_total), jnp.zeros_like(partial_state))
        state_in = carried_in((decay_total, partial_state), "ctx", chain, unit, False)[1]
    scanned = jax.vmap(add_state)(partial_out, carried, read_map, state_in)
    flat_scan = scanned.reshape(row_count, SSM_INNER)
    gated = (flat_scan * jax.nn.silu(gate_part)).astype(jnp.bfloat16)
    residual = (
        source
        + jnp.dot(attended_flat, full_attention_out, preferred_element_type=jnp.float32)
        + jnp.dot(gated, full_mixer_out, preferred_element_type=jnp.float32)
    )
    normed_two = rms_scale(residual, gain_feed).astype(jnp.bfloat16)
    gate_values = jnp.dot(normed_two, full_gate_up, preferred_element_type=jnp.float32)
    gate_in = gate_values[:, :FF]
    up_in = gate_values[:, FF:]
    active = (jax.nn.silu(gate_in) * up_in).astype(jnp.bfloat16)
    output = (residual + jnp.dot(active, full_down, preferred_element_type=jnp.float32)).astype(
        jnp.bfloat16
    )
    cotangent = out_cotangent.reshape(row_count, width)
    grad_down_weight = jnp.dot(active.T, cotangent, preferred_element_type=jnp.float32).astype(
        jnp.bfloat16
    )
    active_grad = jnp.dot(cotangent, full_down.T, preferred_element_type=jnp.float32)
    gate_grad = jnp.concatenate(
        [active_grad * up_in * silu_slope(gate_in), active_grad * jax.nn.silu(gate_in)], axis=1
    ).astype(jnp.bfloat16)
    grad_gate_up = jnp.dot(normed_two.T, gate_grad, preferred_element_type=jnp.float32).astype(
        jnp.bfloat16
    )
    feed_terms = jnp.concatenate(
        [grad_gate_up, fold_rows(grad_down_weight, down_weight.shape[0], own_rows)], axis=1
    )
    feed_sums = lax.psum_scatter(feed_terms, axes, scatter_dimension=0, tiled=True)
    normed_two_grad = jnp.dot(gate_grad, full_gate_up.T, preferred_element_type=jnp.float32)
    _, pull_two = jax.vjp(rms_scale, residual, gain_feed)
    residual_part, grad_gain_feed = pull_two(normed_two_grad)
    residual_grad = cotangent.astype(jnp.float32) + residual_part
    residual_half, _ = lax.optimization_barrier((residual_grad.astype(jnp.bfloat16), feed_terms))
    grad_attention_out = jnp.dot(attended_flat.T, residual_half, preferred_element_type=jnp.float32)
    grad_mixer_out = jnp.dot(gated.T, residual_half, preferred_element_type=jnp.float32)
    attended_grad = jnp.dot(
        residual_half, full_attention_out.T, preferred_element_type=jnp.float32
    ).astype(jnp.bfloat16)
    gated_grad = jnp.dot(residual_half, full_mixer_out.T, preferred_element_type=jnp.float32)
    gate_part_grad = gated_grad * flat_scan * silu_slope(gate_part)
    scan_grad = (gated_grad * jax.nn.silu(gate_part)).reshape(
        seq_count, tok_count, SSM_HEADS, SSM_HEAD
    )
    direct = jnp.einsum("sth,sthp,stn->shpn", carried, scan_grad, read_map, precision=highest)
    if by_heads:
        state_grad = carried_by_heads(decays, direct, True)
    else:
        state_grad = carried_in((decay_total, direct), "ctx", chain, unit, True)[1]

    def block_map(inner_v, write_v, read_v, step_v, decay_v, bias_v, skip_v, state_v):
        mapped = jax.vmap(ssd_block, in_axes=(0, 0, 0, 0, None, None, None, 0, 0, 0))
        return mapped(
            inner_v, write_v, read_v, step_v, decay_v, bias_v, skip_v, starts, segment_ids, state_v
        )

    _, pull_scan = jax.vjp(
        block_map, inner, write_map, read_map, step_raw, decay_log, step_bias, skip_gain, state_in
    )
    pulled = pull_scan((scan_grad, state_grad))
    converted_grad = jnp.concatenate(
        [pulled[0].reshape(seq_count, tok_count, SSM_INNER), pulled[1], pulled[2]], axis=2
    )
    pre_grad = converted_grad * silu_slope(pre)
    after_rows = from_behind(pre_grad[:, :3, :], "ctx", -1)
    ahead = jnp.concatenate([pre_grad, after_rows], axis=1)
    conv_in_grad = conv_weight[3] * pre_grad
    tap_grads = [None, None, None, jnp.sum(pre_grad * conv_in, axis=(0, 1))]
    for offset in (1, 2, 3):
        later_ids = segments_all[jnp.minimum(positions + offset, length - 1)].T
        later_mask = later_ids == segment_ids
        conv_in_grad = (
            conv_in_grad
            + jnp.where(later_mask[..., None], ahead[:, offset : offset + tok_count], 0.0)
            * conv_weight[3 - offset]
        )
        earlier_rows = jnp.where(
            keep_masks[offset - 1][..., None], extended[:, 3 - offset : 3 - offset + tok_count], 0.0
        )
        tap_grads[3 - offset] = jnp.sum(pre_grad * earlier_rows, axis=(0, 1))
    grad_conv_weight = jnp.stack(tap_grads, axis=0)
    grad_conv_bias = jnp.sum(pre_grad, axis=(0, 1))
    mixer_grad = jnp.concatenate(
        [gate_part_grad, conv_in_grad.reshape(row_count, conv_width)], axis=1
    ).astype(jnp.bfloat16)
    step_grad_half = pulled[3].reshape(row_count, SSM_HEADS).astype(jnp.bfloat16)
    out_grad = group_queries(attended_grad, seq_count, tok_count)
    deltas = jnp.sum(out_grad.astype(jnp.float32) * attended.astype(jnp.float32), axis=-1)

    def attention_grads(query_grad, item):
        scores, allowed = scores_of(item[0], item[1], item[2])
        keys = item[0][:, :, :key_width].reshape(block, seq_count, HEADS_KV, HEAD)
        values = item[0][:, :, key_width:].reshape(block, seq_count, HEADS_KV, HEAD)
        probs = jnp.where(allowed, jnp.exp(scores - log_total[..., None]), 0.0)
        value_grad = jnp.einsum(
            "sgrk,sgrd->ksgd",
            probs.astype(jnp.bfloat16),
            out_grad,
            preferred_element_type=jnp.float32,
        )
        prob_grad = jnp.einsum(
            "sgrd,ksgd->sgrk", out_grad, values, preferred_element_type=jnp.float32
        )
        score_grad = (probs * (prob_grad - deltas[..., None])).astype(jnp.bfloat16)
        query_grad = (
            query_grad
            + jnp.einsum("sgrk,ksgd->sgrd", score_grad, keys, preferred_element_type=jnp.float32)
            * score_scale
        )
        key_grad = (
            jnp.einsum("sgrk,sgrd->ksgd", score_grad, queries, preferred_element_type=jnp.float32)
            * score_scale
        )
        both = jnp.concatenate(
            [
                key_grad.reshape(block, seq_count, key_width),
                value_grad.reshape(block, seq_count, key_width),
            ],
            axis=2,
        )
        return (query_grad, both)

    query_grad, key_terms = over_blocks(
        attention_grads,
        jnp.zeros(queries.shape, jnp.float32),
        (key_blocks, segment_blocks, block_ids),
    )
    key_pieces = lax.all_to_all(
        key_terms.reshape(length, seq_count, 2 * key_width).astype(jnp.bfloat16),
        "ctx",
        split_axis=0,
        concat_axis=0,
        tiled=True,
    )
    key_sums = jnp.sum(
        key_pieces.reshape(-1, tok_count, seq_count, 2 * key_width).astype(jnp.float32), axis=0
    )
    kv_grad = key_sums.transpose(1, 0, 2).reshape(row_count, 2 * key_width)
    projected_grad = jnp.concatenate(
        [ungroup(query_grad, seq_count, tok_count), kv_grad], axis=1
    ).astype(jnp.bfloat16)
    grad_attention_in = jnp.dot(normed.T, projected_grad, preferred_element_type=jnp.float32)
    grad_mixer_in = jnp.dot(normed.T, mixer_grad, preferred_element_type=jnp.float32)
    grad_step_in = jnp.dot(normed.T, step_grad_half, preferred_element_type=jnp.float32)
    normed_grad = (
        jnp.dot(projected_grad, full_attention_in.T, preferred_element_type=jnp.float32)
        + jnp.dot(mixer_grad, full_mixer_in.T, preferred_element_type=jnp.float32)
        + jnp.dot(step_grad_half, full_step_in.T, preferred_element_type=jnp.float32)
    )
    _, pull_one = jax.vjp(rms_scale, source, gain_mixing)
    source_part, grad_gain_mixing = pull_one(normed_grad)
    input_grad = residual_grad + source_part
    others = [
        grad_attention_in.astype(jnp.bfloat16),
        grad_mixer_in.astype(jnp.bfloat16),
        fold_rows(grad_attention_out.astype(jnp.bfloat16), attention_out.shape[0], own_rows),
        fold_rows(grad_mixer_out.astype(jnp.bfloat16), mixer_out.shape[0], own_rows),
        pad_columns(grad_step_in.astype(jnp.bfloat16)),
    ]
    other_sums = lax.psum_scatter(
        jnp.concatenate(others, axis=1), axes, scatter_dimension=0, tiled=True
    )
    feed_parts = cut_columns(
        feed_sums, (gate_up.shape[1], feed_sums.shape[1] - gate_up.shape[1])
    )
    other_parts = cut_columns(other_sums, [part.shape[1] for part in others])
    weight_sums = [
        part.astype(jnp.float32)
        for part in (
            other_parts[0],
            other_parts[1],
            other_parts[4][:, :SSM_HEADS],
            unfold_rows(other_parts[2], attention_out.shape[0], own_rows, width),
            unfold_rows(other_parts[3], mixer_out.shape[0], own_rows, width),
            feed_parts[0],
            unfold_rows(feed_parts[1], down_weight.shape[0], own_rows, width),
        )
    ]
    small_sums = lax.psum(
        (
            grad_gain_mixing,
            grad_gain_feed,
            pulled[4],
            pulled[5],
            pulled[6],
            grad_conv_weight,
            grad_conv_bias,
        ),
        ("dp", "ctx"),
    )
    return (
        output.reshape(seq_count, tok_count, width),
        input_grad.reshape(seq_count, tok_count, width),
        weight_sums[0],
        weight_sums[1],
        weight_sums[2],
        weight_sums[3],
        weight_sums[4],
        weight_sums[5],
        weight_sums[6],
        small_sums[0],
        small_sums[1],
        small_sums[2],
        small_sums[3],
        small_sums[4],
        small_sums[5],
        small_sums[6],
    )

def split_heads(ctx):
    return HEADS_Q % ctx == 0 and SSM_HEADS % ctx == 0 and ctx % HEADS_KV == 0


def entry_layout(ctx):
    heads = SSM_HEADS // ctx
    widths = [HEADS_Q // ctx * HEAD, HEAD, HEAD, heads * SSM_HEAD, heads * SSM_HEAD, STATE, STATE, heads]
    return widths + [-sum(widths) % 128]


def entry_slabs(attention_in, mixer_in, step_in, ctx):
    rows = attention_in.shape[0]
    share = ctx // HEADS_KV
    query_width = HEADS_Q * HEAD
    key_width = HEADS_KV * HEAD

    def parts(array, count):
        return array.reshape(rows, count, -1).transpose(1, 0, 2)

    kv = [
        jnp.repeat(parts(attention_in[:, at : at + key_width], HEADS_KV), share, axis=0)
        for at in (query_width, query_width + key_width)
    ]
    both = jnp.broadcast_to(mixer_in[None, :, 2 * SSM_INNER :], (ctx, rows, 2 * STATE))
    pieces = [
        parts(attention_in[:, :query_width], ctx),
        kv[0],
        kv[1],
        parts(mixer_in[:, :SSM_INNER], ctx),
        parts(mixer_in[:, SSM_INNER : 2 * SSM_INNER], ctx),
        both,
        parts(step_in, ctx),
        jnp.zeros((ctx, rows, entry_layout(ctx)[-1]), jnp.bfloat16),
    ]
    return jnp.concatenate(pieces, axis=2)


def entry_unslab(slabs, ctx):
    rows = slabs.shape[1]
    share = ctx // HEADS_KV
    q, k, v, gate, inner, write, read, step, _ = [
        slabs[:, :, at : at + width]
        for at, width in zip(offsets(entry_layout(ctx)), entry_layout(ctx))
    ]

    def flat(part):
        return part.transpose(1, 0, 2).reshape(rows, -1)

    def shared(part):
        return flat(jnp.sum(part.reshape(HEADS_KV, share, rows, HEAD), axis=1))

    attention = jnp.concatenate([flat(q), shared(k), shared(v)], axis=1)
    mixer = jnp.concatenate(
        [flat(gate), flat(inner), jnp.sum(write, axis=0), jnp.sum(read, axis=0)], axis=1
    )
    return attention, mixer, flat(step)


def offsets(widths):
    at, places = 0, []
    for width in widths:
        places.append(at)
        at += width
    return places


def scan_chunks(inner, write_map, read_map, step_raw, decay_log, step_bias, skip_gain, starts, segments):
    local_map = jax.vmap(ssd_local, in_axes=(0, 0, 0, 0, None, None, None, 0, 0))
    result, state, _, carried = local_map(
        inner, write_map, read_map, step_raw, decay_log, step_bias, skip_gain, starts, segments
    )
    chunks = inner.shape[0]
    step = jax.nn.softplus(step_raw + step_bias)
    rates = jnp.sum(step * -jnp.exp(decay_log), axis=1)
    order = jnp.arange(chunks)
    lower = (order[None, :] <= order[:, None]).astype(jnp.float32)
    sums = jnp.dot(lower, rates, precision=highest)
    last = segments[:, -1]
    before = jnp.concatenate([last[:1], last[:-1]])
    open_span = (order[None, :] < order[:, None]) & (last[None, :] == before[:, None])
    sums_before = jnp.concatenate([jnp.zeros_like(sums[:1]), sums[:-1]], axis=0)
    spans = jnp.where(
        open_span[None], sums_before.T[:, :, None] - sums.T[:, None, :], -1e30
    )
    state_in = jnp.einsum("hji,ihpn->jhpn", jnp.exp(spans), state, precision=highest)
    return jax.vmap(add_state)(result, carried, read_map, state_in)


def conv_pre(rows, weight, bias, keeps):
    pre = bias + weight[3] * rows
    for offset in (1, 2, 3):
        shifted = jnp.pad(rows[:-offset], ((offset, 0), (0, 0)))
        pre = pre + jnp.where(keeps[offset - 1][:, None], shifted, 0.0) * weight[3 - offset]
    return pre


def gather_tokens(block):
    return lax.all_gather(block, "ctx", axis=0, tiled=True)


def sum_tokens(terms):
    return lax.psum_scatter(
        terms.astype(jnp.bfloat16), "ctx", scatter_dimension=0, tiled=True
    ).astype(jnp.float32)


def gather_dp(block):
    return lax.all_gather(block, "dp", axis=0, tiled=True)


def sum_dp(terms):
    return lax.psum_scatter(terms.astype(jnp.bfloat16), "dp", scatter_dimension=0, tiled=True)


def swap_ctx(slabs):
    return lax.all_to_all(slabs, "ctx", split_axis=0, concat_axis=0, tiled=True)


def split_local(
    block_input,
    segment_ids,
    out_cotangent,
    attention_in,
    mixer_in,
    step_in,
    attention_out,
    mixer_out,
    gate_up,
    down_weight,
    gain_mixing,
    gain_feed,
    decay_log,
    step_bias,
    skip_gain,
    conv_weight,
    conv_bias,
):
    ctx, dp = lax.axis_size("ctx"), lax.axis_size("dp")
    mine = lax.axis_index("ctx")
    tok_count, width = block_input.shape[1:]
    length = tok_count * ctx
    heads = SSM_HEADS // ctx
    query_heads = HEADS_Q // ctx
    score_scale = HEAD ** (-0.5)
    layout = entry_layout(ctx)
    places = offsets(layout)
    rows = attention_in.shape[0]
    hidden = down_weight.shape[0]
    entry = swap_ctx(entry_slabs(attention_in, mixer_in, step_in, ctx))
    entry = gather_dp(entry.reshape(ctx * rows, -1))
    gate_slabs = gate_up.reshape(rows, 2, dp, ctx, hidden).transpose(3, 0, 1, 2, 4)
    gate_slabs = swap_ctx(gate_slabs.reshape(ctx, rows, 2 * dp * hidden))
    feed_in = gather_dp(gate_slabs.reshape(ctx * rows, -1))
    route = [(i, (i % dp) * ctx + i // dp) for i in range(dp * ctx)]
    back = [(target, start) for start, target in route]
    outs = lax.ppermute(jnp.concatenate([attention_out, mixer_out], axis=0), ("dp", "ctx"), route)
    own_attention, own_mixer = attention_out.shape[0], mixer_out.shape[0]
    outs = gather_dp(outs).reshape(dp, own_attention + own_mixer, width)
    attention_rows = outs[:, :own_attention].reshape(-1, width)
    mixer_rows = outs[:, own_attention:].reshape(-1, width)
    feed_out = gather_dp(down_weight)

    source = block_input.reshape(tok_count, width).astype(jnp.float32)
    cotangent = out_cotangent.reshape(tok_count, width)
    normed = gather_tokens(rms_scale(source, gain_mixing).astype(jnp.bfloat16))
    segments = gather_tokens(segment_ids.reshape(tok_count))
    cotangents = gather_tokens(cotangent)
    mixed = jnp.dot(normed, entry, preferred_element_type=jnp.float32)
    q, k, v, gate_part, inner_in, write_in, read_in, step_raw, _ = [
        mixed[:, at : at + size] for at, size in zip(places, layout)
    ]
    conv_in = mixed[:, places[4] : places[7]]

    queries = q.astype(jnp.bfloat16).reshape(length, query_heads, HEAD).transpose(1, 0, 2)
    keys, values = k.astype(jnp.bfloat16), v.astype(jnp.bfloat16)
    order = jnp.arange(length)
    allowed = (order[None, :] <= order[:, None]) & (segments[None, :] == segments[:, None])
    scores = (
        jnp.einsum("hqd,kd->hqk", queries, keys, preferred_element_type=jnp.float32) * score_scale
    )
    masked = jnp.where(allowed, scores, -1e30)
    top = jnp.max(masked, axis=-1, keepdims=True)
    total = jnp.sum(jnp.where(allowed, jnp.exp(masked - top), 0.0), axis=-1, keepdims=True)
    log_total = top + jnp.log(total)
    probs = jnp.where(allowed, jnp.exp(scores - log_total), 0.0)
    probs_half = probs.astype(jnp.bfloat16)
    attended = jnp.einsum(
        "hqk,kd->hqd", probs_half, values, preferred_element_type=jnp.float32
    ).astype(jnp.bfloat16)
    attended_flat = attended.transpose(1, 0, 2).reshape(length, query_heads * HEAD)

    own = lambda array, at, size: lax.dynamic_slice_in_dim(array, at + mine * size, size, axis=-1)
    conv_own = lambda array: jnp.concatenate(
        [own(array, 0, heads * SSM_HEAD), array[..., SSM_INNER:]], axis=-1
    )
    taps, bias = conv_own(conv_weight), conv_own(conv_bias)
    keeps = []
    for offset in (1, 2, 3):
        earlier = jnp.concatenate([jnp.full((offset,), -1, segments.dtype), segments[:-offset]])
        keeps.append(earlier == segments)
    pre = conv_pre(conv_in, taps, bias, keeps)
    converted = jax.nn.silu(pre)
    starts = jnp.logical_not(keeps[0])
    chunked = lambda array: array.reshape((ctx, tok_count) + array.shape[1:])

    def scan_map(converted_v, step_v, decay_v, bias_v, skip_v):
        inner = converted_v[:, : heads * SSM_HEAD].reshape(length, heads, SSM_HEAD)
        write_map = converted_v[:, heads * SSM_HEAD : heads * SSM_HEAD + STATE]
        read_map = converted_v[:, heads * SSM_HEAD + STATE :]
        return scan_chunks(
            chunked(inner),
            chunked(write_map),
            chunked(read_map),
            chunked(step_v),
            decay_v,
            bias_v,
            skip_v,
            chunked(starts),
            chunked(segments),
        ).reshape(length, heads * SSM_HEAD)

    scanned, pull_scan = jax.vjp(
        scan_map,
        converted,
        step_raw,
        own(decay_log, 0, heads),
        own(step_bias, 0, heads),
        own(skip_gain, 0, heads),
    )
    gated = (scanned * jax.nn.silu(gate_part)).astype(jnp.bfloat16)
    mixing_out = sum_tokens(
        jnp.dot(attended_flat, attention_rows, preferred_element_type=jnp.float32)
        + jnp.dot(gated, mixer_rows, preferred_element_type=jnp.float32)
    )
    residual = source + mixing_out

    normed_two_own, pull_two = jax.vjp(rms_scale, residual, gain_feed)
    normed_two = gather_tokens(normed_two_own.astype(jnp.bfloat16))
    gate_values = jnp.dot(normed_two, feed_in, preferred_element_type=jnp.float32)
    gate_in, up_in = gate_values[:, : dp * hidden], gate_values[:, dp * hidden :]
    active = (jax.nn.silu(gate_in) * up_in).astype(jnp.bfloat16)
    output = (
        residual + sum_tokens(jnp.dot(active, feed_out, preferred_element_type=jnp.float32))
    ).astype(jnp.bfloat16)
    grad_feed_out = sum_dp(jnp.dot(active.T, cotangents, preferred_element_type=jnp.float32))
    active_grad = jnp.dot(cotangents, feed_out.T, preferred_element_type=jnp.float32)
    gate_grad = jnp.concatenate(
        [active_grad * up_in * silu_slope(gate_in), active_grad * jax.nn.silu(gate_in)], axis=1
    ).astype(jnp.bfloat16)
    normed_two_grad = sum_tokens(
        jnp.dot(gate_grad, feed_in.T, preferred_element_type=jnp.float32)
    )
    grad_feed_in = swap_ctx(
        sum_dp(jnp.dot(normed_two.T, gate_grad, preferred_element_type=jnp.float32)).reshape(
            ctx, rows, -1
        )
    )
    residual_part, grad_gain_feed = pull_two(normed_two_grad)
    residual_grad = cotangent.astype(jnp.float32) + residual_part
    residual_half = gather_tokens(residual_grad.astype(jnp.bfloat16))
    grad_outs = jnp.concatenate(
        [
            jnp.dot(attended_flat.T, residual_half, preferred_element_type=jnp.float32).reshape(
                dp, own_attention, width
            ),
            jnp.dot(gated.T, residual_half, preferred_element_type=jnp.float32).reshape(
                dp, own_mixer, width
            ),
        ],
        axis=1,
    )
    grad_outs = lax.ppermute(sum_dp(grad_outs), ("dp", "ctx"), back)[0]
    attended_grad = jnp.dot(
        residual_half, attention_rows.T, preferred_element_type=jnp.float32
    ).astype(jnp.bfloat16)
    gated_grad = jnp.dot(residual_half, mixer_rows.T, preferred_element_type=jnp.float32)
    gate_part_grad = gated_grad * scanned * silu_slope(gate_part)
    scan_grad = gated_grad * jax.nn.silu(gate_part)
    converted_grad, step_grad, own_decay, own_bias, own_skip = pull_scan(scan_grad)
    pre_grad = converted_grad * silu_slope(pre)
    conv_in_grad = taps[3] * pre_grad
    tap_grads = [None, None, None, jnp.sum(pre_grad * conv_in, axis=0)]
    for offset in (1, 2, 3):
        kept = jnp.where(keeps[offset - 1][:, None], pre_grad, 0.0)
        conv_in_grad = (
            conv_in_grad + jnp.pad(kept[offset:], ((0, offset), (0, 0))) * taps[3 - offset]
        )
        tap_grads[3 - offset] = jnp.sum(kept[offset:] * conv_in[:-offset], axis=0)
    tap_grads = jnp.stack(tap_grads + [jnp.sum(pre_grad, axis=0)], axis=0)

    out_grad = attended_grad.reshape(length, query_heads, HEAD).transpose(1, 0, 2)
    deltas = jnp.sum(
        out_grad.astype(jnp.float32) * attended.astype(jnp.float32), axis=-1, keepdims=True
    )
    value_grad = jnp.einsum("hqk,hqd->kd", probs_half, out_grad, preferred_element_type=jnp.float32)
    prob_grad = jnp.einsum("hqd,kd->hqk", out_grad, values, preferred_element_type=jnp.float32)
    score_grad = (probs * (prob_grad - deltas)).astype(jnp.bfloat16)
    query_grad = (
        jnp.einsum("hqk,kd->hqd", score_grad, keys, preferred_element_type=jnp.float32)
        * score_scale
    )
    key_grad = (
        jnp.einsum("hqk,hqd->kd", score_grad, queries, preferred_element_type=jnp.float32)
        * score_scale
    )
    grads = jnp.concatenate(
        [
            query_grad.transpose(1, 0, 2).reshape(length, query_heads * HEAD),
            key_grad,
            value_grad,
            gate_part_grad,
            conv_in_grad,
            step_grad,
            jnp.zeros((length, layout[-1]), jnp.float32),
        ],
        axis=1,
    ).astype(jnp.bfloat16)
    normed_grad = sum_tokens(jnp.dot(grads, entry.T, preferred_element_type=jnp.float32))
    entry_grads = swap_ctx(
        sum_dp(jnp.dot(normed.T, grads, preferred_element_type=jnp.float32)).reshape(ctx, rows, -1)
    )
    grad_attention_in, grad_mixer_in, grad_step_in = entry_unslab(
        entry_grads.astype(jnp.float32), ctx
    )
    _, pull_one = jax.vjp(rms_scale, source, gain_mixing)
    source_part, grad_gain_mixing = pull_one(normed_grad)
    input_grad = residual_grad + source_part

    def spread(part, size):
        whole = jnp.zeros(part.shape[:-1] + (size,), jnp.float32)
        return lax.dynamic_update_slice_in_dim(whole, part, mine * part.shape[-1], axis=-1)

    head_grads = [spread(part, SSM_HEADS) for part in (own_decay, own_bias, own_skip)]
    tap_sums = jnp.concatenate(
        [spread(tap_grads[:, : heads * SSM_HEAD], SSM_INNER), tap_grads[:, heads * SSM_HEAD :]],
        axis=1,
    )
    small = lax.psum((grad_gain_mixing, grad_gain_feed, *head_grads, tap_sums), ("dp", "ctx"))
    grad_gate_up = (
        grad_feed_in.reshape(ctx, rows, 2, dp, hidden)
        .transpose(1, 2, 3, 0, 4)
        .reshape(rows, -1)
        .astype(jnp.float32)
    )
    return (
        output.reshape(block_input.shape),
        input_grad.reshape(block_input.shape),
        grad_attention_in,
        grad_mixer_in,
        grad_step_in,
        grad_outs[:own_attention].astype(jnp.float32),
        grad_outs[own_attention:].astype(jnp.float32),
        grad_gate_up,
        grad_feed_out.astype(jnp.float32),
        small[0],
        small[1],
        small[2],
        small[3],
        small[4],
        small[5][:4],
        small[5][4],
    )


def solution(mesh):
    in_specs = (
        P("dp", "ctx", None),
        P("dp", "ctx"),
        P("dp", "ctx", None),
        P(("dp", "ctx"), None),
        P(("dp", "ctx"), None),
        P(("dp", "ctx"), None),
        P(("dp", "ctx"), None),
        P(("dp", "ctx"), None),
        P(("dp", "ctx"), None),
        P(("dp", "ctx"), None),
        P(),
        P(),
        P(),
        P(),
        P(),
        P(),
        P(),
    )
    out_specs = (
        P("dp", "ctx", None),
        P("dp", "ctx", None),
        P(("dp", "ctx"), None),
        P(("dp", "ctx"), None),
        P(("dp", "ctx"), None),
        P(("dp", "ctx"), None),
        P(("dp", "ctx"), None),
        P(("dp", "ctx"), None),
        P(("dp", "ctx"), None),
        P(),
        P(),
        P(),
        P(),
        P(),
        P(),
        P(),
    )
    sequences = mesh.shape["dp"]

    def choose(*arrays):
        heads = split_heads(mesh.shape["ctx"]) and arrays[0].shape[0] == sequences
        body = split_local if heads else local
        mapped = jax.shard_map(
            body, mesh=mesh, in_specs=in_specs, out_specs=out_specs, check_vma=False
        )
        return mapped(*arrays)

    return choose
```

```python
import functools
import math

import jax
import jax.numpy as jnp
from jax import lax
from jax.experimental import pallas as pl
from jax.experimental.pallas import tpu as pltpu
from jax.sharding import PartitionSpec as P

FF = 2048
HEADS_Q = 8
HEADS_KV = 2
HEAD = 64
SSM_HEADS = 24
SSM_HEAD = 64
STATE = 128
SSM_INNER = 1536


highest = lax.Precision.HIGHEST


def from_behind(block, axis, distance):
    devices = range(lax.axis_size(axis))
    route = [(i - distance, i) for i in devices if i - distance in devices]
    return lax.ppermute(block, axis, route)


def carried_in(value, axis, join, neutral, backward):
    count, mine = (lax.axis_size(axis), lax.axis_index(axis))
    pieces = jax.tree.map(lambda part: lax.all_gather(part, axis), value)
    if backward:
        pieces = jax.tree.map(lambda part: part[::-1], pieces)
        mine = count - 1 - mine
    so_far = jax.tree.map(
        lambda part, zero: jnp.full_like(part, 0) + jnp.asarray(zero, part.dtype), value, neutral
    )

    def hop(position, so_far):
        longer = join(so_far, jax.tree.map(lambda part: part[position], pieces))
        return jax.tree.map(lambda new, old: jnp.where(position < mine, new, old), longer, so_far)

    return lax.fori_loop(0, count - 1, hop, so_far)


def carried_by_heads(decays, state, backward):
    count, mine = (lax.axis_size("ctx"), lax.axis_index("ctx"))
    seq_count, heads = decays.shape[1:]
    share = heads // count
    own = lax.dynamic_slice_in_dim(decays, mine * share, share, axis=2)
    pieces = lax.all_to_all(state, "ctx", split_axis=1, concat_axis=0, tiled=True)
    pieces = pieces.reshape((count, seq_count, share) + state.shape[2:])
    order = list(range(count))[::-1] if backward else list(range(count))
    so_far = jnp.zeros_like(pieces[0])
    reached = [None] * count
    for position in order:
        reached[position] = so_far
        so_far = own[position][:, :, None, None] * so_far + pieces[position]
    return lax.all_to_all(
        jnp.concatenate(reached, axis=0), "ctx", split_axis=0, concat_axis=1, tiled=True
    )


def fold_shape(owned, rows, width):
    step = math.gcd(owned, rows)
    return (step, owned // step, rows // step, width // (rows // step))


def fold_rows(array, owned, rows):
    step, across, down, part = fold_shape(owned, rows, array.shape[1])
    blocks = array.reshape(-1, owned, array.shape[1])
    columns = [
        jnp.concatenate(
            [blocks[:, i * step : (i + 1) * step, j * part : (j + 1) * part] for j in range(down)],
            axis=1,
        )
        for i in range(across)
    ]
    return jnp.concatenate(columns, axis=2).reshape(-1, across * part)


def unfold_rows(array, owned, rows, width):
    step, across, down, part = fold_shape(owned, rows, width)
    blocks = array.reshape(-1, rows, across * part)
    lines = [
        jnp.concatenate(
            [blocks[:, j * step : (j + 1) * step, i * part : (i + 1) * part] for j in range(down)],
            axis=2,
        )
        for i in range(across)
    ]
    return jnp.concatenate(lines, axis=1).reshape(-1, width)


def pad_columns(array):
    return jnp.pad(array, ((0, 0), (0, -array.shape[1] % 128)))


def cut_columns(array, widths):
    pieces, at = ([], 0)
    for width in widths:
        pieces.append(array[:, at : at + width])
        at += width
    return pieces


def rms_scale(values, gain):
    return values * lax.rsqrt(jnp.mean(values * values, axis=-1, keepdims=True) + 1e-05) * gain


def silu_slope(values):
    sigma = jax.nn.sigmoid(values)
    return sigma * (1.0 + values * (1.0 - sigma))


def ssd_local(
    inner, write_map, read_map, step_raw, decay_log, step_bias, skip_gain, starts, segments
):
    step = jax.nn.softplus(step_raw + step_bias)
    rates = step * -jnp.exp(decay_log)
    places = jnp.arange(segments.shape[0])
    lower = places[None, :] <= places[:, None]
    running = jnp.dot(lower.astype(jnp.float32), rates, precision=highest)
    same = (segments[:, None] == segments[None, :]) & lower
    spans = jnp.where(same[None], running.T[:, :, None] - running.T[:, None, :], -1e30)
    intersection = jnp.dot(read_map, write_map.T, precision=highest)
    mixing = jnp.exp(spans) * intersection[None] * step.T[:, None, :]
    result = (
        jnp.einsum("hts,shp->thp", mixing, inner, precision=highest)
        + skip_gain[None, :, None] * inner
    )
    before = jnp.sum((lower & starts[None, :]).astype(jnp.int32), axis=1) == 0
    carried = jnp.where(before[:, None], jnp.exp(running), 0.0)
    tails = jnp.where(
        (segments == segments[-1])[:, None], jnp.exp(running[-1][None, :] - running), 0.0
    )
    state = jnp.einsum("sh,shp,sn->hpn", tails * step, inner, write_map, precision=highest)
    return (result, state, carried[-1], carried)


def add_state(result, carried, read_map, state_in):
    return result + carried[:, :, None] * jnp.einsum(
        "hpn,tn->thp", state_in, read_map, precision=highest
    )


def ssd_block(
    inner,
    write_map,
    read_map,
    step_raw,
    decay_log,
    step_bias,
    skip_gain,
    starts,
    segments,
    state_in,
):
    result, state, decay_total, carried = ssd_local(
        inner, write_map, read_map, step_raw, decay_log, step_bias, skip_gain, starts, segments
    )
    return (
        add_state(result, carried, read_map, state_in),
        decay_total[:, None, None] * state_in + state,
    )


def chain(earlier, later):
    return (earlier[0] * later[0], later[0][:, :, None, None] * earlier[1] + later[1])


def over_blocks(step, start, items):
    if items[2].shape[0] > 1:
        return lax.scan(step, start, items)
    carry, result = step(start, (items[0][0], items[1][0], 0))
    return (carry, None if result is None else result[None])


def group_queries(flat, seq_count, tok_count):
    groups = HEADS_Q // HEADS_KV
    shaped = flat.reshape(seq_count, tok_count, HEADS_KV, groups, HEAD)
    return shaped.transpose(0, 2, 3, 1, 4).reshape(seq_count, HEADS_KV, groups * tok_count, HEAD)


def ungroup(grouped, seq_count, tok_count):
    groups = HEADS_Q // HEADS_KV
    shaped = grouped.reshape(seq_count, HEADS_KV, groups, tok_count, HEAD)
    return shaped.transpose(0, 3, 1, 2, 4).reshape(seq_count * tok_count, HEADS_Q * HEAD)


def local(
    block_input,
    segment_ids,
    out_cotangent,
    attention_in,
    mixer_in,
    step_in,
    attention_out,
    mixer_out,
    gate_up,
    down_weight,
    gain_mixing,
    gain_feed,
    decay_log,
    step_bias,
    skip_gain,
    conv_weight,
    conv_bias,
):
    seq_count, tok_count, width = block_input.shape
    row_count = seq_count * tok_count
    length = tok_count * lax.axis_size("ctx")
    block = length if length <= 1024 else 512
    blocks = length // block
    groups = HEADS_Q // HEADS_KV
    query_width = HEADS_Q * HEAD
    key_width = HEADS_KV * HEAD
    score_scale = HEAD ** (-0.5)
    query_rows = groups * tok_count
    first = lax.axis_index("ctx") * tok_count
    own_rows = attention_in.shape[0]
    axes = ("dp", "ctx")
    entry = jnp.concatenate([attention_in, mixer_in, pad_columns(step_in)], axis=1)
    full_attention_in, full_mixer_in, full_step_in = cut_columns(
        lax.all_gather(entry, axes, axis=0, tiled=True),
        (attention_in.shape[1], mixer_in.shape[1], step_in.shape[1]),
    )
    tall = (attention_out, mixer_out, down_weight)
    folded = [fold_rows(weight, weight.shape[0], own_rows) for weight in tall]
    rest = lax.all_gather(
        jnp.concatenate(folded + [gate_up], axis=1), axes, axis=0, tiled=True
    )
    rest = cut_columns(rest, [weight.shape[1] for weight in folded] + [gate_up.shape[1]])
    full_attention_out, full_mixer_out, full_down = (
        unfold_rows(part, weight.shape[0], own_rows, width) for part, weight in zip(rest, tall)
    )
    full_gate_up = rest[3]
    source = block_input.reshape(row_count, width).astype(jnp.float32)
    normed = rms_scale(source, gain_mixing).astype(jnp.bfloat16)
    projected = jnp.dot(normed, full_attention_in, preferred_element_type=jnp.float32).astype(
        jnp.bfloat16
    )
    mixed_in = jnp.dot(normed, full_mixer_in, preferred_element_type=jnp.float32)
    step_raw = jnp.dot(normed, full_step_in, preferred_element_type=jnp.float32).reshape(
        seq_count, tok_count, SSM_HEADS
    )
    queries = group_queries(projected[:, :query_width], seq_count, tok_count)
    local_keys = (
        projected[:, query_width:].reshape(seq_count, tok_count, 2 * key_width).transpose(1, 0, 2)
    )
    local_segments = segment_ids.T
    keys_all, segments_all = (
        lax.all_gather(local_keys, "ctx", axis=0, tiled=True),
        lax.all_gather(local_segments, "ctx", axis=0, tiled=True),
    )
    query_pos = first + jnp.arange(query_rows) % tok_count
    query_segments = jnp.tile(segment_ids, (1, groups))
    segment_blocks = segments_all.reshape(blocks, block, seq_count)
    block_ids = jnp.arange(blocks)

    def scores_of(key_block, seg_block, block_id):
        keys = key_block[:, :, :key_width].reshape(block, seq_count, HEADS_KV, HEAD)
        scores = (
            jnp.einsum("sgrd,ksgd->sgrk", queries, keys, preferred_element_type=jnp.float32)
            * score_scale
        )
        key_pos = block_id * block + jnp.arange(block)
        allowed = (key_pos[None, None, None, :] <= query_pos[None, None, :, None]) & (
            seg_block.T[:, None, None, :] == query_segments[:, None, :, None]
        )
        return (scores, allowed)

    key_blocks = keys_all.reshape(blocks, block, seq_count, 2 * key_width)

    def gather_stats(carry, item):
        top, total = carry
        scores, allowed = scores_of(item[0], item[1], item[2])
        masked = jnp.where(allowed, scores, -1e30)
        new_top = jnp.maximum(top, jnp.max(masked, axis=-1))
        total = total * jnp.exp(top - new_top) + jnp.sum(
            jnp.where(allowed, jnp.exp(masked - new_top[..., None]), 0.0), axis=-1
        )
        return ((new_top, total), None)

    start_top = jnp.full((seq_count, HEADS_KV, query_rows), -1e30, jnp.float32)
    (top, total), _ = over_blocks(
        gather_stats,
        (start_top, jnp.zeros_like(start_top)),
        (key_blocks, segment_blocks, block_ids),
    )
    log_total = top + jnp.log(total)

    def weigh_values(accum, item):
        scores, allowed = scores_of(item[0], item[1], item[2])
        values = item[0][:, :, key_width:].reshape(block, seq_count, HEADS_KV, HEAD)
        probs = jnp.where(allowed, jnp.exp(scores - log_total[..., None]), 0.0).astype(jnp.bfloat16)
        return (
            accum
            + jnp.einsum("sgrk,ksgd->sgrd", probs, values, preferred_element_type=jnp.float32),
            None,
        )

    attended, _ = over_blocks(
        weigh_values, jnp.zeros(queries.shape, jnp.float32), (key_blocks, segment_blocks, block_ids)
    )
    attended = attended.astype(jnp.bfloat16)
    attended_flat = ungroup(attended, seq_count, tok_count)
    gate_part = mixed_in[:, :SSM_INNER]
    conv_width = mixed_in.shape[1] - SSM_INNER
    conv_in = mixed_in[:, SSM_INNER:].reshape(seq_count, tok_count, conv_width)
    positions = first + jnp.arange(tok_count)
    before_rows = from_behind(conv_in[:, tok_count - 3 :, :], "ctx", 1)
    extended = jnp.concatenate([before_rows, conv_in], axis=1)
    pre = conv_bias + conv_weight[3] * conv_in
    keep_masks = []
    for offset in (1, 2, 3):
        earlier_ids = segments_all[jnp.maximum(positions - offset, 0)].T
        keep_mask = (positions >= offset)[None, :] & (earlier_ids == segment_ids)
        keep_masks.append(keep_mask)
        pre = (
            pre
            + jnp.where(keep_mask[..., None], extended[:, 3 - offset : 3 - offset + tok_count], 0.0)
            * conv_weight[3 - offset]
        )
    converted = jax.nn.silu(pre)
    inner = converted[..., :SSM_INNER].reshape(seq_count, tok_count, SSM_HEADS, SSM_HEAD)
    write_map = converted[..., SSM_INNER : SSM_INNER + STATE]
    read_map = converted[..., SSM_INNER + STATE :]
    starts = (positions == 0)[None, :] | jnp.logical_not(keep_masks[0])
    local_map = jax.vmap(ssd_local, in_axes=(0, 0, 0, 0, None, None, None, 0, 0))
    partial_out, partial_state, decay_total, carried = local_map(
        inner, write_map, read_map, step_raw, decay_log, step_bias, skip_gain, starts, segment_ids
    )
    by_heads = SSM_HEADS % lax.axis_size("ctx") == 0
    if by_heads:
        decays = lax.all_gather(decay_total, "ctx")
        state_in = carried_by_heads(decays, partial_state, False)
    else:
        unit = (jnp.ones_like(decay_total), jnp.zeros_like(partial_state))
        state_in = carried_in((decay_total, partial_state), "ctx", chain, unit, False)[1]
    scanned = jax.vmap(add_state)(partial_out, carried, read_map, state_in)
    flat_scan = scanned.reshape(row_count, SSM_INNER)
    gated = (flat_scan * jax.nn.silu(gate_part)).astype(jnp.bfloat16)
    residual = (
        source
        + jnp.dot(attended_flat, full_attention_out, preferred_element_type=jnp.float32)
        + jnp.dot(gated, full_mixer_out, preferred_element_type=jnp.float32)
    )
    normed_two = rms_scale(residual, gain_feed).astype(jnp.bfloat16)
    gate_values = jnp.dot(normed_two, full_gate_up, preferred_element_type=jnp.float32)
    gate_in = gate_values[:, :FF]
    up_in = gate_values[:, FF:]
    active = (jax.nn.silu(gate_in) * up_in).astype(jnp.bfloat16)
    output = (residual + jnp.dot(active, full_down, preferred_element_type=jnp.float32)).astype(
        jnp.bfloat16
    )
    cotangent = out_cotangent.reshape(row_count, width)
    grad_down_weight = jnp.dot(active.T, cotangent, preferred_element_type=jnp.float32).astype(
        jnp.bfloat16
    )
    active_grad = jnp.dot(cotangent, full_down.T, preferred_element_type=jnp.float32)
    gate_grad = jnp.concatenate(
        [active_grad * up_in * silu_slope(gate_in), active_grad * jax.nn.silu(gate_in)], axis=1
    ).astype(jnp.bfloat16)
    grad_gate_up = jnp.dot(normed_two.T, gate_grad, preferred_element_type=jnp.float32).astype(
        jnp.bfloat16
    )
    feed_terms = jnp.concatenate(
        [grad_gate_up, fold_rows(grad_down_weight, down_weight.shape[0], own_rows)], axis=1
    )
    feed_sums = lax.psum_scatter(feed_terms, axes, scatter_dimension=0, tiled=True)
    normed_two_grad = jnp.dot(gate_grad, full_gate_up.T, preferred_element_type=jnp.float32)
    _, pull_two = jax.vjp(rms_scale, residual, gain_feed)
    residual_part, grad_gain_feed = pull_two(normed_two_grad)
    residual_grad = cotangent.astype(jnp.float32) + residual_part
    residual_half, _ = lax.optimization_barrier((residual_grad.astype(jnp.bfloat16), feed_terms))
    grad_attention_out = jnp.dot(attended_flat.T, residual_half, preferred_element_type=jnp.float32)
    grad_mixer_out = jnp.dot(gated.T, residual_half, preferred_element_type=jnp.float32)
    attended_grad = jnp.dot(
        residual_half, full_attention_out.T, preferred_element_type=jnp.float32
    ).astype(jnp.bfloat16)
    gated_grad = jnp.dot(residual_half, full_mixer_out.T, preferred_element_type=jnp.float32)
    gate_part_grad = gated_grad * flat_scan * silu_slope(gate_part)
    scan_grad = (gated_grad * jax.nn.silu(gate_part)).reshape(
        seq_count, tok_count, SSM_HEADS, SSM_HEAD
    )
    direct = jnp.einsum("sth,sthp,stn->shpn", carried, scan_grad, read_map, precision=highest)
    if by_heads:
        state_grad = carried_by_heads(decays, direct, True)
    else:
        state_grad = carried_in((decay_total, direct), "ctx", chain, unit, True)[1]

    def block_map(inner_v, write_v, read_v, step_v, decay_v, bias_v, skip_v, state_v):
        mapped = jax.vmap(ssd_block, in_axes=(0, 0, 0, 0, None, None, None, 0, 0, 0))
        return mapped(
            inner_v, write_v, read_v, step_v, decay_v, bias_v, skip_v, starts, segment_ids, state_v
        )

    _, pull_scan = jax.vjp(
        block_map, inner, write_map, read_map, step_raw, decay_log, step_bias, skip_gain, state_in
    )
    pulled = pull_scan((scan_grad, state_grad))
    converted_grad = jnp.concatenate(
        [pulled[0].reshape(seq_count, tok_count, SSM_INNER), pulled[1], pulled[2]], axis=2
    )
    pre_grad = converted_grad * silu_slope(pre)
    after_rows = from_behind(pre_grad[:, :3, :], "ctx", -1)
    ahead = jnp.concatenate([pre_grad, after_rows], axis=1)
    conv_in_grad = conv_weight[3] * pre_grad
    tap_grads = [None, None, None, jnp.sum(pre_grad * conv_in, axis=(0, 1))]
    for offset in (1, 2, 3):
        later_ids = segments_all[jnp.minimum(positions + offset, length - 1)].T
        later_mask = later_ids == segment_ids
        conv_in_grad = (
            conv_in_grad
            + jnp.where(later_mask[..., None], ahead[:, offset : offset + tok_count], 0.0)
            * conv_weight[3 - offset]
        )
        earlier_rows = jnp.where(
            keep_masks[offset - 1][..., None], extended[:, 3 - offset : 3 - offset + tok_count], 0.0
        )
        tap_grads[3 - offset] = jnp.sum(pre_grad * earlier_rows, axis=(0, 1))
    grad_conv_weight = jnp.stack(tap_grads, axis=0)
    grad_conv_bias = jnp.sum(pre_grad, axis=(0, 1))
    mixer_grad = jnp.concatenate(
        [gate_part_grad, conv_in_grad.reshape(row_count, conv_width)], axis=1
    ).astype(jnp.bfloat16)
    step_grad_half = pulled[3].reshape(row_count, SSM_HEADS).astype(jnp.bfloat16)
    out_grad = group_queries(attended_grad, seq_count, tok_count)
    deltas = jnp.sum(out_grad.astype(jnp.float32) * attended.astype(jnp.float32), axis=-1)

    def attention_grads(query_grad, item):
        scores, allowed = scores_of(item[0], item[1], item[2])
        keys = item[0][:, :, :key_width].reshape(block, seq_count, HEADS_KV, HEAD)
        values = item[0][:, :, key_width:].reshape(block, seq_count, HEADS_KV, HEAD)
        probs = jnp.where(allowed, jnp.exp(scores - log_total[..., None]), 0.0)
        value_grad = jnp.einsum(
            "sgrk,sgrd->ksgd",
            probs.astype(jnp.bfloat16),
            out_grad,
            preferred_element_type=jnp.float32,
        )
        prob_grad = jnp.einsum(
            "sgrd,ksgd->sgrk", out_grad, values, preferred_element_type=jnp.float32
        )
        score_grad = (probs * (prob_grad - deltas[..., None])).astype(jnp.bfloat16)
        query_grad = (
            query_grad
            + jnp.einsum("sgrk,ksgd->sgrd", score_grad, keys, preferred_element_type=jnp.float32)
            * score_scale
        )
        key_grad = (
            jnp.einsum("sgrk,sgrd->ksgd", score_grad, queries, preferred_element_type=jnp.float32)
            * score_scale
        )
        both = jnp.concatenate(
            [
                key_grad.reshape(block, seq_count, key_width),
                value_grad.reshape(block, seq_count, key_width),
            ],
            axis=2,
        )
        return (query_grad, both)

    query_grad, key_terms = over_blocks(
        attention_grads,
        jnp.zeros(queries.shape, jnp.float32),
        (key_blocks, segment_blocks, block_ids),
    )
    key_pieces = lax.all_to_all(
        key_terms.reshape(length, seq_count, 2 * key_width).astype(jnp.bfloat16),
        "ctx",
        split_axis=0,
        concat_axis=0,
        tiled=True,
    )
    key_sums = jnp.sum(
        key_pieces.reshape(-1, tok_count, seq_count, 2 * key_width).astype(jnp.float32), axis=0
    )
    kv_grad = key_sums.transpose(1, 0, 2).reshape(row_count, 2 * key_width)
    projected_grad = jnp.concatenate(
        [ungroup(query_grad, seq_count, tok_count), kv_grad], axis=1
    ).astype(jnp.bfloat16)
    grad_attention_in = jnp.dot(normed.T, projected_grad, preferred_element_type=jnp.float32)
    grad_mixer_in = jnp.dot(normed.T, mixer_grad, preferred_element_type=jnp.float32)
    grad_step_in = jnp.dot(normed.T, step_grad_half, preferred_element_type=jnp.float32)
    normed_grad = (
        jnp.dot(projected_grad, full_attention_in.T, preferred_element_type=jnp.float32)
        + jnp.dot(mixer_grad, full_mixer_in.T, preferred_element_type=jnp.float32)
        + jnp.dot(step_grad_half, full_step_in.T, preferred_element_type=jnp.float32)
    )
    _, pull_one = jax.vjp(rms_scale, source, gain_mixing)
    source_part, grad_gain_mixing = pull_one(normed_grad)
    input_grad = residual_grad + source_part
    others = [
        grad_attention_in.astype(jnp.bfloat16),
        grad_mixer_in.astype(jnp.bfloat16),
        fold_rows(grad_attention_out.astype(jnp.bfloat16), attention_out.shape[0], own_rows),
        fold_rows(grad_mixer_out.astype(jnp.bfloat16), mixer_out.shape[0], own_rows),
        pad_columns(grad_step_in.astype(jnp.bfloat16)),
    ]
    other_sums = lax.psum_scatter(
        jnp.concatenate(others, axis=1), axes, scatter_dimension=0, tiled=True
    )
    feed_parts = cut_columns(
        feed_sums, (gate_up.shape[1], feed_sums.shape[1] - gate_up.shape[1])
    )
    other_parts = cut_columns(other_sums, [part.shape[1] for part in others])
    weight_sums = [
        part.astype(jnp.float32)
        for part in (
            other_parts[0],
            other_parts[1],
            other_parts[4][:, :SSM_HEADS],
            unfold_rows(other_parts[2], attention_out.shape[0], own_rows, width),
            unfold_rows(other_parts[3], mixer_out.shape[0], own_rows, width),
            feed_parts[0],
            unfold_rows(feed_parts[1], down_weight.shape[0], own_rows, width),
        )
    ]
    small_sums = lax.psum(
        (
            grad_gain_mixing,
            grad_gain_feed,
            pulled[4],
            pulled[5],
            pulled[6],
            grad_conv_weight,
            grad_conv_bias,
        ),
        ("dp", "ctx"),
    )
    return (
        output.reshape(seq_count, tok_count, width),
        input_grad.reshape(seq_count, tok_count, width),
        weight_sums[0],
        weight_sums[1],
        weight_sums[2],
        weight_sums[3],
        weight_sums[4],
        weight_sums[5],
        weight_sums[6],
        small_sums[0],
        small_sums[1],
        small_sums[2],
        small_sums[3],
        small_sums[4],
        small_sums[5],
        small_sums[6],
    )

def split_heads(ctx):
    return HEADS_Q % ctx == 0 and SSM_HEADS % ctx == 0 and ctx % HEADS_KV == 0


def entry_layout(ctx):
    heads = SSM_HEADS // ctx
    widths = [HEADS_Q // ctx * HEAD, HEAD, HEAD, heads * SSM_HEAD, heads * SSM_HEAD, STATE, STATE, heads]
    return widths + [-sum(widths) % 128]


def entry_slabs(attention_in, mixer_in, step_in, ctx):
    rows = attention_in.shape[0]
    share = ctx // HEADS_KV
    query_width = HEADS_Q * HEAD
    key_width = HEADS_KV * HEAD

    def parts(array, count):
        return array.reshape(rows, count, -1).transpose(1, 0, 2)

    kv = [
        jnp.repeat(parts(attention_in[:, at : at + key_width], HEADS_KV), share, axis=0)
        for at in (query_width, query_width + key_width)
    ]
    both = jnp.broadcast_to(mixer_in[None, :, 2 * SSM_INNER :], (ctx, rows, 2 * STATE))
    pieces = [
        parts(attention_in[:, :query_width], ctx),
        kv[0],
        kv[1],
        parts(mixer_in[:, :SSM_INNER], ctx),
        parts(mixer_in[:, SSM_INNER : 2 * SSM_INNER], ctx),
        both,
        parts(step_in, ctx),
        jnp.zeros((ctx, rows, entry_layout(ctx)[-1]), jnp.bfloat16),
    ]
    return jnp.concatenate(pieces, axis=2)


def entry_unslab(slabs, ctx):
    rows = slabs.shape[1]
    share = ctx // HEADS_KV
    q, k, v, gate, inner, write, read, step, _ = [
        slabs[:, :, at : at + width]
        for at, width in zip(offsets(entry_layout(ctx)), entry_layout(ctx))
    ]

    def flat(part):
        return part.transpose(1, 0, 2).reshape(rows, -1)

    def shared(part):
        return flat(jnp.sum(part.reshape(HEADS_KV, share, rows, HEAD), axis=1))

    attention = jnp.concatenate([flat(q), shared(k), shared(v)], axis=1)
    mixer = jnp.concatenate(
        [flat(gate), flat(inner), jnp.sum(write, axis=0), jnp.sum(read, axis=0)], axis=1
    )
    return attention, mixer, flat(step)


def offsets(widths):
    at, places = 0, []
    for width in widths:
        places.append(at)
        at += width
    return places


def scan_chunks(inner, write_map, read_map, step_raw, decay_log, step_bias, skip_gain, starts, segments):
    local_map = jax.vmap(ssd_local, in_axes=(0, 0, 0, 0, None, None, None, 0, 0))
    result, state, _, carried = local_map(
        inner, write_map, read_map, step_raw, decay_log, step_bias, skip_gain, starts, segments
    )
    chunks = inner.shape[0]
    step = jax.nn.softplus(step_raw + step_bias)
    rates = jnp.sum(step * -jnp.exp(decay_log), axis=1)
    order = jnp.arange(chunks)
    lower = (order[None, :] <= order[:, None]).astype(jnp.float32)
    sums = jnp.dot(lower, rates, precision=highest)
    last = segments[:, -1]
    before = jnp.concatenate([last[:1], last[:-1]])
    open_span = (order[None, :] < order[:, None]) & (last[None, :] == before[:, None])
    sums_before = jnp.concatenate([jnp.zeros_like(sums[:1]), sums[:-1]], axis=0)
    spans = jnp.where(
        open_span[None], sums_before.T[:, :, None] - sums.T[:, None, :], -1e30
    )
    state_in = jnp.einsum("hji,ihpn->jhpn", jnp.exp(spans), state, precision=highest)
    return jax.vmap(add_state)(result, carried, read_map, state_in)


def conv_pre(rows, weight, bias, keeps):
    pre = bias + weight[3] * rows
    for offset in (1, 2, 3):
        shifted = jnp.pad(rows[:-offset], ((offset, 0), (0, 0)))
        pre = pre + jnp.where(keeps[offset - 1][:, None], shifted, 0.0) * weight[3 - offset]
    return pre


MESH = pl.DeviceIdType.MESH
IN_VMEM = pl.BlockSpec(memory_space=pltpu.VMEM)
ANYWHERE = pl.BlockSpec(memory_space=pl.ANY)


def remote(source, target, send, recv, peer):
    return pltpu.make_async_remote_copy(
        src_ref=source,
        dst_ref=target,
        send_sem=send,
        recv_sem=recv,
        device_id=peer,
        device_id_type=MESH,
    )


def arrived(ref, recv, peer):
    remote(ref, ref, recv, recv, peer).wait_recv()


class Here:
    def __init__(self, dp, ctx):
        self.dp, self.ctx, self.pairs = dp, ctx, ctx // 2
        self.d, self.me = lax.axis_index("dp"), lax.axis_index("ctx")
        self.z, self.c = self.me // 2, self.me % 2
        self.sibling = (self.d, self.z * 2 + 1 - self.c)

    def dp_peers(self):
        return [(lax.rem(self.d + k, self.dp), self.me) for k in range(1, self.dp)]

    def ctx_peers(self):
        return [(self.d, lax.rem(self.me + k, self.ctx)) for k in range(1, self.ctx)]

    def greet(self, peers):
        sem = pltpu.get_barrier_semaphore()
        for peer in peers:
            pl.semaphore_signal(sem, inc=1, device_id=peer, device_id_type=MESH)
        pl.semaphore_wait(sem, len(peers))


class Relay:
    def __init__(self, here, block, slots, send, recv, local):
        self.here, self.block, self.slots = here, block, slots
        self.send, self.recv, self.local = send, recv, local
        self.up = (here.d, (here.z + 1) * 2 + here.c)
        self.down = (here.d, (here.z - 1) * 2 + here.c)
        self.has_up, self.has_down = here.z < here.pairs - 1, here.z > 0

    @staticmethod
    def scratch(pairs):
        return [
            pltpu.SemaphoreType.DMA((4 * pairs,)),
            pltpu.SemaphoreType.DMA((2 * pairs,)),
            pltpu.SemaphoreType.DMA,
        ]

    def slot(self, z, c):
        return self.slots.at[z * 2 + c]

    def begin(self):
        h, n = self.here, self.here.pairs
        own = self.slot(h.z, h.c)
        pltpu.make_async_copy(self.block, own, self.local).start()

        @pl.when(self.has_up)
        def _():
            remote(self.block, own, self.send.at[0], self.recv.at[h.me], self.up).start()

        @pl.when(self.has_down)
        def _():
            remote(self.block, own, self.send.at[n], self.recv.at[h.me], self.down).start()

        remote(self.block, own, self.send.at[2 * n], self.recv.at[h.me], h.sibling).start()

    def hop(self, s):
        h, n = self.here, self.here.pairs
        low, high = h.z - s, h.z + s

        @pl.when(low >= 0)
        def _():
            ref, recv = self.slot(low, h.c), self.recv.at[low * 2 + h.c]
            arrived(ref, recv, h.sibling)

            @pl.when(self.has_up)
            def _():
                remote(ref, ref, self.send.at[s], recv, self.up).start()

            remote(ref, ref, self.send.at[2 * n + 2 * s - 1], recv, h.sibling).start()

        @pl.when(high < n)
        def _():
            ref, recv = self.slot(high, h.c), self.recv.at[high * 2 + h.c]
            arrived(ref, recv, h.sibling)

            @pl.when(self.has_down)
            def _():
                remote(ref, ref, self.send.at[n + s], recv, self.down).start()

            remote(ref, ref, self.send.at[2 * n + 2 * s], recv, h.sibling).start()

    def end(self):
        h, n = self.here, self.here.pairs
        for z in range(n):
            arrived(self.slot(z, 1 - h.c), self.recv.at[z * 2 + 1 - h.c], h.sibling)
        own = self.slot(h.z, h.c)

        def sent(index):
            remote(own, own, self.send.at[index], self.recv.at[0], h.sibling).wait_send()

        for s in range(n):
            low, high = h.z - s, h.z + s
            pl.when((low >= 0) & self.has_up)(functools.partial(sent, s))
            pl.when((high < n) & self.has_down)(functools.partial(sent, n + s))
            if s == 0:
                sent(2 * n)
            else:
                pl.when(low >= 0)(functools.partial(sent, 2 * n + 2 * s - 1))
                pl.when(high < n)(functools.partial(sent, 2 * n + 2 * s))
        pltpu.make_async_copy(self.block, own, self.local).wait()


class Spread:
    def __init__(self, here, block, slots, send, recv, local):
        self.here, self.block, self.slots = here, block, slots
        self.send, self.recv, self.local = send, recv, local

    @staticmethod
    def scratch(dp):
        return [
            pltpu.SemaphoreType.DMA((dp,)),
            pltpu.SemaphoreType.DMA((dp,)),
            pltpu.SemaphoreType.DMA,
        ]

    def begin(self):
        h = self.here
        pltpu.make_async_copy(self.block, self.slots.at[h.d], self.local).start()
        self.copies = [
            remote(self.block, self.slots.at[h.d], self.send.at[k], self.recv.at[h.d], peer)
            for k, peer in enumerate(h.dp_peers())
        ]
        for copy in self.copies:
            copy.start()

    def end(self):
        h = self.here
        for peer in h.dp_peers():
            arrived(self.slots.at[peer[0]], self.recv.at[peer[0]], peer)
        for copy in self.copies:
            copy.wait_send()
        pltpu.make_async_copy(self.block, self.slots.at[h.d], self.local).wait()


class Total:
    def __init__(self, here, terms, got, result, send, recv):
        self.here, self.terms, self.got, self.result = here, terms, got, result
        self.send, self.recv = send, recv

    @staticmethod
    def scratch(dp, shape):
        return [
            pltpu.VMEM((dp,) + shape, jnp.bfloat16),
            pltpu.SemaphoreType.DMA((dp,)),
            pltpu.SemaphoreType.DMA((dp,)),
        ]

    def begin(self):
        h = self.here
        self.copies = [
            remote(
                self.terms.at[peer[0]], self.got.at[h.d], self.send.at[k], self.recv.at[h.d], peer
            )
            for k, peer in enumerate(h.dp_peers())
        ]
        for copy in self.copies:
            copy.start()

    def end(self):
        h = self.here
        total = self.terms[h.d].astype(jnp.float32)
        for peer in h.dp_peers():
            arrived(self.got.at[peer[0]], self.recv.at[peer[0]], peer)
            total = total + self.got[peer[0]].astype(jnp.float32)
        self.result[...] = total.astype(self.result.dtype)

    def leave(self):
        for copy in self.copies:
            copy.wait_send()


class Swap:
    def __init__(self, here, blocks, slots, send, recv, local):
        self.here, self.blocks, self.slots = here, blocks, slots
        self.send, self.recv, self.local = send, recv, local

    @staticmethod
    def scratch(ctx):
        return [
            pltpu.SemaphoreType.DMA((ctx,)),
            pltpu.SemaphoreType.DMA((ctx,)),
            pltpu.SemaphoreType.DMA,
        ]

    def begin(self):
        h = self.here
        pltpu.make_async_copy(self.blocks.at[h.me], self.slots.at[h.me], self.local).start()
        self.copies = []
        for k, peer in enumerate(h.ctx_peers()):
            copy = remote(
                self.blocks.at[peer[1]],
                self.slots.at[h.me],
                self.send.at[k],
                self.recv.at[h.me],
                peer,
            )
            copy.start()
            self.copies.append(copy)

    def wait(self, index):
        arrived(self.slots.at[index], self.recv.at[index], self.here.sibling)

    def leave(self):
        h = self.here
        for copy in self.copies:
            copy.wait_send()
        pltpu.make_async_copy(self.blocks.at[h.me], self.slots.at[h.me], self.local).wait()


class SumTokens:
    def __init__(self, here, left, right, turned, total, away, pair, out, got, *sems):
        self.here, self.left, self.right, self.turned, self.total = here, left, right, turned, total
        self.away, self.pair, self.out, self.got = away, pair, out, got
        self.away_send, self.away_recv, self.send, self.recv = sems
        self.order = sorted(range(1, here.pairs), key=lambda k: -min(k, here.pairs - k)) + [0]

    @staticmethod
    def scratch(pairs, rows, width):
        block = pltpu.VMEM((pairs, rows, width), jnp.bfloat16)
        return [block] * 4 + [pltpu.SemaphoreType.DMA((pairs,))] * 4

    def term(self, z, c):
        rows = self.total.shape[0]
        part = self.left[pl.ds(pl.multiple_of((z * 2 + c) * rows, rows), rows), :]
        dims = (((1,), (1 if self.turned else 0,)), ((), ()))
        return lax.dot_general(part, self.right[...], dims, preferred_element_type=jnp.float32)

    def peer(self, k):
        h = self.here
        return (h.d, lax.rem(h.z + k, h.pairs) * 2 + h.c)

    def to_sibling(self, k):
        return remote(
            self.away.at[k], self.pair.at[k], self.away_send.at[k], self.away_recv.at[k],
            self.here.sibling,
        )

    def to_pair(self, k):
        return remote(
            self.out.at[k], self.got.at[k], self.send.at[k], self.recv.at[k], self.peer(k)
        )

    def begin(self):
        h = self.here
        for k in self.order:
            self.away[k] = self.term(lax.rem(h.z + k, h.pairs), 1 - h.c).astype(jnp.bfloat16)
            self.to_sibling(k).start()
        for k in self.order:
            term = self.term(lax.rem(h.z + k, h.pairs), h.c)
            self.to_sibling(k).wait_recv()
            term = term + self.pair[k].astype(jnp.float32)
            if k:
                self.out[k] = term.astype(jnp.bfloat16)
                self.to_pair(k).start()
            else:
                self.total[...] = term

    def end(self):
        for k in self.order[::-1]:
            if k:
                self.to_pair(k).wait_recv()
                self.total[...] += self.got[k].astype(jnp.float32)

    def leave(self):
        for k in self.order:
            self.to_sibling(k).wait_send()
            if k:
                self.to_pair(k).wait_send()


def call(kernel, ident, outs, out_specs, in_specs, scratch, *arrays):
    return pl.pallas_call(
        kernel,
        out_shape=outs,
        in_specs=in_specs,
        out_specs=out_specs,
        scratch_shapes=scratch,
        compiler_params=pltpu.CompilerParams(
            collective_id=ident, has_side_effects=True, vmem_limit_bytes=48 * 2**20
        ),
    )(*arrays)


def like(shape, dtype=jnp.bfloat16):
    return jax.ShapeDtypeStruct(shape, dtype)


def gather_tokens(block, ident):
    dp, ctx = lax.axis_size("dp"), lax.axis_size("ctx")

    def kernel(block_ref, slots_ref, *sems):
        here = Here(dp, ctx)
        relay = Relay(here, block_ref, slots_ref, *sems)
        here.greet(here.ctx_peers())
        relay.begin()
        for s in range(1, here.pairs):
            relay.hop(s)
        relay.end()

    whole = call(
        kernel, ident, like((ctx,) + block.shape, block.dtype), ANYWHERE, [ANYWHERE],
        Relay.scratch(ctx // 2), block,
    )
    return whole.reshape((-1,) + block.shape[1:])


def enter(normed, segments, entry, feed):
    dp, ctx = lax.axis_size("dp"), lax.axis_size("ctx")
    relay_sems, swap_sems = Relay.scratch(ctx // 2), Swap.scratch(ctx)

    def kernel(normed_ref, seg_ref, entry_ref, feed_ref, all_ref, segs_ref, full_ref, feeds_ref, *sems):
        here = Here(dp, ctx)
        tokens = Relay(here, normed_ref, all_ref, *sems[0:3])
        ids = Relay(here, seg_ref, segs_ref, *sems[3:6])
        slabs = Swap(here, entry_ref, full_ref.at[here.d], *sems[6:9])
        others = Swap(here, feed_ref, feeds_ref, *sems[9:12])
        pass_send, pass_recv = sems[12:14]
        peers = here.dp_peers()
        here.greet(peers + here.ctx_peers())
        passed = []

        def pass_on(source, index):
            for k, peer in enumerate(peers):
                copy = remote(
                    source,
                    full_ref.at[here.d, index],
                    pass_send.at[k, index],
                    pass_recv.at[here.d, index],
                    peer,
                )
                copy.start()
                passed.append(copy)

        slabs.begin()
        pass_on(entry_ref.at[here.me], here.me)
        tokens.begin()
        ids.begin()

        def forward(index):
            slabs.wait(index)
            pass_on(full_ref.at[here.d, index], index)

        forward(here.z * 2 + 1 - here.c)
        others.begin()
        for s in range(1, here.pairs):
            for core in (0, 1):
                forward(lax.rem(here.z + s, here.pairs) * 2 + core)
            tokens.hop(s)
            ids.hop(s)
        for peer in peers:
            for index in range(ctx):
                arrived(full_ref.at[peer[0], index], pass_recv.at[peer[0], index], peer)
        for peer in here.ctx_peers():
            others.wait(peer[1])
        tokens.end()
        ids.end()
        slabs.leave()
        others.leave()
        for copy in passed:
            copy.wait_send()

    return call(
        kernel,
        0,
        (
            like((ctx,) + normed.shape),
            like((ctx,) + segments.shape, segments.dtype),
            like((dp,) + entry.shape),
            like(feed.shape),
        ),
        (ANYWHERE,) * 4,
        [ANYWHERE] * 4,
        relay_sems * 2 + swap_sems * 2 + [pltpu.SemaphoreType.DMA((dp, ctx))] * 2,
        normed,
        segments,
        entry,
        feed,
    )


def sum_and_spread(left, right, blocks, ident):
    dp, ctx = lax.axis_size("dp"), lax.axis_size("ctx")
    rows, width = left.shape[0] // ctx, right.shape[1]
    count = len(blocks)

    def kernel(left_ref, right_ref, *refs):
        blocks_in, total, slots = refs[:count], refs[count], refs[count + 1 : 2 * count + 1]
        sems = refs[2 * count + 1 :]
        here = Here(dp, ctx)
        sums = SumTokens(here, left_ref, right_ref, False, total, *sems[:8])
        spreads = [
            Spread(here, block, slot, *sems[8 + 3 * i : 11 + 3 * i])
            for i, (block, slot) in enumerate(zip(blocks_in, slots))
        ]
        here.greet(here.dp_peers() + here.ctx_peers())
        for spread in spreads:
            spread.begin()
        sums.begin()
        sums.end()
        for spread in spreads:
            spread.end()
        sums.leave()

    return call(
        kernel,
        ident,
        (like((rows, width), jnp.float32), *[like((dp,) + block.shape) for block in blocks]),
        (IN_VMEM,) + (ANYWHERE,) * count,
        [IN_VMEM, IN_VMEM] + [ANYWHERE] * count,
        SumTokens.scratch(ctx // 2, rows, width) + Spread.scratch(dp) * count,
        left,
        right,
        *blocks,
    )


def sum_and_total(left, right, terms, ident):
    dp, ctx = lax.axis_size("dp"), lax.axis_size("ctx")
    rows, width = left.shape[0] // ctx, right.shape[0]
    count = len(terms)

    def kernel(left_ref, right_ref, *refs):
        terms_in, total, results = refs[:count], refs[count], refs[count + 1 : 2 * count + 1]
        sems = refs[2 * count + 1 :]
        here = Here(dp, ctx)
        sums = SumTokens(here, left_ref, right_ref, True, total, *sems[:8])
        totals = [
            Total(here, term, sems[8 + 3 * i], result, *sems[9 + 3 * i : 11 + 3 * i])
            for i, (term, result) in enumerate(zip(terms_in, results))
        ]
        here.greet(here.dp_peers() + here.ctx_peers())
        for part in totals:
            part.begin()
        sums.begin()
        for part in totals:
            part.end()
        sums.end()
        sums.leave()
        for part in totals:
            part.leave()

    scratch = SumTokens.scratch(ctx // 2, rows, width)
    for term in terms:
        scratch = scratch + Total.scratch(dp, term.shape[1:])
    return call(
        kernel,
        ident,
        (like((rows, width), jnp.float32), *[like(term.shape[1:]) for term in terms]),
        (IN_VMEM,) * (1 + count),
        [IN_VMEM] * (2 + count),
        scratch,
        left,
        right,
        *terms,
    )


def leave(grads, entry, source, residual_grad, gain, entry_terms, feed_sums, small):
    dp, ctx = lax.axis_size("dp"), lax.axis_size("ctx")
    rows, width = source.shape
    slab = entry_terms.shape[2:]

    def kernel(
        grads_ref, entry_ref, source_ref, res_ref, gain_ref, terms_ref, feed_ref, small_ref,
        input_ref, slabs_ref, feeds_ref, smalls_ref, gains_ref, normed_grad, *sems,
    ):
        here = Here(dp, ctx)
        peers = here.dp_peers()
        sums = SumTokens(here, grads_ref, entry_ref, True, normed_grad, *sems[0:8])
        feeds = Swap(here, feed_ref, feeds_ref, *sems[8:11])
        got, term_send, term_recv, mine, slab_send, slab_recv = sems[11:17]
        small_got, gain_got = sems[17:19]
        small_send, small_recv, gain_send, gain_recv = sems[19:23]
        last_send, last_recv, lastg_send, lastg_recv = sems[23:27]
        here.greet(peers + here.ctx_peers())
        order = [lax.rem(here.me + k, ctx) for k in list(range(1, ctx)) + [0]]

        def term_copy(k, index):
            return remote(
                terms_ref.at[peers[k][0], index],
                got.at[here.d, index],
                term_send.at[k, index],
                term_recv.at[here.d, index],
                peers[k],
            )

        for index in order:
            for k in range(dp - 1):
                term_copy(k, index).start()
        small_copies = []
        for k, peer in enumerate(peers):
            copy = remote(
                small_ref, small_got.at[here.d], small_send.at[k], small_recv.at[here.d], peer
            )
            copy.start()
            small_copies.append(copy)
        sums.begin()
        feeds.begin()

        def slab_copy(j):
            return remote(
                mine.at[order[j]], slabs_ref.at[here.me], slab_send.at[j], slab_recv.at[here.me],
                (here.d, order[j]),
            )

        for j, index in enumerate(order):
            total = terms_ref[here.d, index].astype(jnp.float32)
            for peer in peers:
                arrived(got.at[peer[0], index], term_recv.at[peer[0], index], peer)
                total = total + got[peer[0], index].astype(jnp.float32)
            total = total.astype(jnp.bfloat16)
            if j < ctx - 1:
                mine[index] = total
                slab_copy(j).start()
            else:
                slabs_ref[here.me] = total
        sums.end()
        x, grad = source_ref[...], normed_grad[...]
        scale = lax.rsqrt(jnp.mean(x * x, axis=-1, keepdims=True) + 1e-05)
        scaled = grad * gain_ref[...]
        inner = jnp.mean(x * scaled, axis=-1, keepdims=True)
        input_ref[...] = res_ref[...] + scale * scaled - x * (scale * scale * scale * inner)
        gain_got[here.d] = jnp.sum(grad * (x * scale), axis=0, keepdims=True)
        for k, peer in enumerate(peers):
            copy = remote(
                gain_got.at[here.d], gain_got.at[here.d], gain_send.at[k], gain_recv.at[here.d], peer
            )
            copy.start()
            small_copies.append(copy)
        small_got[here.d] = small_ref[...]
        for peer in peers:
            arrived(small_got.at[peer[0]], small_recv.at[peer[0]], peer)
        total = small_got[0]
        for d in range(1, dp):
            total = total + small_got[d]
        smalls_ref[here.me] = total
        last = []
        for k, peer in enumerate(here.ctx_peers()):
            copy = remote(
                smalls_ref.at[here.me], smalls_ref.at[here.me], last_send.at[k],
                last_recv.at[here.me], peer,
            )
            copy.start()
            last.append(copy)
        for peer in peers:
            arrived(gain_got.at[peer[0]], gain_recv.at[peer[0]], peer)
        total = gain_got[0]
        for d in range(1, dp):
            total = total + gain_got[d]
        gains_ref[here.me] = total
        for k, peer in enumerate(here.ctx_peers()):
            copy = remote(
                gains_ref.at[here.me], gains_ref.at[here.me], lastg_send.at[k],
                lastg_recv.at[here.me], peer,
            )
            copy.start()
            last.append(copy)
        for peer in here.ctx_peers():
            arrived(slabs_ref.at[peer[1]], slab_recv.at[peer[1]], peer)
            feeds.wait(peer[1])
            arrived(smalls_ref.at[peer[1]], last_recv.at[peer[1]], peer)
            arrived(gains_ref.at[peer[1]], lastg_recv.at[peer[1]], peer)
        sums.leave()
        feeds.leave()
        for index in order:
            for k in range(dp - 1):
                term_copy(k, index).wait_send()
        for j in range(ctx - 1):
            slab_copy(j).wait_send()
        for copy in small_copies + last:
            copy.wait_send()

    dma = pltpu.SemaphoreType.DMA
    scratch = (
        [pltpu.VMEM((rows, width), jnp.float32)]
        + SumTokens.scratch(ctx // 2, rows, width)
        + Swap.scratch(ctx)
        + [
            pltpu.VMEM((dp, ctx) + slab, jnp.bfloat16),
            dma((dp, ctx)),
            dma((dp, ctx)),
            pltpu.VMEM((ctx,) + slab, jnp.bfloat16),
            dma((ctx,)),
            dma((ctx,)),
        ]
        + [
            pltpu.VMEM((dp,) + small.shape, jnp.float32),
            pltpu.VMEM((dp, 1, width), jnp.float32),
        ]
        + [dma((dp,))] * 4
        + [dma((ctx,))] * 4
    )
    return call(
        kernel,
        5,
        (
            like((rows, width), jnp.float32),
            like((ctx,) + slab),
            like(feed_sums.shape),
            like((ctx,) + small.shape, jnp.float32),
            like((ctx, 1, width), jnp.float32),
        ),
        (IN_VMEM,) * 5,
        [IN_VMEM] * 8,
        scratch,
        grads,
        entry,
        source,
        residual_grad,
        gain,
        entry_terms,
        feed_sums,
        small,
    )


def gather_dp(block):
    return lax.all_gather(block, "dp", axis=0, tiled=True)


def sum_dp(terms):
    return lax.psum_scatter(terms.astype(jnp.bfloat16), "dp", scatter_dimension=0, tiled=True)


def across(left, right):
    return jnp.dot(left.T, right, preferred_element_type=jnp.float32).astype(jnp.bfloat16)


def split_local(
    block_input,
    segment_ids,
    out_cotangent,
    attention_in,
    mixer_in,
    step_in,
    attention_out,
    mixer_out,
    gate_up,
    down_weight,
    gain_mixing,
    gain_feed,
    decay_log,
    step_bias,
    skip_gain,
    conv_weight,
    conv_bias,
):
    ctx, dp = lax.axis_size("ctx"), lax.axis_size("dp")
    mine = lax.axis_index("ctx")
    tok_count, width = block_input.shape[1:]
    length = tok_count * ctx
    heads = SSM_HEADS // ctx
    query_heads = HEADS_Q // ctx
    score_scale = HEAD ** (-0.5)
    layout = entry_layout(ctx)
    places = offsets(layout)
    rows = attention_in.shape[0]
    hidden = down_weight.shape[0]
    slabs = entry_slabs(attention_in, mixer_in, step_in, ctx)
    gate_slabs = gate_up.reshape(rows, 2, dp, ctx, hidden).transpose(3, 0, 1, 2, 4)
    gate_slabs = gate_slabs.reshape(ctx, rows, 2 * dp * hidden)
    route = [(i, (i % dp) * ctx + i // dp) for i in range(dp * ctx)]
    back = [(target, start) for start, target in route]
    outs = lax.ppermute(jnp.concatenate([attention_out, mixer_out], axis=0), ("dp", "ctx"), route)
    own_attention, own_mixer = attention_out.shape[0], mixer_out.shape[0]
    outs = gather_dp(outs).reshape(dp, own_attention + own_mixer, width)
    attention_rows = outs[:, :own_attention].reshape(-1, width)
    mixer_rows = outs[:, own_attention:].reshape(-1, width)

    source = block_input.reshape(tok_count, width).astype(jnp.float32)
    cotangent = out_cotangent.reshape(tok_count, width)
    normed_own = rms_scale(source, gain_mixing).astype(jnp.bfloat16)
    normed, segments, entry, feed_slabs = enter(normed_own, segment_ids, slabs, gate_slabs)
    normed, segments = normed.reshape(length, width), segments.reshape(length)
    entry = entry.reshape(dp * ctx * rows, -1)
    cotangents = lax.all_gather(cotangent, "ctx", axis=0, tiled=True)
    mixed = jnp.dot(normed, entry, preferred_element_type=jnp.float32)
    q, k, v, gate_part, inner_in, write_in, read_in, step_raw, _ = [
        mixed[:, at : at + size] for at, size in zip(places, layout)
    ]
    conv_in = mixed[:, places[4] : places[7]]

    queries = q.astype(jnp.bfloat16).reshape(length, query_heads, HEAD).transpose(1, 0, 2)
    keys, values = k.astype(jnp.bfloat16), v.astype(jnp.bfloat16)
    order = jnp.arange(length)
    allowed = (order[None, :] <= order[:, None]) & (segments[None, :] == segments[:, None])
    scores = (
        jnp.einsum("hqd,kd->hqk", queries, keys, preferred_element_type=jnp.float32) * score_scale
    )
    masked = jnp.where(allowed, scores, -1e30)
    top = jnp.max(masked, axis=-1, keepdims=True)
    total = jnp.sum(jnp.where(allowed, jnp.exp(masked - top), 0.0), axis=-1, keepdims=True)
    log_total = top + jnp.log(total)
    probs = jnp.where(allowed, jnp.exp(scores - log_total), 0.0)
    probs_half = probs.astype(jnp.bfloat16)
    attended = jnp.einsum(
        "hqk,kd->hqd", probs_half, values, preferred_element_type=jnp.float32
    ).astype(jnp.bfloat16)
    attended_flat = attended.transpose(1, 0, 2).reshape(length, query_heads * HEAD)

    own = lambda array, at, size: lax.dynamic_slice_in_dim(array, at + mine * size, size, axis=-1)
    conv_own = lambda array: jnp.concatenate(
        [own(array, 0, heads * SSM_HEAD), array[..., SSM_INNER:]], axis=-1
    )
    taps, bias = conv_own(conv_weight), conv_own(conv_bias)
    keeps = []
    for offset in (1, 2, 3):
        earlier = jnp.concatenate([jnp.full((offset,), -1, segments.dtype), segments[:-offset]])
        keeps.append(earlier == segments)
    pre = conv_pre(conv_in, taps, bias, keeps)
    converted = jax.nn.silu(pre)
    starts = jnp.logical_not(keeps[0])
    chunked = lambda array: array.reshape((ctx, tok_count) + array.shape[1:])

    def scan_map(converted_v, step_v, decay_v, bias_v, skip_v):
        inner = converted_v[:, : heads * SSM_HEAD].reshape(length, heads, SSM_HEAD)
        write_map = converted_v[:, heads * SSM_HEAD : heads * SSM_HEAD + STATE]
        read_map = converted_v[:, heads * SSM_HEAD + STATE :]
        return scan_chunks(
            chunked(inner),
            chunked(write_map),
            chunked(read_map),
            chunked(step_v),
            decay_v,
            bias_v,
            skip_v,
            chunked(starts),
            chunked(segments),
        ).reshape(length, heads * SSM_HEAD)

    scanned, pull_scan = jax.vjp(
        scan_map,
        converted,
        step_raw,
        own(decay_log, 0, heads),
        own(step_bias, 0, heads),
        own(skip_gain, 0, heads),
    )
    gated = (scanned * jax.nn.silu(gate_part)).astype(jnp.bfloat16)
    mixed_out = jnp.concatenate([attended_flat, gated], axis=1)
    out_rows = jnp.concatenate([attention_rows, mixer_rows], axis=0)
    mixing_out, feed_in, feed_out = sum_and_spread(
        mixed_out, out_rows, (feed_slabs.reshape(ctx * rows, -1), down_weight), 1
    )
    feed_in = feed_in.reshape(dp * ctx * rows, -1)
    feed_out = feed_out.reshape(dp * hidden, width)
    residual = source + mixing_out

    normed_two_own, pull_two = jax.vjp(rms_scale, residual, gain_feed)
    normed_two = gather_tokens(normed_two_own.astype(jnp.bfloat16), 2)
    gate_values = jnp.dot(normed_two, feed_in, preferred_element_type=jnp.float32)
    gate_in, up_in = gate_values[:, : dp * hidden], gate_values[:, dp * hidden :]
    active = (jax.nn.silu(gate_in) * up_in).astype(jnp.bfloat16)
    output = (
        residual
        + lax.psum_scatter(
            jnp.dot(active, feed_out, preferred_element_type=jnp.float32).astype(jnp.bfloat16),
            "ctx",
            scatter_dimension=0,
            tiled=True,
        ).astype(jnp.float32)
    ).astype(jnp.bfloat16)
    active_grad = jnp.dot(cotangents, feed_out.T, preferred_element_type=jnp.float32)
    gate_grad = jnp.concatenate(
        [active_grad * up_in * silu_slope(gate_in), active_grad * jax.nn.silu(gate_in)], axis=1
    ).astype(jnp.bfloat16)
    normed_two_grad, feed_sums, grad_feed_out = sum_and_total(
        gate_grad,
        feed_in,
        (
            across(normed_two, gate_grad).reshape(dp, ctx * rows, -1),
            across(active, cotangents).reshape(dp, hidden, width),
        ),
        3,
    )
    residual_part, grad_gain_feed = pull_two(normed_two_grad)
    residual_grad = cotangent.astype(jnp.float32) + residual_part
    residual_half = gather_tokens(residual_grad.astype(jnp.bfloat16), 4)
    grad_outs = jnp.concatenate(
        [
            jnp.dot(attended_flat.T, residual_half, preferred_element_type=jnp.float32).reshape(
                dp, own_attention, width
            ),
            jnp.dot(gated.T, residual_half, preferred_element_type=jnp.float32).reshape(
                dp, own_mixer, width
            ),
        ],
        axis=1,
    )
    grad_outs = lax.ppermute(sum_dp(grad_outs), ("dp", "ctx"), back)[0]
    attended_grad = jnp.dot(
        residual_half, attention_rows.T, preferred_element_type=jnp.float32
    ).astype(jnp.bfloat16)
    gated_grad = jnp.dot(residual_half, mixer_rows.T, preferred_element_type=jnp.float32)
    gate_part_grad = gated_grad * scanned * silu_slope(gate_part)
    scan_grad = gated_grad * jax.nn.silu(gate_part)
    converted_grad, step_grad, own_decay, own_bias, own_skip = pull_scan(scan_grad)
    pre_grad = converted_grad * silu_slope(pre)
    conv_in_grad = taps[3] * pre_grad
    tap_grads = [None, None, None, jnp.sum(pre_grad * conv_in, axis=0)]
    for offset in (1, 2, 3):
        kept = jnp.where(keeps[offset - 1][:, None], pre_grad, 0.0)
        conv_in_grad = (
            conv_in_grad + jnp.pad(kept[offset:], ((0, offset), (0, 0))) * taps[3 - offset]
        )
        tap_grads[3 - offset] = jnp.sum(kept[offset:] * conv_in[:-offset], axis=0)
    tap_grads = jnp.stack(tap_grads + [jnp.sum(pre_grad, axis=0)], axis=0)

    out_grad = attended_grad.reshape(length, query_heads, HEAD).transpose(1, 0, 2)
    deltas = jnp.sum(
        out_grad.astype(jnp.float32) * attended.astype(jnp.float32), axis=-1, keepdims=True
    )
    value_grad = jnp.einsum("hqk,hqd->kd", probs_half, out_grad, preferred_element_type=jnp.float32)
    prob_grad = jnp.einsum("hqd,kd->hqk", out_grad, values, preferred_element_type=jnp.float32)
    score_grad = (probs * (prob_grad - deltas)).astype(jnp.bfloat16)
    query_grad = (
        jnp.einsum("hqk,kd->hqd", score_grad, keys, preferred_element_type=jnp.float32)
        * score_scale
    )
    key_grad = (
        jnp.einsum("hqk,hqd->kd", score_grad, queries, preferred_element_type=jnp.float32)
        * score_scale
    )
    grads = jnp.concatenate(
        [
            query_grad.transpose(1, 0, 2).reshape(length, query_heads * HEAD),
            key_grad,
            value_grad,
            gate_part_grad,
            conv_in_grad,
            step_grad,
            jnp.zeros((length, layout[-1]), jnp.float32),
        ],
        axis=1,
    ).astype(jnp.bfloat16)
    own_small = jnp.concatenate(
        [grad_gain_feed, tap_grads.reshape(-1), own_decay, own_bias, own_skip], axis=0
    )
    own_small = jnp.pad(own_small, (0, -own_small.shape[0] % 1024)).reshape(-1, 128)
    input_grad, entry_grads, grad_feed_in, smalls, gains = leave(
        grads,
        entry,
        source,
        residual_grad,
        gain_mixing.reshape(1, width),
        across(normed, grads).reshape(dp, ctx, rows, -1),
        feed_sums.reshape(ctx, rows, -1),
        own_small,
    )
    grad_attention_in, grad_mixer_in, grad_step_in = entry_unslab(
        entry_grads.astype(jnp.float32), ctx
    )
    smalls = smalls.reshape(ctx, -1)
    tap_width = heads * SSM_HEAD + 2 * STATE
    tap_all = smalls[:, width : width + 5 * tap_width].reshape(ctx, 5, tap_width)
    tap_sums = jnp.concatenate(
        [
            tap_all[:, :, : heads * SSM_HEAD].transpose(1, 0, 2).reshape(5, SSM_INNER),
            jnp.sum(tap_all[:, :, heads * SSM_HEAD :], axis=0),
        ],
        axis=1,
    )
    head_all = smalls[:, width + 5 * tap_width :][:, : 3 * heads].reshape(ctx, 3, heads)
    head_sums = head_all.transpose(1, 0, 2).reshape(3, SSM_HEADS)
    grad_gate_up = (
        grad_feed_in.reshape(ctx, rows, 2, dp, hidden)
        .transpose(1, 2, 3, 0, 4)
        .reshape(rows, -1)
        .astype(jnp.float32)
    )
    return (
        output.reshape(block_input.shape),
        input_grad.reshape(block_input.shape),
        grad_attention_in,
        grad_mixer_in,
        grad_step_in,
        grad_outs[:own_attention].astype(jnp.float32),
        grad_outs[own_attention:].astype(jnp.float32),
        grad_gate_up,
        grad_feed_out.astype(jnp.float32),
        jnp.sum(gains, axis=(0, 1)),
        jnp.sum(smalls[:, :width], axis=0),
        head_sums[0],
        head_sums[1],
        head_sums[2],
        tap_sums[:4],
        tap_sums[4],
    )


def solution(mesh):
    in_specs = (
        P("dp", "ctx", None),
        P("dp", "ctx"),
        P("dp", "ctx", None),
        P(("dp", "ctx"), None),
        P(("dp", "ctx"), None),
        P(("dp", "ctx"), None),
        P(("dp", "ctx"), None),
        P(("dp", "ctx"), None),
        P(("dp", "ctx"), None),
        P(("dp", "ctx"), None),
        P(),
        P(),
        P(),
        P(),
        P(),
        P(),
        P(),
    )
    out_specs = (
        P("dp", "ctx", None),
        P("dp", "ctx", None),
        P(("dp", "ctx"), None),
        P(("dp", "ctx"), None),
        P(("dp", "ctx"), None),
        P(("dp", "ctx"), None),
        P(("dp", "ctx"), None),
        P(("dp", "ctx"), None),
        P(("dp", "ctx"), None),
        P(),
        P(),
        P(),
        P(),
        P(),
        P(),
        P(),
    )
    sequences = mesh.shape["dp"]

    def choose(*arrays):
        heads = split_heads(mesh.shape["ctx"]) and arrays[0].shape[0] == sequences
        body = split_local if heads else local
        mapped = jax.shard_map(
            body, mesh=mesh, in_specs=in_specs, out_specs=out_specs, check_vma=False
        )
        return mapped(*arrays)

    return choose
```

```python
import functools
import math

import jax
import jax.numpy as jnp
from jax import lax
from jax.experimental import pallas as pl
from jax.experimental.pallas import tpu as pltpu
from jax.sharding import PartitionSpec as P

FF = 2048
HEADS_Q = 8
HEADS_KV = 2
HEAD = 64
SSM_HEADS = 24
SSM_HEAD = 64
STATE = 128
SSM_INNER = 1536


highest = lax.Precision.HIGHEST


def from_behind(block, axis, distance):
    devices = range(lax.axis_size(axis))
    route = [(i - distance, i) for i in devices if i - distance in devices]
    return lax.ppermute(block, axis, route)


def carried_in(value, axis, join, neutral, backward):
    count, mine = (lax.axis_size(axis), lax.axis_index(axis))
    pieces = jax.tree.map(lambda part: lax.all_gather(part, axis), value)
    if backward:
        pieces = jax.tree.map(lambda part: part[::-1], pieces)
        mine = count - 1 - mine
    so_far = jax.tree.map(
        lambda part, zero: jnp.full_like(part, 0) + jnp.asarray(zero, part.dtype), value, neutral
    )

    def hop(position, so_far):
        longer = join(so_far, jax.tree.map(lambda part: part[position], pieces))
        return jax.tree.map(lambda new, old: jnp.where(position < mine, new, old), longer, so_far)

    return lax.fori_loop(0, count - 1, hop, so_far)


def carried_by_heads(decays, state, backward):
    count, mine = (lax.axis_size("ctx"), lax.axis_index("ctx"))
    seq_count, heads = decays.shape[1:]
    share = heads // count
    own = lax.dynamic_slice_in_dim(decays, mine * share, share, axis=2)
    pieces = lax.all_to_all(state, "ctx", split_axis=1, concat_axis=0, tiled=True)
    pieces = pieces.reshape((count, seq_count, share) + state.shape[2:])
    order = list(range(count))[::-1] if backward else list(range(count))
    so_far = jnp.zeros_like(pieces[0])
    reached = [None] * count
    for position in order:
        reached[position] = so_far
        so_far = own[position][:, :, None, None] * so_far + pieces[position]
    return lax.all_to_all(
        jnp.concatenate(reached, axis=0), "ctx", split_axis=0, concat_axis=1, tiled=True
    )


def fold_shape(owned, rows, width):
    step = math.gcd(owned, rows)
    return (step, owned // step, rows // step, width // (rows // step))


def fold_rows(array, owned, rows):
    step, across, down, part = fold_shape(owned, rows, array.shape[1])
    blocks = array.reshape(-1, owned, array.shape[1])
    columns = [
        jnp.concatenate(
            [blocks[:, i * step : (i + 1) * step, j * part : (j + 1) * part] for j in range(down)],
            axis=1,
        )
        for i in range(across)
    ]
    return jnp.concatenate(columns, axis=2).reshape(-1, across * part)


def unfold_rows(array, owned, rows, width):
    step, across, down, part = fold_shape(owned, rows, width)
    blocks = array.reshape(-1, rows, across * part)
    lines = [
        jnp.concatenate(
            [blocks[:, j * step : (j + 1) * step, i * part : (i + 1) * part] for j in range(down)],
            axis=2,
        )
        for i in range(across)
    ]
    return jnp.concatenate(lines, axis=1).reshape(-1, width)


def pad_columns(array):
    return jnp.pad(array, ((0, 0), (0, -array.shape[1] % 128)))


def cut_columns(array, widths):
    pieces, at = ([], 0)
    for width in widths:
        pieces.append(array[:, at : at + width])
        at += width
    return pieces


def rms_scale(values, gain):
    return values * lax.rsqrt(jnp.mean(values * values, axis=-1, keepdims=True) + 1e-05) * gain


def silu_slope(values):
    sigma = jax.nn.sigmoid(values)
    return sigma * (1.0 + values * (1.0 - sigma))


def ssd_local(
    inner, write_map, read_map, step_raw, decay_log, step_bias, skip_gain, starts, segments
):
    step = jax.nn.softplus(step_raw + step_bias)
    rates = step * -jnp.exp(decay_log)
    places = jnp.arange(segments.shape[0])
    lower = places[None, :] <= places[:, None]
    running = jnp.dot(lower.astype(jnp.float32), rates, precision=highest)
    same = (segments[:, None] == segments[None, :]) & lower
    spans = jnp.where(same[None], running.T[:, :, None] - running.T[:, None, :], -1e30)
    intersection = jnp.dot(read_map, write_map.T, precision=highest)
    mixing = jnp.exp(spans) * intersection[None] * step.T[:, None, :]
    result = (
        jnp.einsum("hts,shp->thp", mixing, inner, precision=highest)
        + skip_gain[None, :, None] * inner
    )
    before = jnp.sum((lower & starts[None, :]).astype(jnp.int32), axis=1) == 0
    carried = jnp.where(before[:, None], jnp.exp(running), 0.0)
    tails = jnp.where(
        (segments == segments[-1])[:, None], jnp.exp(running[-1][None, :] - running), 0.0
    )
    state = jnp.einsum("sh,shp,sn->hpn", tails * step, inner, write_map, precision=highest)
    return (result, state, carried[-1], carried)


def add_state(result, carried, read_map, state_in):
    return result + carried[:, :, None] * jnp.einsum(
        "hpn,tn->thp", state_in, read_map, precision=highest
    )


def ssd_block(
    inner,
    write_map,
    read_map,
    step_raw,
    decay_log,
    step_bias,
    skip_gain,
    starts,
    segments,
    state_in,
):
    result, state, decay_total, carried = ssd_local(
        inner, write_map, read_map, step_raw, decay_log, step_bias, skip_gain, starts, segments
    )
    return (
        add_state(result, carried, read_map, state_in),
        decay_total[:, None, None] * state_in + state,
    )


def chain(earlier, later):
    return (earlier[0] * later[0], later[0][:, :, None, None] * earlier[1] + later[1])


def over_blocks(step, start, items):
    if items[2].shape[0] > 1:
        return lax.scan(step, start, items)
    carry, result = step(start, (items[0][0], items[1][0], 0))
    return (carry, None if result is None else result[None])


def group_queries(flat, seq_count, tok_count):
    groups = HEADS_Q // HEADS_KV
    shaped = flat.reshape(seq_count, tok_count, HEADS_KV, groups, HEAD)
    return shaped.transpose(0, 2, 3, 1, 4).reshape(seq_count, HEADS_KV, groups * tok_count, HEAD)


def ungroup(grouped, seq_count, tok_count):
    groups = HEADS_Q // HEADS_KV
    shaped = grouped.reshape(seq_count, HEADS_KV, groups, tok_count, HEAD)
    return shaped.transpose(0, 3, 1, 2, 4).reshape(seq_count * tok_count, HEADS_Q * HEAD)


def local(
    block_input,
    segment_ids,
    out_cotangent,
    attention_in,
    mixer_in,
    step_in,
    attention_out,
    mixer_out,
    gate_up,
    down_weight,
    gain_mixing,
    gain_feed,
    decay_log,
    step_bias,
    skip_gain,
    conv_weight,
    conv_bias,
):
    seq_count, tok_count, width = block_input.shape
    row_count = seq_count * tok_count
    length = tok_count * lax.axis_size("ctx")
    block = length if length <= 1024 else 512
    blocks = length // block
    groups = HEADS_Q // HEADS_KV
    query_width = HEADS_Q * HEAD
    key_width = HEADS_KV * HEAD
    score_scale = HEAD ** (-0.5)
    query_rows = groups * tok_count
    first = lax.axis_index("ctx") * tok_count
    own_rows = attention_in.shape[0]
    axes = ("dp", "ctx")
    entry = jnp.concatenate([attention_in, mixer_in, pad_columns(step_in)], axis=1)
    full_attention_in, full_mixer_in, full_step_in = cut_columns(
        lax.all_gather(entry, axes, axis=0, tiled=True),
        (attention_in.shape[1], mixer_in.shape[1], step_in.shape[1]),
    )
    tall = (attention_out, mixer_out, down_weight)
    folded = [fold_rows(weight, weight.shape[0], own_rows) for weight in tall]
    rest = lax.all_gather(
        jnp.concatenate(folded + [gate_up], axis=1), axes, axis=0, tiled=True
    )
    rest = cut_columns(rest, [weight.shape[1] for weight in folded] + [gate_up.shape[1]])
    full_attention_out, full_mixer_out, full_down = (
        unfold_rows(part, weight.shape[0], own_rows, width) for part, weight in zip(rest, tall)
    )
    full_gate_up = rest[3]
    source = block_input.reshape(row_count, width).astype(jnp.float32)
    normed = rms_scale(source, gain_mixing).astype(jnp.bfloat16)
    projected = jnp.dot(normed, full_attention_in, preferred_element_type=jnp.float32).astype(
        jnp.bfloat16
    )
    mixed_in = jnp.dot(normed, full_mixer_in, preferred_element_type=jnp.float32)
    step_raw = jnp.dot(normed, full_step_in, preferred_element_type=jnp.float32).reshape(
        seq_count, tok_count, SSM_HEADS
    )
    queries = group_queries(projected[:, :query_width], seq_count, tok_count)
    local_keys = (
        projected[:, query_width:].reshape(seq_count, tok_count, 2 * key_width).transpose(1, 0, 2)
    )
    local_segments = segment_ids.T
    keys_all, segments_all = (
        lax.all_gather(local_keys, "ctx", axis=0, tiled=True),
        lax.all_gather(local_segments, "ctx", axis=0, tiled=True),
    )
    query_pos = first + jnp.arange(query_rows) % tok_count
    query_segments = jnp.tile(segment_ids, (1, groups))
    segment_blocks = segments_all.reshape(blocks, block, seq_count)
    block_ids = jnp.arange(blocks)

    def scores_of(key_block, seg_block, block_id):
        keys = key_block[:, :, :key_width].reshape(block, seq_count, HEADS_KV, HEAD)
        scores = (
            jnp.einsum("sgrd,ksgd->sgrk", queries, keys, preferred_element_type=jnp.float32)
            * score_scale
        )
        key_pos = block_id * block + jnp.arange(block)
        allowed = (key_pos[None, None, None, :] <= query_pos[None, None, :, None]) & (
            seg_block.T[:, None, None, :] == query_segments[:, None, :, None]
        )
        return (scores, allowed)

    key_blocks = keys_all.reshape(blocks, block, seq_count, 2 * key_width)

    def gather_stats(carry, item):
        top, total = carry
        scores, allowed = scores_of(item[0], item[1], item[2])
        masked = jnp.where(allowed, scores, -1e30)
        new_top = jnp.maximum(top, jnp.max(masked, axis=-1))
        total = total * jnp.exp(top - new_top) + jnp.sum(
            jnp.where(allowed, jnp.exp(masked - new_top[..., None]), 0.0), axis=-1
        )
        return ((new_top, total), None)

    start_top = jnp.full((seq_count, HEADS_KV, query_rows), -1e30, jnp.float32)
    (top, total), _ = over_blocks(
        gather_stats,
        (start_top, jnp.zeros_like(start_top)),
        (key_blocks, segment_blocks, block_ids),
    )
    log_total = top + jnp.log(total)

    def weigh_values(accum, item):
        scores, allowed = scores_of(item[0], item[1], item[2])
        values = item[0][:, :, key_width:].reshape(block, seq_count, HEADS_KV, HEAD)
        probs = jnp.where(allowed, jnp.exp(scores - log_total[..., None]), 0.0).astype(jnp.bfloat16)
        return (
            accum
            + jnp.einsum("sgrk,ksgd->sgrd", probs, values, preferred_element_type=jnp.float32),
            None,
        )

    attended, _ = over_blocks(
        weigh_values, jnp.zeros(queries.shape, jnp.float32), (key_blocks, segment_blocks, block_ids)
    )
    attended = attended.astype(jnp.bfloat16)
    attended_flat = ungroup(attended, seq_count, tok_count)
    gate_part = mixed_in[:, :SSM_INNER]
    conv_width = mixed_in.shape[1] - SSM_INNER
    conv_in = mixed_in[:, SSM_INNER:].reshape(seq_count, tok_count, conv_width)
    positions = first + jnp.arange(tok_count)
    before_rows = from_behind(conv_in[:, tok_count - 3 :, :], "ctx", 1)
    extended = jnp.concatenate([before_rows, conv_in], axis=1)
    pre = conv_bias + conv_weight[3] * conv_in
    keep_masks = []
    for offset in (1, 2, 3):
        earlier_ids = segments_all[jnp.maximum(positions - offset, 0)].T
        keep_mask = (positions >= offset)[None, :] & (earlier_ids == segment_ids)
        keep_masks.append(keep_mask)
        pre = (
            pre
            + jnp.where(keep_mask[..., None], extended[:, 3 - offset : 3 - offset + tok_count], 0.0)
            * conv_weight[3 - offset]
        )
    converted = jax.nn.silu(pre)
    inner = converted[..., :SSM_INNER].reshape(seq_count, tok_count, SSM_HEADS, SSM_HEAD)
    write_map = converted[..., SSM_INNER : SSM_INNER + STATE]
    read_map = converted[..., SSM_INNER + STATE :]
    starts = (positions == 0)[None, :] | jnp.logical_not(keep_masks[0])
    local_map = jax.vmap(ssd_local, in_axes=(0, 0, 0, 0, None, None, None, 0, 0))
    partial_out, partial_state, decay_total, carried = local_map(
        inner, write_map, read_map, step_raw, decay_log, step_bias, skip_gain, starts, segment_ids
    )
    by_heads = SSM_HEADS % lax.axis_size("ctx") == 0
    if by_heads:
        decays = lax.all_gather(decay_total, "ctx")
        state_in = carried_by_heads(decays, partial_state, False)
    else:
        unit = (jnp.ones_like(decay_total), jnp.zeros_like(partial_state))
        state_in = carried_in((decay_total, partial_state), "ctx", chain, unit, False)[1]
    scanned = jax.vmap(add_state)(partial_out, carried, read_map, state_in)
    flat_scan = scanned.reshape(row_count, SSM_INNER)
    gated = (flat_scan * jax.nn.silu(gate_part)).astype(jnp.bfloat16)
    residual = (
        source
        + jnp.dot(attended_flat, full_attention_out, preferred_element_type=jnp.float32)
        + jnp.dot(gated, full_mixer_out, preferred_element_type=jnp.float32)
    )
    normed_two = rms_scale(residual, gain_feed).astype(jnp.bfloat16)
    gate_values = jnp.dot(normed_two, full_gate_up, preferred_element_type=jnp.float32)
    gate_in = gate_values[:, :FF]
    up_in = gate_values[:, FF:]
    active = (jax.nn.silu(gate_in) * up_in).astype(jnp.bfloat16)
    output = (residual + jnp.dot(active, full_down, preferred_element_type=jnp.float32)).astype(
        jnp.bfloat16
    )
    cotangent = out_cotangent.reshape(row_count, width)
    grad_down_weight = jnp.dot(active.T, cotangent, preferred_element_type=jnp.float32).astype(
        jnp.bfloat16
    )
    active_grad = jnp.dot(cotangent, full_down.T, preferred_element_type=jnp.float32)
    gate_grad = jnp.concatenate(
        [active_grad * up_in * silu_slope(gate_in), active_grad * jax.nn.silu(gate_in)], axis=1
    ).astype(jnp.bfloat16)
    grad_gate_up = jnp.dot(normed_two.T, gate_grad, preferred_element_type=jnp.float32).astype(
        jnp.bfloat16
    )
    feed_terms = jnp.concatenate(
        [grad_gate_up, fold_rows(grad_down_weight, down_weight.shape[0], own_rows)], axis=1
    )
    feed_sums = lax.psum_scatter(feed_terms, axes, scatter_dimension=0, tiled=True)
    normed_two_grad = jnp.dot(gate_grad, full_gate_up.T, preferred_element_type=jnp.float32)
    _, pull_two = jax.vjp(rms_scale, residual, gain_feed)
    residual_part, grad_gain_feed = pull_two(normed_two_grad)
    residual_grad = cotangent.astype(jnp.float32) + residual_part
    residual_half, _ = lax.optimization_barrier((residual_grad.astype(jnp.bfloat16), feed_terms))
    grad_attention_out = jnp.dot(attended_flat.T, residual_half, preferred_element_type=jnp.float32)
    grad_mixer_out = jnp.dot(gated.T, residual_half, preferred_element_type=jnp.float32)
    attended_grad = jnp.dot(
        residual_half, full_attention_out.T, preferred_element_type=jnp.float32
    ).astype(jnp.bfloat16)
    gated_grad = jnp.dot(residual_half, full_mixer_out.T, preferred_element_type=jnp.float32)
    gate_part_grad = gated_grad * flat_scan * silu_slope(gate_part)
    scan_grad = (gated_grad * jax.nn.silu(gate_part)).reshape(
        seq_count, tok_count, SSM_HEADS, SSM_HEAD
    )
    direct = jnp.einsum("sth,sthp,stn->shpn", carried, scan_grad, read_map, precision=highest)
    if by_heads:
        state_grad = carried_by_heads(decays, direct, True)
    else:
        state_grad = carried_in((decay_total, direct), "ctx", chain, unit, True)[1]

    def block_map(inner_v, write_v, read_v, step_v, decay_v, bias_v, skip_v, state_v):
        mapped = jax.vmap(ssd_block, in_axes=(0, 0, 0, 0, None, None, None, 0, 0, 0))
        return mapped(
            inner_v, write_v, read_v, step_v, decay_v, bias_v, skip_v, starts, segment_ids, state_v
        )

    _, pull_scan = jax.vjp(
        block_map, inner, write_map, read_map, step_raw, decay_log, step_bias, skip_gain, state_in
    )
    pulled = pull_scan((scan_grad, state_grad))
    converted_grad = jnp.concatenate(
        [pulled[0].reshape(seq_count, tok_count, SSM_INNER), pulled[1], pulled[2]], axis=2
    )
    pre_grad = converted_grad * silu_slope(pre)
    after_rows = from_behind(pre_grad[:, :3, :], "ctx", -1)
    ahead = jnp.concatenate([pre_grad, after_rows], axis=1)
    conv_in_grad = conv_weight[3] * pre_grad
    tap_grads = [None, None, None, jnp.sum(pre_grad * conv_in, axis=(0, 1))]
    for offset in (1, 2, 3):
        later_ids = segments_all[jnp.minimum(positions + offset, length - 1)].T
        later_mask = later_ids == segment_ids
        conv_in_grad = (
            conv_in_grad
            + jnp.where(later_mask[..., None], ahead[:, offset : offset + tok_count], 0.0)
            * conv_weight[3 - offset]
        )
        earlier_rows = jnp.where(
            keep_masks[offset - 1][..., None], extended[:, 3 - offset : 3 - offset + tok_count], 0.0
        )
        tap_grads[3 - offset] = jnp.sum(pre_grad * earlier_rows, axis=(0, 1))
    grad_conv_weight = jnp.stack(tap_grads, axis=0)
    grad_conv_bias = jnp.sum(pre_grad, axis=(0, 1))
    mixer_grad = jnp.concatenate(
        [gate_part_grad, conv_in_grad.reshape(row_count, conv_width)], axis=1
    ).astype(jnp.bfloat16)
    step_grad_half = pulled[3].reshape(row_count, SSM_HEADS).astype(jnp.bfloat16)
    out_grad = group_queries(attended_grad, seq_count, tok_count)
    deltas = jnp.sum(out_grad.astype(jnp.float32) * attended.astype(jnp.float32), axis=-1)

    def attention_grads(query_grad, item):
        scores, allowed = scores_of(item[0], item[1], item[2])
        keys = item[0][:, :, :key_width].reshape(block, seq_count, HEADS_KV, HEAD)
        values = item[0][:, :, key_width:].reshape(block, seq_count, HEADS_KV, HEAD)
        probs = jnp.where(allowed, jnp.exp(scores - log_total[..., None]), 0.0)
        value_grad = jnp.einsum(
            "sgrk,sgrd->ksgd",
            probs.astype(jnp.bfloat16),
            out_grad,
            preferred_element_type=jnp.float32,
        )
        prob_grad = jnp.einsum(
            "sgrd,ksgd->sgrk", out_grad, values, preferred_element_type=jnp.float32
        )
        score_grad = (probs * (prob_grad - deltas[..., None])).astype(jnp.bfloat16)
        query_grad = (
            query_grad
            + jnp.einsum("sgrk,ksgd->sgrd", score_grad, keys, preferred_element_type=jnp.float32)
            * score_scale
        )
        key_grad = (
            jnp.einsum("sgrk,sgrd->ksgd", score_grad, queries, preferred_element_type=jnp.float32)
            * score_scale
        )
        both = jnp.concatenate(
            [
                key_grad.reshape(block, seq_count, key_width),
                value_grad.reshape(block, seq_count, key_width),
            ],
            axis=2,
        )
        return (query_grad, both)

    query_grad, key_terms = over_blocks(
        attention_grads,
        jnp.zeros(queries.shape, jnp.float32),
        (key_blocks, segment_blocks, block_ids),
    )
    key_pieces = lax.all_to_all(
        key_terms.reshape(length, seq_count, 2 * key_width).astype(jnp.bfloat16),
        "ctx",
        split_axis=0,
        concat_axis=0,
        tiled=True,
    )
    key_sums = jnp.sum(
        key_pieces.reshape(-1, tok_count, seq_count, 2 * key_width).astype(jnp.float32), axis=0
    )
    kv_grad = key_sums.transpose(1, 0, 2).reshape(row_count, 2 * key_width)
    projected_grad = jnp.concatenate(
        [ungroup(query_grad, seq_count, tok_count), kv_grad], axis=1
    ).astype(jnp.bfloat16)
    grad_attention_in = jnp.dot(normed.T, projected_grad, preferred_element_type=jnp.float32)
    grad_mixer_in = jnp.dot(normed.T, mixer_grad, preferred_element_type=jnp.float32)
    grad_step_in = jnp.dot(normed.T, step_grad_half, preferred_element_type=jnp.float32)
    normed_grad = (
        jnp.dot(projected_grad, full_attention_in.T, preferred_element_type=jnp.float32)
        + jnp.dot(mixer_grad, full_mixer_in.T, preferred_element_type=jnp.float32)
        + jnp.dot(step_grad_half, full_step_in.T, preferred_element_type=jnp.float32)
    )
    _, pull_one = jax.vjp(rms_scale, source, gain_mixing)
    source_part, grad_gain_mixing = pull_one(normed_grad)
    input_grad = residual_grad + source_part
    others = [
        grad_attention_in.astype(jnp.bfloat16),
        grad_mixer_in.astype(jnp.bfloat16),
        fold_rows(grad_attention_out.astype(jnp.bfloat16), attention_out.shape[0], own_rows),
        fold_rows(grad_mixer_out.astype(jnp.bfloat16), mixer_out.shape[0], own_rows),
        pad_columns(grad_step_in.astype(jnp.bfloat16)),
    ]
    other_sums = lax.psum_scatter(
        jnp.concatenate(others, axis=1), axes, scatter_dimension=0, tiled=True
    )
    feed_parts = cut_columns(
        feed_sums, (gate_up.shape[1], feed_sums.shape[1] - gate_up.shape[1])
    )
    other_parts = cut_columns(other_sums, [part.shape[1] for part in others])
    weight_sums = [
        part.astype(jnp.float32)
        for part in (
            other_parts[0],
            other_parts[1],
            other_parts[4][:, :SSM_HEADS],
            unfold_rows(other_parts[2], attention_out.shape[0], own_rows, width),
            unfold_rows(other_parts[3], mixer_out.shape[0], own_rows, width),
            feed_parts[0],
            unfold_rows(feed_parts[1], down_weight.shape[0], own_rows, width),
        )
    ]
    small_sums = lax.psum(
        (
            grad_gain_mixing,
            grad_gain_feed,
            pulled[4],
            pulled[5],
            pulled[6],
            grad_conv_weight,
            grad_conv_bias,
        ),
        ("dp", "ctx"),
    )
    return (
        output.reshape(seq_count, tok_count, width),
        input_grad.reshape(seq_count, tok_count, width),
        weight_sums[0],
        weight_sums[1],
        weight_sums[2],
        weight_sums[3],
        weight_sums[4],
        weight_sums[5],
        weight_sums[6],
        small_sums[0],
        small_sums[1],
        small_sums[2],
        small_sums[3],
        small_sums[4],
        small_sums[5],
        small_sums[6],
    )

def split_heads(ctx):
    return HEADS_Q == ctx and SSM_HEADS % ctx == 0 and ctx % HEADS_KV == 0


def entry_layout(ctx):
    heads = SSM_HEADS // ctx
    widths = [STATE, STATE, heads * SSM_HEAD, heads * SSM_HEAD, HEAD, HEAD, HEAD, heads]
    return widths + [-sum(widths) % 128]


def entry_slabs(attention_in, mixer_in, step_in, ctx):
    rows = attention_in.shape[0]
    share = ctx // HEADS_KV
    query_width = HEADS_Q * HEAD
    key_width = HEADS_KV * HEAD

    def parts(array, count):
        return array.reshape(rows, count, -1).transpose(1, 0, 2)

    kv = [
        jnp.repeat(parts(attention_in[:, at : at + key_width], HEADS_KV), share, axis=0)
        for at in (query_width, query_width + key_width)
    ]
    both = jnp.broadcast_to(mixer_in[None, :, 2 * SSM_INNER :], (ctx, rows, 2 * STATE))
    pieces = [
        both,
        parts(mixer_in[:, SSM_INNER : 2 * SSM_INNER], ctx),
        parts(mixer_in[:, :SSM_INNER], ctx),
        parts(attention_in[:, :query_width], ctx),
        kv[0],
        kv[1],
        parts(step_in, ctx),
        jnp.zeros((ctx, rows, entry_layout(ctx)[-1]), jnp.bfloat16),
    ]
    return jnp.concatenate(pieces, axis=2)


def entry_unslab(slabs, ctx):
    rows = slabs.shape[1]
    share = ctx // HEADS_KV
    write, read, inner, gate, q, k, v, step, _ = [
        slabs[:, :, at : at + width]
        for at, width in zip(offsets(entry_layout(ctx)), entry_layout(ctx))
    ]

    def flat(part):
        return part.transpose(1, 0, 2).reshape(rows, -1)

    def shared(part):
        return flat(jnp.sum(part.reshape(HEADS_KV, share, rows, HEAD), axis=1))

    attention = jnp.concatenate([flat(q), shared(k), shared(v)], axis=1)
    mixer = jnp.concatenate(
        [flat(gate), flat(inner), jnp.sum(write, axis=0), jnp.sum(read, axis=0)], axis=1
    )
    return attention, mixer, flat(step)


def offsets(widths):
    at, places = 0, []
    for width in widths:
        places.append(at)
        at += width
    return places


MESH = pl.DeviceIdType.MESH
IN_VMEM = pl.BlockSpec(memory_space=pltpu.VMEM)
ANYWHERE = pl.BlockSpec(memory_space=pl.ANY)


def remote(source, target, send, recv, peer):
    return pltpu.make_async_remote_copy(
        src_ref=source,
        dst_ref=target,
        send_sem=send,
        recv_sem=recv,
        device_id=peer,
        device_id_type=MESH,
    )


def arrived(ref, recv, peer):
    remote(ref, ref, recv, recv, peer).wait_recv()


class Here:
    def __init__(self, dp, ctx):
        self.dp, self.ctx, self.pairs = dp, ctx, ctx // 2
        self.d, self.me = lax.axis_index("dp"), lax.axis_index("ctx")
        self.z, self.c = self.me // 2, self.me % 2
        self.sibling = (self.d, self.z * 2 + 1 - self.c)

    def dp_peers(self):
        return [(lax.rem(self.d + k, self.dp), self.me) for k in range(1, self.dp)]

    def ctx_peers(self):
        return [(self.d, lax.rem(self.me + k, self.ctx)) for k in range(1, self.ctx)]

    def greet(self, peers, senders=()):
        sem = pltpu.get_barrier_semaphore()
        for peer in peers:
            pl.semaphore_signal(sem, inc=1, device_id=peer, device_id_type=MESH)
        for peer in senders:

            @pl.when(jnp.logical_not(self.is_me(peer)))
            def _(peer=peer):
                pl.semaphore_signal(sem, inc=1, device_id=peer, device_id_type=MESH)

        count = len(peers)
        if senders:
            count = count + self.dp - (self.group == self.me).astype(jnp.int32)
        pl.semaphore_wait(sem, count)

    @property
    def group(self):
        return (self.d * self.ctx + self.me) // self.dp

    def is_me(self, peer):
        return (peer[0] == self.d) & (peer[1] == self.me)

    def group_devices(self):
        return [(lax.rem(self.d + k, self.dp), self.group) for k in range(self.dp)]

    def owners(self):
        places = [self.me * self.dp + j for j in range(self.dp)]
        return [(place // self.ctx, lax.rem(place, self.ctx)) for place in places]


class Relay:
    def __init__(self, here, block, slots, send, recv, local):
        self.here, self.block, self.slots = here, block, slots
        self.send, self.recv, self.local = send, recv, local
        self.up = (here.d, (here.z + 1) * 2 + here.c)
        self.down = (here.d, (here.z - 1) * 2 + here.c)
        self.has_up, self.has_down = here.z < here.pairs - 1, here.z > 0

    @staticmethod
    def scratch(pairs):
        return [
            pltpu.SemaphoreType.DMA((4 * pairs,)),
            pltpu.SemaphoreType.DMA((2 * pairs,)),
            pltpu.SemaphoreType.DMA,
        ]

    def slot(self, z, c):
        return self.slots.at[z * 2 + c]

    def begin(self):
        h, n = self.here, self.here.pairs
        own = self.slot(h.z, h.c)
        pltpu.make_async_copy(self.block, own, self.local).start()

        @pl.when(self.has_up)
        def _():
            remote(self.block, own, self.send.at[0], self.recv.at[h.me], self.up).start()

        @pl.when(self.has_down)
        def _():
            remote(self.block, own, self.send.at[n], self.recv.at[h.me], self.down).start()

        remote(self.block, own, self.send.at[2 * n], self.recv.at[h.me], h.sibling).start()

    def hop(self, s):
        h, n = self.here, self.here.pairs
        low, high = h.z - s, h.z + s

        @pl.when(low >= 0)
        def _():
            ref, recv = self.slot(low, h.c), self.recv.at[low * 2 + h.c]
            arrived(ref, recv, h.sibling)

            @pl.when(self.has_up)
            def _():
                remote(ref, ref, self.send.at[s], recv, self.up).start()

            remote(ref, ref, self.send.at[2 * n + 2 * s - 1], recv, h.sibling).start()

        @pl.when(high < n)
        def _():
            ref, recv = self.slot(high, h.c), self.recv.at[high * 2 + h.c]
            arrived(ref, recv, h.sibling)

            @pl.when(self.has_down)
            def _():
                remote(ref, ref, self.send.at[n + s], recv, self.down).start()

            remote(ref, ref, self.send.at[2 * n + 2 * s], recv, h.sibling).start()

    def end(self):
        h, n = self.here, self.here.pairs
        for z in range(n):
            arrived(self.slot(z, 1 - h.c), self.recv.at[z * 2 + 1 - h.c], h.sibling)
        own = self.slot(h.z, h.c)

        def sent(index):
            remote(own, own, self.send.at[index], self.recv.at[0], h.sibling).wait_send()

        for s in range(n):
            low, high = h.z - s, h.z + s
            pl.when((low >= 0) & self.has_up)(functools.partial(sent, s))
            pl.when((high < n) & self.has_down)(functools.partial(sent, n + s))
            if s == 0:
                sent(2 * n)
            else:
                pl.when(low >= 0)(functools.partial(sent, 2 * n + 2 * s - 1))
                pl.when(high < n)(functools.partial(sent, 2 * n + 2 * s))
        pltpu.make_async_copy(self.block, own, self.local).wait()


class Spread:
    def __init__(self, here, block, slots, send, recv, local):
        self.here, self.block, self.slots = here, block, slots
        self.send, self.recv, self.local = send, recv, local

    @staticmethod
    def scratch(dp):
        return [
            pltpu.SemaphoreType.DMA((dp,)),
            pltpu.SemaphoreType.DMA((dp,)),
            pltpu.SemaphoreType.DMA,
        ]

    def begin(self):
        h = self.here
        pltpu.make_async_copy(self.block, self.slots.at[h.d], self.local).start()
        self.copies = [
            remote(self.block, self.slots.at[h.d], self.send.at[k], self.recv.at[h.d], peer)
            for k, peer in enumerate(h.dp_peers())
        ]
        for copy in self.copies:
            copy.start()

    def end(self):
        h = self.here
        for peer in h.dp_peers():
            arrived(self.slots.at[peer[0]], self.recv.at[peer[0]], peer)
        for copy in self.copies:
            copy.wait_send()
        pltpu.make_async_copy(self.block, self.slots.at[h.d], self.local).wait()


class Total:
    def __init__(self, here, terms, got, result, send, recv):
        self.here, self.terms, self.got, self.result = here, terms, got, result
        self.send, self.recv = send, recv

    @staticmethod
    def scratch(dp, shape):
        return [
            pltpu.VMEM((dp,) + shape, jnp.bfloat16),
            pltpu.SemaphoreType.DMA((dp,)),
            pltpu.SemaphoreType.DMA((dp,)),
        ]

    def begin(self):
        h = self.here
        self.copies = [
            remote(
                self.terms.at[peer[0]], self.got.at[h.d], self.send.at[k], self.recv.at[h.d], peer
            )
            for k, peer in enumerate(h.dp_peers())
        ]
        for copy in self.copies:
            copy.start()

    def end(self):
        h = self.here
        total = self.terms[h.d].astype(jnp.float32)
        for peer in h.dp_peers():
            arrived(self.got.at[peer[0]], self.recv.at[peer[0]], peer)
            total = total + self.got[peer[0]].astype(jnp.float32)
        self.result[...] = total.astype(self.result.dtype)

    def leave(self):
        for copy in self.copies:
            copy.wait_send()


class Swap:
    def __init__(self, here, blocks, slots, send, recv, local):
        self.here, self.blocks, self.slots = here, blocks, slots
        self.send, self.recv, self.local = send, recv, local

    @staticmethod
    def scratch(ctx):
        return [
            pltpu.SemaphoreType.DMA((ctx,)),
            pltpu.SemaphoreType.DMA((ctx,)),
            pltpu.SemaphoreType.DMA,
        ]

    def begin(self):
        h = self.here
        pltpu.make_async_copy(self.blocks.at[h.me], self.slots.at[h.me], self.local).start()
        self.copies = []
        for k, peer in enumerate(h.ctx_peers()):
            copy = remote(
                self.blocks.at[peer[1]],
                self.slots.at[h.me],
                self.send.at[k],
                self.recv.at[h.me],
                peer,
            )
            copy.start()
            self.copies.append(copy)

    def wait(self, index):
        arrived(self.slots.at[index], self.recv.at[index], self.here.sibling)

    def leave(self):
        h = self.here
        for copy in self.copies:
            copy.wait_send()
        pltpu.make_async_copy(self.blocks.at[h.me], self.slots.at[h.me], self.local).wait()


class SumTokens:
    def __init__(self, here, left, right, turned, total, away, pair, out, got, *sems):
        self.here, self.left, self.right, self.turned, self.total = here, left, right, turned, total
        self.away, self.pair, self.out, self.got = away, pair, out, got
        self.away_send, self.away_recv, self.send, self.recv = sems
        self.order = sorted(range(1, here.pairs), key=lambda k: -min(k, here.pairs - k)) + [0]

    @staticmethod
    def scratch(pairs, rows, width):
        block = pltpu.VMEM((pairs, rows, width), jnp.bfloat16)
        return [block] * 4 + [pltpu.SemaphoreType.DMA((pairs,))] * 4

    def term(self, z, c):
        rows = self.total.shape[0]
        part = self.left[pl.ds(pl.multiple_of((z * 2 + c) * rows, rows), rows), :]
        dims = (((1,), (1 if self.turned else 0,)), ((), ()))
        return lax.dot_general(part, self.right[...], dims, preferred_element_type=jnp.float32)

    def peer(self, k):
        h = self.here
        return (h.d, lax.rem(h.z + k, h.pairs) * 2 + h.c)

    def to_sibling(self, k):
        return remote(
            self.away.at[k], self.pair.at[k], self.away_send.at[k], self.away_recv.at[k],
            self.here.sibling,
        )

    def to_pair(self, k):
        return remote(
            self.out.at[k], self.got.at[k], self.send.at[k], self.recv.at[k], self.peer(k)
        )

    def begin(self):
        h = self.here
        for k in self.order:
            self.away[k] = self.term(lax.rem(h.z + k, h.pairs), 1 - h.c).astype(jnp.bfloat16)
            self.to_sibling(k).start()
        for k in self.order:
            term = self.term(lax.rem(h.z + k, h.pairs), h.c)
            self.to_sibling(k).wait_recv()
            term = term + self.pair[k].astype(jnp.float32)
            if k:
                self.out[k] = term.astype(jnp.bfloat16)
                self.to_pair(k).start()
            else:
                self.total[...] = term

    def end(self):
        for k in self.order[::-1]:
            if k:
                self.to_pair(k).wait_recv()
                self.total[...] += self.got[k].astype(jnp.float32)

    def leave(self):
        for k in self.order:
            self.to_sibling(k).wait_send()
            if k:
                self.to_pair(k).wait_send()


class Scatter:
    def __init__(self, here, blocks, targets, slots, slot, senders, send, recv, local):
        self.here, self.blocks, self.targets, self.slots, self.slot = here, blocks, targets, slots, slot
        self.senders, self.send, self.recv, self.local = senders, send, recv, local

    @staticmethod
    def scratch(dp):
        return [
            pltpu.SemaphoreType.DMA((dp,)),
            pltpu.SemaphoreType.DMA((dp,)),
            pltpu.SemaphoreType.DMA,
        ]

    def each(self, at_home, away):
        for k, target in enumerate(self.targets):
            own = self.here.is_me(target)
            pl.when(own)(functools.partial(at_home, k))
            pl.when(jnp.logical_not(own))(functools.partial(away, k))

    def home_copy(self, k):
        return pltpu.make_async_copy(self.blocks[k], self.slots.at[self.slot], self.local)

    def far_copy(self, k):
        return remote(
            self.blocks[k], self.slots.at[self.slot], self.send.at[k], self.recv.at[self.slot],
            self.targets[k],
        )

    def begin(self):
        self.each(lambda k: self.home_copy(k).start(), lambda k: self.far_copy(k).start())

    def end(self):
        for j, sender in enumerate(self.senders):
            slot = sender[2] if len(sender) > 2 else j
            own = self.here.is_me(sender)

            @pl.when(jnp.logical_not(own))
            def _(slot=slot, sender=sender):
                arrived(self.slots.at[slot], self.recv.at[slot], sender[:2])

        self.each(lambda k: self.home_copy(k).wait(), lambda k: self.far_copy(k).wait_send())


def call(kernel, ident, outs, out_specs, in_specs, scratch, *arrays):
    return pl.pallas_call(
        kernel,
        out_shape=outs,
        in_specs=in_specs,
        out_specs=out_specs,
        scratch_shapes=scratch,
        compiler_params=pltpu.CompilerParams(
            collective_id=ident, has_side_effects=True, vmem_limit_bytes=48 * 2**20
        ),
    )(*arrays)


def like(shape, dtype=jnp.bfloat16):
    return jax.ShapeDtypeStruct(shape, dtype)


def gather_tokens(block, ident):
    dp, ctx = lax.axis_size("dp"), lax.axis_size("ctx")

    def kernel(block_ref, slots_ref, *sems):
        here = Here(dp, ctx)
        relay = Relay(here, block_ref, slots_ref, *sems)
        here.greet(here.ctx_peers())
        relay.begin()
        for s in range(1, here.pairs):
            relay.hop(s)
        relay.end()

    whole = call(
        kernel, ident, like((ctx,) + block.shape, block.dtype), ANYWHERE, [ANYWHERE],
        Relay.scratch(ctx // 2), block,
    )
    return whole.reshape((-1,) + block.shape[1:])


def enter(normed, segments, entry, feed, outs):
    dp, ctx = lax.axis_size("dp"), lax.axis_size("ctx")
    relay_sems, swap_sems = Relay.scratch(ctx // 2), Swap.scratch(ctx)

    def kernel(
        normed_ref, seg_ref, entry_ref, feed_ref, outs_ref,
        all_ref, segs_ref, full_ref, feeds_ref, rows_ref, *sems,
    ):
        here = Here(dp, ctx)
        tokens = Relay(here, normed_ref, all_ref, *sems[0:3])
        ids = Relay(here, seg_ref, segs_ref, *sems[3:6])
        slabs = Swap(here, entry_ref, full_ref.at[here.d], *sems[6:9])
        others = Swap(here, feed_ref, feeds_ref, *sems[9:12])
        pass_send, pass_recv = sems[12:14]
        own_slot = lax.rem(here.d * ctx + here.me, dp)
        outs = Scatter(
            here, [outs_ref] * dp, here.group_devices(), rows_ref, own_slot, here.owners(), *sems[14:17]
        )
        peers = here.dp_peers()
        here.greet(peers + here.ctx_peers(), here.owners())
        passed = []

        def pass_on(source, index):
            for k, peer in enumerate(peers):
                copy = remote(
                    source,
                    full_ref.at[here.d, index],
                    pass_send.at[k, index],
                    pass_recv.at[here.d, index],
                    peer,
                )
                copy.start()
                passed.append(copy)

        slabs.begin()
        pass_on(entry_ref.at[here.me], here.me)
        tokens.begin()
        ids.begin()

        def forward(index):
            slabs.wait(index)
            pass_on(full_ref.at[here.d, index], index)

        forward(here.z * 2 + 1 - here.c)
        outs.begin()
        others.begin()
        for s in range(1, here.pairs):
            for core in (0, 1):
                forward(lax.rem(here.z + s, here.pairs) * 2 + core)
            tokens.hop(s)
            ids.hop(s)
        for peer in peers:
            for index in range(ctx):
                arrived(full_ref.at[peer[0], index], pass_recv.at[peer[0], index], peer)
        for peer in here.ctx_peers():
            others.wait(peer[1])
        tokens.end()
        ids.end()
        outs.end()
        slabs.leave()
        others.leave()
        for copy in passed:
            copy.wait_send()

    return call(
        kernel,
        0,
        (
            like((ctx,) + normed.shape),
            like((ctx,) + segments.shape, segments.dtype),
            like((dp,) + entry.shape),
            like(feed.shape),
            like((dp,) + outs.shape),
        ),
        (ANYWHERE,) * 5,
        [ANYWHERE] * 5,
        relay_sems * 2 + swap_sems * 2 + [pltpu.SemaphoreType.DMA((dp, ctx))] * 2 + Scatter.scratch(dp),
        normed,
        segments,
        entry,
        feed,
        outs,
    )


def sum_and_spread(left, right, blocks, ident):
    dp, ctx = lax.axis_size("dp"), lax.axis_size("ctx")
    rows, width = left.shape[0] // ctx, right.shape[1]
    count = len(blocks)

    def kernel(left_ref, right_ref, *refs):
        blocks_in, total, slots = refs[:count], refs[count], refs[count + 1 : 2 * count + 1]
        sems = refs[2 * count + 1 :]
        here = Here(dp, ctx)
        sums = SumTokens(here, left_ref, right_ref, False, total, *sems[:8])
        spreads = [
            Spread(here, block, slot, *sems[8 + 3 * i : 11 + 3 * i])
            for i, (block, slot) in enumerate(zip(blocks_in, slots))
        ]
        here.greet(here.dp_peers() + here.ctx_peers())
        for spread in spreads:
            spread.begin()
        sums.begin()
        sums.end()
        for spread in spreads:
            spread.end()
        sums.leave()

    return call(
        kernel,
        ident,
        (like((rows, width), jnp.float32), *[like((dp,) + block.shape) for block in blocks]),
        (IN_VMEM,) + (ANYWHERE,) * count,
        [IN_VMEM, IN_VMEM] + [ANYWHERE] * count,
        SumTokens.scratch(ctx // 2, rows, width) + Spread.scratch(dp) * count,
        left,
        right,
        *blocks,
    )


def sum_and_total(left, right, terms, ident):
    dp, ctx = lax.axis_size("dp"), lax.axis_size("ctx")
    rows, width = left.shape[0] // ctx, right.shape[0]
    count = len(terms)

    def kernel(left_ref, right_ref, *refs):
        terms_in, total, results = refs[:count], refs[count], refs[count + 1 : 2 * count + 1]
        sems = refs[2 * count + 1 :]
        here = Here(dp, ctx)
        sums = SumTokens(here, left_ref, right_ref, True, total, *sems[:8])
        totals = [
            Total(here, term, sems[8 + 3 * i], result, *sems[9 + 3 * i : 11 + 3 * i])
            for i, (term, result) in enumerate(zip(terms_in, results))
        ]
        here.greet(here.dp_peers() + here.ctx_peers())
        for part in totals:
            part.begin()
        sums.begin()
        for part in totals:
            part.end()
        sums.end()
        sums.leave()
        for part in totals:
            part.leave()

    scratch = SumTokens.scratch(ctx // 2, rows, width)
    for term in terms:
        scratch = scratch + Total.scratch(dp, term.shape[1:])
    return call(
        kernel,
        ident,
        (like((rows, width), jnp.float32), *[like(term.shape[1:]) for term in terms]),
        (IN_VMEM,) * (1 + count),
        [IN_VMEM] * (2 + count),
        scratch,
        left,
        right,
        *terms,
    )


def leave(grads, entry, source, residual_grad, gain, entry_terms, feed_sums, out_terms, small):
    dp, ctx = lax.axis_size("dp"), lax.axis_size("ctx")
    rows, width = source.shape
    slab = entry_terms.shape[2:]

    def kernel(
        grads_ref, entry_ref, source_ref, res_ref, gain_ref, terms_ref, feed_ref, outs_ref, small_ref,
        input_ref, slabs_ref, feeds_ref, out_sum, smalls_ref, gains_ref, normed_grad, *sems,
    ):
        here = Here(dp, ctx)
        peers = here.dp_peers()
        sums = SumTokens(here, grads_ref, entry_ref, True, normed_grad, *sems[0:8])
        feeds = Swap(here, feed_ref, feeds_ref, *sems[8:11])
        got, term_send, term_recv, mine, slab_send, slab_recv = sems[11:17]
        small_got, gain_got = sems[17:19]
        small_send, small_recv, gain_send, gain_recv = sems[19:23]
        last_send, last_recv, lastg_send, lastg_recv = sems[23:27]
        senders = [device + (device[0],) for device in here.group_devices()]
        outs_got = sems[27]
        outs = Scatter(
            here, [outs_ref.at[j] for j in range(dp)], here.owners(), outs_got, here.d, senders, *sems[28:31]
        )
        here.greet(peers + here.ctx_peers(), here.group_devices())
        order = [lax.rem(here.me + k, ctx) for k in list(range(1, ctx)) + [0]]

        def term_copy(k, index):
            return remote(
                terms_ref.at[peers[k][0], index],
                got.at[here.d, index],
                term_send.at[k, index],
                term_recv.at[here.d, index],
                peers[k],
            )

        for index in order:
            for k in range(dp - 1):
                term_copy(k, index).start()
        outs.begin()
        small_copies = []
        for k, peer in enumerate(peers):
            copy = remote(
                small_ref, small_got.at[here.d], small_send.at[k], small_recv.at[here.d], peer
            )
            copy.start()
            small_copies.append(copy)
        sums.begin()
        feeds.begin()

        def slab_copy(j):
            return remote(
                mine.at[order[j]], slabs_ref.at[here.me], slab_send.at[j], slab_recv.at[here.me],
                (here.d, order[j]),
            )

        for j, index in enumerate(order):
            total = terms_ref[here.d, index].astype(jnp.float32)
            for peer in peers:
                arrived(got.at[peer[0], index], term_recv.at[peer[0], index], peer)
                total = total + got[peer[0], index].astype(jnp.float32)
            total = total.astype(jnp.bfloat16)
            if j < ctx - 1:
                mine[index] = total
                slab_copy(j).start()
            else:
                slabs_ref[here.me] = total
        sums.end()
        x, grad = source_ref[...], normed_grad[...]
        scale = lax.rsqrt(jnp.mean(x * x, axis=-1, keepdims=True) + 1e-05)
        scaled = grad * gain_ref[...]
        inner = jnp.mean(x * scaled, axis=-1, keepdims=True)
        input_ref[...] = res_ref[...] + scale * scaled - x * (scale * scale * scale * inner)
        gain_got[here.d] = jnp.sum(grad * (x * scale), axis=0, keepdims=True)
        for k, peer in enumerate(peers):
            copy = remote(
                gain_got.at[here.d], gain_got.at[here.d], gain_send.at[k], gain_recv.at[here.d], peer
            )
            copy.start()
            small_copies.append(copy)
        small_got[here.d] = small_ref[...]
        for peer in peers:
            arrived(small_got.at[peer[0]], small_recv.at[peer[0]], peer)
        total = small_got[0]
        for d in range(1, dp):
            total = total + small_got[d]
        smalls_ref[here.me] = total
        last = []
        for k, peer in enumerate(here.ctx_peers()):
            copy = remote(
                smalls_ref.at[here.me], smalls_ref.at[here.me], last_send.at[k],
                last_recv.at[here.me], peer,
            )
            copy.start()
            last.append(copy)
        for peer in peers:
            arrived(gain_got.at[peer[0]], gain_recv.at[peer[0]], peer)
        total = gain_got[0]
        for d in range(1, dp):
            total = total + gain_got[d]
        gains_ref[here.me] = total
        for k, peer in enumerate(here.ctx_peers()):
            copy = remote(
                gains_ref.at[here.me], gains_ref.at[here.me], lastg_send.at[k],
                lastg_recv.at[here.me], peer,
            )
            copy.start()
            last.append(copy)
        for peer in here.ctx_peers():
            arrived(slabs_ref.at[peer[1]], slab_recv.at[peer[1]], peer)
            feeds.wait(peer[1])
            arrived(smalls_ref.at[peer[1]], last_recv.at[peer[1]], peer)
            arrived(gains_ref.at[peer[1]], lastg_recv.at[peer[1]], peer)
        outs.end()
        total = outs_got[0].astype(jnp.float32)
        for d in range(1, dp):
            total = total + outs_got[d].astype(jnp.float32)
        out_sum[...] = total
        sums.leave()
        feeds.leave()
        for index in order:
            for k in range(dp - 1):
                term_copy(k, index).wait_send()
        for j in range(ctx - 1):
            slab_copy(j).wait_send()
        for copy in small_copies + last:
            copy.wait_send()

    dma = pltpu.SemaphoreType.DMA
    scratch = (
        [pltpu.VMEM((rows, width), jnp.float32)]
        + SumTokens.scratch(ctx // 2, rows, width)
        + Swap.scratch(ctx)
        + [
            pltpu.VMEM((dp, ctx) + slab, jnp.bfloat16),
            dma((dp, ctx)),
            dma((dp, ctx)),
            pltpu.VMEM((ctx,) + slab, jnp.bfloat16),
            dma((ctx,)),
            dma((ctx,)),
        ]
        + [
            pltpu.VMEM((dp,) + small.shape, jnp.float32),
            pltpu.VMEM((dp, 1, width), jnp.float32),
        ]
        + [dma((dp,))] * 4
        + [dma((ctx,))] * 4
        + [pltpu.VMEM(out_terms.shape, jnp.bfloat16)]
        + Scatter.scratch(dp)
    )
    return call(
        kernel,
        5,
        (
            like((rows, width), jnp.float32),
            like((ctx,) + slab),
            like(feed_sums.shape),
            like(out_terms.shape[1:], jnp.float32),
            like((ctx,) + small.shape, jnp.float32),
            like((ctx, 1, width), jnp.float32),
        ),
        (IN_VMEM,) * 6,
        [IN_VMEM] * 9,
        scratch,
        grads,
        entry,
        source,
        residual_grad,
        gain,
        entry_terms,
        feed_sums,
        out_terms,
        small,
    )


def rows_of(index, size):
    return pl.ds(pl.multiple_of(index * size, size), size)


def product(left, right, dims=((1,), (0,)), precision=None):
    return lax.dot_general(
        left, right, (dims, ((), ())), precision=precision, preferred_element_type=jnp.float32
    )


def sigma(values):
    return 1.0 / (1.0 + jnp.exp(-values))


def lower_of(size):
    down = lax.broadcasted_iota(jnp.int32, (size, size), 0)
    along = lax.broadcasted_iota(jnp.int32, (size, size), 1)
    return along <= down


def widen(columns, heads):
    shape = (columns.shape[0], SSM_HEAD)
    return jnp.concatenate(
        [jnp.broadcast_to(columns[:, h : h + 1], shape) for h in range(heads)], axis=1
    )


def head_sums(array, heads, width):
    sums = [
        jnp.sum(array[:, h * SSM_HEAD : (h + 1) * SSM_HEAD], axis=1, keepdims=True)
        for h in range(heads)
    ]
    return columns_of(sums, width)


def columns_of(columns, width):
    lane = lax.broadcasted_iota(jnp.int32, (columns[0].shape[0], width), 1)
    total = jnp.zeros(lane.shape, jnp.float32)
    for h, column in enumerate(columns):
        total = jnp.where(lane == h, column, total)
    return total


class Layout:
    def __init__(self, heads):
        self.inner = 2 * STATE
        self.conv = self.inner + heads * SSM_HEAD
        self.query = self.conv + heads * SSM_HEAD
        self.key = self.query + HEAD
        self.value = self.key + HEAD
        self.step = self.value + HEAD
        self.width = self.step + heads + (-(self.step + heads)) % 128
        self.steps = self.width - self.step


class Chunk:
    def __init__(self, lay, heads, p, a, seg_row, tap_ref, head_ref, shifted):
        size = p.shape[0]
        self.conv_in = p[:, : lay.conv]
        self.earlier = [jnp.where(a[:, k - 1 : k] > 0.0, shifted(k), 0.0) for k in (1, 2, 3)]
        pre = tap_ref[4:5, :] + tap_ref[3:4, :] * self.conv_in
        for k in (1, 2, 3):
            pre = pre + self.earlier[k - 1] * tap_ref[3 - k : 4 - k, :]
        self.sig = sigma(pre)
        self.pre = pre
        conv = pre * self.sig
        self.write, self.read = conv[:, :STATE], conv[:, STATE : 2 * STATE]
        self.inner = conv[:, lay.inner :]
        self.gate = p[:, lay.conv : lay.query]
        self.biased = p[:, lay.step :] + head_ref[1:2, :]
        self.steps = jnp.maximum(self.biased, 0.0) + jnp.log1p(jnp.exp(-jnp.abs(self.biased)))
        self.rates = self.steps * head_ref[0:1, :]
        lower = lower_of(size)
        self.ones = lower.astype(jnp.float32)
        run = product(self.ones, self.rates, precision=highest)
        run_row = product(self.rates, self.ones, ((0,), (1,)), precision=highest)
        allowed = lower & (a[:, 6:7] == seg_row)
        self.decay = [
            jnp.exp(jnp.where(allowed, run[:, h : h + 1] - run_row[h : h + 1, :], -1e30))
            for h in range(heads)
        ]
        self.carried = a[:, 7:8] * jnp.exp(run)
        self.tails = a[:, 8:9] * jnp.exp(run[size - 1 : size, :] - run)
        self.cross = product(self.read, self.write, ((1,), (1,)))
        self.scaled = self.inner * widen(self.steps, heads)
        self.carried_wide = widen(self.carried, heads)
        self.tails_wide = widen(self.tails, heads)
        self.skip_wide = widen(head_ref[2:3, :], heads)
        last = self.carried[size - 1 : size, :]
        head_row = lax.broadcasted_iota(jnp.int32, (heads * SSM_HEAD, 1), 0) // SSM_HEAD
        self.last = jnp.zeros((heads * SSM_HEAD, 1), jnp.float32)
        for h in range(heads):
            self.last = jnp.where(head_row == h, last[:, h : h + 1], self.last)


def attention_mask(seg_column, seg_row, at):
    rows, keys = seg_column.shape[0], seg_row.shape[1]
    down = lax.broadcasted_iota(jnp.int32, (rows, keys), 0) + at
    along = lax.broadcasted_iota(jnp.int32, (rows, keys), 1)
    return (along <= down) & (seg_column == seg_row)


def mix_forward(normed, entry, columns, seg_row, taps, head_rows, size):
    length = normed.shape[0]
    chunks = length // size
    heads = SSM_HEADS // lax.axis_size("ctx")
    lay = Layout(heads)
    wide = heads * SSM_HEAD
    block = 2 * size if chunks % 2 == 0 else size

    def kernel(
        n_ref, e_ref, col_ref, seg_ref, tap_ref, head_ref,
        mixed_ref, p_ref, y_ref, states_ref, top_ref, ext, state, heads_in,
    ):
        state[...] = jnp.zeros_like(state)
        ext[0:8, :] = jnp.zeros((8, lay.conv), jnp.float32)

        def chunk(j, _):
            at = rows_of(j, size)
            p = product(n_ref[at, :], e_ref[...])
            p_ref[at, :] = p
            ext[8:, :] = p[:, : lay.conv]
            part = Chunk(
                lay, heads, p, col_ref[at, :], seg_ref[:, at], tap_ref, head_ref,
                lambda k: ext[8 - k : 8 - k + size, :],
            )
            ext[0:8, :] = ext[size : size + 8, :]
            reached = state[...]
            states_ref[j] = reached
            local = [
                product(part.decay[h] * part.cross, part.scaled[:, h * SSM_HEAD : (h + 1) * SSM_HEAD])
                for h in range(heads)
            ]
            y = (
                jnp.concatenate(local, axis=1)
                + part.skip_wide * part.inner
                + part.carried_wide * product(part.read, reached, ((1,), (1,)))
            )
            y_ref[at, :] = y
            gated = y * part.gate * sigma(part.gate)
            state[...] = part.last * reached + product(
                part.tails_wide * part.scaled, part.write, ((0,), (0,))
            )
            heads_in[at, :] = p[:, lay.query : lay.query + 3 * HEAD].astype(jnp.bfloat16)
            mixed_ref[at, HEAD:] = gated.astype(jnp.bfloat16)
            return 0

        lax.fori_loop(0, chunks, chunk, 0)
        for b in range(length // block):
            at, keys = slice(b * block, (b + 1) * block), (b + 1) * block
            scores = product(
                heads_in[at, :HEAD], heads_in[:keys, HEAD : 2 * HEAD], ((1,), (1,))
            ) * (HEAD**-0.5)
            allowed = attention_mask(col_ref[at, 6:7], seg_ref[:, :keys], b * block)
            scores = jnp.where(allowed, scores, -1e30)
            top = jnp.max(scores, axis=1, keepdims=True)
            terms = jnp.where(allowed, jnp.exp(scores - top), 0.0)
            total = jnp.sum(terms, axis=1, keepdims=True)
            top_ref[at, :] = top + jnp.log(total)
            probs = (terms * (1.0 / total)).astype(jnp.bfloat16)
            mixed_ref[at, :HEAD] = product(probs, heads_in[:keys, 2 * HEAD :]).astype(jnp.bfloat16)

    return pl.pallas_call(
        kernel,
        out_shape=(
            like((length, HEAD + wide)),
            like((length, lay.width), jnp.float32),
            like((length, wide), jnp.float32),
            like((chunks, wide, STATE), jnp.float32),
            like((length, 1), jnp.float32),
        ),
        in_specs=[IN_VMEM] * 6,
        out_specs=(IN_VMEM,) * 5,
        scratch_shapes=[
            pltpu.VMEM((size + 8, lay.conv), jnp.float32),
            pltpu.VMEM((wide, STATE), jnp.float32),
            pltpu.VMEM((length, 3 * HEAD), jnp.bfloat16),
        ],
        compiler_params=pltpu.CompilerParams(vmem_limit_bytes=48 * 2**20),
    )(normed, entry, columns, seg_row, taps, head_rows)


def mix_backward(
    residual_half, out_rows, mixed_out, p, y, states, log_total, columns, seg_row, taps, head_rows, size
):
    length = p.shape[0]
    chunks = length // size
    heads = SSM_HEADS // lax.axis_size("ctx")
    lay = Layout(heads)
    wide = heads * SSM_HEAD
    block = 2 * size if chunks % 2 == 0 else size

    def kernel(
        r_ref, o_ref, mixed_ref, p_ref, y_ref, states_ref, top_ref, col_ref, seg_ref, tap_ref, head_ref,
        g_ref, tap_sum, head_sum, outs_ref, ext, ahead, out_grad, step_grad, state, heads_in, key_grad, value_grad,
    ):
        state[...] = jnp.zeros_like(state)
        ahead[size:, :] = jnp.zeros((8, lay.conv), jnp.float32)
        tap_sum[...] = jnp.zeros_like(tap_sum)
        head_sum[...] = jnp.zeros_like(head_sum)

        def chunk(step, _):
            j = chunks - 1 - step
            at = rows_of(j, size)
            p, a = p_ref[at, :], col_ref[at, :]
            ext[8:, :] = p[:, : lay.conv]
            ext[0:8, :] = p_ref[pl.ds(pl.multiple_of(jnp.maximum(j * size - 8, 0), 8), 8), : lay.conv]
            part = Chunk(
                lay, heads, p, a, seg_ref[:, at], tap_ref, head_ref,
                lambda k: ext[8 - k : 8 - k + size, :],
            )
            grads = product(r_ref[at, :], o_ref[...], ((1,), (1,)))
            out_grad[at, :] = grads[:, :HEAD].astype(jnp.bfloat16)
            gated_grad = grads[:, HEAD:]
            y = y_ref[at, :]
            gate_sig = sigma(part.gate)
            gate_grad = gated_grad * y * gate_sig * (1.0 + part.gate * (1.0 - gate_sig))
            dy = gated_grad * part.gate * gate_sig
            later = state[...]
            before = states_ref[j]
            reached = part.carried_wide * product(part.read, before, ((1,), (1,)))
            from_later = part.tails_wide * product(part.write, later, ((1,), (1,)))
            cross_grad = jnp.zeros((size, size), jnp.float32)
            local, row_sums, column_sums = [], [], []
            for h in range(heads):
                cut = slice(h * SSM_HEAD, (h + 1) * SSM_HEAD)
                mixing = part.decay[h] * part.cross
                mixing_grad = product(dy[:, cut], part.scaled[:, cut], ((1,), (1,)))
                local.append(product(mixing, dy[:, cut], ((0,), (0,))))
                cross_grad = cross_grad + part.decay[h] * mixing_grad
                weight = mixing * mixing_grad
                row_sums.append(jnp.sum(weight, axis=1, keepdims=True))
                column_sums.append(jnp.sum(weight, axis=0, keepdims=True))
            scaled_grad = jnp.concatenate(local, axis=1) + from_later
            carried_dy = part.carried_wide * dy
            tail_terms = part.tails_wide * part.scaled
            read_grad = product(cross_grad, part.write) + product(carried_dy, before)
            write_grad = product(cross_grad, part.read, ((0,), (0,))) + product(tail_terms, later)
            inner_grad = part.skip_wide * dy + widen(part.steps, heads) * scaled_grad
            tail_sums = head_sums(part.scaled * from_later, heads, lay.steps)
            run_grad = (
                columns_of(row_sums, lay.steps)
                + head_sums(dy * reached, heads, lay.steps)
                - tail_sums
            )
            ends = later * before * part.last
            end_sums = [
                jnp.sum(
                    jnp.sum(ends[h * SSM_HEAD : (h + 1) * SSM_HEAD, :], axis=1, keepdims=True),
                    axis=0,
                    keepdims=True,
                )
                for h in range(heads)
            ]
            final = columns_of(end_sums, lay.steps) + jnp.sum(tail_sums, axis=0, keepdims=True)
            column_rows = jnp.concatenate(
                column_sums + [jnp.zeros((lay.steps - heads, size), jnp.float32)], axis=0
            )
            rate_grad = (
                product(part.ones, run_grad, ((0,), (0,)), precision=highest)
                - product(part.ones, column_rows, ((0,), (1,)), precision=highest)
                + final
            )
            steps_grad = (
                head_sums(scaled_grad * part.inner, heads, lay.steps) + rate_grad * head_ref[0:1, :]
            )
            raw_grad = steps_grad * sigma(part.biased)
            step_grad[at, :] = raw_grad
            head_sum[0:1, :] += jnp.sum(rate_grad * part.rates, axis=0, keepdims=True)
            head_sum[1:2, :] += jnp.sum(raw_grad, axis=0, keepdims=True)
            head_sum[2:3, :] += jnp.sum(
                head_sums(dy * part.inner, heads, lay.steps), axis=0, keepdims=True
            )
            state[...] = part.last * later + product(carried_dy, part.read, ((0,), (0,)))
            converted_grad = jnp.concatenate([write_grad, read_grad, inner_grad], axis=1)
            pre_grad = converted_grad * part.sig * (1.0 + part.pre * (1.0 - part.sig))
            ahead[:size, :] = pre_grad
            conv_grad = tap_ref[3:4, :] * pre_grad
            tap_sum[3:4, :] += jnp.sum(pre_grad * part.conv_in, axis=0, keepdims=True)
            tap_sum[4:5, :] += jnp.sum(pre_grad, axis=0, keepdims=True)
            for k in (1, 2, 3):
                conv_grad = (
                    conv_grad
                    + jnp.where(a[:, 2 + k : 3 + k] > 0.0, ahead[k : k + size, :], 0.0)
                    * tap_ref[3 - k : 4 - k, :]
                )
                tap_sum[3 - k : 4 - k, :] += jnp.sum(
                    pre_grad * part.earlier[k - 1], axis=0, keepdims=True
                )
            ahead[size:, :] = ahead[0:8, :]
            g_ref[at, : lay.query] = jnp.concatenate([conv_grad, gate_grad], axis=1).astype(
                jnp.bfloat16
            )
            heads_in[at, :] = p[:, lay.query : lay.step].astype(jnp.bfloat16)
            return 0

        lax.fori_loop(0, chunks, chunk, 0)
        key_grad[...] = jnp.zeros_like(key_grad)
        value_grad[...] = jnp.zeros_like(value_grad)
        query_grads = []
        for b in range(length // block):
            at, keys = slice(b * block, (b + 1) * block), (b + 1) * block
            queries, grad = heads_in[at, :HEAD], out_grad[at, :]
            key_part, value_part = heads_in[:keys, HEAD : 2 * HEAD], heads_in[:keys, 2 * HEAD :]
            scores = product(queries, key_part, ((1,), (1,))) * (HEAD**-0.5)
            allowed = attention_mask(col_ref[at, 6:7], seg_ref[:, :keys], b * block)
            probs = jnp.where(allowed, jnp.exp(scores - top_ref[at, :]), 0.0)
            deltas = jnp.sum(
                grad.astype(jnp.float32) * mixed_ref[at, :HEAD].astype(jnp.float32),
                axis=1,
                keepdims=True,
            )
            prob_grad = product(grad, value_part, ((1,), (1,)))
            score_grad = (probs * (prob_grad - deltas)).astype(jnp.bfloat16)
            query_grads.append(product(score_grad, key_part) * (HEAD**-0.5))
            key_grad[:keys, :] += product(score_grad, queries, ((0,), (0,))) * (HEAD**-0.5)
            value_grad[:keys, :] += product(probs.astype(jnp.bfloat16), grad, ((0,), (0,)))
        for b, query_grad in enumerate(query_grads):
            at = slice(b * block, (b + 1) * block)
            g_ref[at, lay.query :] = jnp.concatenate(
                [query_grad, key_grad[at, :], value_grad[at, :], step_grad[at, :]], axis=1
            ).astype(jnp.bfloat16)
        outs_ref[...] = product(mixed_ref[...], r_ref[...], ((0,), (0,))).astype(jnp.bfloat16)

    f32 = jnp.float32
    return pl.pallas_call(
        kernel,
        out_shape=(
            like((length, lay.width)),
            like((8, lay.conv), f32),
            like((8, lay.steps), f32),
            like(out_rows.shape),
        ),
        in_specs=[IN_VMEM] * 11,
        out_specs=(IN_VMEM,) * 4,
        scratch_shapes=[
            pltpu.VMEM((size + 8, lay.conv), f32),
            pltpu.VMEM((size + 8, lay.conv), f32),
            pltpu.VMEM((length, HEAD), jnp.bfloat16),
            pltpu.VMEM((length, lay.steps), f32),
            pltpu.VMEM((wide, STATE), f32),
            pltpu.VMEM((length, 3 * HEAD), jnp.bfloat16),
            pltpu.VMEM((length, HEAD), f32),
            pltpu.VMEM((length, HEAD), f32),
        ],
        compiler_params=pltpu.CompilerParams(vmem_limit_bytes=56 * 2**20),
    )(residual_half, out_rows, mixed_out, p, y, states, log_total, columns, seg_row, taps, head_rows)


def across(left, right):
    return jnp.dot(left.T, right, preferred_element_type=jnp.float32).astype(jnp.bfloat16)


def split_local(
    block_input,
    segment_ids,
    out_cotangent,
    attention_in,
    mixer_in,
    step_in,
    attention_out,
    mixer_out,
    gate_up,
    down_weight,
    gain_mixing,
    gain_feed,
    decay_log,
    step_bias,
    skip_gain,
    conv_weight,
    conv_bias,
):
    ctx, dp = lax.axis_size("ctx"), lax.axis_size("dp")
    mine = lax.axis_index("ctx")
    tok_count, width = block_input.shape[1:]
    length = tok_count * ctx
    heads = SSM_HEADS // ctx
    rows = attention_in.shape[0]
    hidden = down_weight.shape[0]
    slabs = entry_slabs(attention_in, mixer_in, step_in, ctx)
    gate_slabs = gate_up.reshape(rows, 2, dp, ctx, hidden).transpose(3, 0, 1, 2, 4)
    gate_slabs = gate_slabs.reshape(ctx, rows, 2 * dp * hidden)
    own_attention = attention_out.shape[0]

    source = block_input.reshape(tok_count, width).astype(jnp.float32)
    cotangent = out_cotangent.reshape(tok_count, width)
    normed_own = rms_scale(source, gain_mixing).astype(jnp.bfloat16)
    outs = jnp.concatenate([attention_out, mixer_out], axis=0)
    normed, segments, entry, feed_slabs, outs = enter(
        normed_own, segment_ids, slabs, gate_slabs, outs
    )
    normed, segments = normed.reshape(length, width), segments.reshape(length)
    entry = entry.reshape(dp * ctx * rows, -1)
    late_cotangent, _ = lax.optimization_barrier((cotangent, segments))
    cotangents = lax.all_gather(late_cotangent, "ctx", axis=0, tiled=True)
    out_rows = jnp.concatenate(
        [outs[:, :own_attention].reshape(-1, width), outs[:, own_attention:].reshape(-1, width)],
        axis=0,
    )

    own = lambda array, at, size: lax.dynamic_slice_in_dim(array, at + mine * size, size, axis=-1)
    conv_own = lambda array: jnp.concatenate(
        [array[:, SSM_INNER:], own(array, 0, heads * SSM_HEAD)], axis=-1
    )
    taps = jnp.pad(conv_own(jnp.concatenate([conv_weight, conv_bias[None]], axis=0)), ((0, 3), (0, 0)))
    head_rows = jnp.stack(
        [own(part, 0, heads) for part in (-jnp.exp(decay_log), step_bias, skip_gain)]
    )
    head_rows = jnp.pad(head_rows, ((0, 5), (0, Layout(heads).steps - heads)))
    keeps = []
    for offset in (1, 2, 3):
        earlier = jnp.concatenate([jnp.full((offset,), -1, segments.dtype), segments[:-offset]])
        keeps.append(earlier == segments)
    nexts = [jnp.pad(keep[k + 1 :], (0, k + 1)) for k, keep in enumerate(keeps)]
    chunk_last = segments.reshape(ctx, tok_count)[:, -1]
    spread = lambda ids: jnp.repeat(ids, tok_count) == segments
    opens = spread(jnp.concatenate([jnp.full((1,), -1, segments.dtype), chunk_last[:-1]]))
    marks = keeps + nexts + [segments, opens, spread(chunk_last)]
    columns = jnp.stack([mark.astype(jnp.float32) for mark in marks], axis=1)
    columns = jnp.pad(columns, ((0, 0), (0, 16 - len(marks))))
    seg_row = segments.astype(jnp.float32).reshape(1, length)
    mixed_out, entry_product, scanned, states, log_total = mix_forward(
        normed, entry, columns, seg_row, taps, head_rows, tok_count
    )
    mixing_out, feed_in, feed_out = sum_and_spread(
        mixed_out, out_rows, (feed_slabs.reshape(ctx * rows, -1), down_weight), 1
    )
    feed_in = feed_in.reshape(dp * ctx * rows, -1)
    feed_out = feed_out.reshape(dp * hidden, width)
    residual = source + mixing_out

    normed_two_own, pull_two = jax.vjp(rms_scale, residual, gain_feed)
    normed_two = gather_tokens(normed_two_own.astype(jnp.bfloat16), 2)
    gate_values = jnp.dot(normed_two, feed_in, preferred_element_type=jnp.float32)
    gate_in, up_in = gate_values[:, : dp * hidden], gate_values[:, dp * hidden :]
    active = (jax.nn.silu(gate_in) * up_in).astype(jnp.bfloat16)
    output_terms = jnp.dot(active, feed_out, preferred_element_type=jnp.float32).astype(jnp.bfloat16)
    active_grad = jnp.dot(cotangents, feed_out.T, preferred_element_type=jnp.float32)
    gate_grad = jnp.concatenate(
        [active_grad * up_in * silu_slope(gate_in), active_grad * jax.nn.silu(gate_in)], axis=1
    ).astype(jnp.bfloat16)
    normed_two_grad, feed_sums, grad_feed_out = sum_and_total(
        gate_grad,
        feed_in,
        (
            across(normed_two, gate_grad).reshape(dp, ctx * rows, -1),
            across(active, cotangents).reshape(dp, hidden, width),
        ),
        3,
    )
    residual_part, grad_gain_feed = pull_two(normed_two_grad)
    residual_grad = cotangent.astype(jnp.float32) + residual_part
    residual_half = gather_tokens(residual_grad.astype(jnp.bfloat16), 4)
    late_terms, _ = lax.optimization_barrier((output_terms, residual_half))
    output_sum = lax.psum_scatter(late_terms, "ctx", scatter_dimension=0, tiled=True)
    output = (residual + output_sum.astype(jnp.float32)).astype(jnp.bfloat16)
    grads, tap_grads, head_grads, out_terms = mix_backward(
        residual_half,
        out_rows,
        mixed_out,
        entry_product,
        scanned,
        states,
        log_total,
        columns,
        seg_row,
        taps,
        head_rows,
        tok_count,
    )
    taken = own_attention * dp
    out_terms = jnp.concatenate(
        [
            out_terms[:taken].reshape(dp, own_attention, width),
            out_terms[taken:].reshape(dp, -1, width),
        ],
        axis=1,
    )
    own_small = jnp.concatenate(
        [grad_gain_feed, tap_grads[:5].reshape(-1), head_grads[:3, :heads].reshape(-1)], axis=0
    )
    own_small = jnp.pad(own_small, (0, -own_small.shape[0] % 1024)).reshape(-1, 128)
    input_grad, entry_grads, grad_feed_in, grad_outs, smalls, gains = leave(
        grads,
        entry,
        source,
        residual_grad,
        gain_mixing.reshape(1, width),
        across(normed, grads).reshape(dp, ctx, rows, -1),
        feed_sums.reshape(ctx, rows, -1),
        out_terms,
        own_small,
    )
    grad_attention_in, grad_mixer_in, grad_step_in = entry_unslab(
        entry_grads.astype(jnp.float32), ctx
    )
    smalls = smalls.reshape(ctx, -1)
    tap_width = heads * SSM_HEAD + 2 * STATE
    tap_all = smalls[:, width : width + 5 * tap_width].reshape(ctx, 5, tap_width)
    tap_sums = jnp.concatenate(
        [
            tap_all[:, :, 2 * STATE :].transpose(1, 0, 2).reshape(5, SSM_INNER),
            jnp.sum(tap_all[:, :, : 2 * STATE], axis=0),
        ],
        axis=1,
    )
    head_all = smalls[:, width + 5 * tap_width :][:, : 3 * heads].reshape(ctx, 3, heads)
    head_sums = head_all.transpose(1, 0, 2).reshape(3, SSM_HEADS)
    grad_gate_up = (
        grad_feed_in.reshape(ctx, rows, 2, dp, hidden)
        .transpose(1, 2, 3, 0, 4)
        .reshape(rows, -1)
        .astype(jnp.float32)
    )
    return (
        output.reshape(block_input.shape),
        input_grad.reshape(block_input.shape),
        grad_attention_in,
        grad_mixer_in,
        grad_step_in,
        grad_outs[:own_attention],
        grad_outs[own_attention:],
        grad_gate_up,
        grad_feed_out.astype(jnp.float32),
        jnp.sum(gains, axis=(0, 1)),
        jnp.sum(smalls[:, :width], axis=0),
        head_sums[0],
        head_sums[1],
        head_sums[2],
        tap_sums[:4],
        tap_sums[4],
    )


def solution(mesh):
    in_specs = (
        P("dp", "ctx", None),
        P("dp", "ctx"),
        P("dp", "ctx", None),
        P(("dp", "ctx"), None),
        P(("dp", "ctx"), None),
        P(("dp", "ctx"), None),
        P(("dp", "ctx"), None),
        P(("dp", "ctx"), None),
        P(("dp", "ctx"), None),
        P(("dp", "ctx"), None),
        P(),
        P(),
        P(),
        P(),
        P(),
        P(),
        P(),
    )
    out_specs = (
        P("dp", "ctx", None),
        P("dp", "ctx", None),
        P(("dp", "ctx"), None),
        P(("dp", "ctx"), None),
        P(("dp", "ctx"), None),
        P(("dp", "ctx"), None),
        P(("dp", "ctx"), None),
        P(("dp", "ctx"), None),
        P(("dp", "ctx"), None),
        P(),
        P(),
        P(),
        P(),
        P(),
        P(),
        P(),
    )
    sequences = mesh.shape["dp"]

    def choose(*arrays):
        heads = split_heads(mesh.shape["ctx"]) and arrays[0].shape[0] == sequences
        body = split_local if heads else local
        mapped = jax.shard_map(
            body, mesh=mesh, in_specs=in_specs, out_specs=out_specs, check_vma=False
        )
        return mapped(*arrays)

    return choose
```

```python
import functools
import math

import jax
import jax.numpy as jnp
from jax import lax
from jax.experimental import pallas as pl
from jax.experimental.pallas import tpu as pltpu
from jax.sharding import PartitionSpec as P

FF = 2048
HEADS_Q = 8
HEADS_KV = 2
HEAD = 64
SSM_HEADS = 24
SSM_HEAD = 64
STATE = 128
SSM_INNER = 1536


highest = lax.Precision.HIGHEST


def from_behind(block, axis, distance):
    devices = range(lax.axis_size(axis))
    route = [(i - distance, i) for i in devices if i - distance in devices]
    return lax.ppermute(block, axis, route)


def carried_in(value, axis, join, neutral, backward):
    count, mine = (lax.axis_size(axis), lax.axis_index(axis))
    pieces = jax.tree.map(lambda part: lax.all_gather(part, axis), value)
    if backward:
        pieces = jax.tree.map(lambda part: part[::-1], pieces)
        mine = count - 1 - mine
    so_far = jax.tree.map(
        lambda part, zero: jnp.full_like(part, 0) + jnp.asarray(zero, part.dtype), value, neutral
    )

    def hop(position, so_far):
        longer = join(so_far, jax.tree.map(lambda part: part[position], pieces))
        return jax.tree.map(lambda new, old: jnp.where(position < mine, new, old), longer, so_far)

    return lax.fori_loop(0, count - 1, hop, so_far)


def carried_by_heads(decays, state, backward):
    count, mine = (lax.axis_size("ctx"), lax.axis_index("ctx"))
    seq_count, heads = decays.shape[1:]
    share = heads // count
    own = lax.dynamic_slice_in_dim(decays, mine * share, share, axis=2)
    pieces = lax.all_to_all(state, "ctx", split_axis=1, concat_axis=0, tiled=True)
    pieces = pieces.reshape((count, seq_count, share) + state.shape[2:])
    order = list(range(count))[::-1] if backward else list(range(count))
    so_far = jnp.zeros_like(pieces[0])
    reached = [None] * count
    for position in order:
        reached[position] = so_far
        so_far = own[position][:, :, None, None] * so_far + pieces[position]
    return lax.all_to_all(
        jnp.concatenate(reached, axis=0), "ctx", split_axis=0, concat_axis=1, tiled=True
    )


def fold_shape(owned, rows, width):
    step = math.gcd(owned, rows)
    return (step, owned // step, rows // step, width // (rows // step))


def fold_rows(array, owned, rows):
    step, across, down, part = fold_shape(owned, rows, array.shape[1])
    blocks = array.reshape(-1, owned, array.shape[1])
    columns = [
        jnp.concatenate(
            [blocks[:, i * step : (i + 1) * step, j * part : (j + 1) * part] for j in range(down)],
            axis=1,
        )
        for i in range(across)
    ]
    return jnp.concatenate(columns, axis=2).reshape(-1, across * part)


def unfold_rows(array, owned, rows, width):
    step, across, down, part = fold_shape(owned, rows, width)
    blocks = array.reshape(-1, rows, across * part)
    lines = [
        jnp.concatenate(
            [blocks[:, j * step : (j + 1) * step, i * part : (i + 1) * part] for j in range(down)],
            axis=2,
        )
        for i in range(across)
    ]
    return jnp.concatenate(lines, axis=1).reshape(-1, width)


def pad_columns(array):
    return jnp.pad(array, ((0, 0), (0, -array.shape[1] % 128)))


def cut_columns(array, widths):
    pieces, at = ([], 0)
    for width in widths:
        pieces.append(array[:, at : at + width])
        at += width
    return pieces


def rms_scale(values, gain):
    return values * lax.rsqrt(jnp.mean(values * values, axis=-1, keepdims=True) + 1e-05) * gain


def silu_slope(values):
    sigma = jax.nn.sigmoid(values)
    return sigma * (1.0 + values * (1.0 - sigma))


def ssd_local(
    inner, write_map, read_map, step_raw, decay_log, step_bias, skip_gain, starts, segments
):
    step = jax.nn.softplus(step_raw + step_bias)
    rates = step * -jnp.exp(decay_log)
    places = jnp.arange(segments.shape[0])
    lower = places[None, :] <= places[:, None]
    running = jnp.dot(lower.astype(jnp.float32), rates, precision=highest)
    same = (segments[:, None] == segments[None, :]) & lower
    spans = jnp.where(same[None], running.T[:, :, None] - running.T[:, None, :], -1e30)
    intersection = jnp.dot(read_map, write_map.T, precision=highest)
    mixing = jnp.exp(spans) * intersection[None] * step.T[:, None, :]
    result = (
        jnp.einsum("hts,shp->thp", mixing, inner, precision=highest)
        + skip_gain[None, :, None] * inner
    )
    before = jnp.sum((lower & starts[None, :]).astype(jnp.int32), axis=1) == 0
    carried = jnp.where(before[:, None], jnp.exp(running), 0.0)
    tails = jnp.where(
        (segments == segments[-1])[:, None], jnp.exp(running[-1][None, :] - running), 0.0
    )
    state = jnp.einsum("sh,shp,sn->hpn", tails * step, inner, write_map, precision=highest)
    return (result, state, carried[-1], carried)


def add_state(result, carried, read_map, state_in):
    return result + carried[:, :, None] * jnp.einsum(
        "hpn,tn->thp", state_in, read_map, precision=highest
    )


def ssd_block(
    inner,
    write_map,
    read_map,
    step_raw,
    decay_log,
    step_bias,
    skip_gain,
    starts,
    segments,
    state_in,
):
    result, state, decay_total, carried = ssd_local(
        inner, write_map, read_map, step_raw, decay_log, step_bias, skip_gain, starts, segments
    )
    return (
        add_state(result, carried, read_map, state_in),
        decay_total[:, None, None] * state_in + state,
    )


def chain(earlier, later):
    return (earlier[0] * later[0], later[0][:, :, None, None] * earlier[1] + later[1])


def over_blocks(step, start, items):
    if items[2].shape[0] > 1:
        return lax.scan(step, start, items)
    carry, result = step(start, (items[0][0], items[1][0], 0))
    return (carry, None if result is None else result[None])


def group_queries(flat, seq_count, tok_count):
    groups = HEADS_Q // HEADS_KV
    shaped = flat.reshape(seq_count, tok_count, HEADS_KV, groups, HEAD)
    return shaped.transpose(0, 2, 3, 1, 4).reshape(seq_count, HEADS_KV, groups * tok_count, HEAD)


def ungroup(grouped, seq_count, tok_count):
    groups = HEADS_Q // HEADS_KV
    shaped = grouped.reshape(seq_count, HEADS_KV, groups, tok_count, HEAD)
    return shaped.transpose(0, 3, 1, 2, 4).reshape(seq_count * tok_count, HEADS_Q * HEAD)


def local(
    block_input,
    segment_ids,
    out_cotangent,
    attention_in,
    mixer_in,
    step_in,
    attention_out,
    mixer_out,
    gate_up,
    down_weight,
    gain_mixing,
    gain_feed,
    decay_log,
    step_bias,
    skip_gain,
    conv_weight,
    conv_bias,
):
    seq_count, tok_count, width = block_input.shape
    row_count = seq_count * tok_count
    length = tok_count * lax.axis_size("ctx")
    block = length if length <= 1024 else 512
    blocks = length // block
    groups = HEADS_Q // HEADS_KV
    query_width = HEADS_Q * HEAD
    key_width = HEADS_KV * HEAD
    score_scale = HEAD ** (-0.5)
    query_rows = groups * tok_count
    first = lax.axis_index("ctx") * tok_count
    own_rows = attention_in.shape[0]
    axes = ("dp", "ctx")
    entry = jnp.concatenate([attention_in, mixer_in, pad_columns(step_in)], axis=1)
    full_attention_in, full_mixer_in, full_step_in = cut_columns(
        lax.all_gather(entry, axes, axis=0, tiled=True),
        (attention_in.shape[1], mixer_in.shape[1], step_in.shape[1]),
    )
    tall = (attention_out, mixer_out, down_weight)
    folded = [fold_rows(weight, weight.shape[0], own_rows) for weight in tall]
    rest = lax.all_gather(
        jnp.concatenate(folded + [gate_up], axis=1), axes, axis=0, tiled=True
    )
    rest = cut_columns(rest, [weight.shape[1] for weight in folded] + [gate_up.shape[1]])
    full_attention_out, full_mixer_out, full_down = (
        unfold_rows(part, weight.shape[0], own_rows, width) for part, weight in zip(rest, tall)
    )
    full_gate_up = rest[3]
    source = block_input.reshape(row_count, width).astype(jnp.float32)
    normed = rms_scale(source, gain_mixing).astype(jnp.bfloat16)
    projected = jnp.dot(normed, full_attention_in, preferred_element_type=jnp.float32).astype(
        jnp.bfloat16
    )
    mixed_in = jnp.dot(normed, full_mixer_in, preferred_element_type=jnp.float32)
    step_raw = jnp.dot(normed, full_step_in, preferred_element_type=jnp.float32).reshape(
        seq_count, tok_count, SSM_HEADS
    )
    queries = group_queries(projected[:, :query_width], seq_count, tok_count)
    local_keys = (
        projected[:, query_width:].reshape(seq_count, tok_count, 2 * key_width).transpose(1, 0, 2)
    )
    local_segments = segment_ids.T
    keys_all, segments_all = (
        lax.all_gather(local_keys, "ctx", axis=0, tiled=True),
        lax.all_gather(local_segments, "ctx", axis=0, tiled=True),
    )
    query_pos = first + jnp.arange(query_rows) % tok_count
    query_segments = jnp.tile(segment_ids, (1, groups))
    segment_blocks = segments_all.reshape(blocks, block, seq_count)
    block_ids = jnp.arange(blocks)

    def scores_of(key_block, seg_block, block_id):
        keys = key_block[:, :, :key_width].reshape(block, seq_count, HEADS_KV, HEAD)
        scores = (
            jnp.einsum("sgrd,ksgd->sgrk", queries, keys, preferred_element_type=jnp.float32)
            * score_scale
        )
        key_pos = block_id * block + jnp.arange(block)
        allowed = (key_pos[None, None, None, :] <= query_pos[None, None, :, None]) & (
            seg_block.T[:, None, None, :] == query_segments[:, None, :, None]
        )
        return (scores, allowed)

    key_blocks = keys_all.reshape(blocks, block, seq_count, 2 * key_width)

    def gather_stats(carry, item):
        top, total = carry
        scores, allowed = scores_of(item[0], item[1], item[2])
        masked = jnp.where(allowed, scores, -1e30)
        new_top = jnp.maximum(top, jnp.max(masked, axis=-1))
        total = total * jnp.exp(top - new_top) + jnp.sum(
            jnp.where(allowed, jnp.exp(masked - new_top[..., None]), 0.0), axis=-1
        )
        return ((new_top, total), None)

    start_top = jnp.full((seq_count, HEADS_KV, query_rows), -1e30, jnp.float32)
    (top, total), _ = over_blocks(
        gather_stats,
        (start_top, jnp.zeros_like(start_top)),
        (key_blocks, segment_blocks, block_ids),
    )
    log_total = top + jnp.log(total)

    def weigh_values(accum, item):
        scores, allowed = scores_of(item[0], item[1], item[2])
        values = item[0][:, :, key_width:].reshape(block, seq_count, HEADS_KV, HEAD)
        probs = jnp.where(allowed, jnp.exp(scores - log_total[..., None]), 0.0).astype(jnp.bfloat16)
        return (
            accum
            + jnp.einsum("sgrk,ksgd->sgrd", probs, values, preferred_element_type=jnp.float32),
            None,
        )

    attended, _ = over_blocks(
        weigh_values, jnp.zeros(queries.shape, jnp.float32), (key_blocks, segment_blocks, block_ids)
    )
    attended = attended.astype(jnp.bfloat16)
    attended_flat = ungroup(attended, seq_count, tok_count)
    gate_part = mixed_in[:, :SSM_INNER]
    conv_width = mixed_in.shape[1] - SSM_INNER
    conv_in = mixed_in[:, SSM_INNER:].reshape(seq_count, tok_count, conv_width)
    positions = first + jnp.arange(tok_count)
    before_rows = from_behind(conv_in[:, tok_count - 3 :, :], "ctx", 1)
    extended = jnp.concatenate([before_rows, conv_in], axis=1)
    pre = conv_bias + conv_weight[3] * conv_in
    keep_masks = []
    for offset in (1, 2, 3):
        earlier_ids = segments_all[jnp.maximum(positions - offset, 0)].T
        keep_mask = (positions >= offset)[None, :] & (earlier_ids == segment_ids)
        keep_masks.append(keep_mask)
        pre = (
            pre
            + jnp.where(keep_mask[..., None], extended[:, 3 - offset : 3 - offset + tok_count], 0.0)
            * conv_weight[3 - offset]
        )
    converted = jax.nn.silu(pre)
    inner = converted[..., :SSM_INNER].reshape(seq_count, tok_count, SSM_HEADS, SSM_HEAD)
    write_map = converted[..., SSM_INNER : SSM_INNER + STATE]
    read_map = converted[..., SSM_INNER + STATE :]
    starts = (positions == 0)[None, :] | jnp.logical_not(keep_masks[0])
    local_map = jax.vmap(ssd_local, in_axes=(0, 0, 0, 0, None, None, None, 0, 0))
    partial_out, partial_state, decay_total, carried = local_map(
        inner, write_map, read_map, step_raw, decay_log, step_bias, skip_gain, starts, segment_ids
    )
    by_heads = SSM_HEADS % lax.axis_size("ctx") == 0
    if by_heads:
        decays = lax.all_gather(decay_total, "ctx")
        state_in = carried_by_heads(decays, partial_state, False)
    else:
        unit = (jnp.ones_like(decay_total), jnp.zeros_like(partial_state))
        state_in = carried_in((decay_total, partial_state), "ctx", chain, unit, False)[1]
    scanned = jax.vmap(add_state)(partial_out, carried, read_map, state_in)
    flat_scan = scanned.reshape(row_count, SSM_INNER)
    gated = (flat_scan * jax.nn.silu(gate_part)).astype(jnp.bfloat16)
    residual = (
        source
        + jnp.dot(attended_flat, full_attention_out, preferred_element_type=jnp.float32)
        + jnp.dot(gated, full_mixer_out, preferred_element_type=jnp.float32)
    )
    normed_two = rms_scale(residual, gain_feed).astype(jnp.bfloat16)
    gate_values = jnp.dot(normed_two, full_gate_up, preferred_element_type=jnp.float32)
    gate_in = gate_values[:, :FF]
    up_in = gate_values[:, FF:]
    active = (jax.nn.silu(gate_in) * up_in).astype(jnp.bfloat16)
    output = (residual + jnp.dot(active, full_down, preferred_element_type=jnp.float32)).astype(
        jnp.bfloat16
    )
    cotangent = out_cotangent.reshape(row_count, width)
    grad_down_weight = jnp.dot(active.T, cotangent, preferred_element_type=jnp.float32).astype(
        jnp.bfloat16
    )
    active_grad = jnp.dot(cotangent, full_down.T, preferred_element_type=jnp.float32)
    gate_grad = jnp.concatenate(
        [active_grad * up_in * silu_slope(gate_in), active_grad * jax.nn.silu(gate_in)], axis=1
    ).astype(jnp.bfloat16)
    grad_gate_up = jnp.dot(normed_two.T, gate_grad, preferred_element_type=jnp.float32).astype(
        jnp.bfloat16
    )
    feed_terms = jnp.concatenate(
        [grad_gate_up, fold_rows(grad_down_weight, down_weight.shape[0], own_rows)], axis=1
    )
    feed_sums = lax.psum_scatter(feed_terms, axes, scatter_dimension=0, tiled=True)
    normed_two_grad = jnp.dot(gate_grad, full_gate_up.T, preferred_element_type=jnp.float32)
    _, pull_two = jax.vjp(rms_scale, residual, gain_feed)
    residual_part, grad_gain_feed = pull_two(normed_two_grad)
    residual_grad = cotangent.astype(jnp.float32) + residual_part
    residual_half, _ = lax.optimization_barrier((residual_grad.astype(jnp.bfloat16), feed_terms))
    grad_attention_out = jnp.dot(attended_flat.T, residual_half, preferred_element_type=jnp.float32)
    grad_mixer_out = jnp.dot(gated.T, residual_half, preferred_element_type=jnp.float32)
    attended_grad = jnp.dot(
        residual_half, full_attention_out.T, preferred_element_type=jnp.float32
    ).astype(jnp.bfloat16)
    gated_grad = jnp.dot(residual_half, full_mixer_out.T, preferred_element_type=jnp.float32)
    gate_part_grad = gated_grad * flat_scan * silu_slope(gate_part)
    scan_grad = (gated_grad * jax.nn.silu(gate_part)).reshape(
        seq_count, tok_count, SSM_HEADS, SSM_HEAD
    )
    direct = jnp.einsum("sth,sthp,stn->shpn", carried, scan_grad, read_map, precision=highest)
    if by_heads:
        state_grad = carried_by_heads(decays, direct, True)
    else:
        state_grad = carried_in((decay_total, direct), "ctx", chain, unit, True)[1]

    def block_map(inner_v, write_v, read_v, step_v, decay_v, bias_v, skip_v, state_v):
        mapped = jax.vmap(ssd_block, in_axes=(0, 0, 0, 0, None, None, None, 0, 0, 0))
        return mapped(
            inner_v, write_v, read_v, step_v, decay_v, bias_v, skip_v, starts, segment_ids, state_v
        )

    _, pull_scan = jax.vjp(
        block_map, inner, write_map, read_map, step_raw, decay_log, step_bias, skip_gain, state_in
    )
    pulled = pull_scan((scan_grad, state_grad))
    converted_grad = jnp.concatenate(
        [pulled[0].reshape(seq_count, tok_count, SSM_INNER), pulled[1], pulled[2]], axis=2
    )
    pre_grad = converted_grad * silu_slope(pre)
    after_rows = from_behind(pre_grad[:, :3, :], "ctx", -1)
    ahead = jnp.concatenate([pre_grad, after_rows], axis=1)
    conv_in_grad = conv_weight[3] * pre_grad
    tap_grads = [None, None, None, jnp.sum(pre_grad * conv_in, axis=(0, 1))]
    for offset in (1, 2, 3):
        later_ids = segments_all[jnp.minimum(positions + offset, length - 1)].T
        later_mask = later_ids == segment_ids
        conv_in_grad = (
            conv_in_grad
            + jnp.where(later_mask[..., None], ahead[:, offset : offset + tok_count], 0.0)
            * conv_weight[3 - offset]
        )
        earlier_rows = jnp.where(
            keep_masks[offset - 1][..., None], extended[:, 3 - offset : 3 - offset + tok_count], 0.0
        )
        tap_grads[3 - offset] = jnp.sum(pre_grad * earlier_rows, axis=(0, 1))
    grad_conv_weight = jnp.stack(tap_grads, axis=0)
    grad_conv_bias = jnp.sum(pre_grad, axis=(0, 1))
    mixer_grad = jnp.concatenate(
        [gate_part_grad, conv_in_grad.reshape(row_count, conv_width)], axis=1
    ).astype(jnp.bfloat16)
    step_grad_half = pulled[3].reshape(row_count, SSM_HEADS).astype(jnp.bfloat16)
    out_grad = group_queries(attended_grad, seq_count, tok_count)
    deltas = jnp.sum(out_grad.astype(jnp.float32) * attended.astype(jnp.float32), axis=-1)

    def attention_grads(query_grad, item):
        scores, allowed = scores_of(item[0], item[1], item[2])
        keys = item[0][:, :, :key_width].reshape(block, seq_count, HEADS_KV, HEAD)
        values = item[0][:, :, key_width:].reshape(block, seq_count, HEADS_KV, HEAD)
        probs = jnp.where(allowed, jnp.exp(scores - log_total[..., None]), 0.0)
        value_grad = jnp.einsum(
            "sgrk,sgrd->ksgd",
            probs.astype(jnp.bfloat16),
            out_grad,
            preferred_element_type=jnp.float32,
        )
        prob_grad = jnp.einsum(
            "sgrd,ksgd->sgrk", out_grad, values, preferred_element_type=jnp.float32
        )
        score_grad = (probs * (prob_grad - deltas[..., None])).astype(jnp.bfloat16)
        query_grad = (
            query_grad
            + jnp.einsum("sgrk,ksgd->sgrd", score_grad, keys, preferred_element_type=jnp.float32)
            * score_scale
        )
        key_grad = (
            jnp.einsum("sgrk,sgrd->ksgd", score_grad, queries, preferred_element_type=jnp.float32)
            * score_scale
        )
        both = jnp.concatenate(
            [
                key_grad.reshape(block, seq_count, key_width),
                value_grad.reshape(block, seq_count, key_width),
            ],
            axis=2,
        )
        return (query_grad, both)

    query_grad, key_terms = over_blocks(
        attention_grads,
        jnp.zeros(queries.shape, jnp.float32),
        (key_blocks, segment_blocks, block_ids),
    )
    key_pieces = lax.all_to_all(
        key_terms.reshape(length, seq_count, 2 * key_width).astype(jnp.bfloat16),
        "ctx",
        split_axis=0,
        concat_axis=0,
        tiled=True,
    )
    key_sums = jnp.sum(
        key_pieces.reshape(-1, tok_count, seq_count, 2 * key_width).astype(jnp.float32), axis=0
    )
    kv_grad = key_sums.transpose(1, 0, 2).reshape(row_count, 2 * key_width)
    projected_grad = jnp.concatenate(
        [ungroup(query_grad, seq_count, tok_count), kv_grad], axis=1
    ).astype(jnp.bfloat16)
    grad_attention_in = jnp.dot(normed.T, projected_grad, preferred_element_type=jnp.float32)
    grad_mixer_in = jnp.dot(normed.T, mixer_grad, preferred_element_type=jnp.float32)
    grad_step_in = jnp.dot(normed.T, step_grad_half, preferred_element_type=jnp.float32)
    normed_grad = (
        jnp.dot(projected_grad, full_attention_in.T, preferred_element_type=jnp.float32)
        + jnp.dot(mixer_grad, full_mixer_in.T, preferred_element_type=jnp.float32)
        + jnp.dot(step_grad_half, full_step_in.T, preferred_element_type=jnp.float32)
    )
    _, pull_one = jax.vjp(rms_scale, source, gain_mixing)
    source_part, grad_gain_mixing = pull_one(normed_grad)
    input_grad = residual_grad + source_part
    others = [
        grad_attention_in.astype(jnp.bfloat16),
        grad_mixer_in.astype(jnp.bfloat16),
        fold_rows(grad_attention_out.astype(jnp.bfloat16), attention_out.shape[0], own_rows),
        fold_rows(grad_mixer_out.astype(jnp.bfloat16), mixer_out.shape[0], own_rows),
        pad_columns(grad_step_in.astype(jnp.bfloat16)),
    ]
    other_sums = lax.psum_scatter(
        jnp.concatenate(others, axis=1), axes, scatter_dimension=0, tiled=True
    )
    feed_parts = cut_columns(
        feed_sums, (gate_up.shape[1], feed_sums.shape[1] - gate_up.shape[1])
    )
    other_parts = cut_columns(other_sums, [part.shape[1] for part in others])
    weight_sums = [
        part.astype(jnp.float32)
        for part in (
            other_parts[0],
            other_parts[1],
            other_parts[4][:, :SSM_HEADS],
            unfold_rows(other_parts[2], attention_out.shape[0], own_rows, width),
            unfold_rows(other_parts[3], mixer_out.shape[0], own_rows, width),
            feed_parts[0],
            unfold_rows(feed_parts[1], down_weight.shape[0], own_rows, width),
        )
    ]
    small_sums = lax.psum(
        (
            grad_gain_mixing,
            grad_gain_feed,
            pulled[4],
            pulled[5],
            pulled[6],
            grad_conv_weight,
            grad_conv_bias,
        ),
        ("dp", "ctx"),
    )
    return (
        output.reshape(seq_count, tok_count, width),
        input_grad.reshape(seq_count, tok_count, width),
        weight_sums[0],
        weight_sums[1],
        weight_sums[2],
        weight_sums[3],
        weight_sums[4],
        weight_sums[5],
        weight_sums[6],
        small_sums[0],
        small_sums[1],
        small_sums[2],
        small_sums[3],
        small_sums[4],
        small_sums[5],
        small_sums[6],
    )

def split_heads(ctx):
    return HEADS_Q == ctx and SSM_HEADS % ctx == 0 and ctx % HEADS_KV == 0


def entry_layout(ctx):
    heads = SSM_HEADS // ctx
    widths = [STATE, STATE, heads * SSM_HEAD, heads * SSM_HEAD, HEAD, HEAD, HEAD, heads]
    return widths + [-sum(widths) % 128]


def entry_slabs(attention_in, mixer_in, step_in, ctx):
    rows = attention_in.shape[0]
    share = ctx // HEADS_KV
    query_width = HEADS_Q * HEAD
    key_width = HEADS_KV * HEAD

    def parts(array, count):
        return array.reshape(rows, count, -1).transpose(1, 0, 2)

    kv = [
        jnp.repeat(parts(attention_in[:, at : at + key_width], HEADS_KV), share, axis=0)
        for at in (query_width, query_width + key_width)
    ]
    both = jnp.broadcast_to(mixer_in[None, :, 2 * SSM_INNER :], (ctx, rows, 2 * STATE))
    pieces = [
        both,
        parts(mixer_in[:, SSM_INNER : 2 * SSM_INNER], ctx),
        parts(mixer_in[:, :SSM_INNER], ctx),
        parts(attention_in[:, :query_width], ctx),
        kv[0],
        kv[1],
        parts(step_in, ctx),
        jnp.zeros((ctx, rows, entry_layout(ctx)[-1]), jnp.bfloat16),
    ]
    return jnp.concatenate(pieces, axis=2)


def entry_unslab(slabs, ctx):
    rows = slabs.shape[1]
    share = ctx // HEADS_KV
    write, read, inner, gate, q, k, v, step, _ = [
        slabs[:, :, at : at + width]
        for at, width in zip(offsets(entry_layout(ctx)), entry_layout(ctx))
    ]

    def flat(part):
        return part.transpose(1, 0, 2).reshape(rows, -1)

    def shared(part):
        return flat(jnp.sum(part.reshape(HEADS_KV, share, rows, HEAD), axis=1))

    attention = jnp.concatenate([flat(q), shared(k), shared(v)], axis=1)
    mixer = jnp.concatenate(
        [flat(gate), flat(inner), jnp.sum(write, axis=0), jnp.sum(read, axis=0)], axis=1
    )
    return attention, mixer, flat(step)


def offsets(widths):
    at, places = 0, []
    for width in widths:
        places.append(at)
        at += width
    return places


MESH = pl.DeviceIdType.MESH
IN_VMEM = pl.BlockSpec(memory_space=pltpu.VMEM)
ANYWHERE = pl.BlockSpec(memory_space=pl.ANY)


def remote(source, target, send, recv, peer):
    return pltpu.make_async_remote_copy(
        src_ref=source,
        dst_ref=target,
        send_sem=send,
        recv_sem=recv,
        device_id=peer,
        device_id_type=MESH,
    )


def arrived(ref, recv, peer):
    remote(ref, ref, recv, recv, peer).wait_recv()


class Here:
    def __init__(self, dp, ctx):
        self.dp, self.ctx, self.pairs = dp, ctx, ctx // 2
        self.d, self.me = lax.axis_index("dp"), lax.axis_index("ctx")
        self.z, self.c = self.me // 2, self.me % 2
        self.sibling = (self.d, self.z * 2 + 1 - self.c)

    def dp_peers(self):
        return [(lax.rem(self.d + k, self.dp), self.me) for k in range(1, self.dp)]

    def ctx_peers(self):
        return [(self.d, lax.rem(self.me + k, self.ctx)) for k in range(1, self.ctx)]

    def greet(self, peers, sender=None):
        sem = pltpu.get_barrier_semaphore()
        for peer in peers:
            pl.semaphore_signal(sem, inc=1, device_id=peer, device_id_type=MESH)
        count = len(peers)
        if sender is not None:
            away = jnp.logical_not(self.is_me(sender))

            @pl.when(away)
            def _():
                pl.semaphore_signal(sem, inc=1, device_id=sender, device_id_type=MESH)

            count = count + away.astype(jnp.int32)
        pl.semaphore_wait(sem, count)

    def is_me(self, peer):
        return (peer[0] == self.d) & (peer[1] == self.me)

    def user(self):
        place = self.d * self.ctx + self.me
        return (lax.rem(place, self.dp), place // self.dp)

    def owner(self):
        place = self.me * self.dp + self.d
        return (place // self.ctx, lax.rem(place, self.ctx))


class Relay:
    def __init__(self, here, block, slots, send, recv, local):
        self.here, self.block, self.slots = here, block, slots
        self.send, self.recv, self.local = send, recv, local
        self.up = (here.d, (here.z + 1) * 2 + here.c)
        self.down = (here.d, (here.z - 1) * 2 + here.c)
        self.has_up, self.has_down = here.z < here.pairs - 1, here.z > 0

    @staticmethod
    def scratch(pairs):
        return [
            pltpu.SemaphoreType.DMA((4 * pairs,)),
            pltpu.SemaphoreType.DMA((2 * pairs,)),
            pltpu.SemaphoreType.DMA,
        ]

    def slot(self, z, c):
        return self.slots.at[z * 2 + c]

    def greet(self):
        sem = pltpu.get_barrier_semaphore()

        def signal(peer):
            pl.semaphore_signal(sem, inc=1, device_id=peer, device_id_type=MESH)

        pl.when(self.has_up)(lambda: signal(self.up))
        pl.when(self.has_down)(lambda: signal(self.down))
        signal(self.here.sibling)
        count = self.has_up.astype(jnp.int32) + self.has_down.astype(jnp.int32)
        pl.semaphore_wait(sem, count + 1)

    def begin(self):
        h, n = self.here, self.here.pairs
        own = self.slot(h.z, h.c)
        pltpu.make_async_copy(self.block, own, self.local).start()

        @pl.when(self.has_up)
        def _():
            remote(self.block, own, self.send.at[0], self.recv.at[h.me], self.up).start()

        @pl.when(self.has_down)
        def _():
            remote(self.block, own, self.send.at[n], self.recv.at[h.me], self.down).start()

        remote(self.block, own, self.send.at[2 * n], self.recv.at[h.me], h.sibling).start()

    def hop(self, s):
        h, n = self.here, self.here.pairs
        low, high = h.z - s, h.z + s

        @pl.when(low >= 0)
        def _():
            ref, recv = self.slot(low, h.c), self.recv.at[low * 2 + h.c]
            arrived(ref, recv, h.sibling)

            @pl.when(self.has_up)
            def _():
                remote(ref, ref, self.send.at[s], recv, self.up).start()

            remote(ref, ref, self.send.at[2 * n + 2 * s - 1], recv, h.sibling).start()

        @pl.when(high < n)
        def _():
            ref, recv = self.slot(high, h.c), self.recv.at[high * 2 + h.c]
            arrived(ref, recv, h.sibling)

            @pl.when(self.has_down)
            def _():
                remote(ref, ref, self.send.at[n + s], recv, self.down).start()

            remote(ref, ref, self.send.at[2 * n + 2 * s], recv, h.sibling).start()

    def end(self):
        h, n = self.here, self.here.pairs
        for z in range(n):
            arrived(self.slot(z, 1 - h.c), self.recv.at[z * 2 + 1 - h.c], h.sibling)
        own = self.slot(h.z, h.c)

        def sent(index):
            remote(own, own, self.send.at[index], self.recv.at[0], h.sibling).wait_send()

        for s in range(n):
            low, high = h.z - s, h.z + s
            pl.when((low >= 0) & self.has_up)(functools.partial(sent, s))
            pl.when((high < n) & self.has_down)(functools.partial(sent, n + s))
            if s == 0:
                sent(2 * n)
            else:
                pl.when(low >= 0)(functools.partial(sent, 2 * n + 2 * s - 1))
                pl.when(high < n)(functools.partial(sent, 2 * n + 2 * s))
        pltpu.make_async_copy(self.block, own, self.local).wait()


class Spread:
    def __init__(self, here, block, slots, send, recv, local):
        self.here, self.block, self.slots = here, block, slots
        self.send, self.recv, self.local = send, recv, local

    @staticmethod
    def scratch(dp):
        return [
            pltpu.SemaphoreType.DMA((dp,)),
            pltpu.SemaphoreType.DMA((dp,)),
            pltpu.SemaphoreType.DMA,
        ]

    def begin(self):
        h = self.here
        pltpu.make_async_copy(self.block, self.slots.at[h.d], self.local).start()
        self.copies = [
            remote(self.block, self.slots.at[h.d], self.send.at[k], self.recv.at[h.d], peer)
            for k, peer in enumerate(h.dp_peers())
        ]
        for copy in self.copies:
            copy.start()

    def end(self):
        h = self.here
        for peer in h.dp_peers():
            arrived(self.slots.at[peer[0]], self.recv.at[peer[0]], peer)
        for copy in self.copies:
            copy.wait_send()
        pltpu.make_async_copy(self.block, self.slots.at[h.d], self.local).wait()


class Total:
    def __init__(self, here, terms, got, result, send, recv):
        self.here, self.terms, self.got, self.result = here, terms, got, result
        self.send, self.recv = send, recv

    @staticmethod
    def scratch(dp, shape):
        return [
            pltpu.VMEM((dp,) + shape, jnp.bfloat16),
            pltpu.SemaphoreType.DMA((dp,)),
            pltpu.SemaphoreType.DMA((dp,)),
        ]

    def begin(self):
        h = self.here
        self.copies = [
            remote(
                self.terms.at[peer[0]], self.got.at[h.d], self.send.at[k], self.recv.at[h.d], peer
            )
            for k, peer in enumerate(h.dp_peers())
        ]
        for copy in self.copies:
            copy.start()

    def end(self):
        h = self.here
        total = self.terms[h.d].astype(jnp.float32)
        for peer in h.dp_peers():
            arrived(self.got.at[peer[0]], self.recv.at[peer[0]], peer)
            total = total + self.got[peer[0]].astype(jnp.float32)
        self.result[...] = total.astype(self.result.dtype)

    def leave(self):
        for copy in self.copies:
            copy.wait_send()


class Swap:
    def __init__(self, here, blocks, slots, send, recv, local):
        self.here, self.blocks, self.slots = here, blocks, slots
        self.send, self.recv, self.local = send, recv, local

    @staticmethod
    def scratch(ctx):
        return [
            pltpu.SemaphoreType.DMA((ctx,)),
            pltpu.SemaphoreType.DMA((ctx,)),
            pltpu.SemaphoreType.DMA,
        ]

    def begin(self):
        h = self.here
        pltpu.make_async_copy(self.blocks.at[h.me], self.slots.at[h.me], self.local).start()
        self.copies = []
        for k, peer in enumerate(h.ctx_peers()):
            copy = remote(
                self.blocks.at[peer[1]],
                self.slots.at[h.me],
                self.send.at[k],
                self.recv.at[h.me],
                peer,
            )
            copy.start()
            self.copies.append(copy)

    def wait(self, index):
        arrived(self.slots.at[index], self.recv.at[index], self.here.sibling)

    def leave(self):
        h = self.here
        for copy in self.copies:
            copy.wait_send()
        pltpu.make_async_copy(self.blocks.at[h.me], self.slots.at[h.me], self.local).wait()


class SumTokens:
    def __init__(self, here, left, right, turned, total, away, pair, out, got, *sems):
        self.here, self.left, self.right, self.turned, self.total = here, left, right, turned, total
        self.away, self.pair, self.out, self.got = away, pair, out, got
        self.away_send, self.away_recv, self.send, self.recv = sems
        self.order = sorted(range(1, here.pairs), key=lambda k: -min(k, here.pairs - k)) + [0]

    @staticmethod
    def scratch(pairs, rows, width):
        block = pltpu.VMEM((pairs, rows, width), jnp.bfloat16)
        return [block] * 4 + [pltpu.SemaphoreType.DMA((pairs,))] * 4

    def term(self, z, c):
        rows = self.total.shape[0]
        part = self.left[pl.ds(pl.multiple_of((z * 2 + c) * rows, rows), rows), :]
        dims = (((1,), (1 if self.turned else 0,)), ((), ()))
        return lax.dot_general(part, self.right[...], dims, preferred_element_type=jnp.float32)

    def peer(self, k):
        h = self.here
        return (h.d, lax.rem(h.z + k, h.pairs) * 2 + h.c)

    def to_sibling(self, k):
        return remote(
            self.away.at[k], self.pair.at[k], self.away_send.at[k], self.away_recv.at[k],
            self.here.sibling,
        )

    def to_pair(self, k):
        return remote(
            self.out.at[k], self.got.at[k], self.send.at[k], self.recv.at[k], self.peer(k)
        )

    def begin(self):
        h = self.here
        for k in self.order:
            self.away[k] = self.term(lax.rem(h.z + k, h.pairs), 1 - h.c).astype(jnp.bfloat16)
            self.to_sibling(k).start()
        for k in self.order:
            term = self.term(lax.rem(h.z + k, h.pairs), h.c)
            self.to_sibling(k).wait_recv()
            term = term + self.pair[k].astype(jnp.float32)
            if k:
                self.out[k] = term.astype(jnp.bfloat16)
                self.to_pair(k).start()
            else:
                self.total[...] = term

    def end(self):
        for k in self.order[::-1]:
            if k:
                self.to_pair(k).wait_recv()
                self.total[...] += self.got[k].astype(jnp.float32)

    def leave(self):
        for k in self.order:
            self.to_sibling(k).wait_send()
            if k:
                self.to_pair(k).wait_send()


class Move:
    def __init__(self, here, block, target, there, landing, sender, send, recv, local):
        self.here, self.landing, self.sender, self.recv = here, landing, sender, recv
        self.own = here.is_me(target)
        self.home = pltpu.make_async_copy(block, landing, local)
        self.far = remote(block, there, send, recv, target)

    @staticmethod
    def scratch():
        return [pltpu.SemaphoreType.DMA] * 3

    def begin(self):
        pl.when(self.own)(lambda: self.home.start())
        pl.when(jnp.logical_not(self.own))(lambda: self.far.start())

    def wait(self):
        pl.when(self.own)(lambda: self.home.wait())
        pl.when(jnp.logical_not(self.own))(lambda: arrived(self.landing, self.recv, self.sender))

    def leave(self):
        pl.when(jnp.logical_not(self.own))(lambda: self.far.wait_send())


def call(kernel, ident, outs, out_specs, in_specs, scratch, *arrays):
    return pl.pallas_call(
        kernel,
        out_shape=outs,
        in_specs=in_specs,
        out_specs=out_specs,
        scratch_shapes=scratch,
        compiler_params=pltpu.CompilerParams(
            collective_id=ident, has_side_effects=True, vmem_limit_bytes=48 * 2**20
        ),
    )(*arrays)


def like(shape, dtype=jnp.bfloat16):
    return jax.ShapeDtypeStruct(shape, dtype)


def gather_tokens(block, ident):
    dp, ctx = lax.axis_size("dp"), lax.axis_size("ctx")

    def kernel(block_ref, slots_ref, *sems):
        here = Here(dp, ctx)
        relay = Relay(here, block_ref, slots_ref, *sems)
        relay.greet()
        relay.begin()
        for s in range(1, here.pairs):
            relay.hop(s)
        relay.end()

    whole = call(
        kernel, ident, like((ctx,) + block.shape, block.dtype), ANYWHERE, [ANYWHERE],
        Relay.scratch(ctx // 2), block,
    )
    return whole.reshape((-1,) + block.shape[1:])


def enter(normed, segments, entry, feed, outs):
    dp, ctx = lax.axis_size("dp"), lax.axis_size("ctx")
    relay_sems, swap_sems = Relay.scratch(ctx // 2), Swap.scratch(ctx)

    def kernel(
        normed_ref, seg_ref, entry_ref, feed_ref, outs_ref,
        all_ref, segs_ref, full_ref, feeds_ref, rows_ref, *sems,
    ):
        here = Here(dp, ctx)
        tokens = Relay(here, normed_ref, all_ref, *sems[0:3])
        ids = Relay(here, seg_ref, segs_ref, *sems[3:6])
        slabs = Swap(here, entry_ref, full_ref.at[here.d], *sems[6:9])
        others = Swap(here, feed_ref, feeds_ref, *sems[9:12])
        pass_send, pass_recv = sems[12:14]
        target = here.user()
        outs = Move(
            here, outs_ref, target, rows_ref.at[target[0]], rows_ref.at[here.d], here.owner(),
            *sems[14:17],
        )
        rows_send, rows_recv = sems[17:19]
        peers = here.dp_peers()
        here.greet(peers + here.ctx_peers(), here.owner())

        def passing(source, k, index):
            return remote(
                source,
                full_ref.at[here.d, index],
                pass_send.at[k, index],
                pass_recv.at[here.d, index],
                peers[k],
            )

        def forward(index):
            slabs.wait(index)
            for k in range(dp - 1):
                passing(full_ref.at[here.d, index], k, index).start()

        def rows_copy(k):
            ref = rows_ref.at[here.d]
            return remote(ref, ref, rows_send.at[k], rows_recv.at[here.d], peers[k])

        slabs.begin()
        for k in range(dp - 1):
            passing(entry_ref.at[here.me], k, here.me).start()
        tokens.begin()
        ids.begin()
        outs.begin()
        forward(here.z * 2 + 1 - here.c)
        for s in range(1, here.pairs):
            for z in (here.z - s, here.z + s):

                @pl.when((z >= 0) & (z < here.pairs))
                def _(z=z):
                    forward(z * 2 + here.c)
                    forward(z * 2 + 1 - here.c)

            tokens.hop(s)
            ids.hop(s)
            if s == 1:
                others.begin()
            if s == max(1, here.pairs - 2):
                outs.wait()
                for k in range(dp - 1):
                    rows_copy(k).start()
        for peer in peers:
            for index in range(ctx):
                arrived(full_ref.at[peer[0], index], pass_recv.at[peer[0], index], peer)
        for peer in here.ctx_peers():
            others.wait(peer[1])
        tokens.end()
        ids.end()
        for k, peer in enumerate(peers):
            arrived(rows_ref.at[peer[0]], rows_recv.at[peer[0]], peer)
            rows_copy(k).wait_send()
        outs.leave()
        slabs.leave()
        others.leave()
        for index in range(ctx):
            for k in range(dp - 1):
                passing(full_ref.at[here.d, index], k, index).wait_send()

    return call(
        kernel,
        0,
        (
            like((ctx,) + normed.shape),
            like((ctx,) + segments.shape, segments.dtype),
            like((dp,) + entry.shape),
            like(feed.shape),
            like((dp,) + outs.shape),
        ),
        (ANYWHERE,) * 5,
        [ANYWHERE] * 5,
        relay_sems * 2 + swap_sems * 2 + [pltpu.SemaphoreType.DMA((dp, ctx))] * 2
        + Move.scratch()
        + [pltpu.SemaphoreType.DMA((dp,))] * 2,
        normed,
        segments,
        entry,
        feed,
        outs,
    )


def sum_and_spread(left, right, blocks, ident):
    dp, ctx = lax.axis_size("dp"), lax.axis_size("ctx")
    rows, width = left.shape[0] // ctx, right.shape[1]
    count = len(blocks)

    def kernel(left_ref, right_ref, *refs):
        blocks_in, total, slots = refs[:count], refs[count], refs[count + 1 : 2 * count + 1]
        sems = refs[2 * count + 1 :]
        here = Here(dp, ctx)
        sums = SumTokens(here, left_ref, right_ref, False, total, *sems[:8])
        spreads = [
            Spread(here, block, slot, *sems[8 + 3 * i : 11 + 3 * i])
            for i, (block, slot) in enumerate(zip(blocks_in, slots))
        ]
        here.greet(here.dp_peers() + here.ctx_peers())
        for spread in spreads:
            spread.begin()
        sums.begin()
        sums.end()
        for spread in spreads:
            spread.end()
        sums.leave()

    return call(
        kernel,
        ident,
        (like((rows, width), jnp.float32), *[like((dp,) + block.shape) for block in blocks]),
        (IN_VMEM,) + (ANYWHERE,) * count,
        [IN_VMEM, IN_VMEM] + [ANYWHERE] * count,
        SumTokens.scratch(ctx // 2, rows, width) + Spread.scratch(dp) * count,
        left,
        right,
        *blocks,
    )


def sum_and_total(left, right, terms, ident):
    dp, ctx = lax.axis_size("dp"), lax.axis_size("ctx")
    rows, width = left.shape[0] // ctx, right.shape[0]
    count = len(terms)

    def kernel(left_ref, right_ref, *refs):
        terms_in, total, results = refs[:count], refs[count], refs[count + 1 : 2 * count + 1]
        sems = refs[2 * count + 1 :]
        here = Here(dp, ctx)
        sums = SumTokens(here, left_ref, right_ref, True, total, *sems[:8])
        totals = [
            Total(here, term, sems[8 + 3 * i], result, *sems[9 + 3 * i : 11 + 3 * i])
            for i, (term, result) in enumerate(zip(terms_in, results))
        ]
        here.greet(here.dp_peers() + here.ctx_peers())
        for part in totals:
            part.begin()
        sums.begin()
        for part in totals:
            part.end()
        sums.end()
        sums.leave()
        for part in totals:
            part.leave()

    scratch = SumTokens.scratch(ctx // 2, rows, width)
    for term in terms:
        scratch = scratch + Total.scratch(dp, term.shape[1:])
    return call(
        kernel,
        ident,
        (like((rows, width), jnp.float32), *[like(term.shape[1:]) for term in terms]),
        (IN_VMEM,) * (1 + count),
        [IN_VMEM] * (2 + count),
        scratch,
        left,
        right,
        *terms,
    )


def leave(grads, entry, source, residual_grad, gain, entry_terms, feed_sums, out_terms, small):
    dp, ctx = lax.axis_size("dp"), lax.axis_size("ctx")
    rows, width = source.shape
    slab = entry_terms.shape[2:]

    def kernel(
        grads_ref, entry_ref, source_ref, res_ref, gain_ref, terms_ref, feed_ref, outs_ref, small_ref,
        input_ref, slabs_ref, feeds_ref, out_sum, smalls_ref, gains_ref, normed_grad, *sems,
    ):
        here = Here(dp, ctx)
        peers = here.dp_peers()
        sums = SumTokens(here, grads_ref, entry_ref, True, normed_grad, *sems[0:8])
        feeds = Swap(here, feed_ref, feeds_ref, *sems[8:11])
        got, term_send, term_recv, mine, slab_send, slab_recv = sems[11:17]
        small_got, gain_got = sems[17:19]
        small_send, small_recv, gain_send, gain_recv = sems[19:23]
        last_send, last_recv, lastg_send, lastg_recv = sems[23:27]
        outs_got, out_half, out_landed = sems[27], sems[30], sems[31]
        outs = Total(here, outs_ref, outs_got, out_half, *sems[28:30])
        home = Move(
            here, out_half, here.owner(), out_landed, out_landed, here.user(), *sems[32:35]
        )
        here.greet(peers + here.ctx_peers(), here.user())
        order = [lax.rem(here.me + k, ctx) for k in list(range(1, ctx)) + [0]]

        def term_copy(k, index):
            return remote(
                terms_ref.at[peers[k][0], index],
                got.at[here.d, index],
                term_send.at[k, index],
                term_recv.at[here.d, index],
                peers[k],
            )

        for index in order:
            for k in range(dp - 1):
                term_copy(k, index).start()
        outs.begin()
        small_copies = []
        for k, peer in enumerate(peers):
            copy = remote(
                small_ref, small_got.at[here.d], small_send.at[k], small_recv.at[here.d], peer
            )
            copy.start()
            small_copies.append(copy)
        sums.begin()
        feeds.begin()

        def slab_copy(j):
            return remote(
                mine.at[order[j]], slabs_ref.at[here.me], slab_send.at[j], slab_recv.at[here.me],
                (here.d, order[j]),
            )

        for j, index in enumerate(order):
            total = terms_ref[here.d, index].astype(jnp.float32)
            for peer in peers:
                arrived(got.at[peer[0], index], term_recv.at[peer[0], index], peer)
                total = total + got[peer[0], index].astype(jnp.float32)
            total = total.astype(jnp.bfloat16)
            if j < ctx - 1:
                mine[index] = total
                slab_copy(j).start()
            else:
                slabs_ref[here.me] = total
        outs.end()
        home.begin()
        sums.end()
        x, grad = source_ref[...], normed_grad[...]
        scale = lax.rsqrt(jnp.mean(x * x, axis=-1, keepdims=True) + 1e-05)
        scaled = grad * gain_ref[...]
        inner = jnp.mean(x * scaled, axis=-1, keepdims=True)
        input_ref[...] = res_ref[...] + scale * scaled - x * (scale * scale * scale * inner)
        gain_got[here.d] = jnp.sum(grad * (x * scale), axis=0, keepdims=True)
        for k, peer in enumerate(peers):
            copy = remote(
                gain_got.at[here.d], gain_got.at[here.d], gain_send.at[k], gain_recv.at[here.d], peer
            )
            copy.start()
            small_copies.append(copy)
        small_got[here.d] = small_ref[...]
        for peer in peers:
            arrived(small_got.at[peer[0]], small_recv.at[peer[0]], peer)
        total = small_got[0]
        for d in range(1, dp):
            total = total + small_got[d]
        smalls_ref[here.me] = total
        last = []
        for k, peer in enumerate(here.ctx_peers()):
            copy = remote(
                smalls_ref.at[here.me], smalls_ref.at[here.me], last_send.at[k],
                last_recv.at[here.me], peer,
            )
            copy.start()
            last.append(copy)
        for peer in peers:
            arrived(gain_got.at[peer[0]], gain_recv.at[peer[0]], peer)
        total = gain_got[0]
        for d in range(1, dp):
            total = total + gain_got[d]
        gains_ref[here.me] = total
        for k, peer in enumerate(here.ctx_peers()):
            copy = remote(
                gains_ref.at[here.me], gains_ref.at[here.me], lastg_send.at[k],
                lastg_recv.at[here.me], peer,
            )
            copy.start()
            last.append(copy)
        for peer in here.ctx_peers():
            arrived(slabs_ref.at[peer[1]], slab_recv.at[peer[1]], peer)
            feeds.wait(peer[1])
            arrived(smalls_ref.at[peer[1]], last_recv.at[peer[1]], peer)
            arrived(gains_ref.at[peer[1]], lastg_recv.at[peer[1]], peer)
        home.wait()
        out_sum[...] = out_landed[...].astype(jnp.float32)
        home.leave()
        outs.leave()
        sums.leave()
        feeds.leave()
        for index in order:
            for k in range(dp - 1):
                term_copy(k, index).wait_send()
        for j in range(ctx - 1):
            slab_copy(j).wait_send()
        for copy in small_copies + last:
            copy.wait_send()

    dma = pltpu.SemaphoreType.DMA
    scratch = (
        [pltpu.VMEM((rows, width), jnp.float32)]
        + SumTokens.scratch(ctx // 2, rows, width)
        + Swap.scratch(ctx)
        + [
            pltpu.VMEM((dp, ctx) + slab, jnp.bfloat16),
            dma((dp, ctx)),
            dma((dp, ctx)),
            pltpu.VMEM((ctx,) + slab, jnp.bfloat16),
            dma((ctx,)),
            dma((ctx,)),
        ]
        + [
            pltpu.VMEM((dp,) + small.shape, jnp.float32),
            pltpu.VMEM((dp, 1, width), jnp.float32),
        ]
        + [dma((dp,))] * 4
        + [dma((ctx,))] * 4
        + Total.scratch(dp, out_terms.shape[1:])
        + [pltpu.VMEM(out_terms.shape[1:], jnp.bfloat16)] * 2
        + Move.scratch()
    )
    return call(
        kernel,
        5,
        (
            like((rows, width), jnp.float32),
            like((ctx,) + slab),
            like(feed_sums.shape),
            like(out_terms.shape[1:], jnp.float32),
            like((ctx,) + small.shape, jnp.float32),
            like((ctx, 1, width), jnp.float32),
        ),
        (IN_VMEM,) * 6,
        [IN_VMEM] * 9,
        scratch,
        grads,
        entry,
        source,
        residual_grad,
        gain,
        entry_terms,
        feed_sums,
        out_terms,
        small,
    )


def rows_of(index, size):
    return pl.ds(pl.multiple_of(index * size, size), size)


def product(left, right, dims=((1,), (0,)), precision=None):
    return lax.dot_general(
        left, right, (dims, ((), ())), precision=precision, preferred_element_type=jnp.float32
    )


def sigma(values):
    return 1.0 / (1.0 + jnp.exp(-values))


def lower_of(size):
    down = lax.broadcasted_iota(jnp.int32, (size, size), 0)
    along = lax.broadcasted_iota(jnp.int32, (size, size), 1)
    return along <= down


def widen(columns, heads):
    shape = (columns.shape[0], SSM_HEAD)
    return jnp.concatenate(
        [jnp.broadcast_to(columns[:, h : h + 1], shape) for h in range(heads)], axis=1
    )


def head_sums(array, heads, width):
    sums = [
        jnp.sum(array[:, h * SSM_HEAD : (h + 1) * SSM_HEAD], axis=1, keepdims=True)
        for h in range(heads)
    ]
    return columns_of(sums, width)


def columns_of(columns, width):
    lane = lax.broadcasted_iota(jnp.int32, (columns[0].shape[0], width), 1)
    total = jnp.zeros(lane.shape, jnp.float32)
    for h, column in enumerate(columns):
        total = jnp.where(lane == h, column, total)
    return total


class Layout:
    def __init__(self, heads):
        self.inner = 2 * STATE
        self.conv = self.inner + heads * SSM_HEAD
        self.query = self.conv + heads * SSM_HEAD
        self.key = self.query + HEAD
        self.value = self.key + HEAD
        self.step = self.value + HEAD
        self.width = self.step + heads + (-(self.step + heads)) % 128
        self.steps = self.width - self.step


class Chunk:
    def __init__(self, lay, heads, p, a, seg_row, tap_ref, head_ref, shifted):
        size = p.shape[0]
        self.conv_in = p[:, : lay.conv]
        self.earlier = [jnp.where(a[:, k - 1 : k] > 0.0, shifted(k), 0.0) for k in (1, 2, 3)]
        pre = tap_ref[4:5, :] + tap_ref[3:4, :] * self.conv_in
        for k in (1, 2, 3):
            pre = pre + self.earlier[k - 1] * tap_ref[3 - k : 4 - k, :]
        self.sig = sigma(pre)
        self.pre = pre
        conv = pre * self.sig
        self.write, self.read = conv[:, :STATE], conv[:, STATE : 2 * STATE]
        self.inner = conv[:, lay.inner :]
        self.gate = p[:, lay.conv : lay.query]
        self.biased = p[:, lay.step :] + head_ref[1:2, :]
        self.steps = jnp.maximum(self.biased, 0.0) + jnp.log1p(jnp.exp(-jnp.abs(self.biased)))
        self.rates = self.steps * head_ref[0:1, :]
        lower = lower_of(size)
        self.ones = lower.astype(jnp.float32)
        run = product(self.ones, self.rates, precision=highest)
        run_row = product(self.rates, self.ones, ((0,), (1,)), precision=highest)
        allowed = lower & (a[:, 6:7] == seg_row)
        self.decay = [
            jnp.exp(jnp.where(allowed, run[:, h : h + 1] - run_row[h : h + 1, :], -1e30))
            for h in range(heads)
        ]
        self.carried = a[:, 7:8] * jnp.exp(run)
        self.tails = a[:, 8:9] * jnp.exp(run[size - 1 : size, :] - run)
        self.cross = product(self.read, self.write, ((1,), (1,)))
        self.scaled = self.inner * widen(self.steps, heads)
        self.carried_wide = widen(self.carried, heads)
        self.tails_wide = widen(self.tails, heads)
        self.skip_wide = widen(head_ref[2:3, :], heads)
        last = self.carried[size - 1 : size, :]
        head_row = lax.broadcasted_iota(jnp.int32, (heads * SSM_HEAD, 1), 0) // SSM_HEAD
        self.last = jnp.zeros((heads * SSM_HEAD, 1), jnp.float32)
        for h in range(heads):
            self.last = jnp.where(head_row == h, last[:, h : h + 1], self.last)


def attention_mask(seg_column, seg_row, at):
    rows, keys = seg_column.shape[0], seg_row.shape[1]
    down = lax.broadcasted_iota(jnp.int32, (rows, keys), 0) + at
    along = lax.broadcasted_iota(jnp.int32, (rows, keys), 1)
    return (along <= down) & (seg_column == seg_row)


def mix_forward(normed, entry, columns, seg_row, taps, head_rows, size):
    length = normed.shape[0]
    chunks = length // size
    heads = SSM_HEADS // lax.axis_size("ctx")
    lay = Layout(heads)
    wide = heads * SSM_HEAD
    block = 2 * size if chunks % 2 == 0 else size

    def kernel(
        n_ref, e_ref, col_ref, seg_ref, tap_ref, head_ref,
        mixed_ref, p_ref, y_ref, states_ref, top_ref, ext, state, heads_in,
    ):
        state[...] = jnp.zeros_like(state)
        ext[0:8, :] = jnp.zeros((8, lay.conv), jnp.float32)

        def chunk(j, _):
            at = rows_of(j, size)
            p = product(n_ref[at, :], e_ref[...])
            p_ref[at, :] = p
            ext[8:, :] = p[:, : lay.conv]
            part = Chunk(
                lay, heads, p, col_ref[at, :], seg_ref[:, at], tap_ref, head_ref,
                lambda k: ext[8 - k : 8 - k + size, :],
            )
            ext[0:8, :] = ext[size : size + 8, :]
            reached = state[...]
            states_ref[j] = reached
            local = [
                product(part.decay[h] * part.cross, part.scaled[:, h * SSM_HEAD : (h + 1) * SSM_HEAD])
                for h in range(heads)
            ]
            y = (
                jnp.concatenate(local, axis=1)
                + part.skip_wide * part.inner
                + part.carried_wide * product(part.read, reached, ((1,), (1,)))
            )
            y_ref[at, :] = y
            gated = y * part.gate * sigma(part.gate)
            state[...] = part.last * reached + product(
                part.tails_wide * part.scaled, part.write, ((0,), (0,))
            )
            heads_in[at, :] = p[:, lay.query : lay.query + 3 * HEAD].astype(jnp.bfloat16)
            mixed_ref[at, HEAD:] = gated.astype(jnp.bfloat16)
            return 0

        lax.fori_loop(0, chunks, chunk, 0)
        for b in range(length // block):
            at, keys = slice(b * block, (b + 1) * block), (b + 1) * block
            scores = product(
                heads_in[at, :HEAD], heads_in[:keys, HEAD : 2 * HEAD], ((1,), (1,))
            ) * (HEAD**-0.5)
            allowed = attention_mask(col_ref[at, 6:7], seg_ref[:, :keys], b * block)
            scores = jnp.where(allowed, scores, -1e30)
            top = jnp.max(scores, axis=1, keepdims=True)
            terms = jnp.where(allowed, jnp.exp(scores - top), 0.0)
            total = jnp.sum(terms, axis=1, keepdims=True)
            top_ref[at, :] = top + jnp.log(total)
            probs = (terms * (1.0 / total)).astype(jnp.bfloat16)
            mixed_ref[at, :HEAD] = product(probs, heads_in[:keys, 2 * HEAD :]).astype(jnp.bfloat16)

    return pl.pallas_call(
        kernel,
        out_shape=(
            like((length, HEAD + wide)),
            like((length, lay.width), jnp.float32),
            like((length, wide), jnp.float32),
            like((chunks, wide, STATE), jnp.float32),
            like((length, 1), jnp.float32),
        ),
        in_specs=[IN_VMEM] * 6,
        out_specs=(IN_VMEM,) * 5,
        scratch_shapes=[
            pltpu.VMEM((size + 8, lay.conv), jnp.float32),
            pltpu.VMEM((wide, STATE), jnp.float32),
            pltpu.VMEM((length, 3 * HEAD), jnp.bfloat16),
        ],
        compiler_params=pltpu.CompilerParams(vmem_limit_bytes=48 * 2**20),
    )(normed, entry, columns, seg_row, taps, head_rows)


def mix_backward(
    residual_half, out_rows, mixed_out, p, y, states, log_total, columns, seg_row, taps, head_rows, size
):
    length = p.shape[0]
    chunks = length // size
    heads = SSM_HEADS // lax.axis_size("ctx")
    lay = Layout(heads)
    wide = heads * SSM_HEAD
    block = 2 * size if chunks % 2 == 0 else size

    def kernel(
        r_ref, o_ref, mixed_ref, p_ref, y_ref, states_ref, top_ref, col_ref, seg_ref, tap_ref, head_ref,
        g_ref, tap_sum, head_sum, outs_ref, ext, ahead, out_grad, step_grad, state, heads_in, key_grad, value_grad,
    ):
        state[...] = jnp.zeros_like(state)
        ahead[size:, :] = jnp.zeros((8, lay.conv), jnp.float32)
        tap_sum[...] = jnp.zeros_like(tap_sum)
        head_sum[...] = jnp.zeros_like(head_sum)

        def chunk(step, _):
            j = chunks - 1 - step
            at = rows_of(j, size)
            p, a = p_ref[at, :], col_ref[at, :]
            ext[8:, :] = p[:, : lay.conv]
            ext[0:8, :] = p_ref[pl.ds(pl.multiple_of(jnp.maximum(j * size - 8, 0), 8), 8), : lay.conv]
            part = Chunk(
                lay, heads, p, a, seg_ref[:, at], tap_ref, head_ref,
                lambda k: ext[8 - k : 8 - k + size, :],
            )
            grads = product(r_ref[at, :], o_ref[...], ((1,), (1,)))
            out_grad[at, :] = grads[:, :HEAD].astype(jnp.bfloat16)
            gated_grad = grads[:, HEAD:]
            y = y_ref[at, :]
            gate_sig = sigma(part.gate)
            gate_grad = gated_grad * y * gate_sig * (1.0 + part.gate * (1.0 - gate_sig))
            dy = gated_grad * part.gate * gate_sig
            later = state[...]
            before = states_ref[j]
            reached = part.carried_wide * product(part.read, before, ((1,), (1,)))
            from_later = part.tails_wide * product(part.write, later, ((1,), (1,)))
            cross_grad = jnp.zeros((size, size), jnp.float32)
            local, row_sums, column_sums = [], [], []
            for h in range(heads):
                cut = slice(h * SSM_HEAD, (h + 1) * SSM_HEAD)
                mixing = part.decay[h] * part.cross
                mixing_grad = product(dy[:, cut], part.scaled[:, cut], ((1,), (1,)))
                local.append(product(mixing, dy[:, cut], ((0,), (0,))))
                cross_grad = cross_grad + part.decay[h] * mixing_grad
                weight = mixing * mixing_grad
                row_sums.append(jnp.sum(weight, axis=1, keepdims=True))
                column_sums.append(jnp.sum(weight, axis=0, keepdims=True))
            scaled_grad = jnp.concatenate(local, axis=1) + from_later
            carried_dy = part.carried_wide * dy
            tail_terms = part.tails_wide * part.scaled
            read_grad = product(cross_grad, part.write) + product(carried_dy, before)
            write_grad = product(cross_grad, part.read, ((0,), (0,))) + product(tail_terms, later)
            inner_grad = part.skip_wide * dy + widen(part.steps, heads) * scaled_grad
            tail_sums = head_sums(part.scaled * from_later, heads, lay.steps)
            run_grad = (
                columns_of(row_sums, lay.steps)
                + head_sums(dy * reached, heads, lay.steps)
                - tail_sums
            )
            ends = later * before * part.last
            end_sums = [
                jnp.sum(
                    jnp.sum(ends[h * SSM_HEAD : (h + 1) * SSM_HEAD, :], axis=1, keepdims=True),
                    axis=0,
                    keepdims=True,
                )
                for h in range(heads)
            ]
            final = columns_of(end_sums, lay.steps) + jnp.sum(tail_sums, axis=0, keepdims=True)
            column_rows = jnp.concatenate(
                column_sums + [jnp.zeros((lay.steps - heads, size), jnp.float32)], axis=0
            )
            rate_grad = (
                product(part.ones, run_grad, ((0,), (0,)), precision=highest)
                - product(part.ones, column_rows, ((0,), (1,)), precision=highest)
                + final
            )
            steps_grad = (
                head_sums(scaled_grad * part.inner, heads, lay.steps) + rate_grad * head_ref[0:1, :]
            )
            raw_grad = steps_grad * sigma(part.biased)
            step_grad[at, :] = raw_grad
            head_sum[0:1, :] += jnp.sum(rate_grad * part.rates, axis=0, keepdims=True)
            head_sum[1:2, :] += jnp.sum(raw_grad, axis=0, keepdims=True)
            head_sum[2:3, :] += jnp.sum(
                head_sums(dy * part.inner, heads, lay.steps), axis=0, keepdims=True
            )
            state[...] = part.last * later + product(carried_dy, part.read, ((0,), (0,)))
            converted_grad = jnp.concatenate([write_grad, read_grad, inner_grad], axis=1)
            pre_grad = converted_grad * part.sig * (1.0 + part.pre * (1.0 - part.sig))
            ahead[:size, :] = pre_grad
            conv_grad = tap_ref[3:4, :] * pre_grad
            tap_sum[3:4, :] += jnp.sum(pre_grad * part.conv_in, axis=0, keepdims=True)
            tap_sum[4:5, :] += jnp.sum(pre_grad, axis=0, keepdims=True)
            for k in (1, 2, 3):
                conv_grad = (
                    conv_grad
                    + jnp.where(a[:, 2 + k : 3 + k] > 0.0, ahead[k : k + size, :], 0.0)
                    * tap_ref[3 - k : 4 - k, :]
                )
                tap_sum[3 - k : 4 - k, :] += jnp.sum(
                    pre_grad * part.earlier[k - 1], axis=0, keepdims=True
                )
            ahead[size:, :] = ahead[0:8, :]
            g_ref[at, : lay.query] = jnp.concatenate([conv_grad, gate_grad], axis=1).astype(
                jnp.bfloat16
            )
            heads_in[at, :] = p[:, lay.query : lay.step].astype(jnp.bfloat16)
            return 0

        lax.fori_loop(0, chunks, chunk, 0)
        key_grad[...] = jnp.zeros_like(key_grad)
        value_grad[...] = jnp.zeros_like(value_grad)
        query_grads = []
        for b in range(length // block):
            at, keys = slice(b * block, (b + 1) * block), (b + 1) * block
            queries, grad = heads_in[at, :HEAD], out_grad[at, :]
            key_part, value_part = heads_in[:keys, HEAD : 2 * HEAD], heads_in[:keys, 2 * HEAD :]
            scores = product(queries, key_part, ((1,), (1,))) * (HEAD**-0.5)
            allowed = attention_mask(col_ref[at, 6:7], seg_ref[:, :keys], b * block)
            probs = jnp.where(allowed, jnp.exp(scores - top_ref[at, :]), 0.0)
            deltas = jnp.sum(
                grad.astype(jnp.float32) * mixed_ref[at, :HEAD].astype(jnp.float32),
                axis=1,
                keepdims=True,
            )
            prob_grad = product(grad, value_part, ((1,), (1,)))
            score_grad = (probs * (prob_grad - deltas)).astype(jnp.bfloat16)
            query_grads.append(product(score_grad, key_part) * (HEAD**-0.5))
            key_grad[:keys, :] += product(score_grad, queries, ((0,), (0,))) * (HEAD**-0.5)
            value_grad[:keys, :] += product(probs.astype(jnp.bfloat16), grad, ((0,), (0,)))
        for b, query_grad in enumerate(query_grads):
            at = slice(b * block, (b + 1) * block)
            g_ref[at, lay.query :] = jnp.concatenate(
                [query_grad, key_grad[at, :], value_grad[at, :], step_grad[at, :]], axis=1
            ).astype(jnp.bfloat16)
        outs_ref[...] = product(mixed_ref[...], r_ref[...], ((0,), (0,))).astype(jnp.bfloat16)

    f32 = jnp.float32
    return pl.pallas_call(
        kernel,
        out_shape=(
            like((length, lay.width)),
            like((8, lay.conv), f32),
            like((8, lay.steps), f32),
            like(out_rows.shape),
        ),
        in_specs=[IN_VMEM] * 11,
        out_specs=(IN_VMEM,) * 4,
        scratch_shapes=[
            pltpu.VMEM((size + 8, lay.conv), f32),
            pltpu.VMEM((size + 8, lay.conv), f32),
            pltpu.VMEM((length, HEAD), jnp.bfloat16),
            pltpu.VMEM((length, lay.steps), f32),
            pltpu.VMEM((wide, STATE), f32),
            pltpu.VMEM((length, 3 * HEAD), jnp.bfloat16),
            pltpu.VMEM((length, HEAD), f32),
            pltpu.VMEM((length, HEAD), f32),
        ],
        compiler_params=pltpu.CompilerParams(vmem_limit_bytes=56 * 2**20),
    )(residual_half, out_rows, mixed_out, p, y, states, log_total, columns, seg_row, taps, head_rows)


def across(left, right):
    return jnp.dot(left.T, right, preferred_element_type=jnp.float32).astype(jnp.bfloat16)


def split_local(
    block_input,
    segment_ids,
    out_cotangent,
    attention_in,
    mixer_in,
    step_in,
    attention_out,
    mixer_out,
    gate_up,
    down_weight,
    gain_mixing,
    gain_feed,
    decay_log,
    step_bias,
    skip_gain,
    conv_weight,
    conv_bias,
):
    ctx, dp = lax.axis_size("ctx"), lax.axis_size("dp")
    mine = lax.axis_index("ctx")
    tok_count, width = block_input.shape[1:]
    length = tok_count * ctx
    heads = SSM_HEADS // ctx
    rows = attention_in.shape[0]
    hidden = down_weight.shape[0]
    slabs = entry_slabs(attention_in, mixer_in, step_in, ctx)
    gate_slabs = gate_up.reshape(rows, 2, dp, ctx, hidden).transpose(3, 0, 1, 2, 4)
    gate_slabs = gate_slabs.reshape(ctx, rows, 2 * dp * hidden)
    own_attention = attention_out.shape[0]

    source = block_input.reshape(tok_count, width).astype(jnp.float32)
    cotangent = out_cotangent.reshape(tok_count, width)
    normed_own = rms_scale(source, gain_mixing).astype(jnp.bfloat16)
    outs = jnp.concatenate([attention_out, mixer_out], axis=0)
    normed, segments, entry, feed_slabs, outs = enter(
        normed_own, segment_ids, slabs, gate_slabs, outs
    )
    normed, segments = normed.reshape(length, width), segments.reshape(length)
    entry = entry.reshape(dp * ctx * rows, -1)
    late_cotangent, _ = lax.optimization_barrier((cotangent, segments))
    cotangents = lax.all_gather(late_cotangent, "ctx", axis=0, tiled=True)
    out_rows = jnp.concatenate(
        [outs[:, :own_attention].reshape(-1, width), outs[:, own_attention:].reshape(-1, width)],
        axis=0,
    )

    own = lambda array, at, size: lax.dynamic_slice_in_dim(array, at + mine * size, size, axis=-1)
    conv_own = lambda array: jnp.concatenate(
        [array[:, SSM_INNER:], own(array, 0, heads * SSM_HEAD)], axis=-1
    )
    taps = jnp.pad(conv_own(jnp.concatenate([conv_weight, conv_bias[None]], axis=0)), ((0, 3), (0, 0)))
    head_rows = jnp.stack(
        [own(part, 0, heads) for part in (-jnp.exp(decay_log), step_bias, skip_gain)]
    )
    head_rows = jnp.pad(head_rows, ((0, 5), (0, Layout(heads).steps - heads)))
    keeps = []
    for offset in (1, 2, 3):
        earlier = jnp.concatenate([jnp.full((offset,), -1, segments.dtype), segments[:-offset]])
        keeps.append(earlier == segments)
    nexts = [jnp.pad(keep[k + 1 :], (0, k + 1)) for k, keep in enumerate(keeps)]
    chunk_last = segments.reshape(ctx, tok_count)[:, -1]
    spread = lambda ids: jnp.repeat(ids, tok_count) == segments
    opens = spread(jnp.concatenate([jnp.full((1,), -1, segments.dtype), chunk_last[:-1]]))
    marks = keeps + nexts + [segments, opens, spread(chunk_last)]
    columns = jnp.stack([mark.astype(jnp.float32) for mark in marks], axis=1)
    columns = jnp.pad(columns, ((0, 0), (0, 16 - len(marks))))
    seg_row = segments.astype(jnp.float32).reshape(1, length)
    mixed_out, entry_product, scanned, states, log_total = mix_forward(
        normed, entry, columns, seg_row, taps, head_rows, tok_count
    )
    mixing_out, feed_in, feed_out = sum_and_spread(
        mixed_out, out_rows, (feed_slabs.reshape(ctx * rows, -1), down_weight), 1
    )
    feed_in = feed_in.reshape(dp * ctx * rows, -1)
    feed_out = feed_out.reshape(dp * hidden, width)
    residual = source + mixing_out

    normed_two_own, pull_two = jax.vjp(rms_scale, residual, gain_feed)
    normed_two = gather_tokens(normed_two_own.astype(jnp.bfloat16), 2)
    gate_values = jnp.dot(normed_two, feed_in, preferred_element_type=jnp.float32)
    gate_in, up_in = gate_values[:, : dp * hidden], gate_values[:, dp * hidden :]
    active = (jax.nn.silu(gate_in) * up_in).astype(jnp.bfloat16)
    output_terms = jnp.dot(active, feed_out, preferred_element_type=jnp.float32).astype(jnp.bfloat16)
    active_grad = jnp.dot(cotangents, feed_out.T, preferred_element_type=jnp.float32)
    gate_grad = jnp.concatenate(
        [active_grad * up_in * silu_slope(gate_in), active_grad * jax.nn.silu(gate_in)], axis=1
    ).astype(jnp.bfloat16)
    normed_two_grad, feed_sums, grad_feed_out = sum_and_total(
        gate_grad,
        feed_in,
        (
            across(normed_two, gate_grad).reshape(dp, ctx * rows, -1),
            across(active, cotangents).reshape(dp, hidden, width),
        ),
        3,
    )
    residual_part, grad_gain_feed = pull_two(normed_two_grad)
    residual_grad = cotangent.astype(jnp.float32) + residual_part
    residual_half = gather_tokens(residual_grad.astype(jnp.bfloat16), 4)
    late_terms, _ = lax.optimization_barrier((output_terms, residual_half))
    output_sum = lax.psum_scatter(late_terms, "ctx", scatter_dimension=0, tiled=True)
    output = (residual + output_sum.astype(jnp.float32)).astype(jnp.bfloat16)
    grads, tap_grads, head_grads, out_terms = mix_backward(
        residual_half,
        out_rows,
        mixed_out,
        entry_product,
        scanned,
        states,
        log_total,
        columns,
        seg_row,
        taps,
        head_rows,
        tok_count,
    )
    taken = own_attention * dp
    out_terms = jnp.concatenate(
        [
            out_terms[:taken].reshape(dp, own_attention, width),
            out_terms[taken:].reshape(dp, -1, width),
        ],
        axis=1,
    )
    own_small = jnp.concatenate(
        [grad_gain_feed, tap_grads[:5].reshape(-1), head_grads[:3, :heads].reshape(-1)], axis=0
    )
    own_small = jnp.pad(own_small, (0, -own_small.shape[0] % 1024)).reshape(-1, 128)
    input_grad, entry_grads, grad_feed_in, grad_outs, smalls, gains = leave(
        grads,
        entry,
        source,
        residual_grad,
        gain_mixing.reshape(1, width),
        across(normed, grads).reshape(dp, ctx, rows, -1),
        feed_sums.reshape(ctx, rows, -1),
        out_terms,
        own_small,
    )
    grad_attention_in, grad_mixer_in, grad_step_in = entry_unslab(
        entry_grads.astype(jnp.float32), ctx
    )
    smalls = smalls.reshape(ctx, -1)
    tap_width = heads * SSM_HEAD + 2 * STATE
    tap_all = smalls[:, width : width + 5 * tap_width].reshape(ctx, 5, tap_width)
    tap_sums = jnp.concatenate(
        [
            tap_all[:, :, 2 * STATE :].transpose(1, 0, 2).reshape(5, SSM_INNER),
            jnp.sum(tap_all[:, :, : 2 * STATE], axis=0),
        ],
        axis=1,
    )
    head_all = smalls[:, width + 5 * tap_width :][:, : 3 * heads].reshape(ctx, 3, heads)
    head_sums = head_all.transpose(1, 0, 2).reshape(3, SSM_HEADS)
    grad_gate_up = (
        grad_feed_in.reshape(ctx, rows, 2, dp, hidden)
        .transpose(1, 2, 3, 0, 4)
        .reshape(rows, -1)
        .astype(jnp.float32)
    )
    return (
        output.reshape(block_input.shape),
        input_grad.reshape(block_input.shape),
        grad_attention_in,
        grad_mixer_in,
        grad_step_in,
        grad_outs[:own_attention],
        grad_outs[own_attention:],
        grad_gate_up,
        grad_feed_out.astype(jnp.float32),
        jnp.sum(gains, axis=(0, 1)),
        jnp.sum(smalls[:, :width], axis=0),
        head_sums[0],
        head_sums[1],
        head_sums[2],
        tap_sums[:4],
        tap_sums[4],
    )


def solution(mesh):
    in_specs = (
        P("dp", "ctx", None),
        P("dp", "ctx"),
        P("dp", "ctx", None),
        P(("dp", "ctx"), None),
        P(("dp", "ctx"), None),
        P(("dp", "ctx"), None),
        P(("dp", "ctx"), None),
        P(("dp", "ctx"), None),
        P(("dp", "ctx"), None),
        P(("dp", "ctx"), None),
        P(),
        P(),
        P(),
        P(),
        P(),
        P(),
        P(),
    )
    out_specs = (
        P("dp", "ctx", None),
        P("dp", "ctx", None),
        P(("dp", "ctx"), None),
        P(("dp", "ctx"), None),
        P(("dp", "ctx"), None),
        P(("dp", "ctx"), None),
        P(("dp", "ctx"), None),
        P(("dp", "ctx"), None),
        P(("dp", "ctx"), None),
        P(),
        P(),
        P(),
        P(),
        P(),
        P(),
        P(),
    )
    sequences = mesh.shape["dp"]

    def choose(*arrays):
        heads = split_heads(mesh.shape["ctx"]) and arrays[0].shape[0] == sequences
        body = split_local if heads else local
        mapped = jax.shard_map(
            body, mesh=mesh, in_specs=in_specs, out_specs=out_specs, check_vma=False
        )
        return mapped(*arrays)

    return choose
```

```python
import functools
import math

import jax
import jax.numpy as jnp
from jax import lax
from jax.experimental import pallas as pl
from jax.experimental.pallas import tpu as pltpu
from jax.sharding import PartitionSpec as P

FF = 2048
HEADS_Q = 8
HEADS_KV = 2
HEAD = 64
SSM_HEADS = 24
SSM_HEAD = 64
STATE = 128
SSM_INNER = 1536


highest = lax.Precision.HIGHEST


def from_behind(block, axis, distance):
    devices = range(lax.axis_size(axis))
    route = [(i - distance, i) for i in devices if i - distance in devices]
    return lax.ppermute(block, axis, route)


def carried_in(value, axis, join, neutral, backward):
    count, mine = (lax.axis_size(axis), lax.axis_index(axis))
    pieces = jax.tree.map(lambda part: lax.all_gather(part, axis), value)
    if backward:
        pieces = jax.tree.map(lambda part: part[::-1], pieces)
        mine = count - 1 - mine
    so_far = jax.tree.map(
        lambda part, zero: jnp.full_like(part, 0) + jnp.asarray(zero, part.dtype), value, neutral
    )

    def hop(position, so_far):
        longer = join(so_far, jax.tree.map(lambda part: part[position], pieces))
        return jax.tree.map(lambda new, old: jnp.where(position < mine, new, old), longer, so_far)

    return lax.fori_loop(0, count - 1, hop, so_far)


def carried_by_heads(decays, state, backward):
    count, mine = (lax.axis_size("ctx"), lax.axis_index("ctx"))
    seq_count, heads = decays.shape[1:]
    share = heads // count
    own = lax.dynamic_slice_in_dim(decays, mine * share, share, axis=2)
    pieces = lax.all_to_all(state, "ctx", split_axis=1, concat_axis=0, tiled=True)
    pieces = pieces.reshape((count, seq_count, share) + state.shape[2:])
    order = list(range(count))[::-1] if backward else list(range(count))
    so_far = jnp.zeros_like(pieces[0])
    reached = [None] * count
    for position in order:
        reached[position] = so_far
        so_far = own[position][:, :, None, None] * so_far + pieces[position]
    return lax.all_to_all(
        jnp.concatenate(reached, axis=0), "ctx", split_axis=0, concat_axis=1, tiled=True
    )


def fold_shape(owned, rows, width):
    step = math.gcd(owned, rows)
    return (step, owned // step, rows // step, width // (rows // step))


def fold_rows(array, owned, rows):
    step, across, down, part = fold_shape(owned, rows, array.shape[1])
    blocks = array.reshape(-1, owned, array.shape[1])
    columns = [
        jnp.concatenate(
            [blocks[:, i * step : (i + 1) * step, j * part : (j + 1) * part] for j in range(down)],
            axis=1,
        )
        for i in range(across)
    ]
    return jnp.concatenate(columns, axis=2).reshape(-1, across * part)


def unfold_rows(array, owned, rows, width):
    step, across, down, part = fold_shape(owned, rows, width)
    blocks = array.reshape(-1, rows, across * part)
    lines = [
        jnp.concatenate(
            [blocks[:, j * step : (j + 1) * step, i * part : (i + 1) * part] for j in range(down)],
            axis=2,
        )
        for i in range(across)
    ]
    return jnp.concatenate(lines, axis=1).reshape(-1, width)


def pad_columns(array):
    return jnp.pad(array, ((0, 0), (0, -array.shape[1] % 128)))


def cut_columns(array, widths):
    pieces, at = ([], 0)
    for width in widths:
        pieces.append(array[:, at : at + width])
        at += width
    return pieces


def rms_scale(values, gain):
    return values * lax.rsqrt(jnp.mean(values * values, axis=-1, keepdims=True) + 1e-05) * gain


def silu_slope(values):
    sigma = jax.nn.sigmoid(values)
    return sigma * (1.0 + values * (1.0 - sigma))


def ssd_local(
    inner, write_map, read_map, step_raw, decay_log, step_bias, skip_gain, starts, segments
):
    step = jax.nn.softplus(step_raw + step_bias)
    rates = step * -jnp.exp(decay_log)
    places = jnp.arange(segments.shape[0])
    lower = places[None, :] <= places[:, None]
    running = jnp.dot(lower.astype(jnp.float32), rates, precision=highest)
    same = (segments[:, None] == segments[None, :]) & lower
    spans = jnp.where(same[None], running.T[:, :, None] - running.T[:, None, :], -1e30)
    intersection = jnp.dot(read_map, write_map.T, precision=highest)
    mixing = jnp.exp(spans) * intersection[None] * step.T[:, None, :]
    result = (
        jnp.einsum("hts,shp->thp", mixing, inner, precision=highest)
        + skip_gain[None, :, None] * inner
    )
    before = jnp.sum((lower & starts[None, :]).astype(jnp.int32), axis=1) == 0
    carried = jnp.where(before[:, None], jnp.exp(running), 0.0)
    tails = jnp.where(
        (segments == segments[-1])[:, None], jnp.exp(running[-1][None, :] - running), 0.0
    )
    state = jnp.einsum("sh,shp,sn->hpn", tails * step, inner, write_map, precision=highest)
    return (result, state, carried[-1], carried)


def add_state(result, carried, read_map, state_in):
    return result + carried[:, :, None] * jnp.einsum(
        "hpn,tn->thp", state_in, read_map, precision=highest
    )


def ssd_block(
    inner,
    write_map,
    read_map,
    step_raw,
    decay_log,
    step_bias,
    skip_gain,
    starts,
    segments,
    state_in,
):
    result, state, decay_total, carried = ssd_local(
        inner, write_map, read_map, step_raw, decay_log, step_bias, skip_gain, starts, segments
    )
    return (
        add_state(result, carried, read_map, state_in),
        decay_total[:, None, None] * state_in + state,
    )


def chain(earlier, later):
    return (earlier[0] * later[0], later[0][:, :, None, None] * earlier[1] + later[1])


def over_blocks(step, start, items):
    if items[2].shape[0] > 1:
        return lax.scan(step, start, items)
    carry, result = step(start, (items[0][0], items[1][0], 0))
    return (carry, None if result is None else result[None])


def group_queries(flat, seq_count, tok_count):
    groups = HEADS_Q // HEADS_KV
    shaped = flat.reshape(seq_count, tok_count, HEADS_KV, groups, HEAD)
    return shaped.transpose(0, 2, 3, 1, 4).reshape(seq_count, HEADS_KV, groups * tok_count, HEAD)


def ungroup(grouped, seq_count, tok_count):
    groups = HEADS_Q // HEADS_KV
    shaped = grouped.reshape(seq_count, HEADS_KV, groups, tok_count, HEAD)
    return shaped.transpose(0, 3, 1, 2, 4).reshape(seq_count * tok_count, HEADS_Q * HEAD)


def local(
    block_input,
    segment_ids,
    out_cotangent,
    attention_in,
    mixer_in,
    step_in,
    attention_out,
    mixer_out,
    gate_up,
    down_weight,
    gain_mixing,
    gain_feed,
    decay_log,
    step_bias,
    skip_gain,
    conv_weight,
    conv_bias,
):
    seq_count, tok_count, width = block_input.shape
    row_count = seq_count * tok_count
    length = tok_count * lax.axis_size("ctx")
    block = length if length <= 1024 else 512
    blocks = length // block
    groups = HEADS_Q // HEADS_KV
    query_width = HEADS_Q * HEAD
    key_width = HEADS_KV * HEAD
    score_scale = HEAD ** (-0.5)
    query_rows = groups * tok_count
    first = lax.axis_index("ctx") * tok_count
    own_rows = attention_in.shape[0]
    axes = ("dp", "ctx")
    entry = jnp.concatenate([attention_in, mixer_in, pad_columns(step_in)], axis=1)
    full_attention_in, full_mixer_in, full_step_in = cut_columns(
        lax.all_gather(entry, axes, axis=0, tiled=True),
        (attention_in.shape[1], mixer_in.shape[1], step_in.shape[1]),
    )
    tall = (attention_out, mixer_out, down_weight)
    folded = [fold_rows(weight, weight.shape[0], own_rows) for weight in tall]
    rest = lax.all_gather(
        jnp.concatenate(folded + [gate_up], axis=1), axes, axis=0, tiled=True
    )
    rest = cut_columns(rest, [weight.shape[1] for weight in folded] + [gate_up.shape[1]])
    full_attention_out, full_mixer_out, full_down = (
        unfold_rows(part, weight.shape[0], own_rows, width) for part, weight in zip(rest, tall)
    )
    full_gate_up = rest[3]
    source = block_input.reshape(row_count, width).astype(jnp.float32)
    normed = rms_scale(source, gain_mixing).astype(jnp.bfloat16)
    projected = jnp.dot(normed, full_attention_in, preferred_element_type=jnp.float32).astype(
        jnp.bfloat16
    )
    mixed_in = jnp.dot(normed, full_mixer_in, preferred_element_type=jnp.float32)
    step_raw = jnp.dot(normed, full_step_in, preferred_element_type=jnp.float32).reshape(
        seq_count, tok_count, SSM_HEADS
    )
    queries = group_queries(projected[:, :query_width], seq_count, tok_count)
    local_keys = (
        projected[:, query_width:].reshape(seq_count, tok_count, 2 * key_width).transpose(1, 0, 2)
    )
    local_segments = segment_ids.T
    keys_all, segments_all = (
        lax.all_gather(local_keys, "ctx", axis=0, tiled=True),
        lax.all_gather(local_segments, "ctx", axis=0, tiled=True),
    )
    query_pos = first + jnp.arange(query_rows) % tok_count
    query_segments = jnp.tile(segment_ids, (1, groups))
    segment_blocks = segments_all.reshape(blocks, block, seq_count)
    block_ids = jnp.arange(blocks)

    def scores_of(key_block, seg_block, block_id):
        keys = key_block[:, :, :key_width].reshape(block, seq_count, HEADS_KV, HEAD)
        scores = (
            jnp.einsum("sgrd,ksgd->sgrk", queries, keys, preferred_element_type=jnp.float32)
            * score_scale
        )
        key_pos = block_id * block + jnp.arange(block)
        allowed = (key_pos[None, None, None, :] <= query_pos[None, None, :, None]) & (
            seg_block.T[:, None, None, :] == query_segments[:, None, :, None]
        )
        return (scores, allowed)

    key_blocks = keys_all.reshape(blocks, block, seq_count, 2 * key_width)

    def gather_stats(carry, item):
        top, total = carry
        scores, allowed = scores_of(item[0], item[1], item[2])
        masked = jnp.where(allowed, scores, -1e30)
        new_top = jnp.maximum(top, jnp.max(masked, axis=-1))
        total = total * jnp.exp(top - new_top) + jnp.sum(
            jnp.where(allowed, jnp.exp(masked - new_top[..., None]), 0.0), axis=-1
        )
        return ((new_top, total), None)

    start_top = jnp.full((seq_count, HEADS_KV, query_rows), -1e30, jnp.float32)
    (top, total), _ = over_blocks(
        gather_stats,
        (start_top, jnp.zeros_like(start_top)),
        (key_blocks, segment_blocks, block_ids),
    )
    log_total = top + jnp.log(total)

    def weigh_values(accum, item):
        scores, allowed = scores_of(item[0], item[1], item[2])
        values = item[0][:, :, key_width:].reshape(block, seq_count, HEADS_KV, HEAD)
        probs = jnp.where(allowed, jnp.exp(scores - log_total[..., None]), 0.0).astype(jnp.bfloat16)
        return (
            accum
            + jnp.einsum("sgrk,ksgd->sgrd", probs, values, preferred_element_type=jnp.float32),
            None,
        )

    attended, _ = over_blocks(
        weigh_values, jnp.zeros(queries.shape, jnp.float32), (key_blocks, segment_blocks, block_ids)
    )
    attended = attended.astype(jnp.bfloat16)
    attended_flat = ungroup(attended, seq_count, tok_count)
    gate_part = mixed_in[:, :SSM_INNER]
    conv_width = mixed_in.shape[1] - SSM_INNER
    conv_in = mixed_in[:, SSM_INNER:].reshape(seq_count, tok_count, conv_width)
    positions = first + jnp.arange(tok_count)
    before_rows = from_behind(conv_in[:, tok_count - 3 :, :], "ctx", 1)
    extended = jnp.concatenate([before_rows, conv_in], axis=1)
    pre = conv_bias + conv_weight[3] * conv_in
    keep_masks = []
    for offset in (1, 2, 3):
        earlier_ids = segments_all[jnp.maximum(positions - offset, 0)].T
        keep_mask = (positions >= offset)[None, :] & (earlier_ids == segment_ids)
        keep_masks.append(keep_mask)
        pre = (
            pre
            + jnp.where(keep_mask[..., None], extended[:, 3 - offset : 3 - offset + tok_count], 0.0)
            * conv_weight[3 - offset]
        )
    converted = jax.nn.silu(pre)
    inner = converted[..., :SSM_INNER].reshape(seq_count, tok_count, SSM_HEADS, SSM_HEAD)
    write_map = converted[..., SSM_INNER : SSM_INNER + STATE]
    read_map = converted[..., SSM_INNER + STATE :]
    starts = (positions == 0)[None, :] | jnp.logical_not(keep_masks[0])
    local_map = jax.vmap(ssd_local, in_axes=(0, 0, 0, 0, None, None, None, 0, 0))
    partial_out, partial_state, decay_total, carried = local_map(
        inner, write_map, read_map, step_raw, decay_log, step_bias, skip_gain, starts, segment_ids
    )
    by_heads = SSM_HEADS % lax.axis_size("ctx") == 0
    if by_heads:
        decays = lax.all_gather(decay_total, "ctx")
        state_in = carried_by_heads(decays, partial_state, False)
    else:
        unit = (jnp.ones_like(decay_total), jnp.zeros_like(partial_state))
        state_in = carried_in((decay_total, partial_state), "ctx", chain, unit, False)[1]
    scanned = jax.vmap(add_state)(partial_out, carried, read_map, state_in)
    flat_scan = scanned.reshape(row_count, SSM_INNER)
    gated = (flat_scan * jax.nn.silu(gate_part)).astype(jnp.bfloat16)
    residual = (
        source
        + jnp.dot(attended_flat, full_attention_out, preferred_element_type=jnp.float32)
        + jnp.dot(gated, full_mixer_out, preferred_element_type=jnp.float32)
    )
    normed_two = rms_scale(residual, gain_feed).astype(jnp.bfloat16)
    gate_values = jnp.dot(normed_two, full_gate_up, preferred_element_type=jnp.float32)
    gate_in = gate_values[:, :FF]
    up_in = gate_values[:, FF:]
    active = (jax.nn.silu(gate_in) * up_in).astype(jnp.bfloat16)
    output = (residual + jnp.dot(active, full_down, preferred_element_type=jnp.float32)).astype(
        jnp.bfloat16
    )
    cotangent = out_cotangent.reshape(row_count, width)
    grad_down_weight = jnp.dot(active.T, cotangent, preferred_element_type=jnp.float32).astype(
        jnp.bfloat16
    )
    active_grad = jnp.dot(cotangent, full_down.T, preferred_element_type=jnp.float32)
    gate_grad = jnp.concatenate(
        [active_grad * up_in * silu_slope(gate_in), active_grad * jax.nn.silu(gate_in)], axis=1
    ).astype(jnp.bfloat16)
    grad_gate_up = jnp.dot(normed_two.T, gate_grad, preferred_element_type=jnp.float32).astype(
        jnp.bfloat16
    )
    feed_terms = jnp.concatenate(
        [grad_gate_up, fold_rows(grad_down_weight, down_weight.shape[0], own_rows)], axis=1
    )
    feed_sums = lax.psum_scatter(feed_terms, axes, scatter_dimension=0, tiled=True)
    normed_two_grad = jnp.dot(gate_grad, full_gate_up.T, preferred_element_type=jnp.float32)
    _, pull_two = jax.vjp(rms_scale, residual, gain_feed)
    residual_part, grad_gain_feed = pull_two(normed_two_grad)
    residual_grad = cotangent.astype(jnp.float32) + residual_part
    residual_half, _ = lax.optimization_barrier((residual_grad.astype(jnp.bfloat16), feed_terms))
    grad_attention_out = jnp.dot(attended_flat.T, residual_half, preferred_element_type=jnp.float32)
    grad_mixer_out = jnp.dot(gated.T, residual_half, preferred_element_type=jnp.float32)
    attended_grad = jnp.dot(
        residual_half, full_attention_out.T, preferred_element_type=jnp.float32
    ).astype(jnp.bfloat16)
    gated_grad = jnp.dot(residual_half, full_mixer_out.T, preferred_element_type=jnp.float32)
    gate_part_grad = gated_grad * flat_scan * silu_slope(gate_part)
    scan_grad = (gated_grad * jax.nn.silu(gate_part)).reshape(
        seq_count, tok_count, SSM_HEADS, SSM_HEAD
    )
    direct = jnp.einsum("sth,sthp,stn->shpn", carried, scan_grad, read_map, precision=highest)
    if by_heads:
        state_grad = carried_by_heads(decays, direct, True)
    else:
        state_grad = carried_in((decay_total, direct), "ctx", chain, unit, True)[1]

    def block_map(inner_v, write_v, read_v, step_v, decay_v, bias_v, skip_v, state_v):
        mapped = jax.vmap(ssd_block, in_axes=(0, 0, 0, 0, None, None, None, 0, 0, 0))
        return mapped(
            inner_v, write_v, read_v, step_v, decay_v, bias_v, skip_v, starts, segment_ids, state_v
        )

    _, pull_scan = jax.vjp(
        block_map, inner, write_map, read_map, step_raw, decay_log, step_bias, skip_gain, state_in
    )
    pulled = pull_scan((scan_grad, state_grad))
    converted_grad = jnp.concatenate(
        [pulled[0].reshape(seq_count, tok_count, SSM_INNER), pulled[1], pulled[2]], axis=2
    )
    pre_grad = converted_grad * silu_slope(pre)
    after_rows = from_behind(pre_grad[:, :3, :], "ctx", -1)
    ahead = jnp.concatenate([pre_grad, after_rows], axis=1)
    conv_in_grad = conv_weight[3] * pre_grad
    tap_grads = [None, None, None, jnp.sum(pre_grad * conv_in, axis=(0, 1))]
    for offset in (1, 2, 3):
        later_ids = segments_all[jnp.minimum(positions + offset, length - 1)].T
        later_mask = later_ids == segment_ids
        conv_in_grad = (
            conv_in_grad
            + jnp.where(later_mask[..., None], ahead[:, offset : offset + tok_count], 0.0)
            * conv_weight[3 - offset]
        )
        earlier_rows = jnp.where(
            keep_masks[offset - 1][..., None], extended[:, 3 - offset : 3 - offset + tok_count], 0.0
        )
        tap_grads[3 - offset] = jnp.sum(pre_grad * earlier_rows, axis=(0, 1))
    grad_conv_weight = jnp.stack(tap_grads, axis=0)
    grad_conv_bias = jnp.sum(pre_grad, axis=(0, 1))
    mixer_grad = jnp.concatenate(
        [gate_part_grad, conv_in_grad.reshape(row_count, conv_width)], axis=1
    ).astype(jnp.bfloat16)
    step_grad_half = pulled[3].reshape(row_count, SSM_HEADS).astype(jnp.bfloat16)
    out_grad = group_queries(attended_grad, seq_count, tok_count)
    deltas = jnp.sum(out_grad.astype(jnp.float32) * attended.astype(jnp.float32), axis=-1)

    def attention_grads(query_grad, item):
        scores, allowed = scores_of(item[0], item[1], item[2])
        keys = item[0][:, :, :key_width].reshape(block, seq_count, HEADS_KV, HEAD)
        values = item[0][:, :, key_width:].reshape(block, seq_count, HEADS_KV, HEAD)
        probs = jnp.where(allowed, jnp.exp(scores - log_total[..., None]), 0.0)
        value_grad = jnp.einsum(
            "sgrk,sgrd->ksgd",
            probs.astype(jnp.bfloat16),
            out_grad,
            preferred_element_type=jnp.float32,
        )
        prob_grad = jnp.einsum(
            "sgrd,ksgd->sgrk", out_grad, values, preferred_element_type=jnp.float32
        )
        score_grad = (probs * (prob_grad - deltas[..., None])).astype(jnp.bfloat16)
        query_grad = (
            query_grad
            + jnp.einsum("sgrk,ksgd->sgrd", score_grad, keys, preferred_element_type=jnp.float32)
            * score_scale
        )
        key_grad = (
            jnp.einsum("sgrk,sgrd->ksgd", score_grad, queries, preferred_element_type=jnp.float32)
            * score_scale
        )
        both = jnp.concatenate(
            [
                key_grad.reshape(block, seq_count, key_width),
                value_grad.reshape(block, seq_count, key_width),
            ],
            axis=2,
        )
        return (query_grad, both)

    query_grad, key_terms = over_blocks(
        attention_grads,
        jnp.zeros(queries.shape, jnp.float32),
        (key_blocks, segment_blocks, block_ids),
    )
    key_pieces = lax.all_to_all(
        key_terms.reshape(length, seq_count, 2 * key_width).astype(jnp.bfloat16),
        "ctx",
        split_axis=0,
        concat_axis=0,
        tiled=True,
    )
    key_sums = jnp.sum(
        key_pieces.reshape(-1, tok_count, seq_count, 2 * key_width).astype(jnp.float32), axis=0
    )
    kv_grad = key_sums.transpose(1, 0, 2).reshape(row_count, 2 * key_width)
    projected_grad = jnp.concatenate(
        [ungroup(query_grad, seq_count, tok_count), kv_grad], axis=1
    ).astype(jnp.bfloat16)
    grad_attention_in = jnp.dot(normed.T, projected_grad, preferred_element_type=jnp.float32)
    grad_mixer_in = jnp.dot(normed.T, mixer_grad, preferred_element_type=jnp.float32)
    grad_step_in = jnp.dot(normed.T, step_grad_half, preferred_element_type=jnp.float32)
    normed_grad = (
        jnp.dot(projected_grad, full_attention_in.T, preferred_element_type=jnp.float32)
        + jnp.dot(mixer_grad, full_mixer_in.T, preferred_element_type=jnp.float32)
        + jnp.dot(step_grad_half, full_step_in.T, preferred_element_type=jnp.float32)
    )
    _, pull_one = jax.vjp(rms_scale, source, gain_mixing)
    source_part, grad_gain_mixing = pull_one(normed_grad)
    input_grad = residual_grad + source_part
    others = [
        grad_attention_in.astype(jnp.bfloat16),
        grad_mixer_in.astype(jnp.bfloat16),
        fold_rows(grad_attention_out.astype(jnp.bfloat16), attention_out.shape[0], own_rows),
        fold_rows(grad_mixer_out.astype(jnp.bfloat16), mixer_out.shape[0], own_rows),
        pad_columns(grad_step_in.astype(jnp.bfloat16)),
    ]
    other_sums = lax.psum_scatter(
        jnp.concatenate(others, axis=1), axes, scatter_dimension=0, tiled=True
    )
    feed_parts = cut_columns(
        feed_sums, (gate_up.shape[1], feed_sums.shape[1] - gate_up.shape[1])
    )
    other_parts = cut_columns(other_sums, [part.shape[1] for part in others])
    weight_sums = [
        part.astype(jnp.float32)
        for part in (
            other_parts[0],
            other_parts[1],
            other_parts[4][:, :SSM_HEADS],
            unfold_rows(other_parts[2], attention_out.shape[0], own_rows, width),
            unfold_rows(other_parts[3], mixer_out.shape[0], own_rows, width),
            feed_parts[0],
            unfold_rows(feed_parts[1], down_weight.shape[0], own_rows, width),
        )
    ]
    small_sums = lax.psum(
        (
            grad_gain_mixing,
            grad_gain_feed,
            pulled[4],
            pulled[5],
            pulled[6],
            grad_conv_weight,
            grad_conv_bias,
        ),
        ("dp", "ctx"),
    )
    return (
        output.reshape(seq_count, tok_count, width),
        input_grad.reshape(seq_count, tok_count, width),
        weight_sums[0],
        weight_sums[1],
        weight_sums[2],
        weight_sums[3],
        weight_sums[4],
        weight_sums[5],
        weight_sums[6],
        small_sums[0],
        small_sums[1],
        small_sums[2],
        small_sums[3],
        small_sums[4],
        small_sums[5],
        small_sums[6],
    )

def split_heads(ctx):
    return HEADS_Q == ctx and SSM_HEADS % ctx == 0 and ctx % HEADS_KV == 0


def entry_layout(ctx):
    heads = SSM_HEADS // ctx
    widths = [STATE, STATE, heads * SSM_HEAD, heads * SSM_HEAD, HEAD, HEAD, HEAD, heads]
    return widths + [-sum(widths) % 128]


def entry_slabs(attention_in, mixer_in, step_in, ctx):
    rows = attention_in.shape[0]
    share = ctx // HEADS_KV
    query_width = HEADS_Q * HEAD
    key_width = HEADS_KV * HEAD

    def parts(array, count):
        return array.reshape(rows, count, -1).transpose(1, 0, 2)

    kv = [
        jnp.repeat(parts(attention_in[:, at : at + key_width], HEADS_KV), share, axis=0)
        for at in (query_width, query_width + key_width)
    ]
    both = jnp.broadcast_to(mixer_in[None, :, 2 * SSM_INNER :], (ctx, rows, 2 * STATE))
    pieces = [
        both,
        parts(mixer_in[:, SSM_INNER : 2 * SSM_INNER], ctx),
        parts(mixer_in[:, :SSM_INNER], ctx),
        parts(attention_in[:, :query_width], ctx),
        kv[0],
        kv[1],
        parts(step_in, ctx),
        jnp.zeros((ctx, rows, entry_layout(ctx)[-1]), jnp.bfloat16),
    ]
    return jnp.concatenate(pieces, axis=2)


def offsets(widths):
    at, places = 0, []
    for width in widths:
        places.append(at)
        at += width
    return places


MESH = pl.DeviceIdType.MESH
IN_VMEM = pl.BlockSpec(memory_space=pltpu.VMEM)
ANYWHERE = pl.BlockSpec(memory_space=pl.ANY)


def remote(source, target, send, recv, peer):
    return pltpu.make_async_remote_copy(
        src_ref=source,
        dst_ref=target,
        send_sem=send,
        recv_sem=recv,
        device_id=peer,
        device_id_type=MESH,
    )


def arrived(ref, recv, peer):
    remote(ref, ref, recv, recv, peer).wait_recv()


class Here:
    def __init__(self, dp, ctx):
        self.dp, self.ctx, self.pairs = dp, ctx, ctx // 2
        self.d, self.me = lax.axis_index("dp"), lax.axis_index("ctx")
        self.z, self.c = self.me // 2, self.me % 2
        self.sibling = (self.d, self.z * 2 + 1 - self.c)

    def dp_peers(self):
        return [(lax.rem(self.d + k, self.dp), self.me) for k in range(1, self.dp)]

    def ctx_peers(self):
        return [(self.d, lax.rem(self.me + k, self.ctx)) for k in range(1, self.ctx)]

    def greet(self, peers, sender=None):
        sem = pltpu.get_barrier_semaphore()
        for peer in peers:
            pl.semaphore_signal(sem, inc=1, device_id=peer, device_id_type=MESH)
        count = len(peers)
        if sender is not None:
            away = jnp.logical_not(self.is_me(sender))

            @pl.when(away)
            def _():
                pl.semaphore_signal(sem, inc=1, device_id=sender, device_id_type=MESH)

            count = count + away.astype(jnp.int32)
        pl.semaphore_wait(sem, count)

    def is_me(self, peer):
        return (peer[0] == self.d) & (peer[1] == self.me)

    def user(self):
        place = self.d * self.ctx + self.me
        return (lax.rem(place, self.dp), place // self.dp)

    def owner(self):
        place = self.me * self.dp + self.d
        return (place // self.ctx, lax.rem(place, self.ctx))


class Relay:
    def __init__(self, here, block, slots, send, recv, local, cut=None):
        self.here, self.slots, self.cut = here, slots, cut
        self.block = block if cut is None else block.at[cut]
        self.send, self.recv, self.local = send, recv, local
        self.up = (here.d, (here.z + 1) * 2 + here.c)
        self.down = (here.d, (here.z - 1) * 2 + here.c)
        self.has_up, self.has_down = here.z < here.pairs - 1, here.z > 0

    @staticmethod
    def scratch(pairs):
        return [
            pltpu.SemaphoreType.DMA((4 * pairs,)),
            pltpu.SemaphoreType.DMA((2 * pairs,)),
            pltpu.SemaphoreType.DMA,
        ]

    @staticmethod
    def cuts(rows):
        count = 2 if rows % (16 * 2) == 0 else 1
        return [pl.ds(i * (rows // count), rows // count) for i in range(count)]

    def slot(self, z, c):
        ref = self.slots.at[z * 2 + c]
        return ref if self.cut is None else ref.at[self.cut]

    def greet(self):
        sem = pltpu.get_barrier_semaphore()

        def signal(peer):
            pl.semaphore_signal(sem, inc=1, device_id=peer, device_id_type=MESH)

        pl.when(self.has_up)(lambda: signal(self.up))
        pl.when(self.has_down)(lambda: signal(self.down))
        signal(self.here.sibling)
        count = self.has_up.astype(jnp.int32) + self.has_down.astype(jnp.int32)
        pl.semaphore_wait(sem, count + 1)

    def begin(self):
        h, n = self.here, self.here.pairs
        own = self.slot(h.z, h.c)
        pltpu.make_async_copy(self.block, own, self.local).start()

        @pl.when(self.has_up)
        def _():
            remote(self.block, own, self.send.at[0], self.recv.at[h.me], self.up).start()

        @pl.when(self.has_down)
        def _():
            remote(self.block, own, self.send.at[n], self.recv.at[h.me], self.down).start()

        remote(self.block, own, self.send.at[2 * n], self.recv.at[h.me], h.sibling).start()

    def hop(self, s):
        h, n = self.here, self.here.pairs
        low, high = h.z - s, h.z + s

        @pl.when(low >= 0)
        def _():
            ref, recv = self.slot(low, h.c), self.recv.at[low * 2 + h.c]
            arrived(ref, recv, h.sibling)

            @pl.when(self.has_up)
            def _():
                remote(ref, ref, self.send.at[s], recv, self.up).start()

            remote(ref, ref, self.send.at[2 * n + 2 * s - 1], recv, h.sibling).start()

        @pl.when(high < n)
        def _():
            ref, recv = self.slot(high, h.c), self.recv.at[high * 2 + h.c]
            arrived(ref, recv, h.sibling)

            @pl.when(self.has_down)
            def _():
                remote(ref, ref, self.send.at[n + s], recv, self.down).start()

            remote(ref, ref, self.send.at[2 * n + 2 * s], recv, h.sibling).start()

    def end(self):
        h, n = self.here, self.here.pairs
        for z in range(n):
            arrived(self.slot(z, 1 - h.c), self.recv.at[z * 2 + 1 - h.c], h.sibling)
        own = self.slot(h.z, h.c)

        def sent(index):
            remote(own, own, self.send.at[index], self.recv.at[0], h.sibling).wait_send()

        for s in range(n):
            low, high = h.z - s, h.z + s
            pl.when((low >= 0) & self.has_up)(functools.partial(sent, s))
            pl.when((high < n) & self.has_down)(functools.partial(sent, n + s))
            if s == 0:
                sent(2 * n)
            else:
                pl.when(low >= 0)(functools.partial(sent, 2 * n + 2 * s - 1))
                pl.when(high < n)(functools.partial(sent, 2 * n + 2 * s))
        pltpu.make_async_copy(self.block, own, self.local).wait()


class Spread:
    def __init__(self, here, block, slots, send, recv, local):
        self.here, self.block, self.slots = here, block, slots
        self.send, self.recv, self.local = send, recv, local

    @staticmethod
    def scratch(dp):
        return [
            pltpu.SemaphoreType.DMA((dp,)),
            pltpu.SemaphoreType.DMA((dp,)),
            pltpu.SemaphoreType.DMA,
        ]

    def begin(self):
        h = self.here
        pltpu.make_async_copy(self.block, self.slots.at[h.d], self.local).start()
        self.copies = [
            remote(self.block, self.slots.at[h.d], self.send.at[k], self.recv.at[h.d], peer)
            for k, peer in enumerate(h.dp_peers())
        ]
        for copy in self.copies:
            copy.start()

    def end(self):
        h = self.here
        for peer in h.dp_peers():
            arrived(self.slots.at[peer[0]], self.recv.at[peer[0]], peer)
        for copy in self.copies:
            copy.wait_send()
        pltpu.make_async_copy(self.block, self.slots.at[h.d], self.local).wait()


class Total:
    def __init__(self, here, terms, got, result, send, recv):
        self.here, self.terms, self.got, self.result = here, terms, got, result
        self.send, self.recv = send, recv

    @staticmethod
    def scratch(dp, shape):
        return [
            pltpu.VMEM((dp,) + shape, jnp.bfloat16),
            pltpu.SemaphoreType.DMA((dp,)),
            pltpu.SemaphoreType.DMA((dp,)),
        ]

    def begin(self):
        h = self.here
        self.copies = [
            remote(
                self.terms.at[peer[0]], self.got.at[h.d], self.send.at[k], self.recv.at[h.d], peer
            )
            for k, peer in enumerate(h.dp_peers())
        ]
        for copy in self.copies:
            copy.start()

    def end(self):
        h = self.here
        total = self.terms[h.d].astype(jnp.float32)
        for peer in h.dp_peers():
            arrived(self.got.at[peer[0]], self.recv.at[peer[0]], peer)
            total = total + self.got[peer[0]].astype(jnp.float32)
        self.result[...] = total.astype(self.result.dtype)

    def leave(self):
        for copy in self.copies:
            copy.wait_send()


class Swap:
    def __init__(self, here, blocks, slots, send, recv, local):
        self.here, self.blocks, self.slots = here, blocks, slots
        self.send, self.recv, self.local = send, recv, local

    @staticmethod
    def scratch(ctx):
        return [
            pltpu.SemaphoreType.DMA((ctx,)),
            pltpu.SemaphoreType.DMA((ctx,)),
            pltpu.SemaphoreType.DMA,
        ]

    def begin(self):
        h = self.here
        pltpu.make_async_copy(self.blocks.at[h.me], self.slots.at[h.me], self.local).start()
        self.copies = []
        for k, peer in enumerate(h.ctx_peers()):
            copy = remote(
                self.blocks.at[peer[1]],
                self.slots.at[h.me],
                self.send.at[k],
                self.recv.at[h.me],
                peer,
            )
            copy.start()
            self.copies.append(copy)

    def wait(self, index):
        arrived(self.slots.at[index], self.recv.at[index], self.here.sibling)

    def leave(self):
        h = self.here
        for copy in self.copies:
            copy.wait_send()
        pltpu.make_async_copy(self.blocks.at[h.me], self.slots.at[h.me], self.local).wait()


class SumTokens:
    def __init__(self, here, left, right, turned, total, away, pair, out, got, *sems):
        self.here, self.left, self.right, self.turned, self.total = here, left, right, turned, total
        self.away, self.pair, self.out, self.got = away, pair, out, got
        self.away_send, self.away_recv, self.send, self.recv = sems
        self.order = sorted(range(1, here.pairs), key=lambda k: -min(k, here.pairs - k)) + [0]

    @staticmethod
    def scratch(pairs, rows, width):
        block = pltpu.VMEM((pairs, rows, width), jnp.bfloat16)
        return [block] * 4 + [pltpu.SemaphoreType.DMA((pairs,))] * 4

    def term(self, z, c):
        rows = self.total.shape[0]
        part = self.left[pl.ds(pl.multiple_of((z * 2 + c) * rows, rows), rows), :]
        dims = (((1,), (1 if self.turned else 0,)), ((), ()))
        return lax.dot_general(part, self.right[...], dims, preferred_element_type=jnp.float32)

    def peer(self, k):
        h = self.here
        return (h.d, lax.rem(h.z + k, h.pairs) * 2 + h.c)

    def to_sibling(self, k):
        return remote(
            self.away.at[k], self.pair.at[k], self.away_send.at[k], self.away_recv.at[k],
            self.here.sibling,
        )

    def to_pair(self, k):
        return remote(
            self.out.at[k], self.got.at[k], self.send.at[k], self.recv.at[k], self.peer(k)
        )

    def begin(self):
        h = self.here
        for k in self.order:
            self.away[k] = self.term(lax.rem(h.z + k, h.pairs), 1 - h.c).astype(jnp.bfloat16)
            self.to_sibling(k).start()
        for k in self.order:
            term = self.term(lax.rem(h.z + k, h.pairs), h.c)
            self.to_sibling(k).wait_recv()
            term = term + self.pair[k].astype(jnp.float32)
            if k:
                self.out[k] = term.astype(jnp.bfloat16)
                self.to_pair(k).start()
            else:
                self.total[...] = term

    def end(self):
        for k in self.order[::-1]:
            if k:
                self.to_pair(k).wait_recv()
                self.total[...] += self.got[k].astype(jnp.float32)

    def leave(self):
        for k in self.order:
            self.to_sibling(k).wait_send()
            if k:
                self.to_pair(k).wait_send()


class Move:
    def __init__(self, here, block, target, there, landing, sender, send, recv, local):
        self.here, self.landing, self.sender, self.recv = here, landing, sender, recv
        self.own = here.is_me(target)
        self.home = pltpu.make_async_copy(block, landing, local)
        self.far = remote(block, there, send, recv, target)

    @staticmethod
    def scratch():
        return [pltpu.SemaphoreType.DMA] * 3

    def begin(self):
        pl.when(self.own)(lambda: self.home.start())
        pl.when(jnp.logical_not(self.own))(lambda: self.far.start())

    def wait(self):
        pl.when(self.own)(lambda: self.home.wait())
        pl.when(jnp.logical_not(self.own))(lambda: arrived(self.landing, self.recv, self.sender))

    def leave(self):
        pl.when(jnp.logical_not(self.own))(lambda: self.far.wait_send())


def call(kernel, ident, outs, out_specs, in_specs, scratch, *arrays):
    return pl.pallas_call(
        kernel,
        out_shape=outs,
        in_specs=in_specs,
        out_specs=out_specs,
        scratch_shapes=scratch,
        compiler_params=pltpu.CompilerParams(
            collective_id=ident, has_side_effects=True, vmem_limit_bytes=48 * 2**20
        ),
    )(*arrays)


def like(shape, dtype=jnp.bfloat16):
    return jax.ShapeDtypeStruct(shape, dtype)


def gather_tokens(block, ident):
    dp, ctx = lax.axis_size("dp"), lax.axis_size("ctx")
    cuts = Relay.cuts(block.shape[0])

    def kernel(block_ref, slots_ref, *sems):
        here = Here(dp, ctx)
        relays = [
            Relay(here, block_ref, slots_ref, *sems[3 * i : 3 * i + 3], cut)
            for i, cut in enumerate(cuts)
        ]
        relays[0].greet()
        for relay in relays:
            relay.begin()
        for s in range(1, here.pairs):
            for relay in relays:
                relay.hop(s)
        for relay in relays:
            relay.end()

    whole = call(
        kernel, ident, like((ctx,) + block.shape, block.dtype), ANYWHERE, [ANYWHERE],
        Relay.scratch(ctx // 2) * len(cuts), block,
    )
    return whole.reshape((-1,) + block.shape[1:])


def enter(normed, segments, entry, feed, outs):
    dp, ctx = lax.axis_size("dp"), lax.axis_size("ctx")
    relay_sems, swap_sems = Relay.scratch(ctx // 2), Swap.scratch(ctx)
    cuts = Relay.cuts(normed.shape[0])

    def kernel(
        normed_ref, seg_ref, entry_ref, feed_ref, outs_ref,
        all_ref, segs_ref, full_ref, feeds_ref, rows_ref, *sems,
    ):
        here = Here(dp, ctx)
        tokens = [
            Relay(here, normed_ref, all_ref, *sems[16 + 3 * i : 19 + 3 * i], cut)
            for i, cut in enumerate(cuts)
        ]
        ids = Relay(here, seg_ref, segs_ref, *sems[0:3])
        slabs = Swap(here, entry_ref, full_ref.at[here.d], *sems[3:6])
        others = Swap(here, feed_ref, feeds_ref, *sems[6:9])
        pass_send, pass_recv = sems[9:11]
        target = here.user()
        outs = Move(
            here, outs_ref, target, rows_ref.at[target[0]], rows_ref.at[here.d], here.owner(),
            *sems[11:14],
        )
        rows_send, rows_recv = sems[14:16]
        peers = here.dp_peers()
        here.greet(peers + here.ctx_peers(), here.owner())

        def passing(source, k, index):
            return remote(
                source,
                full_ref.at[here.d, index],
                pass_send.at[k, index],
                pass_recv.at[here.d, index],
                peers[k],
            )

        def forward(index):
            slabs.wait(index)
            for k in range(dp - 1):
                passing(full_ref.at[here.d, index], k, index).start()

        def rows_copy(k):
            ref = rows_ref.at[here.d]
            return remote(ref, ref, rows_send.at[k], rows_recv.at[here.d], peers[k])

        slabs.begin()
        for k in range(dp - 1):
            passing(entry_ref.at[here.me], k, here.me).start()
        for part in tokens:
            part.begin()
        ids.begin()
        outs.begin()
        forward(here.z * 2 + 1 - here.c)
        for s in range(1, here.pairs):
            for z in (here.z - s, here.z + s):

                @pl.when((z >= 0) & (z < here.pairs))
                def _(z=z):
                    forward(z * 2 + here.c)
                    forward(z * 2 + 1 - here.c)

            for part in tokens:
                part.hop(s)
            ids.hop(s)
            if s == 1:
                others.begin()
            if s == max(1, here.pairs - 2):
                outs.wait()
                for k in range(dp - 1):
                    rows_copy(k).start()
        for peer in peers:
            for index in range(ctx):
                arrived(full_ref.at[peer[0], index], pass_recv.at[peer[0], index], peer)
        for peer in here.ctx_peers():
            others.wait(peer[1])
        for part in tokens:
            part.end()
        ids.end()
        for k, peer in enumerate(peers):
            arrived(rows_ref.at[peer[0]], rows_recv.at[peer[0]], peer)
            rows_copy(k).wait_send()
        outs.leave()
        slabs.leave()
        others.leave()
        for index in range(ctx):
            for k in range(dp - 1):
                passing(full_ref.at[here.d, index], k, index).wait_send()

    return call(
        kernel,
        0,
        (
            like((ctx,) + normed.shape),
            like((ctx,) + segments.shape, segments.dtype),
            like((dp,) + entry.shape),
            like(feed.shape),
            like((dp,) + outs.shape),
        ),
        (ANYWHERE,) * 5,
        [ANYWHERE] * 5,
        relay_sems + swap_sems * 2 + [pltpu.SemaphoreType.DMA((dp, ctx))] * 2
        + Move.scratch()
        + [pltpu.SemaphoreType.DMA((dp,))] * 2
        + relay_sems * len(cuts),
        normed,
        segments,
        entry,
        feed,
        outs,
    )


def sum_and_spread(left, right, blocks, ident):
    dp, ctx = lax.axis_size("dp"), lax.axis_size("ctx")
    rows, width = left.shape[0] // ctx, right.shape[1]
    count = len(blocks)

    def kernel(left_ref, right_ref, *refs):
        blocks_in, total, slots = refs[:count], refs[count], refs[count + 1 : 2 * count + 1]
        sems = refs[2 * count + 1 :]
        here = Here(dp, ctx)
        sums = SumTokens(here, left_ref, right_ref, False, total, *sems[:8])
        spreads = [
            Spread(here, block, slot, *sems[8 + 3 * i : 11 + 3 * i])
            for i, (block, slot) in enumerate(zip(blocks_in, slots))
        ]
        here.greet(here.dp_peers() + here.ctx_peers())
        for spread in spreads:
            spread.begin()
        sums.begin()
        sums.end()
        for spread in spreads:
            spread.end()
        sums.leave()

    return call(
        kernel,
        ident,
        (like((rows, width), jnp.float32), *[like((dp,) + block.shape) for block in blocks]),
        (IN_VMEM,) + (ANYWHERE,) * count,
        [IN_VMEM, IN_VMEM] + [ANYWHERE] * count,
        SumTokens.scratch(ctx // 2, rows, width) + Spread.scratch(dp) * count,
        left,
        right,
        *blocks,
    )


def sum_and_total(left, right, terms, ident):
    dp, ctx = lax.axis_size("dp"), lax.axis_size("ctx")
    rows, width = left.shape[0] // ctx, right.shape[0]
    count = len(terms)

    def kernel(left_ref, right_ref, *refs):
        terms_in, total, results = refs[:count], refs[count], refs[count + 1 : 2 * count + 1]
        sems = refs[2 * count + 1 :]
        here = Here(dp, ctx)
        sums = SumTokens(here, left_ref, right_ref, True, total, *sems[:8])
        totals = [
            Total(here, term, sems[8 + 3 * i], result, *sems[9 + 3 * i : 11 + 3 * i])
            for i, (term, result) in enumerate(zip(terms_in, results))
        ]
        here.greet(here.dp_peers() + here.ctx_peers())
        for part in totals:
            part.begin()
        sums.begin()
        for part in totals:
            part.end()
        sums.end()
        sums.leave()
        for part in totals:
            part.leave()

    scratch = SumTokens.scratch(ctx // 2, rows, width)
    for term in terms:
        scratch = scratch + Total.scratch(dp, term.shape[1:])
    return call(
        kernel,
        ident,
        (like((rows, width), jnp.float32), *[like(term.shape[1:]) for term in terms]),
        (IN_VMEM,) * (1 + count),
        [IN_VMEM] * (2 + count),
        scratch,
        left,
        right,
        *terms,
    )


def leave(grads, entry, source, residual_grad, gain, entry_terms, feed_sums, out_terms, small):
    dp, ctx = lax.axis_size("dp"), lax.axis_size("ctx")
    rows, width = source.shape
    slab = entry_terms.shape[2:]
    layout = entry_layout(ctx)
    hidden = feed_sums.shape[2] // (2 * dp)
    own_rows = slab[0]

    def kernel(
        grads_ref, entry_ref, source_ref, res_ref, gain_ref, terms_ref, feed_ref, outs_ref, small_ref,
        input_ref, attention_ref, mixer_ref, step_ref, gate_up_ref, out_sum, smalls_ref, gain_ref_out,
        slabs_ref, feeds_ref, gains_ref, normed_grad, *sems,
    ):
        here = Here(dp, ctx)
        peers = here.dp_peers()
        sums = SumTokens(here, grads_ref, entry_ref, True, normed_grad, *sems[0:8])
        feeds = Swap(here, feed_ref, feeds_ref, *sems[8:11])
        got, term_send, term_recv, mine, slab_send, slab_recv = sems[11:17]
        small_got, gain_got = sems[17:19]
        small_send, small_recv, gain_send, gain_recv = sems[19:23]
        last_send, last_recv, lastg_send, lastg_recv = sems[23:27]
        outs_got, out_half, out_landed = sems[27], sems[30], sems[31]
        outs = Total(here, outs_ref, outs_got, out_half, *sems[28:30])
        home = Move(
            here, out_half, here.owner(), out_landed, out_landed, here.user(), *sems[32:35]
        )
        here.greet(peers + here.ctx_peers(), here.user())
        order = [lax.rem(here.me + k, ctx) for k in list(range(1, ctx)) + [0]]

        def term_copy(k, index):
            return remote(
                terms_ref.at[peers[k][0], index],
                got.at[here.d, index],
                term_send.at[k, index],
                term_recv.at[here.d, index],
                peers[k],
            )

        for index in order:
            for k in range(dp - 1):
                term_copy(k, index).start()
        outs.begin()
        small_copies = []
        for k, peer in enumerate(peers):
            copy = remote(
                small_ref, small_got.at[here.d], small_send.at[k], small_recv.at[here.d], peer
            )
            copy.start()
            small_copies.append(copy)
        sums.begin()
        feeds.begin()

        def slab_copy(j):
            return remote(
                mine.at[order[j]], slabs_ref.at[here.me], slab_send.at[j], slab_recv.at[here.me],
                (here.d, order[j]),
            )

        for j, index in enumerate(order):
            total = terms_ref[here.d, index].astype(jnp.float32)
            for peer in peers:
                arrived(got.at[peer[0], index], term_recv.at[peer[0], index], peer)
                total = total + got[peer[0], index].astype(jnp.float32)
            total = total.astype(jnp.bfloat16)
            if j < ctx - 1:
                mine[index] = total
                slab_copy(j).start()
            else:
                slabs_ref[here.me] = total
        outs.end()
        home.begin()
        sums.end()
        x, grad = source_ref[...], normed_grad[...]
        scale = lax.rsqrt(jnp.mean(x * x, axis=-1, keepdims=True) + 1e-05)
        scaled = grad * gain_ref[...]
        inner = jnp.mean(x * scaled, axis=-1, keepdims=True)
        input_ref[...] = res_ref[...] + scale * scaled - x * (scale * scale * scale * inner)
        gain_got[here.d] = jnp.sum(grad * (x * scale), axis=0, keepdims=True)
        for k, peer in enumerate(peers):
            copy = remote(
                gain_got.at[here.d], gain_got.at[here.d], gain_send.at[k], gain_recv.at[here.d], peer
            )
            copy.start()
            small_copies.append(copy)
        small_got[here.d] = small_ref[...]
        for peer in peers:
            arrived(small_got.at[peer[0]], small_recv.at[peer[0]], peer)
        total = small_got[0]
        for d in range(1, dp):
            total = total + small_got[d]
        smalls_ref[here.me] = total
        last = []
        for k, peer in enumerate(here.ctx_peers()):
            copy = remote(
                smalls_ref.at[here.me], smalls_ref.at[here.me], last_send.at[k],
                last_recv.at[here.me], peer,
            )
            copy.start()
            last.append(copy)
        for peer in peers:
            arrived(gain_got.at[peer[0]], gain_recv.at[peer[0]], peer)
        total = gain_got[0]
        for d in range(1, dp):
            total = total + gain_got[d]
        gains_ref[here.me] = total
        for k, peer in enumerate(here.ctx_peers()):
            copy = remote(
                gains_ref.at[here.me], gains_ref.at[here.me], lastg_send.at[k],
                lastg_recv.at[here.me], peer,
            )
            copy.start()
            last.append(copy)
        for peer in here.ctx_peers():
            arrived(slabs_ref.at[peer[1]], slab_recv.at[peer[1]], peer)
            feeds.wait(peer[1])
            arrived(smalls_ref.at[peer[1]], last_recv.at[peer[1]], peer)
            arrived(gains_ref.at[peer[1]], lastg_recv.at[peer[1]], peer)
        feeds.leave()
        slabs = [slabs_ref[c].astype(jnp.float32) for c in range(ctx)]

        def columns(i, members=range(ctx)):
            at, size = offsets(layout)[i], layout[i]
            return [slabs[c][:, at : at + size] for c in members]

        share = ctx // HEADS_KV
        shared = [
            sum(columns(i, range(g * share, (g + 1) * share)))
            for i in (5, 6)
            for g in range(HEADS_KV)
        ]
        attention_ref[...] = jnp.concatenate(columns(4) + shared, axis=1)
        mixer_ref[:, :SSM_INNER] = jnp.concatenate(columns(3), axis=1)
        mixer_ref[:, SSM_INNER : 2 * SSM_INNER] = jnp.concatenate(columns(2), axis=1)
        mixer_ref[:, 2 * SSM_INNER : 2 * SSM_INNER + STATE] = sum(columns(0))
        mixer_ref[:, 2 * SSM_INNER + STATE :] = sum(columns(1))
        steps_at = offsets(layout)[7]
        for c in range(ctx):
            step_ref[c] = slabs[c][:, steps_at:]
        for m in range(2 * dp):
            part = [feeds_ref[c, :, m * hidden : (m + 1) * hidden] for c in range(ctx)]
            span = ctx * hidden
            gate_up_ref[:, m * span : (m + 1) * span] = jnp.concatenate(
                [piece.astype(jnp.float32) for piece in part], axis=1
            )
        total = gains_ref[0]
        for c in range(1, ctx):
            total = total + gains_ref[c]
        gain_ref_out[...] = total
        home.wait()
        out_sum[...] = out_landed[...].astype(jnp.float32)
        home.leave()
        outs.leave()
        sums.leave()
        for index in order:
            for k in range(dp - 1):
                term_copy(k, index).wait_send()
        for j in range(ctx - 1):
            slab_copy(j).wait_send()
        for copy in small_copies + last:
            copy.wait_send()

    dma = pltpu.SemaphoreType.DMA
    scratch = (
        [
            pltpu.VMEM((ctx,) + slab, jnp.bfloat16),
            pltpu.VMEM(feed_sums.shape, jnp.bfloat16),
            pltpu.VMEM((ctx, 1, width), jnp.float32),
            pltpu.VMEM((rows, width), jnp.float32),
        ]
        + SumTokens.scratch(ctx // 2, rows, width)
        + Swap.scratch(ctx)
        + [
            pltpu.VMEM((dp, ctx) + slab, jnp.bfloat16),
            dma((dp, ctx)),
            dma((dp, ctx)),
            pltpu.VMEM((ctx,) + slab, jnp.bfloat16),
            dma((ctx,)),
            dma((ctx,)),
        ]
        + [
            pltpu.VMEM((dp,) + small.shape, jnp.float32),
            pltpu.VMEM((dp, 1, width), jnp.float32),
        ]
        + [dma((dp,))] * 4
        + [dma((ctx,))] * 4
        + Total.scratch(dp, out_terms.shape[1:])
        + [pltpu.VMEM(out_terms.shape[1:], jnp.bfloat16)] * 2
        + Move.scratch()
    )
    return call(
        kernel,
        5,
        (
            like((rows, width), jnp.float32),
            like((own_rows, (HEADS_Q + 2 * HEADS_KV) * HEAD), jnp.float32),
            like((own_rows, 2 * SSM_INNER + 2 * STATE), jnp.float32),
            like((ctx, own_rows, layout[7] + layout[8]), jnp.float32),
            like((own_rows, ctx * feed_sums.shape[2]), jnp.float32),
            like(out_terms.shape[1:], jnp.float32),
            like((ctx,) + small.shape, jnp.float32),
            like((1, width), jnp.float32),
        ),
        (IN_VMEM,) * 8,
        [IN_VMEM] * 9,
        scratch,
        grads,
        entry,
        source,
        residual_grad,
        gain,
        entry_terms,
        feed_sums,
        out_terms,
        small,
    )


def rows_of(index, size):
    return pl.ds(pl.multiple_of(index * size, size), size)


def product(left, right, dims=((1,), (0,)), precision=None):
    return lax.dot_general(
        left, right, (dims, ((), ())), precision=precision, preferred_element_type=jnp.float32
    )


def sigma(values):
    return 1.0 / (1.0 + jnp.exp(-values))


def lower_of(size):
    down = lax.broadcasted_iota(jnp.int32, (size, size), 0)
    along = lax.broadcasted_iota(jnp.int32, (size, size), 1)
    return along <= down


def widen(columns, heads):
    shape = (columns.shape[0], SSM_HEAD)
    return jnp.concatenate(
        [jnp.broadcast_to(columns[:, h : h + 1], shape) for h in range(heads)], axis=1
    )


def head_sums(array, heads, width):
    sums = [
        jnp.sum(array[:, h * SSM_HEAD : (h + 1) * SSM_HEAD], axis=1, keepdims=True)
        for h in range(heads)
    ]
    return columns_of(sums, width)


def columns_of(columns, width):
    lane = lax.broadcasted_iota(jnp.int32, (columns[0].shape[0], width), 1)
    total = jnp.zeros(lane.shape, jnp.float32)
    for h, column in enumerate(columns):
        total = jnp.where(lane == h, column, total)
    return total


class Layout:
    def __init__(self, heads):
        self.inner = 2 * STATE
        self.conv = self.inner + heads * SSM_HEAD
        self.query = self.conv + heads * SSM_HEAD
        self.key = self.query + HEAD
        self.value = self.key + HEAD
        self.step = self.value + HEAD
        self.width = self.step + heads + (-(self.step + heads)) % 128
        self.steps = self.width - self.step


class Chunk:
    def __init__(self, lay, heads, p, a, seg_row, tap_ref, head_ref, shifted):
        size = p.shape[0]
        self.conv_in = p[:, : lay.conv]
        self.earlier = [jnp.where(a[:, k - 1 : k] > 0.0, shifted(k), 0.0) for k in (1, 2, 3)]
        pre = tap_ref[4:5, :] + tap_ref[3:4, :] * self.conv_in
        for k in (1, 2, 3):
            pre = pre + self.earlier[k - 1] * tap_ref[3 - k : 4 - k, :]
        self.sig = sigma(pre)
        self.pre = pre
        conv = pre * self.sig
        self.write, self.read = conv[:, :STATE], conv[:, STATE : 2 * STATE]
        self.inner = conv[:, lay.inner :]
        self.gate = p[:, lay.conv : lay.query]
        self.biased = p[:, lay.step :] + head_ref[1:2, :]
        self.steps = jnp.maximum(self.biased, 0.0) + jnp.log1p(jnp.exp(-jnp.abs(self.biased)))
        self.rates = self.steps * head_ref[0:1, :]
        lower = lower_of(size)
        self.ones = lower.astype(jnp.float32)
        run = product(self.ones, self.rates, precision=highest)
        run_row = product(self.rates, self.ones, ((0,), (1,)), precision=highest)
        allowed = lower & (a[:, 6:7] == seg_row)
        self.decay = [
            jnp.exp(jnp.where(allowed, run[:, h : h + 1] - run_row[h : h + 1, :], -1e30))
            for h in range(heads)
        ]
        self.carried = a[:, 7:8] * jnp.exp(run)
        self.tails = a[:, 8:9] * jnp.exp(run[size - 1 : size, :] - run)
        self.cross = product(self.read, self.write, ((1,), (1,)))
        self.scaled = self.inner * widen(self.steps, heads)
        self.carried_wide = widen(self.carried, heads)
        self.tails_wide = widen(self.tails, heads)
        self.skip_wide = widen(head_ref[2:3, :], heads)
        last = self.carried[size - 1 : size, :]
        head_row = lax.broadcasted_iota(jnp.int32, (heads * SSM_HEAD, 1), 0) // SSM_HEAD
        self.last = jnp.zeros((heads * SSM_HEAD, 1), jnp.float32)
        for h in range(heads):
            self.last = jnp.where(head_row == h, last[:, h : h + 1], self.last)


def attention_mask(seg_column, seg_row, at):
    rows, keys = seg_column.shape[0], seg_row.shape[1]
    down = lax.broadcasted_iota(jnp.int32, (rows, keys), 0) + at
    along = lax.broadcasted_iota(jnp.int32, (rows, keys), 1)
    return (along <= down) & (seg_column == seg_row)


def mix_forward(normed, entry, columns, seg_row, taps, head_rows, size):
    length = normed.shape[0]
    chunks = length // size
    heads = SSM_HEADS // lax.axis_size("ctx")
    lay = Layout(heads)
    wide = heads * SSM_HEAD
    block = 2 * size if chunks % 2 == 0 else size

    def kernel(
        n_ref, e_ref, col_ref, seg_ref, tap_ref, head_ref,
        mixed_ref, p_ref, y_ref, states_ref, top_ref, ext, state, heads_in,
    ):
        state[...] = jnp.zeros_like(state)
        ext[0:8, :] = jnp.zeros((8, lay.conv), jnp.float32)

        def chunk(j, _):
            at = rows_of(j, size)
            p = product(n_ref[at, :], e_ref[...])
            p_ref[at, :] = p
            ext[8:, :] = p[:, : lay.conv]
            part = Chunk(
                lay, heads, p, col_ref[at, :], seg_ref[:, at], tap_ref, head_ref,
                lambda k: ext[8 - k : 8 - k + size, :],
            )
            ext[0:8, :] = ext[size : size + 8, :]
            reached = state[...]
            states_ref[j] = reached
            local = [
                product(part.decay[h] * part.cross, part.scaled[:, h * SSM_HEAD : (h + 1) * SSM_HEAD])
                for h in range(heads)
            ]
            y = (
                jnp.concatenate(local, axis=1)
                + part.skip_wide * part.inner
                + part.carried_wide * product(part.read, reached, ((1,), (1,)))
            )
            y_ref[at, :] = y
            gated = y * part.gate * sigma(part.gate)
            state[...] = part.last * reached + product(
                part.tails_wide * part.scaled, part.write, ((0,), (0,))
            )
            heads_in[at, :] = p[:, lay.query : lay.query + 3 * HEAD].astype(jnp.bfloat16)
            mixed_ref[at, HEAD:] = gated.astype(jnp.bfloat16)
            return 0

        lax.fori_loop(0, chunks, chunk, 0)
        for b in range(length // block):
            at, keys = slice(b * block, (b + 1) * block), (b + 1) * block
            scores = product(
                heads_in[at, :HEAD], heads_in[:keys, HEAD : 2 * HEAD], ((1,), (1,))
            ) * (HEAD**-0.5)
            allowed = attention_mask(col_ref[at, 6:7], seg_ref[:, :keys], b * block)
            scores = jnp.where(allowed, scores, -1e30)
            top = jnp.max(scores, axis=1, keepdims=True)
            terms = jnp.where(allowed, jnp.exp(scores - top), 0.0)
            total = jnp.sum(terms, axis=1, keepdims=True)
            top_ref[at, :] = top + jnp.log(total)
            probs = (terms * (1.0 / total)).astype(jnp.bfloat16)
            mixed_ref[at, :HEAD] = product(probs, heads_in[:keys, 2 * HEAD :]).astype(jnp.bfloat16)

    return pl.pallas_call(
        kernel,
        out_shape=(
            like((length, HEAD + wide)),
            like((length, lay.width), jnp.float32),
            like((length, wide), jnp.float32),
            like((chunks, wide, STATE), jnp.float32),
            like((length, 1), jnp.float32),
        ),
        in_specs=[IN_VMEM] * 6,
        out_specs=(IN_VMEM,) * 5,
        scratch_shapes=[
            pltpu.VMEM((size + 8, lay.conv), jnp.float32),
            pltpu.VMEM((wide, STATE), jnp.float32),
            pltpu.VMEM((length, 3 * HEAD), jnp.bfloat16),
        ],
        compiler_params=pltpu.CompilerParams(vmem_limit_bytes=48 * 2**20),
    )(normed, entry, columns, seg_row, taps, head_rows)


def mix_backward(
    residual_half, out_rows, mixed_out, p, y, states, log_total, columns, seg_row, taps, head_rows, size
):
    length = p.shape[0]
    dp = lax.axis_size("dp")
    chunks = length // size
    heads = SSM_HEADS // lax.axis_size("ctx")
    lay = Layout(heads)
    wide = heads * SSM_HEAD
    block = 2 * size if chunks % 2 == 0 else size

    def kernel(
        r_ref, o_ref, mixed_ref, p_ref, y_ref, states_ref, top_ref, col_ref, seg_ref, tap_ref, head_ref,
        g_ref, tap_sum, head_sum, outs_ref, ext, ahead, out_grad, step_grad, state, heads_in, key_grad, value_grad,
    ):
        state[...] = jnp.zeros_like(state)
        ahead[size:, :] = jnp.zeros((8, lay.conv), jnp.float32)
        tap_sum[...] = jnp.zeros_like(tap_sum)
        head_sum[...] = jnp.zeros_like(head_sum)

        def chunk(step, _):
            j = chunks - 1 - step
            at = rows_of(j, size)
            p, a = p_ref[at, :], col_ref[at, :]
            ext[8:, :] = p[:, : lay.conv]
            ext[0:8, :] = p_ref[pl.ds(pl.multiple_of(jnp.maximum(j * size - 8, 0), 8), 8), : lay.conv]
            part = Chunk(
                lay, heads, p, a, seg_ref[:, at], tap_ref, head_ref,
                lambda k: ext[8 - k : 8 - k + size, :],
            )
            grads = product(r_ref[at, :], o_ref[...], ((1,), (1,)))
            out_grad[at, :] = grads[:, :HEAD].astype(jnp.bfloat16)
            gated_grad = grads[:, HEAD:]
            y = y_ref[at, :]
            gate_sig = sigma(part.gate)
            gate_grad = gated_grad * y * gate_sig * (1.0 + part.gate * (1.0 - gate_sig))
            dy = gated_grad * part.gate * gate_sig
            later = state[...]
            before = states_ref[j]
            reached = part.carried_wide * product(part.read, before, ((1,), (1,)))
            from_later = part.tails_wide * product(part.write, later, ((1,), (1,)))
            cross_grad = jnp.zeros((size, size), jnp.float32)
            local, row_sums, column_sums = [], [], []
            for h in range(heads):
                cut = slice(h * SSM_HEAD, (h + 1) * SSM_HEAD)
                mixing = part.decay[h] * part.cross
                mixing_grad = product(dy[:, cut], part.scaled[:, cut], ((1,), (1,)))
                local.append(product(mixing, dy[:, cut], ((0,), (0,))))
                cross_grad = cross_grad + part.decay[h] * mixing_grad
                weight = mixing * mixing_grad
                row_sums.append(jnp.sum(weight, axis=1, keepdims=True))
                column_sums.append(jnp.sum(weight, axis=0, keepdims=True))
            scaled_grad = jnp.concatenate(local, axis=1) + from_later
            carried_dy = part.carried_wide * dy
            tail_terms = part.tails_wide * part.scaled
            read_grad = product(cross_grad, part.write) + product(carried_dy, before)
            write_grad = product(cross_grad, part.read, ((0,), (0,))) + product(tail_terms, later)
            inner_grad = part.skip_wide * dy + widen(part.steps, heads) * scaled_grad
            tail_sums = head_sums(part.scaled * from_later, heads, lay.steps)
            run_grad = (
                columns_of(row_sums, lay.steps)
                + head_sums(dy * reached, heads, lay.steps)
                - tail_sums
            )
            ends = later * before * part.last
            end_sums = [
                jnp.sum(
                    jnp.sum(ends[h * SSM_HEAD : (h + 1) * SSM_HEAD, :], axis=1, keepdims=True),
                    axis=0,
                    keepdims=True,
                )
                for h in range(heads)
            ]
            final = columns_of(end_sums, lay.steps) + jnp.sum(tail_sums, axis=0, keepdims=True)
            column_rows = jnp.concatenate(
                column_sums + [jnp.zeros((lay.steps - heads, size), jnp.float32)], axis=0
            )
            rate_grad = (
                product(part.ones, run_grad, ((0,), (0,)), precision=highest)
                - product(part.ones, column_rows, ((0,), (1,)), precision=highest)
                + final
            )
            steps_grad = (
                head_sums(scaled_grad * part.inner, heads, lay.steps) + rate_grad * head_ref[0:1, :]
            )
            raw_grad = steps_grad * sigma(part.biased)
            step_grad[at, :] = raw_grad
            head_sum[0:1, :] += jnp.sum(rate_grad * part.rates, axis=0, keepdims=True)
            head_sum[1:2, :] += jnp.sum(raw_grad, axis=0, keepdims=True)
            head_sum[2:3, :] += jnp.sum(
                head_sums(dy * part.inner, heads, lay.steps), axis=0, keepdims=True
            )
            state[...] = part.last * later + product(carried_dy, part.read, ((0,), (0,)))
            converted_grad = jnp.concatenate([write_grad, read_grad, inner_grad], axis=1)
            pre_grad = converted_grad * part.sig * (1.0 + part.pre * (1.0 - part.sig))
            ahead[:size, :] = pre_grad
            conv_grad = tap_ref[3:4, :] * pre_grad
            tap_sum[3:4, :] += jnp.sum(pre_grad * part.conv_in, axis=0, keepdims=True)
            tap_sum[4:5, :] += jnp.sum(pre_grad, axis=0, keepdims=True)
            for k in (1, 2, 3):
                conv_grad = (
                    conv_grad
                    + jnp.where(a[:, 2 + k : 3 + k] > 0.0, ahead[k : k + size, :], 0.0)
                    * tap_ref[3 - k : 4 - k, :]
                )
                tap_sum[3 - k : 4 - k, :] += jnp.sum(
                    pre_grad * part.earlier[k - 1], axis=0, keepdims=True
                )
            ahead[size:, :] = ahead[0:8, :]
            g_ref[at, : lay.query] = jnp.concatenate([conv_grad, gate_grad], axis=1).astype(
                jnp.bfloat16
            )
            heads_in[at, :] = p[:, lay.query : lay.step].astype(jnp.bfloat16)
            return 0

        lax.fori_loop(0, chunks, chunk, 0)
        key_grad[...] = jnp.zeros_like(key_grad)
        value_grad[...] = jnp.zeros_like(value_grad)
        query_grads = []
        for b in range(length // block):
            at, keys = slice(b * block, (b + 1) * block), (b + 1) * block
            queries, grad = heads_in[at, :HEAD], out_grad[at, :]
            key_part, value_part = heads_in[:keys, HEAD : 2 * HEAD], heads_in[:keys, 2 * HEAD :]
            scores = product(queries, key_part, ((1,), (1,))) * (HEAD**-0.5)
            allowed = attention_mask(col_ref[at, 6:7], seg_ref[:, :keys], b * block)
            probs = jnp.where(allowed, jnp.exp(scores - top_ref[at, :]), 0.0)
            deltas = jnp.sum(
                grad.astype(jnp.float32) * mixed_ref[at, :HEAD].astype(jnp.float32),
                axis=1,
                keepdims=True,
            )
            prob_grad = product(grad, value_part, ((1,), (1,)))
            score_grad = (probs * (prob_grad - deltas)).astype(jnp.bfloat16)
            query_grads.append(product(score_grad, key_part) * (HEAD**-0.5))
            key_grad[:keys, :] += product(score_grad, queries, ((0,), (0,))) * (HEAD**-0.5)
            value_grad[:keys, :] += product(probs.astype(jnp.bfloat16), grad, ((0,), (0,)))
        for b, query_grad in enumerate(query_grads):
            at = slice(b * block, (b + 1) * block)
            g_ref[at, lay.query :] = jnp.concatenate(
                [query_grad, key_grad[at, :], value_grad[at, :], step_grad[at, :]], axis=1
            ).astype(jnp.bfloat16)
        terms = product(mixed_ref[...], r_ref[...], ((0,), (0,))).astype(jnp.bfloat16)
        few, many = HEAD // dp, wide // dp
        for j in range(dp):
            outs_ref[j, :few, :] = terms[j * few : (j + 1) * few, :]
            outs_ref[j, few:, :] = terms[HEAD + j * many : HEAD + (j + 1) * many, :]

    f32 = jnp.float32
    return pl.pallas_call(
        kernel,
        out_shape=(
            like((length, lay.width)),
            like((8, lay.conv), f32),
            like((8, lay.steps), f32),
            like((dp, out_rows.shape[0] // dp, out_rows.shape[1])),
        ),
        in_specs=[IN_VMEM] * 11,
        out_specs=(IN_VMEM,) * 4,
        scratch_shapes=[
            pltpu.VMEM((size + 8, lay.conv), f32),
            pltpu.VMEM((size + 8, lay.conv), f32),
            pltpu.VMEM((length, HEAD), jnp.bfloat16),
            pltpu.VMEM((length, lay.steps), f32),
            pltpu.VMEM((wide, STATE), f32),
            pltpu.VMEM((length, 3 * HEAD), jnp.bfloat16),
            pltpu.VMEM((length, HEAD), f32),
            pltpu.VMEM((length, HEAD), f32),
        ],
        compiler_params=pltpu.CompilerParams(vmem_limit_bytes=56 * 2**20),
    )(residual_half, out_rows, mixed_out, p, y, states, log_total, columns, seg_row, taps, head_rows)


def across(left, right):
    return jnp.dot(left.T, right, preferred_element_type=jnp.float32).astype(jnp.bfloat16)


def split_local(
    block_input,
    segment_ids,
    out_cotangent,
    attention_in,
    mixer_in,
    step_in,
    attention_out,
    mixer_out,
    gate_up,
    down_weight,
    gain_mixing,
    gain_feed,
    decay_log,
    step_bias,
    skip_gain,
    conv_weight,
    conv_bias,
):
    ctx, dp = lax.axis_size("ctx"), lax.axis_size("dp")
    mine = lax.axis_index("ctx")
    tok_count, width = block_input.shape[1:]
    length = tok_count * ctx
    heads = SSM_HEADS // ctx
    rows = attention_in.shape[0]
    hidden = down_weight.shape[0]
    slabs = entry_slabs(attention_in, mixer_in, step_in, ctx)
    gate_slabs = gate_up.reshape(rows, 2, dp, ctx, hidden).transpose(3, 0, 1, 2, 4)
    gate_slabs = gate_slabs.reshape(ctx, rows, 2 * dp * hidden)
    own_attention = attention_out.shape[0]

    source = block_input.reshape(tok_count, width).astype(jnp.float32)
    cotangent = out_cotangent.reshape(tok_count, width)
    normed_own = rms_scale(source, gain_mixing).astype(jnp.bfloat16)
    outs = jnp.concatenate([attention_out, mixer_out], axis=0)
    normed, segments, entry, feed_slabs, outs = enter(
        normed_own, segment_ids, slabs, gate_slabs, outs
    )
    normed, segments = normed.reshape(length, width), segments.reshape(length)
    entry = entry.reshape(dp * ctx * rows, -1)
    late_cotangent, _ = lax.optimization_barrier((cotangent, segments))
    cotangents = lax.all_gather(late_cotangent, "ctx", axis=0, tiled=True)
    out_rows = jnp.concatenate(
        [outs[:, :own_attention].reshape(-1, width), outs[:, own_attention:].reshape(-1, width)],
        axis=0,
    )

    own = lambda array, at, size: lax.dynamic_slice_in_dim(array, at + mine * size, size, axis=-1)
    conv_own = lambda array: jnp.concatenate(
        [array[:, SSM_INNER:], own(array, 0, heads * SSM_HEAD)], axis=-1
    )
    taps = jnp.pad(conv_own(jnp.concatenate([conv_weight, conv_bias[None]], axis=0)), ((0, 3), (0, 0)))
    head_rows = jnp.stack(
        [own(part, 0, heads) for part in (-jnp.exp(decay_log), step_bias, skip_gain)]
    )
    head_rows = jnp.pad(head_rows, ((0, 5), (0, Layout(heads).steps - heads)))
    keeps = []
    for offset in (1, 2, 3):
        earlier = jnp.concatenate([jnp.full((offset,), -1, segments.dtype), segments[:-offset]])
        keeps.append(earlier == segments)
    nexts = [jnp.pad(keep[k + 1 :], (0, k + 1)) for k, keep in enumerate(keeps)]
    chunk_last = segments.reshape(ctx, tok_count)[:, -1]
    spread = lambda ids: jnp.repeat(ids, tok_count) == segments
    opens = spread(jnp.concatenate([jnp.full((1,), -1, segments.dtype), chunk_last[:-1]]))
    marks = keeps + nexts + [segments, opens, spread(chunk_last)]
    columns = jnp.stack([mark.astype(jnp.float32) for mark in marks], axis=1)
    columns = jnp.pad(columns, ((0, 0), (0, 16 - len(marks))))
    seg_row = segments.astype(jnp.float32).reshape(1, length)
    mixed_out, entry_product, scanned, states, log_total = mix_forward(
        normed, entry, columns, seg_row, taps, head_rows, tok_count
    )
    mixing_out, feed_in, feed_out = sum_and_spread(
        mixed_out, out_rows, (feed_slabs.reshape(ctx * rows, -1), down_weight), 1
    )
    feed_in = feed_in.reshape(dp * ctx * rows, -1)
    feed_out = feed_out.reshape(dp * hidden, width)
    residual = source + mixing_out

    normed_two_own, pull_two = jax.vjp(rms_scale, residual, gain_feed)
    normed_two = gather_tokens(normed_two_own.astype(jnp.bfloat16), 2)
    gate_values = jnp.dot(normed_two, feed_in, preferred_element_type=jnp.float32)
    gate_in, up_in = gate_values[:, : dp * hidden], gate_values[:, dp * hidden :]
    active = (jax.nn.silu(gate_in) * up_in).astype(jnp.bfloat16)
    output_terms = jnp.dot(active, feed_out, preferred_element_type=jnp.float32).astype(jnp.bfloat16)
    active_grad = jnp.dot(cotangents, feed_out.T, preferred_element_type=jnp.float32)
    gate_grad = jnp.concatenate(
        [active_grad * up_in * silu_slope(gate_in), active_grad * jax.nn.silu(gate_in)], axis=1
    ).astype(jnp.bfloat16)
    normed_two_grad, feed_sums, grad_feed_out = sum_and_total(
        gate_grad,
        feed_in,
        (
            across(normed_two, gate_grad).reshape(dp, ctx * rows, -1),
            across(active, cotangents).reshape(dp, hidden, width),
        ),
        3,
    )
    residual_part, grad_gain_feed = pull_two(normed_two_grad)
    residual_grad = cotangent.astype(jnp.float32) + residual_part
    residual_half = gather_tokens(residual_grad.astype(jnp.bfloat16), 4)
    late_terms, _ = lax.optimization_barrier((output_terms, residual_half))
    output_sum = lax.psum_scatter(late_terms, "ctx", scatter_dimension=0, tiled=True)
    output = (residual + output_sum.astype(jnp.float32)).astype(jnp.bfloat16)
    grads, tap_grads, head_grads, out_terms = mix_backward(
        residual_half,
        out_rows,
        mixed_out,
        entry_product,
        scanned,
        states,
        log_total,
        columns,
        seg_row,
        taps,
        head_rows,
        tok_count,
    )
    own_small = jnp.concatenate(
        [grad_gain_feed, tap_grads[:5].reshape(-1), head_grads[:3, :heads].reshape(-1)], axis=0
    )
    own_small = jnp.pad(own_small, (0, -own_small.shape[0] % 1024)).reshape(-1, 128)
    input_grad, grad_attention_in, grad_mixer_in, step_slabs, grad_gate_up, grad_outs, smalls, gains = leave(
        grads,
        entry,
        source,
        residual_grad,
        gain_mixing.reshape(1, width),
        across(normed, grads).reshape(dp, ctx, rows, -1),
        feed_sums.reshape(ctx, rows, -1),
        out_terms,
        own_small,
    )
    grad_step_in = step_slabs[:, :, :heads].transpose(1, 0, 2).reshape(rows, SSM_HEADS)
    smalls = smalls.reshape(ctx, -1)
    tap_width = heads * SSM_HEAD + 2 * STATE
    tap_all = smalls[:, width : width + 5 * tap_width].reshape(ctx, 5, tap_width)
    tap_sums = jnp.concatenate(
        [
            tap_all[:, :, 2 * STATE :].transpose(1, 0, 2).reshape(5, SSM_INNER),
            jnp.sum(tap_all[:, :, : 2 * STATE], axis=0),
        ],
        axis=1,
    )
    head_all = smalls[:, width + 5 * tap_width :][:, : 3 * heads].reshape(ctx, 3, heads)
    head_sums = head_all.transpose(1, 0, 2).reshape(3, SSM_HEADS)
    return (
        output.reshape(block_input.shape),
        input_grad.reshape(block_input.shape),
        grad_attention_in,
        grad_mixer_in,
        grad_step_in,
        grad_outs[:own_attention],
        grad_outs[own_attention:],
        grad_gate_up,
        grad_feed_out.astype(jnp.float32),
        gains.reshape(width),
        jnp.sum(smalls[:, :width], axis=0),
        head_sums[0],
        head_sums[1],
        head_sums[2],
        tap_sums[:4],
        tap_sums[4],
    )


def solution(mesh):
    in_specs = (
        P("dp", "ctx", None),
        P("dp", "ctx"),
        P("dp", "ctx", None),
        P(("dp", "ctx"), None),
        P(("dp", "ctx"), None),
        P(("dp", "ctx"), None),
        P(("dp", "ctx"), None),
        P(("dp", "ctx"), None),
        P(("dp", "ctx"), None),
        P(("dp", "ctx"), None),
        P(),
        P(),
        P(),
        P(),
        P(),
        P(),
        P(),
    )
    out_specs = (
        P("dp", "ctx", None),
        P("dp", "ctx", None),
        P(("dp", "ctx"), None),
        P(("dp", "ctx"), None),
        P(("dp", "ctx"), None),
        P(("dp", "ctx"), None),
        P(("dp", "ctx"), None),
        P(("dp", "ctx"), None),
        P(("dp", "ctx"), None),
        P(),
        P(),
        P(),
        P(),
        P(),
        P(),
        P(),
    )
    sequences = mesh.shape["dp"]

    def choose(*arrays):
        heads = split_heads(mesh.shape["ctx"]) and arrays[0].shape[0] == sequences
        body = split_local if heads else local
        mapped = jax.shard_map(
            body, mesh=mesh, in_specs=in_specs, out_specs=out_specs, check_vma=False
        )
        return mapped(*arrays)

    return choose
```

```python
import functools
import math

import jax
import jax.numpy as jnp
from jax import lax
from jax.experimental import pallas as pl
from jax.experimental.pallas import tpu as pltpu
from jax.sharding import PartitionSpec as P

FF = 2048
HEADS_Q = 8
HEADS_KV = 2
HEAD = 64
SSM_HEADS = 24
SSM_HEAD = 64
STATE = 128
SSM_INNER = 1536


highest = lax.Precision.HIGHEST


def from_behind(block, axis, distance):
    devices = range(lax.axis_size(axis))
    route = [(i - distance, i) for i in devices if i - distance in devices]
    return lax.ppermute(block, axis, route)


def carried_in(value, axis, join, neutral, backward):
    count, mine = (lax.axis_size(axis), lax.axis_index(axis))
    pieces = jax.tree.map(lambda part: lax.all_gather(part, axis), value)
    if backward:
        pieces = jax.tree.map(lambda part: part[::-1], pieces)
        mine = count - 1 - mine
    so_far = jax.tree.map(
        lambda part, zero: jnp.full_like(part, 0) + jnp.asarray(zero, part.dtype), value, neutral
    )

    def hop(position, so_far):
        longer = join(so_far, jax.tree.map(lambda part: part[position], pieces))
        return jax.tree.map(lambda new, old: jnp.where(position < mine, new, old), longer, so_far)

    return lax.fori_loop(0, count - 1, hop, so_far)


def carried_by_heads(decays, state, backward):
    count, mine = (lax.axis_size("ctx"), lax.axis_index("ctx"))
    seq_count, heads = decays.shape[1:]
    share = heads // count
    own = lax.dynamic_slice_in_dim(decays, mine * share, share, axis=2)
    pieces = lax.all_to_all(state, "ctx", split_axis=1, concat_axis=0, tiled=True)
    pieces = pieces.reshape((count, seq_count, share) + state.shape[2:])
    order = list(range(count))[::-1] if backward else list(range(count))
    so_far = jnp.zeros_like(pieces[0])
    reached = [None] * count
    for position in order:
        reached[position] = so_far
        so_far = own[position][:, :, None, None] * so_far + pieces[position]
    return lax.all_to_all(
        jnp.concatenate(reached, axis=0), "ctx", split_axis=0, concat_axis=1, tiled=True
    )


def fold_shape(owned, rows, width):
    step = math.gcd(owned, rows)
    return (step, owned // step, rows // step, width // (rows // step))


def fold_rows(array, owned, rows):
    step, across, down, part = fold_shape(owned, rows, array.shape[1])
    blocks = array.reshape(-1, owned, array.shape[1])
    columns = [
        jnp.concatenate(
            [blocks[:, i * step : (i + 1) * step, j * part : (j + 1) * part] for j in range(down)],
            axis=1,
        )
        for i in range(across)
    ]
    return jnp.concatenate(columns, axis=2).reshape(-1, across * part)


def unfold_rows(array, owned, rows, width):
    step, across, down, part = fold_shape(owned, rows, width)
    blocks = array.reshape(-1, rows, across * part)
    lines = [
        jnp.concatenate(
            [blocks[:, j * step : (j + 1) * step, i * part : (i + 1) * part] for j in range(down)],
            axis=2,
        )
        for i in range(across)
    ]
    return jnp.concatenate(lines, axis=1).reshape(-1, width)


def pad_columns(array):
    return jnp.pad(array, ((0, 0), (0, -array.shape[1] % 128)))


def cut_columns(array, widths):
    pieces, at = ([], 0)
    for width in widths:
        pieces.append(array[:, at : at + width])
        at += width
    return pieces


def rms_scale(values, gain):
    return values * lax.rsqrt(jnp.mean(values * values, axis=-1, keepdims=True) + 1e-05) * gain


def silu_slope(values):
    sigma = jax.nn.sigmoid(values)
    return sigma * (1.0 + values * (1.0 - sigma))


def ssd_local(
    inner, write_map, read_map, step_raw, decay_log, step_bias, skip_gain, starts, segments
):
    step = jax.nn.softplus(step_raw + step_bias)
    rates = step * -jnp.exp(decay_log)
    places = jnp.arange(segments.shape[0])
    lower = places[None, :] <= places[:, None]
    running = jnp.dot(lower.astype(jnp.float32), rates, precision=highest)
    same = (segments[:, None] == segments[None, :]) & lower
    spans = jnp.where(same[None], running.T[:, :, None] - running.T[:, None, :], -1e30)
    intersection = jnp.dot(read_map, write_map.T, precision=highest)
    mixing = jnp.exp(spans) * intersection[None] * step.T[:, None, :]
    result = (
        jnp.einsum("hts,shp->thp", mixing, inner, precision=highest)
        + skip_gain[None, :, None] * inner
    )
    before = jnp.sum((lower & starts[None, :]).astype(jnp.int32), axis=1) == 0
    carried = jnp.where(before[:, None], jnp.exp(running), 0.0)
    tails = jnp.where(
        (segments == segments[-1])[:, None], jnp.exp(running[-1][None, :] - running), 0.0
    )
    state = jnp.einsum("sh,shp,sn->hpn", tails * step, inner, write_map, precision=highest)
    return (result, state, carried[-1], carried)


def add_state(result, carried, read_map, state_in):
    return result + carried[:, :, None] * jnp.einsum(
        "hpn,tn->thp", state_in, read_map, precision=highest
    )


def ssd_block(
    inner,
    write_map,
    read_map,
    step_raw,
    decay_log,
    step_bias,
    skip_gain,
    starts,
    segments,
    state_in,
):
    result, state, decay_total, carried = ssd_local(
        inner, write_map, read_map, step_raw, decay_log, step_bias, skip_gain, starts, segments
    )
    return (
        add_state(result, carried, read_map, state_in),
        decay_total[:, None, None] * state_in + state,
    )


def chain(earlier, later):
    return (earlier[0] * later[0], later[0][:, :, None, None] * earlier[1] + later[1])


def over_blocks(step, start, items):
    if items[2].shape[0] > 1:
        return lax.scan(step, start, items)
    carry, result = step(start, (items[0][0], items[1][0], 0))
    return (carry, None if result is None else result[None])


def group_queries(flat, seq_count, tok_count):
    groups = HEADS_Q // HEADS_KV
    shaped = flat.reshape(seq_count, tok_count, HEADS_KV, groups, HEAD)
    return shaped.transpose(0, 2, 3, 1, 4).reshape(seq_count, HEADS_KV, groups * tok_count, HEAD)


def ungroup(grouped, seq_count, tok_count):
    groups = HEADS_Q // HEADS_KV
    shaped = grouped.reshape(seq_count, HEADS_KV, groups, tok_count, HEAD)
    return shaped.transpose(0, 3, 1, 2, 4).reshape(seq_count * tok_count, HEADS_Q * HEAD)


def local(
    block_input,
    segment_ids,
    out_cotangent,
    attention_in,
    mixer_in,
    step_in,
    attention_out,
    mixer_out,
    gate_up,
    down_weight,
    gain_mixing,
    gain_feed,
    decay_log,
    step_bias,
    skip_gain,
    conv_weight,
    conv_bias,
):
    seq_count, tok_count, width = block_input.shape
    row_count = seq_count * tok_count
    length = tok_count * lax.axis_size("ctx")
    block = length if length <= 1024 else 512
    blocks = length // block
    groups = HEADS_Q // HEADS_KV
    query_width = HEADS_Q * HEAD
    key_width = HEADS_KV * HEAD
    score_scale = HEAD ** (-0.5)
    query_rows = groups * tok_count
    first = lax.axis_index("ctx") * tok_count
    own_rows = attention_in.shape[0]
    axes = ("dp", "ctx")
    entry = jnp.concatenate([attention_in, mixer_in, pad_columns(step_in)], axis=1)
    full_attention_in, full_mixer_in, full_step_in = cut_columns(
        lax.all_gather(entry, axes, axis=0, tiled=True),
        (attention_in.shape[1], mixer_in.shape[1], step_in.shape[1]),
    )
    tall = (attention_out, mixer_out, down_weight)
    folded = [fold_rows(weight, weight.shape[0], own_rows) for weight in tall]
    rest = lax.all_gather(
        jnp.concatenate(folded + [gate_up], axis=1), axes, axis=0, tiled=True
    )
    rest = cut_columns(rest, [weight.shape[1] for weight in folded] + [gate_up.shape[1]])
    full_attention_out, full_mixer_out, full_down = (
        unfold_rows(part, weight.shape[0], own_rows, width) for part, weight in zip(rest, tall)
    )
    full_gate_up = rest[3]
    source = block_input.reshape(row_count, width).astype(jnp.float32)
    normed = rms_scale(source, gain_mixing).astype(jnp.bfloat16)
    projected = jnp.dot(normed, full_attention_in, preferred_element_type=jnp.float32).astype(
        jnp.bfloat16
    )
    mixed_in = jnp.dot(normed, full_mixer_in, preferred_element_type=jnp.float32)
    step_raw = jnp.dot(normed, full_step_in, preferred_element_type=jnp.float32).reshape(
        seq_count, tok_count, SSM_HEADS
    )
    queries = group_queries(projected[:, :query_width], seq_count, tok_count)
    local_keys = (
        projected[:, query_width:].reshape(seq_count, tok_count, 2 * key_width).transpose(1, 0, 2)
    )
    local_segments = segment_ids.T
    keys_all, segments_all = (
        lax.all_gather(local_keys, "ctx", axis=0, tiled=True),
        lax.all_gather(local_segments, "ctx", axis=0, tiled=True),
    )
    query_pos = first + jnp.arange(query_rows) % tok_count
    query_segments = jnp.tile(segment_ids, (1, groups))
    segment_blocks = segments_all.reshape(blocks, block, seq_count)
    block_ids = jnp.arange(blocks)

    def scores_of(key_block, seg_block, block_id):
        keys = key_block[:, :, :key_width].reshape(block, seq_count, HEADS_KV, HEAD)
        scores = (
            jnp.einsum("sgrd,ksgd->sgrk", queries, keys, preferred_element_type=jnp.float32)
            * score_scale
        )
        key_pos = block_id * block + jnp.arange(block)
        allowed = (key_pos[None, None, None, :] <= query_pos[None, None, :, None]) & (
            seg_block.T[:, None, None, :] == query_segments[:, None, :, None]
        )
        return (scores, allowed)

    key_blocks = keys_all.reshape(blocks, block, seq_count, 2 * key_width)

    def gather_stats(carry, item):
        top, total = carry
        scores, allowed = scores_of(item[0], item[1], item[2])
        masked = jnp.where(allowed, scores, -1e30)
        new_top = jnp.maximum(top, jnp.max(masked, axis=-1))
        total = total * jnp.exp(top - new_top) + jnp.sum(
            jnp.where(allowed, jnp.exp(masked - new_top[..., None]), 0.0), axis=-1
        )
        return ((new_top, total), None)

    start_top = jnp.full((seq_count, HEADS_KV, query_rows), -1e30, jnp.float32)
    (top, total), _ = over_blocks(
        gather_stats,
        (start_top, jnp.zeros_like(start_top)),
        (key_blocks, segment_blocks, block_ids),
    )
    log_total = top + jnp.log(total)

    def weigh_values(accum, item):
        scores, allowed = scores_of(item[0], item[1], item[2])
        values = item[0][:, :, key_width:].reshape(block, seq_count, HEADS_KV, HEAD)
        probs = jnp.where(allowed, jnp.exp(scores - log_total[..., None]), 0.0).astype(jnp.bfloat16)
        return (
            accum
            + jnp.einsum("sgrk,ksgd->sgrd", probs, values, preferred_element_type=jnp.float32),
            None,
        )

    attended, _ = over_blocks(
        weigh_values, jnp.zeros(queries.shape, jnp.float32), (key_blocks, segment_blocks, block_ids)
    )
    attended = attended.astype(jnp.bfloat16)
    attended_flat = ungroup(attended, seq_count, tok_count)
    gate_part = mixed_in[:, :SSM_INNER]
    conv_width = mixed_in.shape[1] - SSM_INNER
    conv_in = mixed_in[:, SSM_INNER:].reshape(seq_count, tok_count, conv_width)
    positions = first + jnp.arange(tok_count)
    before_rows = from_behind(conv_in[:, tok_count - 3 :, :], "ctx", 1)
    extended = jnp.concatenate([before_rows, conv_in], axis=1)
    pre = conv_bias + conv_weight[3] * conv_in
    keep_masks = []
    for offset in (1, 2, 3):
        earlier_ids = segments_all[jnp.maximum(positions - offset, 0)].T
        keep_mask = (positions >= offset)[None, :] & (earlier_ids == segment_ids)
        keep_masks.append(keep_mask)
        pre = (
            pre
            + jnp.where(keep_mask[..., None], extended[:, 3 - offset : 3 - offset + tok_count], 0.0)
            * conv_weight[3 - offset]
        )
    converted = jax.nn.silu(pre)
    inner = converted[..., :SSM_INNER].reshape(seq_count, tok_count, SSM_HEADS, SSM_HEAD)
    write_map = converted[..., SSM_INNER : SSM_INNER + STATE]
    read_map = converted[..., SSM_INNER + STATE :]
    starts = (positions == 0)[None, :] | jnp.logical_not(keep_masks[0])
    local_map = jax.vmap(ssd_local, in_axes=(0, 0, 0, 0, None, None, None, 0, 0))
    partial_out, partial_state, decay_total, carried = local_map(
        inner, write_map, read_map, step_raw, decay_log, step_bias, skip_gain, starts, segment_ids
    )
    by_heads = SSM_HEADS % lax.axis_size("ctx") == 0
    if by_heads:
        decays = lax.all_gather(decay_total, "ctx")
        state_in = carried_by_heads(decays, partial_state, False)
    else:
        unit = (jnp.ones_like(decay_total), jnp.zeros_like(partial_state))
        state_in = carried_in((decay_total, partial_state), "ctx", chain, unit, False)[1]
    scanned = jax.vmap(add_state)(partial_out, carried, read_map, state_in)
    flat_scan = scanned.reshape(row_count, SSM_INNER)
    gated = (flat_scan * jax.nn.silu(gate_part)).astype(jnp.bfloat16)
    residual = (
        source
        + jnp.dot(attended_flat, full_attention_out, preferred_element_type=jnp.float32)
        + jnp.dot(gated, full_mixer_out, preferred_element_type=jnp.float32)
    )
    normed_two = rms_scale(residual, gain_feed).astype(jnp.bfloat16)
    gate_values = jnp.dot(normed_two, full_gate_up, preferred_element_type=jnp.float32)
    gate_in = gate_values[:, :FF]
    up_in = gate_values[:, FF:]
    active = (jax.nn.silu(gate_in) * up_in).astype(jnp.bfloat16)
    output = (residual + jnp.dot(active, full_down, preferred_element_type=jnp.float32)).astype(
        jnp.bfloat16
    )
    cotangent = out_cotangent.reshape(row_count, width)
    grad_down_weight = jnp.dot(active.T, cotangent, preferred_element_type=jnp.float32).astype(
        jnp.bfloat16
    )
    active_grad = jnp.dot(cotangent, full_down.T, preferred_element_type=jnp.float32)
    gate_grad = jnp.concatenate(
        [active_grad * up_in * silu_slope(gate_in), active_grad * jax.nn.silu(gate_in)], axis=1
    ).astype(jnp.bfloat16)
    grad_gate_up = jnp.dot(normed_two.T, gate_grad, preferred_element_type=jnp.float32).astype(
        jnp.bfloat16
    )
    feed_terms = jnp.concatenate(
        [grad_gate_up, fold_rows(grad_down_weight, down_weight.shape[0], own_rows)], axis=1
    )
    feed_sums = lax.psum_scatter(feed_terms, axes, scatter_dimension=0, tiled=True)
    normed_two_grad = jnp.dot(gate_grad, full_gate_up.T, preferred_element_type=jnp.float32)
    _, pull_two = jax.vjp(rms_scale, residual, gain_feed)
    residual_part, grad_gain_feed = pull_two(normed_two_grad)
    residual_grad = cotangent.astype(jnp.float32) + residual_part
    residual_half, _ = lax.optimization_barrier((residual_grad.astype(jnp.bfloat16), feed_terms))
    grad_attention_out = jnp.dot(attended_flat.T, residual_half, preferred_element_type=jnp.float32)
    grad_mixer_out = jnp.dot(gated.T, residual_half, preferred_element_type=jnp.float32)
    attended_grad = jnp.dot(
        residual_half, full_attention_out.T, preferred_element_type=jnp.float32
    ).astype(jnp.bfloat16)
    gated_grad = jnp.dot(residual_half, full_mixer_out.T, preferred_element_type=jnp.float32)
    gate_part_grad = gated_grad * flat_scan * silu_slope(gate_part)
    scan_grad = (gated_grad * jax.nn.silu(gate_part)).reshape(
        seq_count, tok_count, SSM_HEADS, SSM_HEAD
    )
    direct = jnp.einsum("sth,sthp,stn->shpn", carried, scan_grad, read_map, precision=highest)
    if by_heads:
        state_grad = carried_by_heads(decays, direct, True)
    else:
        state_grad = carried_in((decay_total, direct), "ctx", chain, unit, True)[1]

    def block_map(inner_v, write_v, read_v, step_v, decay_v, bias_v, skip_v, state_v):
        mapped = jax.vmap(ssd_block, in_axes=(0, 0, 0, 0, None, None, None, 0, 0, 0))
        return mapped(
            inner_v, write_v, read_v, step_v, decay_v, bias_v, skip_v, starts, segment_ids, state_v
        )

    _, pull_scan = jax.vjp(
        block_map, inner, write_map, read_map, step_raw, decay_log, step_bias, skip_gain, state_in
    )
    pulled = pull_scan((scan_grad, state_grad))
    converted_grad = jnp.concatenate(
        [pulled[0].reshape(seq_count, tok_count, SSM_INNER), pulled[1], pulled[2]], axis=2
    )
    pre_grad = converted_grad * silu_slope(pre)
    after_rows = from_behind(pre_grad[:, :3, :], "ctx", -1)
    ahead = jnp.concatenate([pre_grad, after_rows], axis=1)
    conv_in_grad = conv_weight[3] * pre_grad
    tap_grads = [None, None, None, jnp.sum(pre_grad * conv_in, axis=(0, 1))]
    for offset in (1, 2, 3):
        later_ids = segments_all[jnp.minimum(positions + offset, length - 1)].T
        later_mask = later_ids == segment_ids
        conv_in_grad = (
            conv_in_grad
            + jnp.where(later_mask[..., None], ahead[:, offset : offset + tok_count], 0.0)
            * conv_weight[3 - offset]
        )
        earlier_rows = jnp.where(
            keep_masks[offset - 1][..., None], extended[:, 3 - offset : 3 - offset + tok_count], 0.0
        )
        tap_grads[3 - offset] = jnp.sum(pre_grad * earlier_rows, axis=(0, 1))
    grad_conv_weight = jnp.stack(tap_grads, axis=0)
    grad_conv_bias = jnp.sum(pre_grad, axis=(0, 1))
    mixer_grad = jnp.concatenate(
        [gate_part_grad, conv_in_grad.reshape(row_count, conv_width)], axis=1
    ).astype(jnp.bfloat16)
    step_grad_half = pulled[3].reshape(row_count, SSM_HEADS).astype(jnp.bfloat16)
    out_grad = group_queries(attended_grad, seq_count, tok_count)
    deltas = jnp.sum(out_grad.astype(jnp.float32) * attended.astype(jnp.float32), axis=-1)

    def attention_grads(query_grad, item):
        scores, allowed = scores_of(item[0], item[1], item[2])
        keys = item[0][:, :, :key_width].reshape(block, seq_count, HEADS_KV, HEAD)
        values = item[0][:, :, key_width:].reshape(block, seq_count, HEADS_KV, HEAD)
        probs = jnp.where(allowed, jnp.exp(scores - log_total[..., None]), 0.0)
        value_grad = jnp.einsum(
            "sgrk,sgrd->ksgd",
            probs.astype(jnp.bfloat16),
            out_grad,
            preferred_element_type=jnp.float32,
        )
        prob_grad = jnp.einsum(
            "sgrd,ksgd->sgrk", out_grad, values, preferred_element_type=jnp.float32
        )
        score_grad = (probs * (prob_grad - deltas[..., None])).astype(jnp.bfloat16)
        query_grad = (
            query_grad
            + jnp.einsum("sgrk,ksgd->sgrd", score_grad, keys, preferred_element_type=jnp.float32)
            * score_scale
        )
        key_grad = (
            jnp.einsum("sgrk,sgrd->ksgd", score_grad, queries, preferred_element_type=jnp.float32)
            * score_scale
        )
        both = jnp.concatenate(
            [
                key_grad.reshape(block, seq_count, key_width),
                value_grad.reshape(block, seq_count, key_width),
            ],
            axis=2,
        )
        return (query_grad, both)

    query_grad, key_terms = over_blocks(
        attention_grads,
        jnp.zeros(queries.shape, jnp.float32),
        (key_blocks, segment_blocks, block_ids),
    )
    key_pieces = lax.all_to_all(
        key_terms.reshape(length, seq_count, 2 * key_width).astype(jnp.bfloat16),
        "ctx",
        split_axis=0,
        concat_axis=0,
        tiled=True,
    )
    key_sums = jnp.sum(
        key_pieces.reshape(-1, tok_count, seq_count, 2 * key_width).astype(jnp.float32), axis=0
    )
    kv_grad = key_sums.transpose(1, 0, 2).reshape(row_count, 2 * key_width)
    projected_grad = jnp.concatenate(
        [ungroup(query_grad, seq_count, tok_count), kv_grad], axis=1
    ).astype(jnp.bfloat16)
    grad_attention_in = jnp.dot(normed.T, projected_grad, preferred_element_type=jnp.float32)
    grad_mixer_in = jnp.dot(normed.T, mixer_grad, preferred_element_type=jnp.float32)
    grad_step_in = jnp.dot(normed.T, step_grad_half, preferred_element_type=jnp.float32)
    normed_grad = (
        jnp.dot(projected_grad, full_attention_in.T, preferred_element_type=jnp.float32)
        + jnp.dot(mixer_grad, full_mixer_in.T, preferred_element_type=jnp.float32)
        + jnp.dot(step_grad_half, full_step_in.T, preferred_element_type=jnp.float32)
    )
    _, pull_one = jax.vjp(rms_scale, source, gain_mixing)
    source_part, grad_gain_mixing = pull_one(normed_grad)
    input_grad = residual_grad + source_part
    others = [
        grad_attention_in.astype(jnp.bfloat16),
        grad_mixer_in.astype(jnp.bfloat16),
        fold_rows(grad_attention_out.astype(jnp.bfloat16), attention_out.shape[0], own_rows),
        fold_rows(grad_mixer_out.astype(jnp.bfloat16), mixer_out.shape[0], own_rows),
        pad_columns(grad_step_in.astype(jnp.bfloat16)),
    ]
    other_sums = lax.psum_scatter(
        jnp.concatenate(others, axis=1), axes, scatter_dimension=0, tiled=True
    )
    feed_parts = cut_columns(
        feed_sums, (gate_up.shape[1], feed_sums.shape[1] - gate_up.shape[1])
    )
    other_parts = cut_columns(other_sums, [part.shape[1] for part in others])
    weight_sums = [
        part.astype(jnp.float32)
        for part in (
            other_parts[0],
            other_parts[1],
            other_parts[4][:, :SSM_HEADS],
            unfold_rows(other_parts[2], attention_out.shape[0], own_rows, width),
            unfold_rows(other_parts[3], mixer_out.shape[0], own_rows, width),
            feed_parts[0],
            unfold_rows(feed_parts[1], down_weight.shape[0], own_rows, width),
        )
    ]
    small_sums = lax.psum(
        (
            grad_gain_mixing,
            grad_gain_feed,
            pulled[4],
            pulled[5],
            pulled[6],
            grad_conv_weight,
            grad_conv_bias,
        ),
        ("dp", "ctx"),
    )
    return (
        output.reshape(seq_count, tok_count, width),
        input_grad.reshape(seq_count, tok_count, width),
        weight_sums[0],
        weight_sums[1],
        weight_sums[2],
        weight_sums[3],
        weight_sums[4],
        weight_sums[5],
        weight_sums[6],
        small_sums[0],
        small_sums[1],
        small_sums[2],
        small_sums[3],
        small_sums[4],
        small_sums[5],
        small_sums[6],
    )

def split_heads(ctx):
    return HEADS_Q == ctx and SSM_HEADS % ctx == 0 and ctx % HEADS_KV == 0


def entry_layout(ctx):
    heads = SSM_HEADS // ctx
    widths = [STATE, STATE, heads * SSM_HEAD, heads * SSM_HEAD, HEAD, HEAD, HEAD, heads]
    return widths + [-sum(widths) % 128]


def entry_slabs(attention_in, mixer_in, step_in, ctx):
    rows = attention_in.shape[0]
    share = ctx // HEADS_KV
    query_width = HEADS_Q * HEAD
    key_width = HEADS_KV * HEAD

    def parts(array, count):
        return array.reshape(rows, count, -1).transpose(1, 0, 2)

    kv = [
        jnp.repeat(parts(attention_in[:, at : at + key_width], HEADS_KV), share, axis=0)
        for at in (query_width, query_width + key_width)
    ]
    both = jnp.broadcast_to(mixer_in[None, :, 2 * SSM_INNER :], (ctx, rows, 2 * STATE))
    pieces = [
        both,
        parts(mixer_in[:, SSM_INNER : 2 * SSM_INNER], ctx),
        parts(mixer_in[:, :SSM_INNER], ctx),
        parts(attention_in[:, :query_width], ctx),
        kv[0],
        kv[1],
        parts(step_in, ctx),
        jnp.zeros((ctx, rows, entry_layout(ctx)[-1]), jnp.bfloat16),
    ]
    return jnp.concatenate(pieces, axis=2)


def offsets(widths):
    at, places = 0, []
    for width in widths:
        places.append(at)
        at += width
    return places


MESH = pl.DeviceIdType.MESH
IN_VMEM = pl.BlockSpec(memory_space=pltpu.VMEM)
ANYWHERE = pl.BlockSpec(memory_space=pl.ANY)


def remote(source, target, send, recv, peer):
    return pltpu.make_async_remote_copy(
        src_ref=source,
        dst_ref=target,
        send_sem=send,
        recv_sem=recv,
        device_id=peer,
        device_id_type=MESH,
    )


def arrived(ref, recv, peer):
    remote(ref, ref, recv, recv, peer).wait_recv()


class Here:
    def __init__(self, dp, ctx):
        self.dp, self.ctx, self.pairs = dp, ctx, ctx // 2
        self.d, self.me = lax.axis_index("dp"), lax.axis_index("ctx")
        self.z, self.c = self.me // 2, self.me % 2
        self.sibling = (self.d, self.z * 2 + 1 - self.c)

    def dp_peers(self):
        return [(lax.rem(self.d + k, self.dp), self.me) for k in range(1, self.dp)]

    def ctx_peers(self):
        return [(self.d, lax.rem(self.me + k, self.ctx)) for k in range(1, self.ctx)]

    def greet(self, peers, sender=None):
        sem = pltpu.get_barrier_semaphore()
        for peer in peers:
            pl.semaphore_signal(sem, inc=1, device_id=peer, device_id_type=MESH)
        count = len(peers)
        if sender is not None:
            away = jnp.logical_not(self.is_me(sender))

            @pl.when(away)
            def _():
                pl.semaphore_signal(sem, inc=1, device_id=sender, device_id_type=MESH)

            count = count + away.astype(jnp.int32)
        pl.semaphore_wait(sem, count)

    def is_me(self, peer):
        return (peer[0] == self.d) & (peer[1] == self.me)

    def user(self):
        place = self.d * self.ctx + self.me
        return (lax.rem(place, self.dp), place // self.dp)

    def owner(self):
        place = self.me * self.dp + self.d
        return (place // self.ctx, lax.rem(place, self.ctx))


class Relay:
    def __init__(self, here, block, slots, send, recv, local, cut=None):
        self.here, self.slots, self.cut = here, slots, cut
        self.block = block if cut is None else block.at[cut]
        self.send, self.recv, self.local = send, recv, local
        self.up = (here.d, (here.z + 1) * 2 + here.c)
        self.down = (here.d, (here.z - 1) * 2 + here.c)
        self.has_up, self.has_down = here.z < here.pairs - 1, here.z > 0

    @staticmethod
    def scratch(pairs):
        return [
            pltpu.SemaphoreType.DMA((4 * pairs,)),
            pltpu.SemaphoreType.DMA((2 * pairs,)),
            pltpu.SemaphoreType.DMA,
        ]

    @staticmethod
    def cuts(rows):
        count = 2 if rows % (16 * 2) == 0 else 1
        return [pl.ds(i * (rows // count), rows // count) for i in range(count)]

    def slot(self, z, c):
        ref = self.slots.at[z * 2 + c]
        return ref if self.cut is None else ref.at[self.cut]

    def greet(self):
        sem = pltpu.get_barrier_semaphore()

        def signal(peer):
            pl.semaphore_signal(sem, inc=1, device_id=peer, device_id_type=MESH)

        pl.when(self.has_up)(lambda: signal(self.up))
        pl.when(self.has_down)(lambda: signal(self.down))
        signal(self.here.sibling)
        count = self.has_up.astype(jnp.int32) + self.has_down.astype(jnp.int32)
        pl.semaphore_wait(sem, count + 1)

    def begin(self):
        h, n = self.here, self.here.pairs
        own = self.slot(h.z, h.c)
        pltpu.make_async_copy(self.block, own, self.local).start()

        @pl.when(self.has_up)
        def _():
            remote(self.block, own, self.send.at[0], self.recv.at[h.me], self.up).start()

        @pl.when(self.has_down)
        def _():
            remote(self.block, own, self.send.at[n], self.recv.at[h.me], self.down).start()

        remote(self.block, own, self.send.at[2 * n], self.recv.at[h.me], h.sibling).start()

    def hop(self, s):
        h, n = self.here, self.here.pairs
        low, high = h.z - s, h.z + s

        @pl.when(low >= 0)
        def _():
            ref, recv = self.slot(low, h.c), self.recv.at[low * 2 + h.c]
            arrived(ref, recv, h.sibling)

            @pl.when(self.has_up)
            def _():
                remote(ref, ref, self.send.at[s], recv, self.up).start()

            remote(ref, ref, self.send.at[2 * n + 2 * s - 1], recv, h.sibling).start()

        @pl.when(high < n)
        def _():
            ref, recv = self.slot(high, h.c), self.recv.at[high * 2 + h.c]
            arrived(ref, recv, h.sibling)

            @pl.when(self.has_down)
            def _():
                remote(ref, ref, self.send.at[n + s], recv, self.down).start()

            remote(ref, ref, self.send.at[2 * n + 2 * s], recv, h.sibling).start()

    def end(self):
        h, n = self.here, self.here.pairs
        for z in range(n):
            arrived(self.slot(z, 1 - h.c), self.recv.at[z * 2 + 1 - h.c], h.sibling)
        own = self.slot(h.z, h.c)

        def sent(index):
            remote(own, own, self.send.at[index], self.recv.at[0], h.sibling).wait_send()

        for s in range(n):
            low, high = h.z - s, h.z + s
            pl.when((low >= 0) & self.has_up)(functools.partial(sent, s))
            pl.when((high < n) & self.has_down)(functools.partial(sent, n + s))
            if s == 0:
                sent(2 * n)
            else:
                pl.when(low >= 0)(functools.partial(sent, 2 * n + 2 * s - 1))
                pl.when(high < n)(functools.partial(sent, 2 * n + 2 * s))
        pltpu.make_async_copy(self.block, own, self.local).wait()


class Spread:
    def __init__(self, here, block, slots, send, recv, local):
        self.here, self.block, self.slots = here, block, slots
        self.send, self.recv, self.local = send, recv, local

    @staticmethod
    def scratch(dp):
        return [
            pltpu.SemaphoreType.DMA((dp,)),
            pltpu.SemaphoreType.DMA((dp,)),
            pltpu.SemaphoreType.DMA,
        ]

    def begin(self):
        h = self.here
        pltpu.make_async_copy(self.block, self.slots.at[h.d], self.local).start()
        self.copies = [
            remote(self.block, self.slots.at[h.d], self.send.at[k], self.recv.at[h.d], peer)
            for k, peer in enumerate(h.dp_peers())
        ]
        for copy in self.copies:
            copy.start()

    def end(self):
        h = self.here
        for peer in h.dp_peers():
            arrived(self.slots.at[peer[0]], self.recv.at[peer[0]], peer)
        for copy in self.copies:
            copy.wait_send()
        pltpu.make_async_copy(self.block, self.slots.at[h.d], self.local).wait()


class Total:
    def __init__(self, here, terms, got, result, send, recv):
        self.here, self.terms, self.got, self.result = here, terms, got, result
        self.send, self.recv = send, recv

    @staticmethod
    def scratch(dp, shape):
        return [
            pltpu.VMEM((dp,) + shape, jnp.bfloat16),
            pltpu.SemaphoreType.DMA((dp,)),
            pltpu.SemaphoreType.DMA((dp,)),
        ]

    def begin(self):
        h = self.here
        self.copies = [
            remote(
                self.terms.at[peer[0]], self.got.at[h.d], self.send.at[k], self.recv.at[h.d], peer
            )
            for k, peer in enumerate(h.dp_peers())
        ]
        for copy in self.copies:
            copy.start()

    def end(self):
        h = self.here
        total = self.terms[h.d].astype(jnp.float32)
        for peer in h.dp_peers():
            arrived(self.got.at[peer[0]], self.recv.at[peer[0]], peer)
            total = total + self.got[peer[0]].astype(jnp.float32)
        self.result[...] = total.astype(self.result.dtype)

    def leave(self):
        for copy in self.copies:
            copy.wait_send()


class Swap:
    def __init__(self, here, blocks, slots, send, recv, local):
        self.here, self.blocks, self.slots = here, blocks, slots
        self.send, self.recv, self.local = send, recv, local

    @staticmethod
    def scratch(ctx):
        return [
            pltpu.SemaphoreType.DMA((ctx,)),
            pltpu.SemaphoreType.DMA((ctx,)),
            pltpu.SemaphoreType.DMA,
        ]

    def begin(self):
        h = self.here
        pltpu.make_async_copy(self.blocks.at[h.me], self.slots.at[h.me], self.local).start()
        self.copies = []
        for k, peer in enumerate(h.ctx_peers()):
            copy = remote(
                self.blocks.at[peer[1]],
                self.slots.at[h.me],
                self.send.at[k],
                self.recv.at[h.me],
                peer,
            )
            copy.start()
            self.copies.append(copy)

    def wait(self, index):
        arrived(self.slots.at[index], self.recv.at[index], self.here.sibling)

    def leave(self):
        h = self.here
        for copy in self.copies:
            copy.wait_send()
        pltpu.make_async_copy(self.blocks.at[h.me], self.slots.at[h.me], self.local).wait()


class SumTokens:
    def __init__(self, here, left, right, turned, total, away, pair, out, got, *sems):
        self.here, self.left, self.right, self.turned, self.total = here, left, right, turned, total
        self.away, self.pair, self.out, self.got = away, pair, out, got
        self.away_send, self.away_recv, self.send, self.recv = sems
        self.order = sorted(range(1, here.pairs), key=lambda k: -min(k, here.pairs - k)) + [0]

    @staticmethod
    def scratch(pairs, rows, width):
        block = pltpu.VMEM((pairs, rows, width), jnp.bfloat16)
        return [block] * 4 + [pltpu.SemaphoreType.DMA((pairs,))] * 4

    def term(self, z, c):
        rows = self.total.shape[0]
        part = self.left[pl.ds(pl.multiple_of((z * 2 + c) * rows, rows), rows), :]
        dims = (((1,), (1 if self.turned else 0,)), ((), ()))
        return lax.dot_general(part, self.right[...], dims, preferred_element_type=jnp.float32)

    def peer(self, k):
        h = self.here
        return (h.d, lax.rem(h.z + k, h.pairs) * 2 + h.c)

    def to_sibling(self, k):
        return remote(
            self.away.at[k], self.pair.at[k], self.away_send.at[k], self.away_recv.at[k],
            self.here.sibling,
        )

    def to_pair(self, k):
        return remote(
            self.out.at[k], self.got.at[k], self.send.at[k], self.recv.at[k], self.peer(k)
        )

    def begin(self):
        h = self.here

        def give(k):
            self.away[k] = self.term(lax.rem(h.z + k, h.pairs), 1 - h.c).astype(jnp.bfloat16)
            self.to_sibling(k).start()

        give(self.order[0])
        for i, k in enumerate(self.order):
            if i + 1 < len(self.order):
                give(self.order[i + 1])
            term = self.term(lax.rem(h.z + k, h.pairs), h.c)
            self.to_sibling(k).wait_recv()
            term = term + self.pair[k].astype(jnp.float32)
            if k:
                self.out[k] = term.astype(jnp.bfloat16)
                self.to_pair(k).start()
            else:
                self.total[...] = term

    def end(self):
        for k in self.order[::-1]:
            if k:
                self.to_pair(k).wait_recv()
                self.total[...] += self.got[k].astype(jnp.float32)

    def leave(self):
        for k in self.order:
            self.to_sibling(k).wait_send()
            if k:
                self.to_pair(k).wait_send()


class Move:
    def __init__(self, here, block, target, there, landing, sender, send, recv, local):
        self.here, self.landing, self.sender, self.recv = here, landing, sender, recv
        self.own = here.is_me(target)
        self.home = pltpu.make_async_copy(block, landing, local)
        self.far = remote(block, there, send, recv, target)

    @staticmethod
    def scratch():
        return [pltpu.SemaphoreType.DMA] * 3

    def begin(self):
        pl.when(self.own)(lambda: self.home.start())
        pl.when(jnp.logical_not(self.own))(lambda: self.far.start())

    def wait(self):
        pl.when(self.own)(lambda: self.home.wait())
        pl.when(jnp.logical_not(self.own))(lambda: arrived(self.landing, self.recv, self.sender))

    def leave(self):
        pl.when(jnp.logical_not(self.own))(lambda: self.far.wait_send())


def call(kernel, ident, outs, out_specs, in_specs, scratch, *arrays):
    return pl.pallas_call(
        kernel,
        out_shape=outs,
        in_specs=in_specs,
        out_specs=out_specs,
        scratch_shapes=scratch,
        compiler_params=pltpu.CompilerParams(
            collective_id=ident, has_side_effects=True, vmem_limit_bytes=48 * 2**20
        ),
    )(*arrays)


def like(shape, dtype=jnp.bfloat16):
    return jax.ShapeDtypeStruct(shape, dtype)


def gather_tokens(block, ident):
    dp, ctx = lax.axis_size("dp"), lax.axis_size("ctx")
    cuts = Relay.cuts(block.shape[0])

    def kernel(block_ref, slots_ref, *sems):
        here = Here(dp, ctx)
        relays = [
            Relay(here, block_ref, slots_ref, *sems[3 * i : 3 * i + 3], cut)
            for i, cut in enumerate(cuts)
        ]
        relays[0].greet()
        for relay in relays:
            relay.begin()
        for s in range(1, here.pairs):
            for relay in relays:
                relay.hop(s)
        for relay in relays:
            relay.end()

    whole = call(
        kernel, ident, like((ctx,) + block.shape, block.dtype), ANYWHERE, [ANYWHERE],
        Relay.scratch(ctx // 2) * len(cuts), block,
    )
    return whole.reshape((-1,) + block.shape[1:])


def enter(normed, segments, entry, feed, outs):
    dp, ctx = lax.axis_size("dp"), lax.axis_size("ctx")
    relay_sems, swap_sems = Relay.scratch(ctx // 2), Swap.scratch(ctx)
    cuts = Relay.cuts(normed.shape[0])

    def kernel(
        normed_ref, seg_ref, entry_ref, feed_ref, outs_ref,
        all_ref, segs_ref, full_ref, feeds_ref, rows_ref, *sems,
    ):
        here = Here(dp, ctx)
        tokens = [
            Relay(here, normed_ref, all_ref, *sems[16 + 3 * i : 19 + 3 * i], cut)
            for i, cut in enumerate(cuts)
        ]
        ids = Relay(here, seg_ref, segs_ref, *sems[0:3])
        slabs = Swap(here, entry_ref, full_ref.at[here.d], *sems[3:6])
        others = Swap(here, feed_ref, feeds_ref, *sems[6:9])
        pass_send, pass_recv = sems[9:11]
        target = here.user()
        outs = Move(
            here, outs_ref, target, rows_ref.at[target[0]], rows_ref.at[here.d], here.owner(),
            *sems[11:14],
        )
        rows_send, rows_recv = sems[14:16]
        peers = here.dp_peers()
        here.greet(peers + here.ctx_peers(), here.owner())

        def passing(source, k, index):
            return remote(
                source,
                full_ref.at[here.d, index],
                pass_send.at[k, index],
                pass_recv.at[here.d, index],
                peers[k],
            )

        def forward(index):
            slabs.wait(index)
            for k in range(dp - 1):
                passing(full_ref.at[here.d, index], k, index).start()

        def rows_copy(k):
            ref = rows_ref.at[here.d]
            return remote(ref, ref, rows_send.at[k], rows_recv.at[here.d], peers[k])

        slabs.begin()
        for k in range(dp - 1):
            passing(entry_ref.at[here.me], k, here.me).start()
        for part in tokens:
            part.begin()
        ids.begin()
        outs.begin()
        forward(here.z * 2 + 1 - here.c)
        for s in range(1, here.pairs):
            for z in (here.z - s, here.z + s):

                @pl.when((z >= 0) & (z < here.pairs))
                def _(z=z):
                    forward(z * 2 + here.c)
                    forward(z * 2 + 1 - here.c)

            for part in tokens:
                part.hop(s)
            ids.hop(s)
            if s == 1:
                others.begin()
            if s == max(1, here.pairs - 2):
                outs.wait()
                for k in range(dp - 1):
                    rows_copy(k).start()
        for peer in peers:
            for index in range(ctx):
                arrived(full_ref.at[peer[0], index], pass_recv.at[peer[0], index], peer)
        for peer in here.ctx_peers():
            others.wait(peer[1])
        for part in tokens:
            part.end()
        ids.end()
        for k, peer in enumerate(peers):
            arrived(rows_ref.at[peer[0]], rows_recv.at[peer[0]], peer)
            rows_copy(k).wait_send()
        outs.leave()
        slabs.leave()
        others.leave()
        for index in range(ctx):
            for k in range(dp - 1):
                passing(full_ref.at[here.d, index], k, index).wait_send()

    return call(
        kernel,
        0,
        (
            like((ctx,) + normed.shape),
            like((ctx,) + segments.shape, segments.dtype),
            like((dp,) + entry.shape),
            like(feed.shape),
            like((dp,) + outs.shape),
        ),
        (ANYWHERE,) * 5,
        [ANYWHERE] * 5,
        relay_sems + swap_sems * 2 + [pltpu.SemaphoreType.DMA((dp, ctx))] * 2
        + Move.scratch()
        + [pltpu.SemaphoreType.DMA((dp,))] * 2
        + relay_sems * len(cuts),
        normed,
        segments,
        entry,
        feed,
        outs,
    )


def sum_and_spread(left, right, blocks, ident):
    dp, ctx = lax.axis_size("dp"), lax.axis_size("ctx")
    rows, width = left.shape[0] // ctx, right.shape[1]
    count = len(blocks)

    def kernel(left_ref, right_ref, *refs):
        blocks_in, total, slots = refs[:count], refs[count], refs[count + 1 : 2 * count + 1]
        sems = refs[2 * count + 1 :]
        here = Here(dp, ctx)
        sums = SumTokens(here, left_ref, right_ref, False, total, *sems[:8])
        spreads = [
            Spread(here, block, slot, *sems[8 + 3 * i : 11 + 3 * i])
            for i, (block, slot) in enumerate(zip(blocks_in, slots))
        ]
        here.greet(here.dp_peers() + here.ctx_peers())
        for spread in spreads:
            spread.begin()
        sums.begin()
        sums.end()
        for spread in spreads:
            spread.end()
        sums.leave()

    return call(
        kernel,
        ident,
        (like((rows, width), jnp.float32), *[like((dp,) + block.shape) for block in blocks]),
        (IN_VMEM,) + (ANYWHERE,) * count,
        [IN_VMEM, IN_VMEM] + [ANYWHERE] * count,
        SumTokens.scratch(ctx // 2, rows, width) + Spread.scratch(dp) * count,
        left,
        right,
        *blocks,
    )


def sum_and_total(left, right, terms, ident):
    dp, ctx = lax.axis_size("dp"), lax.axis_size("ctx")
    rows, width = left.shape[0] // ctx, right.shape[0]
    count = len(terms)

    def kernel(left_ref, right_ref, *refs):
        terms_in, total, results = refs[:count], refs[count], refs[count + 1 : 2 * count + 1]
        sems = refs[2 * count + 1 :]
        here = Here(dp, ctx)
        sums = SumTokens(here, left_ref, right_ref, True, total, *sems[:8])
        totals = [
            Total(here, term, sems[8 + 3 * i], result, *sems[9 + 3 * i : 11 + 3 * i])
            for i, (term, result) in enumerate(zip(terms_in, results))
        ]
        here.greet(here.dp_peers() + here.ctx_peers())
        for part in totals:
            part.begin()
        sums.begin()
        for part in totals:
            part.end()
        sums.end()
        sums.leave()
        for part in totals:
            part.leave()

    scratch = SumTokens.scratch(ctx // 2, rows, width)
    for term in terms:
        scratch = scratch + Total.scratch(dp, term.shape[1:])
    return call(
        kernel,
        ident,
        (like((rows, width), jnp.float32), *[like(term.shape[1:]) for term in terms]),
        (IN_VMEM,) * (1 + count),
        [IN_VMEM] * (2 + count),
        scratch,
        left,
        right,
        *terms,
    )


def leave(grads, entry, source, residual_grad, gain, entry_terms, feed_sums, out_terms, small):
    dp, ctx = lax.axis_size("dp"), lax.axis_size("ctx")
    rows, width = source.shape
    slab = entry_terms.shape[2:]
    layout = entry_layout(ctx)
    hidden = feed_sums.shape[2] // (2 * dp)
    own_rows = slab[0]

    def kernel(
        grads_ref, entry_ref, source_ref, res_ref, gain_ref, terms_ref, feed_ref, outs_ref, small_ref,
        input_ref, attention_ref, mixer_ref, step_ref, gate_up_ref, out_sum, smalls_ref, gain_ref_out,
        slabs_ref, feeds_ref, gains_ref, normed_grad, *sems,
    ):
        here = Here(dp, ctx)
        peers = here.dp_peers()
        sums = SumTokens(here, grads_ref, entry_ref, True, normed_grad, *sems[0:8])
        feeds = Swap(here, feed_ref, feeds_ref, *sems[8:11])
        got, term_send, term_recv, mine, slab_send, slab_recv = sems[11:17]
        small_got, gain_got = sems[17:19]
        small_send, small_recv, gain_send, gain_recv = sems[19:23]
        last_send, last_recv, lastg_send, lastg_recv = sems[23:27]
        outs_got, out_half, out_landed = sems[27], sems[30], sems[31]
        outs = Total(here, outs_ref, outs_got, out_half, *sems[28:30])
        home = Move(
            here, out_half, here.owner(), out_landed, out_landed, here.user(), *sems[32:35]
        )
        here.greet(peers + here.ctx_peers(), here.user())
        order = [lax.rem(here.me + k, ctx) for k in list(range(1, ctx)) + [0]]

        def term_copy(k, index):
            return remote(
                terms_ref.at[peers[k][0], index],
                got.at[here.d, index],
                term_send.at[k, index],
                term_recv.at[here.d, index],
                peers[k],
            )

        for index in order:
            for k in range(dp - 1):
                term_copy(k, index).start()
        outs.begin()
        small_copies = []
        for k, peer in enumerate(peers):
            copy = remote(
                small_ref, small_got.at[here.d], small_send.at[k], small_recv.at[here.d], peer
            )
            copy.start()
            small_copies.append(copy)
        sums.begin()
        feeds.begin()

        def slab_copy(j):
            return remote(
                mine.at[order[j]], slabs_ref.at[here.me], slab_send.at[j], slab_recv.at[here.me],
                (here.d, order[j]),
            )

        for j, index in enumerate(order):
            total = terms_ref[here.d, index].astype(jnp.float32)
            for peer in peers:
                arrived(got.at[peer[0], index], term_recv.at[peer[0], index], peer)
                total = total + got[peer[0], index].astype(jnp.float32)
            total = total.astype(jnp.bfloat16)
            if j < ctx - 1:
                mine[index] = total
                slab_copy(j).start()
            else:
                slabs_ref[here.me] = total
        small_got[here.d] = small_ref[...]
        for peer in peers:
            arrived(small_got.at[peer[0]], small_recv.at[peer[0]], peer)
        total = small_got[0]
        for d in range(1, dp):
            total = total + small_got[d]
        smalls_ref[here.me] = total
        last = []
        for k, peer in enumerate(here.ctx_peers()):
            copy = remote(
                smalls_ref.at[here.me], smalls_ref.at[here.me], last_send.at[k],
                last_recv.at[here.me], peer,
            )
            copy.start()
            last.append(copy)
        outs.end()
        home.begin()
        sums.end()
        x, grad = source_ref[...], normed_grad[...]
        scale = lax.rsqrt(jnp.mean(x * x, axis=-1, keepdims=True) + 1e-05)
        scaled = grad * gain_ref[...]
        inner = jnp.mean(x * scaled, axis=-1, keepdims=True)
        input_ref[...] = res_ref[...] + scale * scaled - x * (scale * scale * scale * inner)
        gain_got[here.d] = jnp.sum(grad * (x * scale), axis=0, keepdims=True)
        for k, peer in enumerate(peers):
            copy = remote(
                gain_got.at[here.d], gain_got.at[here.d], gain_send.at[k], gain_recv.at[here.d], peer
            )
            copy.start()
            small_copies.append(copy)
        for peer in peers:
            arrived(gain_got.at[peer[0]], gain_recv.at[peer[0]], peer)
        total = gain_got[0]
        for d in range(1, dp):
            total = total + gain_got[d]
        gains_ref[here.me] = total
        for k, peer in enumerate(here.ctx_peers()):
            copy = remote(
                gains_ref.at[here.me], gains_ref.at[here.me], lastg_send.at[k],
                lastg_recv.at[here.me], peer,
            )
            copy.start()
            last.append(copy)
        for peer in here.ctx_peers():
            arrived(slabs_ref.at[peer[1]], slab_recv.at[peer[1]], peer)
            feeds.wait(peer[1])
            arrived(smalls_ref.at[peer[1]], last_recv.at[peer[1]], peer)
            arrived(gains_ref.at[peer[1]], lastg_recv.at[peer[1]], peer)
        feeds.leave()
        slabs = [slabs_ref[c].astype(jnp.float32) for c in range(ctx)]

        def columns(i, members=range(ctx)):
            at, size = offsets(layout)[i], layout[i]
            return [slabs[c][:, at : at + size] for c in members]

        share = ctx // HEADS_KV
        shared = [
            sum(columns(i, range(g * share, (g + 1) * share)))
            for i in (5, 6)
            for g in range(HEADS_KV)
        ]
        attention_ref[...] = jnp.concatenate(columns(4) + shared, axis=1)
        mixer_ref[:, :SSM_INNER] = jnp.concatenate(columns(3), axis=1)
        mixer_ref[:, SSM_INNER : 2 * SSM_INNER] = jnp.concatenate(columns(2), axis=1)
        mixer_ref[:, 2 * SSM_INNER : 2 * SSM_INNER + STATE] = sum(columns(0))
        mixer_ref[:, 2 * SSM_INNER + STATE :] = sum(columns(1))
        steps_at = offsets(layout)[7]
        for c in range(ctx):
            step_ref[c] = slabs[c][:, steps_at:]
        for m in range(2 * dp):
            part = [feeds_ref[c, :, m * hidden : (m + 1) * hidden] for c in range(ctx)]
            span = ctx * hidden
            gate_up_ref[:, m * span : (m + 1) * span] = jnp.concatenate(
                [piece.astype(jnp.float32) for piece in part], axis=1
            )
        total = gains_ref[0]
        for c in range(1, ctx):
            total = total + gains_ref[c]
        gain_ref_out[...] = total
        home.wait()
        out_sum[...] = out_landed[...].astype(jnp.float32)
        home.leave()
        outs.leave()
        sums.leave()
        for index in order:
            for k in range(dp - 1):
                term_copy(k, index).wait_send()
        for j in range(ctx - 1):
            slab_copy(j).wait_send()
        for copy in small_copies + last:
            copy.wait_send()

    dma = pltpu.SemaphoreType.DMA
    scratch = (
        [
            pltpu.VMEM((ctx,) + slab, jnp.bfloat16),
            pltpu.VMEM(feed_sums.shape, jnp.bfloat16),
            pltpu.VMEM((ctx, 1, width), jnp.float32),
            pltpu.VMEM((rows, width), jnp.float32),
        ]
        + SumTokens.scratch(ctx // 2, rows, width)
        + Swap.scratch(ctx)
        + [
            pltpu.VMEM((dp, ctx) + slab, jnp.bfloat16),
            dma((dp, ctx)),
            dma((dp, ctx)),
            pltpu.VMEM((ctx,) + slab, jnp.bfloat16),
            dma((ctx,)),
            dma((ctx,)),
        ]
        + [
            pltpu.VMEM((dp,) + small.shape, jnp.float32),
            pltpu.VMEM((dp, 1, width), jnp.float32),
        ]
        + [dma((dp,))] * 4
        + [dma((ctx,))] * 4
        + Total.scratch(dp, out_terms.shape[1:])
        + [pltpu.VMEM(out_terms.shape[1:], jnp.bfloat16)] * 2
        + Move.scratch()
    )
    return call(
        kernel,
        5,
        (
            like((rows, width), jnp.float32),
            like((own_rows, (HEADS_Q + 2 * HEADS_KV) * HEAD), jnp.float32),
            like((own_rows, 2 * SSM_INNER + 2 * STATE), jnp.float32),
            like((ctx, own_rows, layout[7] + layout[8]), jnp.float32),
            like((own_rows, ctx * feed_sums.shape[2]), jnp.float32),
            like(out_terms.shape[1:], jnp.float32),
            like((ctx,) + small.shape, jnp.float32),
            like((1, width), jnp.float32),
        ),
        (IN_VMEM,) * 8,
        [IN_VMEM] * 9,
        scratch,
        grads,
        entry,
        source,
        residual_grad,
        gain,
        entry_terms,
        feed_sums,
        out_terms,
        small,
    )


def rows_of(index, size):
    return pl.ds(pl.multiple_of(index * size, size), size)


def product(left, right, dims=((1,), (0,)), precision=None):
    return lax.dot_general(
        left, right, (dims, ((), ())), precision=precision, preferred_element_type=jnp.float32
    )


def sigma(values):
    return 1.0 / (1.0 + jnp.exp(-values))


def lower_of(size):
    down = lax.broadcasted_iota(jnp.int32, (size, size), 0)
    along = lax.broadcasted_iota(jnp.int32, (size, size), 1)
    return along <= down


def widen(columns, heads):
    shape = (columns.shape[0], SSM_HEAD)
    return jnp.concatenate(
        [jnp.broadcast_to(columns[:, h : h + 1], shape) for h in range(heads)], axis=1
    )


def head_sums(array, heads, width):
    sums = [
        jnp.sum(array[:, h * SSM_HEAD : (h + 1) * SSM_HEAD], axis=1, keepdims=True)
        for h in range(heads)
    ]
    return columns_of(sums, width)


def columns_of(columns, width):
    lane = lax.broadcasted_iota(jnp.int32, (columns[0].shape[0], width), 1)
    total = jnp.zeros(lane.shape, jnp.float32)
    for h, column in enumerate(columns):
        total = jnp.where(lane == h, column, total)
    return total


class Layout:
    def __init__(self, heads):
        self.inner = 2 * STATE
        self.conv = self.inner + heads * SSM_HEAD
        self.query = self.conv + heads * SSM_HEAD
        self.key = self.query + HEAD
        self.value = self.key + HEAD
        self.step = self.value + HEAD
        self.width = self.step + heads + (-(self.step + heads)) % 128
        self.steps = self.width - self.step


class Chunk:
    def __init__(self, lay, heads, p, a, seg_row, tap_ref, head_ref, shifted):
        size = p.shape[0]
        self.conv_in = p[:, : lay.conv]
        self.earlier = [jnp.where(a[:, k - 1 : k] > 0.0, shifted(k), 0.0) for k in (1, 2, 3)]
        pre = tap_ref[4:5, :] + tap_ref[3:4, :] * self.conv_in
        for k in (1, 2, 3):
            pre = pre + self.earlier[k - 1] * tap_ref[3 - k : 4 - k, :]
        self.sig = sigma(pre)
        self.pre = pre
        conv = pre * self.sig
        self.write, self.read = conv[:, :STATE], conv[:, STATE : 2 * STATE]
        self.inner = conv[:, lay.inner :]
        self.gate = p[:, lay.conv : lay.query]
        self.biased = p[:, lay.step :] + head_ref[1:2, :]
        self.steps = jnp.maximum(self.biased, 0.0) + jnp.log1p(jnp.exp(-jnp.abs(self.biased)))
        self.rates = self.steps * head_ref[0:1, :]
        lower = lower_of(size)
        self.ones = lower.astype(jnp.float32)
        run = product(self.ones, self.rates, precision=highest)
        run_row = product(self.rates, self.ones, ((0,), (1,)), precision=highest)
        allowed = lower & (a[:, 6:7] == seg_row)
        self.decay = [
            jnp.exp(jnp.where(allowed, run[:, h : h + 1] - run_row[h : h + 1, :], -1e30))
            for h in range(heads)
        ]
        self.carried = a[:, 7:8] * jnp.exp(run)
        self.tails = a[:, 8:9] * jnp.exp(run[size - 1 : size, :] - run)
        self.cross = product(self.read, self.write, ((1,), (1,)))
        self.scaled = self.inner * widen(self.steps, heads)
        self.carried_wide = widen(self.carried, heads)
        self.tails_wide = widen(self.tails, heads)
        self.skip_wide = widen(head_ref[2:3, :], heads)
        last = self.carried[size - 1 : size, :]
        head_row = lax.broadcasted_iota(jnp.int32, (heads * SSM_HEAD, 1), 0) // SSM_HEAD
        self.last = jnp.zeros((heads * SSM_HEAD, 1), jnp.float32)
        for h in range(heads):
            self.last = jnp.where(head_row == h, last[:, h : h + 1], self.last)


def attention_mask(seg_column, seg_row, at):
    rows, keys = seg_column.shape[0], seg_row.shape[1]
    down = lax.broadcasted_iota(jnp.int32, (rows, keys), 0) + at
    along = lax.broadcasted_iota(jnp.int32, (rows, keys), 1)
    return (along <= down) & (seg_column == seg_row)


def mix_forward(normed, entry, columns, seg_row, taps, head_rows, size):
    length = normed.shape[0]
    chunks = length // size
    heads = SSM_HEADS // lax.axis_size("ctx")
    lay = Layout(heads)
    wide = heads * SSM_HEAD
    block = 2 * size if chunks % 2 == 0 else size

    def kernel(
        n_ref, e_ref, col_ref, seg_ref, tap_ref, head_ref,
        mixed_ref, p_ref, y_ref, states_ref, top_ref, ext, state, heads_in,
    ):
        state[...] = jnp.zeros_like(state)
        ext[0:8, :] = jnp.zeros((8, lay.conv), jnp.float32)

        def chunk(j, _):
            at = rows_of(j, size)
            p = product(n_ref[at, :], e_ref[...])
            p_ref[at, :] = p
            ext[8:, :] = p[:, : lay.conv]
            part = Chunk(
                lay, heads, p, col_ref[at, :], seg_ref[:, at], tap_ref, head_ref,
                lambda k: ext[8 - k : 8 - k + size, :],
            )
            ext[0:8, :] = ext[size : size + 8, :]
            reached = state[...]
            states_ref[j] = reached
            local = [
                product(part.decay[h] * part.cross, part.scaled[:, h * SSM_HEAD : (h + 1) * SSM_HEAD])
                for h in range(heads)
            ]
            y = (
                jnp.concatenate(local, axis=1)
                + part.skip_wide * part.inner
                + part.carried_wide * product(part.read, reached, ((1,), (1,)))
            )
            y_ref[at, :] = y
            gated = y * part.gate * sigma(part.gate)
            state[...] = part.last * reached + product(
                part.tails_wide * part.scaled, part.write, ((0,), (0,))
            )
            heads_in[at, :] = p[:, lay.query : lay.query + 3 * HEAD].astype(jnp.bfloat16)
            mixed_ref[at, HEAD:] = gated.astype(jnp.bfloat16)
            return 0

        lax.fori_loop(0, chunks, chunk, 0)
        for b in range(length // block):
            at, keys = slice(b * block, (b + 1) * block), (b + 1) * block
            scores = product(
                heads_in[at, :HEAD], heads_in[:keys, HEAD : 2 * HEAD], ((1,), (1,))
            ) * (HEAD**-0.5)
            allowed = attention_mask(col_ref[at, 6:7], seg_ref[:, :keys], b * block)
            scores = jnp.where(allowed, scores, -1e30)
            top = jnp.max(scores, axis=1, keepdims=True)
            terms = jnp.where(allowed, jnp.exp(scores - top), 0.0)
            total = jnp.sum(terms, axis=1, keepdims=True)
            top_ref[at, :] = top + jnp.log(total)
            probs = (terms * (1.0 / total)).astype(jnp.bfloat16)
            mixed_ref[at, :HEAD] = product(probs, heads_in[:keys, 2 * HEAD :]).astype(jnp.bfloat16)

    return pl.pallas_call(
        kernel,
        out_shape=(
            like((length, HEAD + wide)),
            like((length, lay.width), jnp.float32),
            like((length, wide), jnp.float32),
            like((chunks, wide, STATE), jnp.float32),
            like((length, 1), jnp.float32),
        ),
        in_specs=[IN_VMEM] * 6,
        out_specs=(IN_VMEM,) * 5,
        scratch_shapes=[
            pltpu.VMEM((size + 8, lay.conv), jnp.float32),
            pltpu.VMEM((wide, STATE), jnp.float32),
            pltpu.VMEM((length, 3 * HEAD), jnp.bfloat16),
        ],
        compiler_params=pltpu.CompilerParams(vmem_limit_bytes=48 * 2**20),
    )(normed, entry, columns, seg_row, taps, head_rows)


def mix_backward(
    residual_half, out_rows, mixed_out, p, y, states, log_total, columns, seg_row, taps, head_rows, size
):
    length = p.shape[0]
    dp = lax.axis_size("dp")
    chunks = length // size
    heads = SSM_HEADS // lax.axis_size("ctx")
    lay = Layout(heads)
    wide = heads * SSM_HEAD
    block = 2 * size if chunks % 2 == 0 else size

    def kernel(
        r_ref, o_ref, mixed_ref, p_ref, y_ref, states_ref, top_ref, col_ref, seg_ref, tap_ref, head_ref,
        g_ref, tap_sum, head_sum, outs_ref, ext, ahead, out_grad, step_grad, state, heads_in, key_grad, value_grad,
    ):
        state[...] = jnp.zeros_like(state)
        ahead[size:, :] = jnp.zeros((8, lay.conv), jnp.float32)
        tap_sum[...] = jnp.zeros_like(tap_sum)
        head_sum[...] = jnp.zeros_like(head_sum)

        def chunk(step, _):
            j = chunks - 1 - step
            at = rows_of(j, size)
            p, a = p_ref[at, :], col_ref[at, :]
            ext[8:, :] = p[:, : lay.conv]
            ext[0:8, :] = p_ref[pl.ds(pl.multiple_of(jnp.maximum(j * size - 8, 0), 8), 8), : lay.conv]
            part = Chunk(
                lay, heads, p, a, seg_ref[:, at], tap_ref, head_ref,
                lambda k: ext[8 - k : 8 - k + size, :],
            )
            grads = product(r_ref[at, :], o_ref[...], ((1,), (1,)))
            out_grad[at, :] = grads[:, :HEAD].astype(jnp.bfloat16)
            gated_grad = grads[:, HEAD:]
            y = y_ref[at, :]
            gate_sig = sigma(part.gate)
            gate_grad = gated_grad * y * gate_sig * (1.0 + part.gate * (1.0 - gate_sig))
            dy = gated_grad * part.gate * gate_sig
            later = state[...]
            before = states_ref[j]
            reached = part.carried_wide * product(part.read, before, ((1,), (1,)))
            from_later = part.tails_wide * product(part.write, later, ((1,), (1,)))
            cross_grad = jnp.zeros((size, size), jnp.float32)
            local, row_sums, column_sums = [], [], []
            for h in range(heads):
                cut = slice(h * SSM_HEAD, (h + 1) * SSM_HEAD)
                mixing = part.decay[h] * part.cross
                mixing_grad = product(dy[:, cut], part.scaled[:, cut], ((1,), (1,)))
                local.append(product(mixing, dy[:, cut], ((0,), (0,))))
                cross_grad = cross_grad + part.decay[h] * mixing_grad
                weight = mixing * mixing_grad
                row_sums.append(jnp.sum(weight, axis=1, keepdims=True))
                column_sums.append(jnp.sum(weight, axis=0, keepdims=True))
            scaled_grad = jnp.concatenate(local, axis=1) + from_later
            carried_dy = part.carried_wide * dy
            tail_terms = part.tails_wide * part.scaled
            read_grad = product(cross_grad, part.write) + product(carried_dy, before)
            write_grad = product(cross_grad, part.read, ((0,), (0,))) + product(tail_terms, later)
            inner_grad = part.skip_wide * dy + widen(part.steps, heads) * scaled_grad
            tail_sums = head_sums(part.scaled * from_later, heads, lay.steps)
            run_grad = (
                columns_of(row_sums, lay.steps)
                + head_sums(dy * reached, heads, lay.steps)
                - tail_sums
            )
            ends = later * before * part.last
            end_sums = [
                jnp.sum(
                    jnp.sum(ends[h * SSM_HEAD : (h + 1) * SSM_HEAD, :], axis=1, keepdims=True),
                    axis=0,
                    keepdims=True,
                )
                for h in range(heads)
            ]
            final = columns_of(end_sums, lay.steps) + jnp.sum(tail_sums, axis=0, keepdims=True)
            column_rows = jnp.concatenate(
                column_sums + [jnp.zeros((lay.steps - heads, size), jnp.float32)], axis=0
            )
            rate_grad = (
                product(part.ones, run_grad, ((0,), (0,)), precision=highest)
                - product(part.ones, column_rows, ((0,), (1,)), precision=highest)
                + final
            )
            steps_grad = (
                head_sums(scaled_grad * part.inner, heads, lay.steps) + rate_grad * head_ref[0:1, :]
            )
            raw_grad = steps_grad * sigma(part.biased)
            step_grad[at, :] = raw_grad
            head_sum[0:1, :] += jnp.sum(rate_grad * part.rates, axis=0, keepdims=True)
            head_sum[1:2, :] += jnp.sum(raw_grad, axis=0, keepdims=True)
            head_sum[2:3, :] += jnp.sum(
                head_sums(dy * part.inner, heads, lay.steps), axis=0, keepdims=True
            )
            state[...] = part.last * later + product(carried_dy, part.read, ((0,), (0,)))
            converted_grad = jnp.concatenate([write_grad, read_grad, inner_grad], axis=1)
            pre_grad = converted_grad * part.sig * (1.0 + part.pre * (1.0 - part.sig))
            ahead[:size, :] = pre_grad
            conv_grad = tap_ref[3:4, :] * pre_grad
            tap_sum[3:4, :] += jnp.sum(pre_grad * part.conv_in, axis=0, keepdims=True)
            tap_sum[4:5, :] += jnp.sum(pre_grad, axis=0, keepdims=True)
            for k in (1, 2, 3):
                conv_grad = (
                    conv_grad
                    + jnp.where(a[:, 2 + k : 3 + k] > 0.0, ahead[k : k + size, :], 0.0)
                    * tap_ref[3 - k : 4 - k, :]
                )
                tap_sum[3 - k : 4 - k, :] += jnp.sum(
                    pre_grad * part.earlier[k - 1], axis=0, keepdims=True
                )
            ahead[size:, :] = ahead[0:8, :]
            g_ref[at, : lay.query] = jnp.concatenate([conv_grad, gate_grad], axis=1).astype(
                jnp.bfloat16
            )
            heads_in[at, :] = p[:, lay.query : lay.step].astype(jnp.bfloat16)
            return 0

        lax.fori_loop(0, chunks, chunk, 0)
        key_grad[...] = jnp.zeros_like(key_grad)
        value_grad[...] = jnp.zeros_like(value_grad)
        query_grads = []
        for b in range(length // block):
            at, keys = slice(b * block, (b + 1) * block), (b + 1) * block
            queries, grad = heads_in[at, :HEAD], out_grad[at, :]
            key_part, value_part = heads_in[:keys, HEAD : 2 * HEAD], heads_in[:keys, 2 * HEAD :]
            scores = product(queries, key_part, ((1,), (1,))) * (HEAD**-0.5)
            allowed = attention_mask(col_ref[at, 6:7], seg_ref[:, :keys], b * block)
            probs = jnp.where(allowed, jnp.exp(scores - top_ref[at, :]), 0.0)
            deltas = jnp.sum(
                grad.astype(jnp.float32) * mixed_ref[at, :HEAD].astype(jnp.float32),
                axis=1,
                keepdims=True,
            )
            prob_grad = product(grad, value_part, ((1,), (1,)))
            score_grad = (probs * (prob_grad - deltas)).astype(jnp.bfloat16)
            query_grads.append(product(score_grad, key_part) * (HEAD**-0.5))
            key_grad[:keys, :] += product(score_grad, queries, ((0,), (0,))) * (HEAD**-0.5)
            value_grad[:keys, :] += product(probs.astype(jnp.bfloat16), grad, ((0,), (0,)))
        for b, query_grad in enumerate(query_grads):
            at = slice(b * block, (b + 1) * block)
            g_ref[at, lay.query :] = jnp.concatenate(
                [query_grad, key_grad[at, :], value_grad[at, :], step_grad[at, :]], axis=1
            ).astype(jnp.bfloat16)
        terms = product(mixed_ref[...], r_ref[...], ((0,), (0,))).astype(jnp.bfloat16)
        few, many = HEAD // dp, wide // dp
        for j in range(dp):
            outs_ref[j, :few, :] = terms[j * few : (j + 1) * few, :]
            outs_ref[j, few:, :] = terms[HEAD + j * many : HEAD + (j + 1) * many, :]

    f32 = jnp.float32
    return pl.pallas_call(
        kernel,
        out_shape=(
            like((length, lay.width)),
            like((8, lay.conv), f32),
            like((8, lay.steps), f32),
            like((dp, out_rows.shape[0] // dp, out_rows.shape[1])),
        ),
        in_specs=[IN_VMEM] * 11,
        out_specs=(IN_VMEM,) * 4,
        scratch_shapes=[
            pltpu.VMEM((size + 8, lay.conv), f32),
            pltpu.VMEM((size + 8, lay.conv), f32),
            pltpu.VMEM((length, HEAD), jnp.bfloat16),
            pltpu.VMEM((length, lay.steps), f32),
            pltpu.VMEM((wide, STATE), f32),
            pltpu.VMEM((length, 3 * HEAD), jnp.bfloat16),
            pltpu.VMEM((length, HEAD), f32),
            pltpu.VMEM((length, HEAD), f32),
        ],
        compiler_params=pltpu.CompilerParams(vmem_limit_bytes=56 * 2**20),
    )(residual_half, out_rows, mixed_out, p, y, states, log_total, columns, seg_row, taps, head_rows)


def across(left, right):
    return jnp.dot(left.T, right, preferred_element_type=jnp.float32).astype(jnp.bfloat16)


def split_local(
    block_input,
    segment_ids,
    out_cotangent,
    attention_in,
    mixer_in,
    step_in,
    attention_out,
    mixer_out,
    gate_up,
    down_weight,
    gain_mixing,
    gain_feed,
    decay_log,
    step_bias,
    skip_gain,
    conv_weight,
    conv_bias,
):
    ctx, dp = lax.axis_size("ctx"), lax.axis_size("dp")
    mine = lax.axis_index("ctx")
    tok_count, width = block_input.shape[1:]
    length = tok_count * ctx
    heads = SSM_HEADS // ctx
    rows = attention_in.shape[0]
    hidden = down_weight.shape[0]
    slabs = entry_slabs(attention_in, mixer_in, step_in, ctx)
    gate_slabs = gate_up.reshape(rows, 2, dp, ctx, hidden).transpose(3, 0, 1, 2, 4)
    gate_slabs = gate_slabs.reshape(ctx, rows, 2 * dp * hidden)
    own_attention = attention_out.shape[0]

    source = block_input.reshape(tok_count, width).astype(jnp.float32)
    cotangent = out_cotangent.reshape(tok_count, width)
    normed_own = rms_scale(source, gain_mixing).astype(jnp.bfloat16)
    outs = jnp.concatenate([attention_out, mixer_out], axis=0)
    normed, segments, entry, feed_slabs, outs = enter(
        normed_own, segment_ids, slabs, gate_slabs, outs
    )
    normed, segments = normed.reshape(length, width), segments.reshape(length)
    entry = entry.reshape(dp * ctx * rows, -1)
    late_cotangent, _ = lax.optimization_barrier((cotangent, segments))
    cotangents = lax.all_gather(late_cotangent, "ctx", axis=0, tiled=True)
    out_rows = jnp.concatenate(
        [outs[:, :own_attention].reshape(-1, width), outs[:, own_attention:].reshape(-1, width)],
        axis=0,
    )

    own = lambda array, at, size: lax.dynamic_slice_in_dim(array, at + mine * size, size, axis=-1)
    conv_own = lambda array: jnp.concatenate(
        [array[:, SSM_INNER:], own(array, 0, heads * SSM_HEAD)], axis=-1
    )
    taps = jnp.pad(conv_own(jnp.concatenate([conv_weight, conv_bias[None]], axis=0)), ((0, 3), (0, 0)))
    head_rows = jnp.stack(
        [own(part, 0, heads) for part in (-jnp.exp(decay_log), step_bias, skip_gain)]
    )
    head_rows = jnp.pad(head_rows, ((0, 5), (0, Layout(heads).steps - heads)))
    keeps = []
    for offset in (1, 2, 3):
        earlier = jnp.concatenate([jnp.full((offset,), -1, segments.dtype), segments[:-offset]])
        keeps.append(earlier == segments)
    nexts = [jnp.pad(keep[k + 1 :], (0, k + 1)) for k, keep in enumerate(keeps)]
    chunk_last = segments.reshape(ctx, tok_count)[:, -1]
    spread = lambda ids: jnp.repeat(ids, tok_count) == segments
    opens = spread(jnp.concatenate([jnp.full((1,), -1, segments.dtype), chunk_last[:-1]]))
    marks = keeps + nexts + [segments, opens, spread(chunk_last)]
    columns = jnp.stack([mark.astype(jnp.float32) for mark in marks], axis=1)
    columns = jnp.pad(columns, ((0, 0), (0, 16 - len(marks))))
    seg_row = segments.astype(jnp.float32).reshape(1, length)
    mixed_out, entry_product, scanned, states, log_total = mix_forward(
        normed, entry, columns, seg_row, taps, head_rows, tok_count
    )
    mixing_out, feed_in, feed_out = sum_and_spread(
        mixed_out, out_rows, (feed_slabs.reshape(ctx * rows, -1), down_weight), 1
    )
    feed_in = feed_in.reshape(dp * ctx * rows, -1)
    feed_out = feed_out.reshape(dp * hidden, width)
    residual = source + mixing_out

    normed_two_own, pull_two = jax.vjp(rms_scale, residual, gain_feed)
    normed_two = gather_tokens(normed_two_own.astype(jnp.bfloat16), 2)
    gate_values = jnp.dot(normed_two, feed_in, preferred_element_type=jnp.float32)
    gate_in, up_in = gate_values[:, : dp * hidden], gate_values[:, dp * hidden :]
    active = (jax.nn.silu(gate_in) * up_in).astype(jnp.bfloat16)
    output_terms = jnp.dot(active, feed_out, preferred_element_type=jnp.float32).astype(jnp.bfloat16)
    active_grad = jnp.dot(cotangents, feed_out.T, preferred_element_type=jnp.float32)
    gate_grad = jnp.concatenate(
        [active_grad * up_in * silu_slope(gate_in), active_grad * jax.nn.silu(gate_in)], axis=1
    ).astype(jnp.bfloat16)
    normed_two_grad, feed_sums, grad_feed_out = sum_and_total(
        gate_grad,
        feed_in,
        (
            across(normed_two, gate_grad).reshape(dp, ctx * rows, -1),
            across(active, cotangents).reshape(dp, hidden, width),
        ),
        3,
    )
    residual_part, grad_gain_feed = pull_two(normed_two_grad)
    residual_grad = cotangent.astype(jnp.float32) + residual_part
    residual_half = gather_tokens(residual_grad.astype(jnp.bfloat16), 4)
    late_terms, _ = lax.optimization_barrier((output_terms, residual_half))
    output_sum = lax.psum_scatter(late_terms, "ctx", scatter_dimension=0, tiled=True)
    output = (residual + output_sum.astype(jnp.float32)).astype(jnp.bfloat16)
    grads, tap_grads, head_grads, out_terms = mix_backward(
        residual_half,
        out_rows,
        mixed_out,
        entry_product,
        scanned,
        states,
        log_total,
        columns,
        seg_row,
        taps,
        head_rows,
        tok_count,
    )
    own_small = jnp.concatenate(
        [grad_gain_feed, tap_grads[:5].reshape(-1), head_grads[:3, :heads].reshape(-1)], axis=0
    )
    own_small = jnp.pad(own_small, (0, -own_small.shape[0] % 1024)).reshape(-1, 128)
    input_grad, grad_attention_in, grad_mixer_in, step_slabs, grad_gate_up, grad_outs, smalls, gains = leave(
        grads,
        entry,
        source,
        residual_grad,
        gain_mixing.reshape(1, width),
        across(normed, grads).reshape(dp, ctx, rows, -1),
        feed_sums.reshape(ctx, rows, -1),
        out_terms,
        own_small,
    )
    grad_step_in = step_slabs[:, :, :heads].transpose(1, 0, 2).reshape(rows, SSM_HEADS)
    smalls = smalls.reshape(ctx, -1)
    tap_width = heads * SSM_HEAD + 2 * STATE
    tap_all = smalls[:, width : width + 5 * tap_width].reshape(ctx, 5, tap_width)
    tap_sums = jnp.concatenate(
        [
            tap_all[:, :, 2 * STATE :].transpose(1, 0, 2).reshape(5, SSM_INNER),
            jnp.sum(tap_all[:, :, : 2 * STATE], axis=0),
        ],
        axis=1,
    )
    head_all = smalls[:, width + 5 * tap_width :][:, : 3 * heads].reshape(ctx, 3, heads)
    head_sums = head_all.transpose(1, 0, 2).reshape(3, SSM_HEADS)
    return (
        output.reshape(block_input.shape),
        input_grad.reshape(block_input.shape),
        grad_attention_in,
        grad_mixer_in,
        grad_step_in,
        grad_outs[:own_attention],
        grad_outs[own_attention:],
        grad_gate_up,
        grad_feed_out.astype(jnp.float32),
        gains.reshape(width),
        jnp.sum(smalls[:, :width], axis=0),
        head_sums[0],
        head_sums[1],
        head_sums[2],
        tap_sums[:4],
        tap_sums[4],
    )


def solution(mesh):
    in_specs = (
        P("dp", "ctx", None),
        P("dp", "ctx"),
        P("dp", "ctx", None),
        P(("dp", "ctx"), None),
        P(("dp", "ctx"), None),
        P(("dp", "ctx"), None),
        P(("dp", "ctx"), None),
        P(("dp", "ctx"), None),
        P(("dp", "ctx"), None),
        P(("dp", "ctx"), None),
        P(),
        P(),
        P(),
        P(),
        P(),
        P(),
        P(),
    )
    out_specs = (
        P("dp", "ctx", None),
        P("dp", "ctx", None),
        P(("dp", "ctx"), None),
        P(("dp", "ctx"), None),
        P(("dp", "ctx"), None),
        P(("dp", "ctx"), None),
        P(("dp", "ctx"), None),
        P(("dp", "ctx"), None),
        P(("dp", "ctx"), None),
        P(),
        P(),
        P(),
        P(),
        P(),
        P(),
        P(),
    )
    sequences = mesh.shape["dp"]

    def choose(*arrays):
        heads = split_heads(mesh.shape["ctx"]) and arrays[0].shape[0] == sequences
        body = split_local if heads else local
        mapped = jax.shard_map(
            body, mesh=mesh, in_specs=in_specs, out_specs=out_specs, check_vma=False
        )
        return mapped(*arrays)

    return choose
```
